32 devices in a mesh: dp: 16 (over z, y, x), dim: 2 (over core).
Axes of the slice: x: 2, y: 2, z: 4, core: 2. Of those that a mesh axis runs over, the one named last changes fastest.
Arguments:
- tokens: bfloat16 [49152, 768], P(('dp', 'dim')), may hold values from -6 to 6
- doc_lengths: int32 [16, 2], P('dp'), may hold values from 1024 to 1820, as said below
- pair_index: int32 [32], P('dp'), may hold values from 0 to 255
- target_bank: bfloat16 [256, 768], P(None, 'dim'), may hold values from -6 to 6
- mixer_in: float32 [1, 768, 2304], P(None, ('dp', 'dim')), may hold values from -0.21875 to 0.21875
- mixer_out: float32 [1, 768, 768], P(None, ('dp', 'dim')), may hold values from -1.75 to 1.75
- expand: float32 [1, 768, 6144], P(None, ('dp', 'dim')), may hold values from -0.21875 to 0.21875
- contract: float32 [1, 3072, 768], P(None, ('dp', 'dim')), may hold values from -0.109375 to 0.109375
- norm_params: float32 [1, 4, 768], P(None, None, ('dp', 'dim')), as said below
- mixer_in_moment: float32 [1, 768, 2304], P(None, ('dp', 'dim')), may hold values from -64 to 64
- mixer_out_moment: float32 [1, 768, 768], P(None, ('dp', 'dim')), may hold values from -64 to 64
- expand_moment: float32 [1, 768, 6144], P(None, ('dp', 'dim')), may hold values from -64 to 64
- contract_moment: float32 [1, 3072, 768], P(None, ('dp', 'dim')), may hold values from -64 to 64
- norm_moment: float32 [1, 4, 768], P(None, None, ('dp', 'dim')), may hold values from -128 to 128
- mixer_in_average: float32 [1, 768, 2304], P(None, ('dp', 'dim')), may hold values from -0.21875 to 0.21875
- mixer_out_average: float32 [1, 768, 768], P(None, ('dp', 'dim')), may hold values from -1.75 to 1.75
- expand_average: float32 [1, 768, 6144], P(None, ('dp', 'dim')), may hold values from -0.21875 to 0.21875
- contract_average: float32 [1, 3072, 768], P(None, ('dp', 'dim')), may hold values from -0.109375 to 0.109375
- norm_average: float32 [1, 4, 768], P(None, None, ('dp', 'dim')), as said below
Outputs:
- embeddings: float32 [32, 768], P('dp', 'dim')
- token_grads: float32 [49152, 768], P(('dp', 'dim'))
- mixer_in_grad: float32 [1, 768, 2304], P(None, ('dp', 'dim'))
- mixer_out_grad: float32 [1, 768, 768], P(None, ('dp', 'dim'))
- expand_grad: float32 [1, 768, 6144], P(None, ('dp', 'dim'))
- contract_grad: float32 [1, 3072, 768], P(None, ('dp', 'dim'))
- norm_grad: float32 [1, 4, 768], P(None, None, ('dp', 'dim'))
- mixer_in_next: float32 [1, 768, 2304], P(None, ('dp', 'dim'))
- mixer_out_next: float32 [1, 768, 768], P(None, ('dp', 'dim'))
- expand_next: float32 [1, 768, 6144], P(None, ('dp', 'dim'))
- contract_next: float32 [1, 3072, 768], P(None, ('dp', 'dim'))
- norm_next: float32 [1, 4, 768], P(None, None, ('dp', 'dim'))
- mixer_in_moment_next: float32 [1, 768, 2304], P(None, ('dp', 'dim'))
- mixer_out_moment_next: float32 [1, 768, 768], P(None, ('dp', 'dim'))
- expand_moment_next: float32 [1, 768, 6144], P(None, ('dp', 'dim'))
- contract_moment_next: float32 [1, 3072, 768], P(None, ('dp', 'dim'))
- norm_moment_next: float32 [1, 4, 768], P(None, None, ('dp', 'dim'))
- mixer_in_average_next: float32 [1, 768, 2304], P(None, ('dp', 'dim'))
- mixer_out_average_next: float32 [1, 768, 768], P(None, ('dp', 'dim'))
- expand_average_next: float32 [1, 768, 6144], P(None, ('dp', 'dim'))
- contract_average_next: float32 [1, 3072, 768], P(None, ('dp', 'dim'))
- norm_average_next: float32 [1, 4, 768], P(None, None, ('dp', 'dim'))
- mixer_in_copy: bfloat16 [1, 768, 2304], P(None, ('dp', 'dim'))
- mixer_out_copy: bfloat16 [1, 768, 768], P(None, ('dp', 'dim'))
- expand_copy: bfloat16 [1, 768, 6144], P(None, ('dp', 'dim'))
- contract_copy: bfloat16 [1, 3072, 768], P(None, ('dp', 'dim'))
- norm_copy: bfloat16 [1, 4, 768], P(None, None, ('dp', 'dim'))
The draws below stay inside these ranges and needn't reach their ends.
Inputs may be any that keep to these rules, and one draw needn't show every extreme that they name: `doc_lengths`: each document of a group holds at least 1024 rows, and a group's documents together hold fewer than 3072 rows. `norm_params`: rows 0 and 2 of each layer are gains, rows 1 and 3 biases. `norm_average`: laid out as norm_params.
All inputs are finite; a program needn't handle non-finite values.
Results may differ from the reference program's by a relative error of at most 0.015.
Values may be sent and summed in bfloat16 or wider, within the bound.
A program may use at most 256 MiB of HBM per device.

```python
import math
import jax
import jax.numpy as jnp
from jax import lax

D = 768
HEAD = 64
FF = 3072
LAYERS = 1
DOCS = 2
BANK = 256
GROUP_TOK = 3072
MINLEN = 1024
GROUPS = 16
DOCS_ALL = 32
TOKENS = 49152
QKV = 2304


def draw_doc_lengths(key, part):
    powers = jax.random.randint(key, (GROUPS, DOCS), 0, 4)
    shares = jnp.left_shift(jnp.ones((GROUPS, DOCS), jnp.int32), powers.astype(jnp.int32))
    first_row = jnp.where(jnp.arange(DOCS) == 0, 8, 1).astype(jnp.int32)
    shares = jnp.concatenate([first_row[None, :], shares[1:]], axis=0)
    spare = GROUP_TOK - DOCS * MINLEN
    extra = spare * (shares - 1) // jnp.sum(shares, axis=1, keepdims=True)
    return (MINLEN + extra).astype(jnp.int32)


def norm_like(key):
    noise = jnp.clip(jax.random.normal(key, (LAYERS, 4, D), jnp.float32), -4.0, 4.0)
    is_gain = (jnp.arange(4) % 2 == 0)[None, :, None]
    return jnp.where(is_gain, 1.0 + 0.1 * noise, 0.05 * noise).astype(jnp.float32)


def draw_norm_params(key, part):
    return norm_like(jax.random.fold_in(key, 1))


def draw_norm_average(key, part):
    return norm_like(jax.random.fold_in(key, 2))


def plant(entries, stream_key, least, high):
    shape = entries.shape
    spot = [jax.random.randint(jax.random.fold_in(stream_key, axis), (), 0, shape[axis]) for axis in range(len(shape))]
    entries = entries.at[tuple(spot)].set(least)
    longest = shape.index(max(shape))
    spot[longest] = (spot[longest] + 1) % shape[longest]
    return entries.at[tuple(spot)].set(high)


def levels(rng, dims, cuts, low, high):
    def one(axis_at, blocks):
        heights = jax.random.uniform(jax.random.fold_in(jax.random.fold_in(rng, 6), axis_at), (blocks,), jnp.float32, low / len(cuts), high / len(cuts))
        return jnp.repeat(jnp.exp(heights), dims[axis_at] // blocks).reshape((-1,) + (1,) * (len(dims) - axis_at - 1))

    loudness = one(*cuts[0])
    for cut in cuts[1:]:
        loudness = loudness * one(*cut)
    return loudness


def bell_draw(rng, extent, width, limit, shards=(), kind=jnp.bfloat16):
    level = levels(rng, extent, shards, -0.22, 0.18) if shards else 1.0
    values = jax.random.normal(rng, extent, jnp.float32) * width * level
    return jnp.minimum(jnp.maximum(values, -limit), limit).astype(kind)


def setup_inputs(seed: int = 0) -> dict:
    arg_keys = jax.random.split(jax.random.key(seed), 20)
    return {
        "tokens": bell_draw(arg_keys[0], (TOKENS, D), 1.0, 6.0, ((0, 32),)),
        "doc_lengths": draw_doc_lengths(jax.random.fold_in(arg_keys[19], 71), 0),
        "pair_index": plant(jax.random.randint(arg_keys[2], (DOCS_ALL,), 0, BANK), jax.random.fold_in(arg_keys[2], 1), 0, BANK - 1).astype(jnp.int32),
        "target_bank": bell_draw(arg_keys[3], (BANK, D), 1.0, 6.0, ((1, 2),)),
        "mixer_in": bell_draw(arg_keys[4], (LAYERS, D, QKV), D ** -0.5, 0.21875, ((1, 32),), jnp.float32),
        "mixer_out": bell_draw(arg_keys[5], (LAYERS, D, D), (D // 64) ** -0.5, 1.75, ((1, 32),), jnp.float32),
        "expand": bell_draw(arg_keys[6], (LAYERS, D, 2 * FF), D ** -0.5, 0.21875, ((1, 32),), jnp.float32),
        "contract": bell_draw(arg_keys[7], (LAYERS, FF, D), FF ** -0.5, 0.109375, ((1, 32),), jnp.float32),
        "norm_params": draw_norm_params(jax.random.fold_in(arg_keys[19], 71), 0),
        "mixer_in_moment": bell_draw(arg_keys[9], (LAYERS, D, QKV), (0.05 * TOKENS ** 0.5), 64.0, ((1, 32),), jnp.float32),
        "mixer_out_moment": bell_draw(arg_keys[10], (LAYERS, D, D), (0.05 * TOKENS ** 0.5), 64.0, ((1, 32),), jnp.float32),
        "expand_moment": bell_draw(arg_keys[11], (LAYERS, D, 2 * FF), (0.05 * TOKENS ** 0.5), 64.0, ((1, 32),), jnp.float32),
        "contract_moment": bell_draw(arg_keys[12], (LAYERS, FF, D), (0.05 * TOKENS ** 0.5), 64.0, ((1, 32),), jnp.float32),
        "norm_moment": bell_draw(arg_keys[13], (LAYERS, 4, D), (0.1 * TOKENS ** 0.5), 128.0, ((2, 32),), jnp.float32),
        "mixer_in_average": bell_draw(arg_keys[14], (LAYERS, D, QKV), D ** -0.5, 0.21875, ((1, 32),), jnp.float32),
        "mixer_out_average": bell_draw(arg_keys[15], (LAYERS, D, D), (D // 64) ** -0.5, 1.75, ((1, 32),), jnp.float32),
        "expand_average": bell_draw(arg_keys[16], (LAYERS, D, 2 * FF), D ** -0.5, 0.21875, ((1, 32),), jnp.float32),
        "contract_average": bell_draw(arg_keys[17], (LAYERS, FF, D), FF ** -0.5, 0.109375, ((1, 32),), jnp.float32),
        "norm_average": draw_norm_average(jax.random.fold_in(arg_keys[19], 71), 0),
    }


NORM_EPSILON = 1e-05
COSINE_EPSILON = 1e-06
MOMENTUM = 0.5
AVERAGE_DECAY = 0.5
PRECISE = lax.Precision.HIGHEST
MASKED = -1e+30

@jax.custom_vjp
def low(v):
    return lax.optimization_barrier(v.astype(jnp.bfloat16)).astype(jnp.float32)

@jax.custom_vjp
def low_back(v):
    return v

def low_keep(v):
    return (low(v), None)

def low_pass(kept, grad):
    return (grad,)

def back_keep(v):
    return (v, None)

def back_low(kept, grad):
    return (low(grad),)
low.defvjp(low_keep, low_pass)
low_back.defvjp(back_keep, back_low)

def matmul_exact(left_op, right_op):
    return jnp.dot(left_op, right_op, precision=PRECISE, preferred_element_type=jnp.float32)

def rotate(values, cosines, sines):
    row_count = values.shape[0]
    shaped = values.reshape(row_count, -1, 2, HEAD // 2)
    former = shaped[:, :, 0, :]
    latter = shaped[:, :, 1, :]
    cosine_b = cosines[:, None, :]
    sine_b = sines[:, None, :]
    turned = jnp.stack([former * cosine_b - latter * sine_b, latter * cosine_b + former * sine_b], axis=2)
    return turned.reshape(values.shape)

def normalize(summed, gain_vec, bias_vec):
    centred = summed - lax.optimization_barrier(jnp.mean(summed, axis=1, keepdims=True))
    scaling = lax.rsqrt(lax.optimization_barrier(jnp.mean(centred * centred, axis=1, keepdims=True)) + NORM_EPSILON)
    return centred * scaling * gain_vec + bias_vec

def attend(q_rot, k_rot, values, segment):
    same_doc = segment[:, None] == segment[None, :]

    def one_head(head_pos):
        offset = head_pos * HEAD
        query_part = lax.dynamic_slice_in_dim(q_rot, offset, HEAD, 1)
        key_part = lax.dynamic_slice_in_dim(k_rot, offset, HEAD, 1)
        value_part = lax.dynamic_slice_in_dim(values, offset, HEAD, 1)
        scores = matmul_exact(query_part, key_part.T) * 0.125
        scores = low_back(jnp.where(same_doc, scores, MASKED))
        row_max = lax.optimization_barrier(jnp.max(scores, axis=1, keepdims=True))
        exponent = jnp.exp(scores - row_max)
        attn_probs = exponent / lax.optimization_barrier(jnp.sum(exponent, axis=1, keepdims=True))
        return matmul_exact(low(attn_probs), value_part)
    outputs = lax.map(jax.checkpoint(one_head), jnp.arange(D // HEAD, dtype=jnp.int32))
    return outputs.transpose(1, 0, 2).reshape(q_rot.shape[0], D)

def layer_apply(stream, params, segment, cosines, sines):
    w_mix, w_out, w_exp, w_con, w_norm = params
    x_low = low(stream)
    mixed = low_back(matmul_exact(x_low, w_mix))
    q_rot = low(rotate(mixed[:, 0:D], cosines, sines))
    k_rot = low(rotate(mixed[:, D:2 * D], cosines, sines))
    v_low = low(mixed[:, 2 * D:3 * D])
    attended = attend(q_rot, k_rot, v_low, segment)
    att_low = low(low_back(attended))
    branch = low_back(matmul_exact(att_low, w_out))
    normed = normalize(stream + branch, w_norm[0], w_norm[1])
    gate_up = low_back(matmul_exact(low(normed), w_exp))
    hidden = low(jax.nn.silu(gate_up[:, 0:FF]) * gate_up[:, FF:2 * FF])
    second = low_back(matmul_exact(hidden, w_con))
    return normalize(normed + second, w_norm[2], w_norm[3])

def advance(weight, moment, average, grad_in, rate):
    moment_next = MOMENTUM * moment + grad_in
    weight_next = weight - rate * (grad_in + MOMENTUM * moment_next)
    average_next = AVERAGE_DECAY * average + (1.0 - AVERAGE_DECAY) * weight_next
    return (weight_next, moment_next, average_next, weight_next.astype(jnp.bfloat16))

def reference(tokens, doc_lengths, pair_index, target_bank, mixer_in, mixer_out, expand, contract, norm_params, mixer_in_moment, mixer_out_moment, expand_moment, contract_moment, norm_moment, mixer_in_average, mixer_out_average, expand_average, contract_average, norm_average):
    doc_ends = jnp.cumsum(doc_lengths, axis=1)
    doc_starts = doc_ends - doc_lengths
    row_ids = jnp.arange(GROUP_TOK, dtype=jnp.int32)
    segment = lax.optimization_barrier(jnp.sum((row_ids[None, :, None] >= doc_ends[:, None, :]).astype(jnp.int32), axis=2))
    first_rows = jnp.concatenate([doc_starts, doc_ends[:, -1:]], axis=1)
    segment_ids = jnp.arange(DOCS + 1, dtype=jnp.int32)
    row_begin = lax.optimization_barrier(jnp.sum(jnp.where(segment[:, :, None] == segment_ids[None, None, :], first_rows[:, None, :], 0), axis=2))
    frequency = jnp.power(1000.0, -jnp.arange(0, HEAD, 2).astype(jnp.float32) / HEAD)
    angles = (row_ids[None, :] - row_begin).astype(jnp.float32)[:, :, None] * frequency[None, None, :]
    cosines = jnp.cos(angles)
    sines = jnp.sin(angles)
    member = (segment[:, :, None] == jnp.arange(DOCS, dtype=jnp.int32)[None, None, :]).astype(jnp.float32)
    length_f = doc_lengths.astype(jnp.float32)
    targets = target_bank.astype(jnp.float32)[pair_index]
    cuts = jnp.array([D // 12, D // 6, D // 3, 2 * D // 3, D], dtype=jnp.int32)
    masks = (jnp.arange(D, dtype=jnp.int32)[None, :] < cuts[:, None]).astype(jnp.float32)

    def network(stream, w_mix, w_out, w_exp, w_con, w_norm):
        params = (low(w_mix), low(w_out), low(w_exp), low(w_con), low(w_norm))

        def group(pack):
            group_stream, group_seg, group_cos, group_sin = pack
            for layer_pos in range(LAYERS):
                layer_params = tuple((p[layer_pos] for p in params))
                group_stream = layer_apply(group_stream, layer_params, group_seg, group_cos, group_sin)
            return group_stream
        final = lax.map(jax.checkpoint(group), (stream.reshape(GROUPS, GROUP_TOK, D), segment, cosines, sines))
        sums = jnp.einsum('gtn,gtf->gnf', member, final, precision=PRECISE)
        pooled = (sums / length_f[:, :, None]).reshape(GROUPS * DOCS, D)
        cross = matmul_exact(pooled * targets, masks.T)
        own = matmul_exact(pooled * pooled, masks.T)
        other = matmul_exact(targets * targets, masks.T)
        cosine = cross * lax.rsqrt(own + COSINE_EPSILON) * lax.rsqrt(other + COSINE_EPSILON)
        loss = jnp.sum(length_f.reshape(-1)[:, None] * (1.0 - cosine))
        return (loss, pooled)
    loss, pull, embeddings = jax.vjp(network, tokens.astype(jnp.float32), mixer_in, mixer_out, expand, contract, norm_params, has_aux=True)
    grads = pull(jnp.ones_like(loss))
    token_grads = grads[0].reshape(TOKENS, D)
    matrix_rate = 1.0 / math.sqrt(TOKENS)
    norm_rate = 0.3 / math.sqrt(TOKENS)
    weights = (mixer_in, mixer_out, expand, contract, norm_params)
    moments = (mixer_in_moment, mixer_out_moment, expand_moment, contract_moment, norm_moment)
    averages = (mixer_in_average, mixer_out_average, expand_average, contract_average, norm_average)
    rates = (matrix_rate, matrix_rate, matrix_rate, matrix_rate, norm_rate)
    results = [advance(weights[k], moments[k], averages[k], grads[k + 1], rates[k]) for k in range(5)]
    return (embeddings, token_grads, grads[1], grads[2], grads[3], grads[4], grads[5], results[0][0], results[1][0], results[2][0], results[3][0], results[4][0], results[0][1], results[1][1], results[2][1], results[3][1], results[4][1], results[0][2], results[1][2], results[2][2], results[3][2], results[4][2], results[0][3], results[1][3], results[2][3], results[3][3], results[4][3])
```

```python
import math

import jax
import jax.numpy as jnp
from jax import lax
from jax.experimental import pallas as pl
from jax.experimental.pallas import tpu as pltpu
from jax.sharding import PartitionSpec as P

HEAD = 64


NORM_EPSILON = 1e-05
COSINE_EPSILON = 1e-06
MOMENTUM = 0.5
AVERAGE_DECAY = 0.5
PRECISE = lax.Precision.HIGHEST
MASKED = -1e30


def matmul(left_op, right_op):
    return jnp.dot(left_op, right_op, preferred_element_type=jnp.float32)


def matmul_exact(left_op, right_op):
    return jnp.dot(left_op, right_op, precision=PRECISE, preferred_element_type=jnp.float32)


def inner_rows(left_op, right_op):
    return lax.dot_general(
        left_op, right_op, (((0,), (0,)), ((), ())), preferred_element_type=jnp.float32
    )


def inner_cols(left_op, right_op):
    return lax.dot_general(
        left_op, right_op, (((1,), (1,)), ((), ())), preferred_element_type=jnp.float32
    )


def rotate(values, cosines, sines):
    row_count = values.shape[0]
    shaped = values.reshape(row_count, -1, 2, HEAD // 2)
    former = shaped[:, :, 0, :]
    latter = shaped[:, :, 1, :]
    cosine_b = cosines[:, None, :]
    sine_b = sines[:, None, :]
    turned = jnp.stack(
        [former * cosine_b - latter * sine_b, latter * cosine_b + former * sine_b], axis=2
    )
    return turned.reshape(values.shape)


def rotate_back(grads_in, cosines, sines):
    row_count = grads_in.shape[0]
    shaped = grads_in.reshape(row_count, -1, 2, HEAD // 2)
    former = shaped[:, :, 0, :]
    latter = shaped[:, :, 1, :]
    cosine_b = cosines[:, None, :]
    sine_b = sines[:, None, :]
    turned = jnp.stack(
        [former * cosine_b + latter * sine_b, latter * cosine_b - former * sine_b], axis=2
    )
    return turned.reshape(grads_in.shape)


def normalize(summed, gain_vec, bias_vec):
    centred = summed - jnp.mean(summed, axis=1, keepdims=True)
    scaling = lax.rsqrt(jnp.mean(centred * centred, axis=1, keepdims=True) + NORM_EPSILON)
    return centred * scaling * gain_vec + bias_vec


def normalize_back(grad_in, summed, gain_vec):
    centred = summed - jnp.mean(summed, axis=1, keepdims=True)
    scaling = lax.rsqrt(jnp.mean(centred * centred, axis=1, keepdims=True) + NORM_EPSILON)
    unit = centred * scaling
    grad_unit = grad_in * gain_vec
    grad_sum = scaling * (
        grad_unit
        - jnp.mean(grad_unit, axis=1, keepdims=True)
        - unit * jnp.mean(grad_unit * unit, axis=1, keepdims=True)
    )
    return (grad_sum, jnp.sum(grad_in * unit, axis=0), jnp.sum(grad_in, axis=0))


def flatten(stacked):
    return stacked.transpose(1, 0, 2).reshape(stacked.shape[1], -1)


def attend(q_rot, all_keys, all_values, same_doc):
    head_count = q_rot.shape[1] // HEAD

    def one_head(head_pos):
        offset = head_pos * HEAD
        query_part = lax.dynamic_slice_in_dim(q_rot, offset, HEAD, 1)
        key_part = lax.dynamic_slice_in_dim(all_keys, offset, HEAD, 1)
        value_part = lax.dynamic_slice_in_dim(all_values, offset, HEAD, 1)
        scores = jnp.where(same_doc, inner_cols(query_part, key_part) * 0.125, MASKED)
        row_max = jnp.max(scores, axis=1, keepdims=True)
        exponent = jnp.exp(scores - row_max)
        row_total = jnp.sum(exponent, axis=1, keepdims=True)
        attn_probs = (exponent / row_total).astype(jnp.bfloat16)
        return (matmul(attn_probs, value_part), (row_max + jnp.log(row_total))[:, 0])

    outputs, log_totals = lax.map(one_head, jnp.arange(head_count, dtype=jnp.int32))
    return (flatten(outputs), log_totals)


def attend_back(q_rot, all_keys, all_values, same_doc, grad_out, log_totals):
    head_count = q_rot.shape[1] // HEAD

    def one_head(pack):
        head_pos, log_total = pack
        offset = head_pos * HEAD
        query_part = lax.dynamic_slice_in_dim(q_rot, offset, HEAD, 1)
        key_part = lax.dynamic_slice_in_dim(all_keys, offset, HEAD, 1)
        value_part = lax.dynamic_slice_in_dim(all_values, offset, HEAD, 1)
        grad_part = lax.dynamic_slice_in_dim(grad_out, offset, HEAD, 1)
        scores = jnp.where(same_doc, inner_cols(query_part, key_part) * 0.125, MASKED)
        attn_probs = jnp.exp(scores - log_total[:, None])
        grad_probs = inner_cols(grad_part, value_part)
        row_dot = jnp.sum(attn_probs * grad_probs, axis=1, keepdims=True)
        grad_scores = (attn_probs * (grad_probs - row_dot)).astype(jnp.bfloat16)
        grad_query = matmul(grad_scores, key_part) * 0.125
        grad_key = inner_rows(grad_scores, query_part) * 0.125
        grad_value = inner_rows(attn_probs.astype(jnp.bfloat16), grad_part)
        return (grad_query, grad_key, grad_value)

    mapped = lax.map(one_head, (jnp.arange(head_count, dtype=jnp.int32), log_totals))
    return (flatten(mapped[0]), flatten(mapped[1]), flatten(mapped[2]))


def advance(weight, moment, average, grad_in, rate):
    moment_next = MOMENTUM * moment + grad_in
    weight_next = weight - rate * (grad_in + MOMENTUM * moment_next)
    average_next = AVERAGE_DECAY * average + (1.0 - AVERAGE_DECAY) * weight_next
    return (weight_next, moment_next, average_next, weight_next.astype(jnp.bfloat16))


def body_general(
    tokens,
    doc_lengths,
    pair_index,
    target_bank,
    mixer_in,
    mixer_out,
    expand,
    contract,
    norm_params,
    mixer_in_moment,
    mixer_out_moment,
    expand_moment,
    contract_moment,
    norm_moment,
    mixer_in_average,
    mixer_out_average,
    expand_average,
    contract_average,
    norm_average,
):
    local_rows, model_width = tokens.shape
    slices = lax.axis_size("dim")
    group_rows = local_rows * slices
    position = lax.axis_index("dim")
    layer_count = mixer_in.shape[0]
    doc_count = doc_lengths.shape[1]
    lengths = doc_lengths[0]
    doc_ends = jnp.cumsum(lengths)
    doc_starts = doc_ends - lengths
    row_ids = position * local_rows + jnp.arange(local_rows, dtype=jnp.int32)
    key_ids = jnp.arange(group_rows, dtype=jnp.int32)
    seg_rows = jnp.sum((row_ids[:, None] >= doc_ends[None, :]).astype(jnp.int32), axis=1)
    seg_keys = jnp.sum((key_ids[:, None] >= doc_ends[None, :]).astype(jnp.int32), axis=1)
    first_rows = jnp.concatenate([doc_starts, doc_ends[-1:]])
    segment_ids = jnp.arange(doc_count + 1, dtype=jnp.int32)
    row_begin = jnp.sum(
        jnp.where(seg_rows[:, None] == segment_ids[None, :], first_rows[None, :], 0), axis=1
    )
    frequency = jnp.power(1000.0, -jnp.arange(0, HEAD, 2).astype(jnp.float32) / HEAD)
    angles = (row_ids - row_begin).astype(jnp.float32)[:, None] * frequency[None, :]
    cosines = jnp.cos(angles)
    sines = jnp.sin(angles)
    same_doc = seg_rows[:, None] == seg_keys[None, :]
    stream = tokens.astype(jnp.float32)
    layer_pos = 0
    layer_weights = (
        lax.all_gather(mixer_in[layer_pos].astype(jnp.bfloat16), ("dp", "dim"), axis=0, tiled=True),
        lax.all_gather(
            mixer_out[layer_pos].astype(jnp.bfloat16), ("dp", "dim"), axis=0, tiled=True
        ),
        lax.all_gather(expand[layer_pos].astype(jnp.bfloat16), ("dp", "dim"), axis=0, tiled=True),
        lax.all_gather(contract[layer_pos].astype(jnp.bfloat16), ("dp", "dim"), axis=0, tiled=True),
        lax.all_gather(
            norm_params[layer_pos].astype(jnp.bfloat16), ("dp", "dim"), axis=1, tiled=True
        ),
    )
    w_mix, w_out, w_exp, w_con, w_norm = layer_weights
    norm_gains = w_norm.astype(jnp.float32)
    x_low = stream.astype(jnp.bfloat16)
    mixed = matmul(x_low, w_mix)
    q_rot = rotate(mixed[:, 0:model_width], cosines, sines).astype(jnp.bfloat16)
    k_rot = rotate(mixed[:, model_width : 2 * model_width], cosines, sines).astype(jnp.bfloat16)
    v_low = mixed[:, 2 * model_width : 3 * model_width].astype(jnp.bfloat16)
    all_keys = lax.all_gather(k_rot, "dim", axis=0, tiled=True)
    all_values = lax.all_gather(v_low, "dim", axis=0, tiled=True)
    attended, log_totals = attend(q_rot, all_keys, all_values, same_doc)
    att_low = attended.astype(jnp.bfloat16)
    first_sum = stream + matmul(att_low, w_out)
    normed = normalize(first_sum, norm_gains[0], norm_gains[1])
    y_low = normed.astype(jnp.bfloat16)
    gate_up = matmul(y_low, w_exp)
    half = gate_up.shape[1] // 2
    hidden = (jax.nn.silu(gate_up[:, 0:half]) * gate_up[:, half : 2 * half]).astype(jnp.bfloat16)
    second_sum = normed + matmul(hidden, w_con)
    saved = [
        (
            stream,
            layer_weights,
            q_rot,
            k_rot,
            v_low,
            all_keys,
            all_values,
            log_totals,
            attended,
            att_low,
            first_sum,
            normed,
            y_low,
            gate_up,
            hidden,
            second_sum,
        )
    ]
    stream = normalize(second_sum, norm_gains[2], norm_gains[3])
    member = (seg_rows[None, :] == jnp.arange(doc_count, dtype=jnp.int32)[:, None]).astype(
        jnp.float32
    )
    partial_value = matmul_exact(member, stream)
    pooled = lax.psum_scatter(partial_value, "dim", scatter_dimension=1, tiled=True)
    length_f = lengths.astype(jnp.float32)
    embeddings = pooled / length_f[:, None]
    share = embeddings.shape[1]
    pick = (
        pair_index[:, None] == jnp.arange(target_bank.shape[0], dtype=jnp.int32)[None, :]
    ).astype(jnp.bfloat16)
    targets = matmul(pick, target_bank)
    feature_ids = position * share + jnp.arange(share, dtype=jnp.int32)
    cuts = jnp.array(
        [model_width // 12, model_width // 6, model_width // 3, 2 * model_width // 3, model_width],
        dtype=jnp.int32,
    )
    masks = (feature_ids[None, :] < cuts[:, None]).astype(jnp.float32)
    cross = matmul_exact(embeddings * targets, masks.T)
    own = matmul_exact(embeddings * embeddings, masks.T)
    other = matmul_exact(targets * targets, masks.T)
    cross, own, other = lax.psum((cross, own, other), "dim")
    own_root = lax.rsqrt(own + COSINE_EPSILON)
    other_root = lax.rsqrt(other + COSINE_EPSILON)
    cosine = cross * own_root * other_root
    coef_target = -length_f[:, None] * own_root * other_root
    coef_self = length_f[:, None] * cosine * own_root * own_root
    grad_emb = (
        matmul_exact(coef_target, masks) * targets + matmul_exact(coef_self, masks) * embeddings
    )
    grad_full = lax.all_gather(grad_emb, "dim", axis=1, tiled=True)
    spread_rows = member / length_f[:, None]
    grad_stream = lax.dot_general(
        spread_rows,
        grad_full,
        (((0,), (0,)), ((), ())),
        precision=PRECISE,
        preferred_element_type=jnp.float32,
    )
    grad_list = [None] * layer_count
    for layer_pos in reversed(range(layer_count)):
        (
            layer_input,
            layer_weights,
            q_rot,
            k_rot,
            v_low,
            all_keys,
            all_values,
            log_totals,
            attended,
            att_low,
            first_sum,
            normed,
            y_low,
            gate_up,
            hidden,
            second_sum,
        ) = saved[layer_pos]
        w_mix = lax.all_gather(
            mixer_in[layer_pos].astype(jnp.bfloat16), ("dp", "dim"), axis=0, tiled=True
        )
        w_out = lax.all_gather(
            mixer_out[layer_pos].astype(jnp.bfloat16), ("dp", "dim"), axis=0, tiled=True
        )
        w_exp = lax.all_gather(
            expand[layer_pos].astype(jnp.bfloat16), ("dp", "dim"), axis=0, tiled=True
        )
        w_con = lax.all_gather(
            contract[layer_pos].astype(jnp.bfloat16), ("dp", "dim"), axis=0, tiled=True
        )
        w_norm = lax.all_gather(
            norm_params[layer_pos].astype(jnp.bfloat16), ("dp", "dim"), axis=1, tiled=True
        )
        norm_gains = w_norm.astype(jnp.float32)
        grad_second, grad_gain2, grad_bias2 = normalize_back(grad_stream, second_sum, norm_gains[2])
        grad_m_low = grad_second.astype(jnp.bfloat16)
        grad_con = inner_rows(hidden, grad_m_low)
        grad_hidden = inner_cols(grad_m_low, w_con)
        half = gate_up.shape[1] // 2
        gate_part = gate_up[:, 0:half]
        up_part = gate_up[:, half : 2 * half]
        sigmoid_gate = jax.nn.sigmoid(gate_part)
        activated = gate_part * sigmoid_gate
        grad_gate = grad_hidden * up_part * sigmoid_gate * (1.0 + gate_part * (1.0 - sigmoid_gate))
        grad_up = grad_hidden * activated
        grad_both = jnp.concatenate([grad_gate, grad_up], axis=1).astype(jnp.bfloat16)
        grad_exp = inner_rows(y_low, grad_both)
        grad_normed = grad_second + inner_cols(grad_both, w_exp)
        grad_first, grad_gain1, grad_bias1 = normalize_back(grad_normed, first_sum, norm_gains[0])
        grad_a_low = grad_first.astype(jnp.bfloat16)
        grad_out = inner_rows(att_low, grad_a_low)
        grad_attended = inner_cols(grad_a_low, w_out).astype(jnp.bfloat16)
        keys_back, values_back = (
            lax.all_gather(k_rot, "dim", axis=0, tiled=True),
            lax.all_gather(v_low, "dim", axis=0, tiled=True),
        )
        grad_query, grad_key_all, grad_value_all = attend_back(
            q_rot, keys_back, values_back, same_doc, grad_attended, log_totals
        )
        grad_kv = lax.psum_scatter(
            jnp.concatenate([grad_key_all, grad_value_all], axis=1).astype(jnp.bfloat16),
            "dim",
            scatter_dimension=0,
            tiled=True,
        ).astype(jnp.float32)
        grad_mixed = jnp.concatenate(
            [
                rotate_back(grad_query, cosines, sines),
                rotate_back(grad_kv[:, 0:model_width], cosines, sines),
                grad_kv[:, model_width : 2 * model_width],
            ],
            axis=1,
        ).astype(jnp.bfloat16)
        x_low = layer_input.astype(jnp.bfloat16)
        grad_mix = inner_rows(x_low, grad_mixed)
        grad_stream = grad_first + inner_cols(grad_mixed, w_mix)
        grad_norm = jnp.stack([grad_gain1, grad_bias1, grad_gain2, grad_bias2])
        grad_list[layer_pos] = (
            lax.psum_scatter(grad_mix, ("dp", "dim"), scatter_dimension=0, tiled=True),
            lax.psum_scatter(grad_out, ("dp", "dim"), scatter_dimension=0, tiled=True),
            lax.psum_scatter(grad_exp, ("dp", "dim"), scatter_dimension=0, tiled=True),
            lax.psum_scatter(grad_con, ("dp", "dim"), scatter_dimension=0, tiled=True),
            lax.psum_scatter(grad_norm, ("dp", "dim"), scatter_dimension=1, tiled=True),
        )
    total_rows = group_rows * lax.axis_size("dp")
    matrix_rate = 1.0 / math.sqrt(total_rows)
    norm_rate = 0.3 / math.sqrt(total_rows)
    grads = [jnp.stack([grad_list[0][kind]]) for kind in range(5)]
    weights = (mixer_in, mixer_out, expand, contract, norm_params)
    moments = (mixer_in_moment, mixer_out_moment, expand_moment, contract_moment, norm_moment)
    averages = (mixer_in_average, mixer_out_average, expand_average, contract_average, norm_average)
    rates = (matrix_rate, matrix_rate, matrix_rate, matrix_rate, norm_rate)
    results = [
        advance(weights[kind], moments[kind], averages[kind], grads[kind], rates[kind])
        for kind in range(5)
    ]
    return (
        embeddings,
        grad_stream,
        grads[0],
        grads[1],
        grads[2],
        grads[3],
        grads[4],
        results[0][0],
        results[1][0],
        results[2][0],
        results[3][0],
        results[4][0],
        results[0][1],
        results[1][1],
        results[2][1],
        results[3][1],
        results[4][1],
        results[0][2],
        results[1][2],
        results[2][2],
        results[3][2],
        results[4][2],
        results[0][3],
        results[1][3],
        results[2][3],
        results[3][3],
        results[4][3],
    )


NEG=-1e30
BQ=256
BK=512
F32=jnp.float32
BF=jnp.bfloat16

def nt(a,b): return lax.dot_general(a,b,(((1,),(1,)),((),())),preferred_element_type=F32)
def nn(a,b): return jnp.dot(a,b,preferred_element_type=F32)

def fill_masks(e0,e1,kaug,q0,q1,rows,pad):
    r=lax.broadcasted_iota(jnp.int32,(rows+pad,128),0)
    l=lax.broadcasted_iota(jnp.int32,(rows+pad,128),1)
    seg=(r>=e0).astype(jnp.int32)+(r>=e1).astype(jnp.int32)
    kaug[:,128:256]=jnp.where((l<3)&(l!=seg),NEG,0.0).astype(BF)
    qm=jnp.where(l==seg,1.0,0.0).astype(BF)[0:rows]
    q0[:,128:256]=qm
    q1[:,128:256]=qm

def key_range(i,e0,e1):
    first=i*BQ
    last=jnp.minimum(first+BQ,e1)-1
    lo=jnp.where(first>=e0,e0,0)
    hi=jnp.where(last>=e0,e1,e0)
    base=(lo//128)*128
    return pl.multiple_of(base,128),(hi-base+BK-1)//BK

def fwd_kernel(ctl,qo,ko,vo,qr,kr,vr,oo,ox,lse,kaug,q0,q1,vt):
    rows=kaug.shape[0]-BK
    half=rows//2
    pos,e0,e1=ctl[0],ctl[1],ctl[2]
    p=pl.program_id(0)
    @pl.when(p==0)
    def _():
        fill_masks(e0,e1,kaug,q0,q1,rows,BK)
        kaug[rows:,0:128]=jnp.zeros((BK,128),BF)
        vt[:,:]=jnp.where(lax.broadcasted_iota(jnp.int32,vt.shape,0)%80>=64,1.0,0.0).astype(BF)
    lane=lax.broadcasted_iota(jnp.int32,(half,128),1)
    for own,(q,k,v) in ((True,(qo,ko,vo)),(False,(qr,kr,vr))):
        at=pl.multiple_of((pos if own else 1-pos)*half,half)
        scaled=q[...]*jnp.asarray(0.125,BF)
        zero=jnp.zeros_like(scaled)
        q0[pl.ds(at,half),0:128]=jnp.where(lane<64,scaled,zero)
        q1[pl.ds(at,half),0:128]=jnp.where(lane<64,zero,scaled)
        kaug[pl.ds(at,half),0:128]=k[...]
        turned=v[...].T
        vt[0:64,pl.ds(at,half)]=turned[0:64]
        vt[80:144,pl.ds(at,half)]=turned[64:128]
    def qblock(i,_):
        r0=pl.multiple_of(i*BQ,BQ)
        base,count=key_range(i,e0,e1)
        qs=(q0[pl.ds(r0,BQ),:],q1[pl.ds(r0,BQ),:])
        def step(j,carry):
            k0=pl.multiple_of(base+j*BK,128)
            kb=kaug[pl.ds(k0,BK),:]
            out=[]
            for h in range(2):
                m,acc=carry[h]
                st=nt(kb,qs[h])
                mn=jnp.maximum(m,jnp.max(st,axis=0,keepdims=True))
                pt=jnp.exp(st-mn).astype(BF)
                acc=acc*jnp.exp(m-mn)+nn(vt[80*h:80*h+80,pl.ds(k0,BK)],pt)
                out.append((mn,acc))
            return tuple(out)
        init=(jnp.full((1,BQ),-jnp.inf,F32),jnp.zeros((80,BQ),F32))
        res=lax.fori_loop(0,count,step,(init,init))
        outs=[]
        for h in range(2):
            m,acc=res[h]
            l=acc[64:65]
            outs.append(acc[0:64]/l)
            lse[0,h:h+1,pl.ds(r0,BQ)]=m+jnp.log(l)
        ob=jnp.concatenate(outs,axis=0).T.astype(BF)
        put(i,ob)
        return 0
    def put(i,ob):
        local=i*BQ-pos*half
        @pl.when((local>=0)&(local<half))
        def _(): oo[pl.ds(pl.multiple_of(local,BQ),BQ),:]=ob
        @pl.when((local<0)|(local>=half))
        def _(): ox[pl.ds(pl.multiple_of(i*BQ-(1-pos)*half,BQ),BQ),:]=ob
    used=(e1+BQ-1)//BQ
    lax.fori_loop(0,used,qblock,0)
    def blank(i,_):
        r0=pl.multiple_of(i*BQ,BQ)
        lse[0,:,pl.ds(r0,BQ)]=jnp.zeros((8,BQ),F32)
        put(i,jnp.zeros((BQ,128),BF))
        return 0
    lax.fori_loop(used,rows//BQ,blank,0)

def attend_fwd(ctl,own,recv):
    half,width=own.shape
    pairs=width//384
    rows=2*half
    sp=[pl.BlockSpec((half,128),(lambda p,c,s=s:(0,s*pairs+p))) for s in range(3)]
    outw=pairs*128
    return pl.pallas_call(fwd_kernel,
        grid_spec=pltpu.PrefetchScalarGridSpec(num_scalar_prefetch=1,grid=(pairs,),
          in_specs=sp+sp,
          out_specs=[pl.BlockSpec((half,128),lambda p,c:(0,p))]*2+[pl.BlockSpec((1,8,rows),lambda p,c:(p,0,0))],
          scratch_shapes=[pltpu.VMEM((rows+BK,256),BF),pltpu.VMEM((rows,256),BF),pltpu.VMEM((rows,256),BF),pltpu.VMEM((160,rows+BK),BF)]),
        out_shape=[jax.ShapeDtypeStruct((half,outw),BF)]*2+[jax.ShapeDtypeStruct((pairs,8,rows),F32)],
        compiler_params=pltpu.CompilerParams(vmem_limit_bytes=56<<20,dimension_semantics=("arbitrary",)),
        cost_estimate=pl.CostEstimate(flops=4*rows*rows*64*2*pairs//2,bytes_accessed=10*half*width,transcendentals=rows*rows*pairs),
        name="attend_fwd",
    )(ctl,own,own,own,recv,recv,recv)

def bwd_kernel(ctl,qo,ko,vo,qr,kr,vr,do_o,do_r,oo,ox,lse,cos,sin,go,gx,kaug,q0,q1,vs,d0,d1,kt,delta,dk,dv):
    rows=kaug.shape[0]-BK
    half=rows//2
    pos,e0,e1=ctl[0],ctl[1],ctl[2]
    p=pl.program_id(0)
    @pl.when(p==0)
    def _():
        fill_masks(e0,e1,kaug,q0,q1,rows,BK)
        kaug[rows:,0:128]=jnp.zeros((BK,128),BF)
        vs[rows:,:]=jnp.zeros((BK,128),BF)
        kt[:,rows:]=jnp.zeros((128,BK),BF)
    lane=lax.broadcasted_iota(jnp.int32,(half,128),1)
    pick_r=lax.broadcasted_iota(jnp.int32,(16,128),0)
    pick_l=lax.broadcasted_iota(jnp.int32,(16,128),1)
    pick=jnp.where(pick_l//64==pick_r,1.0,0.0).astype(BF)
    for own,(q,k,v,d,o) in ((True,(qo,ko,vo,do_o,oo)),(False,(qr,kr,vr,do_r,ox))):
        at=pl.multiple_of((pos if own else 1-pos)*half,half)
        scaled=q[...]*jnp.asarray(0.125,BF)
        zero=jnp.zeros_like(scaled)
        q0[pl.ds(at,half),0:128]=jnp.where(lane<64,scaled,zero)
        q1[pl.ds(at,half),0:128]=jnp.where(lane<64,zero,scaled)
        kb=k[...]
        kaug[pl.ds(at,half),0:128]=kb
        kt[:,pl.ds(at,half)]=kb.T
        vs[pl.ds(at,half),:]=v[...]
        db=d[...]
        d0[pl.ds(at,half),:]=jnp.where(lane<64,db,zero)
        d1[pl.ds(at,half),:]=jnp.where(lane<64,zero,db)
        prod=db.astype(F32)*o[...].astype(F32)
        hi=prod.astype(BF)
        lo=(prod-hi.astype(F32)).astype(BF)
        delta[:,pl.ds(at,half)]=nt(pick,hi)+nt(pick,lo)
    dk[...]=jnp.zeros_like(dk)
    dv[...]=jnp.zeros_like(dv)
    def spread(i,col,val):
        local=i*BQ-pos*half
        @pl.when((local>=0)&(local<half))
        def _(): go[pl.ds(pl.multiple_of(local,BQ),BQ),col*128:(col+1)*128] = val
        @pl.when((local<0)|(local>=half))
        def _(): gx[pl.ds(pl.multiple_of(i*BQ-(1-pos)*half,BQ),BQ),col*128:(col+1)*128] = val
    def unturn(x,r0):
        ln=lax.broadcasted_iota(jnp.int32,x.shape,1)
        swapped=jnp.where((ln%64)<32,pltpu.roll(x,96,1),pltpu.roll(x,32,1))
        return x*cos[pl.ds(r0,BQ),:]-swapped*sin[pl.ds(r0,BQ),:]
    def qblock(i,_):
        r0=pl.multiple_of(i*BQ,BQ)
        base,count=key_range(i,e0,e1)
        qs=(q0[pl.ds(r0,BQ),:],q1[pl.ds(r0,BQ),:])
        ds_=(d0[pl.ds(r0,BQ),:],d1[pl.ds(r0,BQ),:])
        ls=[lse[0,h:h+1,pl.ds(r0,BQ)] for h in range(2)]
        de=[delta[h:h+1,pl.ds(r0,BQ)] for h in range(2)]
        def step(j,carry):
            k0=pl.multiple_of(base+j*BK,128)
            kb=kaug[pl.ds(k0,BK),:]
            vb=vs[pl.ds(k0,BK),:]
            out=[]
            dva=dv[pl.ds(k0,BK),:]
            dka=dk[pl.ds(k0,BK),:]
            for h in range(2):
                st=nt(kb,qs[h])
                pt=jnp.exp(st-ls[h])
                dpt=nt(vb,ds_[h])
                dst=(pt*(dpt-de[h])).astype(BF)
                dva=dva+nn(pt.astype(BF),ds_[h])
                dka=dka+nn(dst,qs[h][:,0:128])
                out.append(carry[h]+nn(kt[64*h:64*h+64,pl.ds(k0,BK)],dst))
            dv[pl.ds(k0,BK),:]=dva
            dk[pl.ds(k0,BK),:]=dka
            return tuple(out)
        init=jnp.zeros((64,BQ),F32)
        res=lax.fori_loop(0,count,step,(init,init))
        dq=jnp.concatenate(res,axis=0).T*0.125
        spread(i,0,unturn(dq,r0).astype(BF))
        return 0
    used=(e1+BQ-1)//BQ
    lax.fori_loop(0,used,qblock,0)
    def blank(i,_):
        spread(i,0,jnp.zeros((BQ,128),BF))
        return 0
    lax.fori_loop(used,rows//BQ,blank,0)
    def last(i,_):
        r0=pl.multiple_of(i*BQ,BQ)
        spread(i,1,unturn(dk[pl.ds(r0,BQ),:],r0).astype(BF))
        spread(i,2,dv[pl.ds(r0,BQ),:].astype(BF))
        return 0
    lax.fori_loop(0,rows//BQ,last,0)

def attend_bwd(ctl,own,recv,d_own,d_recv,o_own,o_oth,lse,cos,sin):
    half,width=own.shape
    pairs=width//384
    rows=2*half
    sp=[pl.BlockSpec((half,128),(lambda p,c,s=s:(0,s*pairs+p))) for s in range(3)]
    one=pl.BlockSpec((half,128),lambda p,c:(0,p))
    full=pl.BlockSpec((rows,128),lambda p,c:(0,0))
    return pl.pallas_call(bwd_kernel,
        grid_spec=pltpu.PrefetchScalarGridSpec(num_scalar_prefetch=1,grid=(pairs,),
          in_specs=sp+sp+[one]*4+[pl.BlockSpec((1,8,rows),lambda p,c:(p,0,0)),full,full],
          out_specs=[pl.BlockSpec((half,384),lambda p,c:(0,p))]*2,
          scratch_shapes=[pltpu.VMEM((rows+BK,256),BF),pltpu.VMEM((rows,256),BF),pltpu.VMEM((rows,256),BF),
             pltpu.VMEM((rows+BK,128),BF),pltpu.VMEM((rows,128),BF),pltpu.VMEM((rows,128),BF),
             pltpu.VMEM((128,rows+BK),BF),pltpu.VMEM((16,rows),F32),pltpu.VMEM((rows+BK,128),F32),pltpu.VMEM((rows+BK,128),F32)]),
        out_shape=[jax.ShapeDtypeStruct((half,width),BF)]*2,
        compiler_params=pltpu.CompilerParams(vmem_limit_bytes=56<<20,dimension_semantics=("arbitrary",)),
        cost_estimate=pl.CostEstimate(flops=10*rows*rows*64*2*pairs//2,bytes_accessed=20*half*width,transcendentals=rows*rows*pairs),
        name="attend_bwd",
    )(ctl,own,own,own,recv,recv,recv,d_own,d_recv,o_own,o_oth,lse,cos,sin)

def mix_kernel(ctl,x,w,cos,sin,own,oth):
    pos=ctl[0]
    width=x.shape[1]
    share=width//2
    xb=x[...]
    c=cos[...]
    s=sin[...]
    lane=lax.broadcasted_iota(jnp.int32,c.shape,1)
    first=(lane%64)<32
    for out,side in ((own,pos),(oth,1-pos)):
        for part in range(3):
            cols=pl.ds(pl.multiple_of(part*width+side*share,128),share)
            y=nn(xb,w[:,cols])
            for t in range(share//128):
                z=y[:,t*128:(t+1)*128]
                if part<2:
                    swapped=jnp.where(first,pltpu.roll(z,96,1),pltpu.roll(z,32,1))
                    z=z*c+swapped*s
                out[:,part*share+t*128:part*share+(t+1)*128]=z.astype(BF)

def mix(ctl,x,w,cos,sin):
    rows,width=x.shape
    cols=w.shape[1]
    block=256
    row=lambda n: pl.BlockSpec((block,n),lambda i,c:(i,0))
    return pl.pallas_call(mix_kernel,
        grid_spec=pltpu.PrefetchScalarGridSpec(num_scalar_prefetch=1,grid=(rows//block,),
          in_specs=[row(width),pl.BlockSpec((width,cols),lambda i,c:(0,0)),row(128),row(128)],
          out_specs=[row(cols//2)]*2),
        out_shape=[jax.ShapeDtypeStruct((rows,cols//2),BF)]*2,
        compiler_params=pltpu.CompilerParams(vmem_limit_bytes=40<<20,dimension_semantics=("arbitrary",)),
        cost_estimate=pl.CostEstimate(flops=2*rows*width*cols,bytes_accessed=2*(rows*width+width*cols+rows*cols),transcendentals=0),
        name="mix",
    )(ctl,x,w,cos,sin)

def fold_rows(x,per):
    rows,cols=x.shape
    return x.reshape(per,rows//per,cols).transpose(1,0,2).reshape(rows//per,per*cols)

def unfold_rows(x,per,share):
    count=x.shape[0]//share
    cols=x.shape[1]//per
    return x.reshape(count,share,per,cols).transpose(0,2,1,3).reshape(count*per*share,cols)

def swap_cores(x):
    return lax.ppermute(x,"dim",[(0,1),(1,0)])

def join(pos,own,recv,axis=1):
    return jnp.where(pos==0,jnp.concatenate([own,recv],axis),jnp.concatenate([recv,own],axis))

def join_parts(pos,own,recv):
    share=own.shape[1]//3
    pieces=[]
    for s in range(3):
        pieces.append(own[:,s*share:(s+1)*share])
        pieces.append(recv[:,s*share:(s+1)*share])
    flip=[pieces[i^1] for i in range(6)]
    return jnp.where(pos==0,jnp.concatenate(pieces,1),jnp.concatenate(flip,1))

def body(tokens,doc_lengths,pair_index,target_bank,mixer_in,mixer_out,expand,contract,norm_params,*rest):
    slices=lax.axis_size("dim")
    if slices!=2 or doc_lengths.shape[1]!=2:
        return body_general(tokens,doc_lengths,pair_index,target_bank,mixer_in,mixer_out,expand,contract,norm_params,*rest)
    (mixer_in_moment,mixer_out_moment,expand_moment,contract_moment,norm_moment,
     mixer_in_average,mixer_out_average,expand_average,contract_average,norm_average)=rest
    local_rows,model_width=tokens.shape
    group_rows=local_rows*slices
    pos=lax.axis_index("dim")
    doc_count=2
    gather=lambda w,axis=0: lax.all_gather(w[0].astype(BF),("dp","dim"),axis=axis,tiled=True)
    w_mix=gather(mixer_in)
    share_rows=mixer_out.shape[1]
    per=contract.shape[1]//share_rows
    count=model_width//share_rows
    con_cols=fold_rows(contract[0],per)
    norm_cols=jnp.pad(norm_params[0],((0,share_rows-4),(0,128-share_rows)))
    bundle=jnp.concatenate([mixer_out[0],expand[0],con_cols,norm_cols],1).astype(BF)
    bundle=lax.all_gather(bundle,("dp","dim"),axis=0,tiled=True)
    at1=model_width
    at2=at1+expand.shape[2]
    at3=at2+per*model_width
    w_out=bundle[:,0:at1]
    w_exp=bundle[:,at1:at2]
    w_con=unfold_rows(bundle[:,at2:at3],per,share_rows)
    w_norm=bundle[:,at3:].reshape(count,share_rows,128)[:,0:4,0:share_rows].transpose(1,0,2).reshape(4,model_width)
    lengths=doc_lengths[0]
    e0=lengths[0]
    e1=lengths[0]+lengths[1]
    ctl=jnp.stack([pos.astype(jnp.int32),e0,e1])
    ids=jnp.arange(group_rows,dtype=jnp.int32)
    seg=(ids>=e0).astype(jnp.int32)+(ids>=e1).astype(jnp.int32)
    begin=jnp.where(seg==0,0,jnp.where(seg==1,e0,e1))
    lane=jnp.arange(128,dtype=jnp.int32)
    frequency=jnp.power(1000.0,-(2*(lane%32)).astype(F32)/HEAD)
    angles=(ids-begin).astype(F32)[:,None]*frequency[None,:]
    cos=jnp.cos(angles)
    sin=jnp.sin(angles)*jnp.where((lane%64)<32,-1.0,1.0)[None,:]
    cos_own=lax.dynamic_slice_in_dim(cos,pos*local_rows,local_rows,0)
    sin_own=lax.dynamic_slice_in_dim(sin,pos*local_rows,local_rows,0)
    seg_rows=lax.dynamic_slice_in_dim(seg,pos*local_rows,local_rows,0)
    stream=tokens.astype(F32)
    own,oth=mix(ctl,tokens,w_mix,cos_own,sin_own)
    recv=swap_cores(oth)
    o_own,o_oth,lse=attend_fwd(ctl,own,recv)
    att_low=join(pos,o_own,swap_cores(o_oth))
    norm_gains=w_norm.astype(F32)
    first_sum=stream+matmul(att_low,w_out)
    normed=normalize(first_sum,norm_gains[0],norm_gains[1])
    y_low=normed.astype(BF)
    gate_up=matmul(y_low,w_exp)
    half=gate_up.shape[1]//2
    hidden=(jax.nn.silu(gate_up[:,0:half])*gate_up[:,half:2*half]).astype(BF)
    second_sum=normed+matmul(hidden,w_con)
    final=normalize(second_sum,norm_gains[2],norm_gains[3])
    member=(seg_rows[None,:]==jnp.arange(doc_count,dtype=jnp.int32)[:,None]).astype(F32)
    partial_value=matmul_exact(member,final)
    pooled=lax.psum_scatter(partial_value,"dim",scatter_dimension=1,tiled=True)
    length_f=lengths.astype(F32)
    embeddings=pooled/length_f[:,None]
    share=embeddings.shape[1]
    pick=(pair_index[:,None]==jnp.arange(target_bank.shape[0],dtype=jnp.int32)[None,:]).astype(BF)
    targets=matmul(pick,target_bank)
    feature_ids=pos*share+jnp.arange(share,dtype=jnp.int32)
    cuts=jnp.array([model_width//12,model_width//6,model_width//3,2*model_width//3,model_width],dtype=jnp.int32)
    masks=(feature_ids[None,:]<cuts[:,None]).astype(F32)
    cross=matmul_exact(embeddings*targets,masks.T)
    own_sq=matmul_exact(embeddings*embeddings,masks.T)
    other=matmul_exact(targets*targets,masks.T)
    cross,own_sq,other=lax.psum((cross,own_sq,other),"dim")
    own_root=lax.rsqrt(own_sq+COSINE_EPSILON)
    other_root=lax.rsqrt(other+COSINE_EPSILON)
    cosine=cross*own_root*other_root
    coef_target=-length_f[:,None]*own_root*other_root
    coef_self=length_f[:,None]*cosine*own_root*own_root
    grad_emb=matmul_exact(coef_target,masks)*targets+matmul_exact(coef_self,masks)*embeddings
    grad_full=lax.all_gather(grad_emb,"dim",axis=1,tiled=True)
    spread_rows=member/length_f[:,None]
    grad_stream=lax.dot_general(spread_rows,grad_full,(((0,),(0,)),((),())),precision=PRECISE,preferred_element_type=F32)
    grad_second,grad_gain2,grad_bias2=normalize_back(grad_stream,second_sum,norm_gains[2])
    grad_m_low=grad_second.astype(BF)
    grad_con=inner_rows(hidden,grad_m_low)
    grad_hidden=inner_cols(grad_m_low,w_con)
    gate_part=gate_up[:,0:half]
    up_part=gate_up[:,half:2*half]
    sigmoid_gate=jax.nn.sigmoid(gate_part)
    activated=gate_part*sigmoid_gate
    grad_gate=grad_hidden*up_part*sigmoid_gate*(1.0+gate_part*(1.0-sigmoid_gate))
    grad_up=grad_hidden*activated
    grad_both=jnp.concatenate([grad_gate,grad_up],axis=1).astype(BF)
    grad_exp=inner_rows(y_low,grad_both)
    grad_normed=grad_second+inner_cols(grad_both,w_exp)
    grad_first,grad_gain1,grad_bias1=normalize_back(grad_normed,first_sum,norm_gains[0])
    grad_a_low=grad_first.astype(BF)
    grad_out=inner_rows(att_low,grad_a_low)
    grad_attended=inner_cols(grad_a_low,w_out).astype(BF)
    width=model_width//2
    d_own=lax.dynamic_slice_in_dim(grad_attended,pos*width,width,1)
    d_oth=lax.dynamic_slice_in_dim(grad_attended,(1-pos)*width,width,1)
    d_recv=swap_cores(d_oth)
    scatter=lambda g: lax.psum_scatter(g,("dp","dim"),scatter_dimension=0,tiled=True).astype(F32)
    grad_norm=jnp.stack([grad_gain1,grad_bias1,grad_gain2,grad_bias2]).reshape(4,count,share_rows).transpose(1,0,2)
    grad_norm=jnp.pad(grad_norm,((0,0),(0,share_rows-4),(0,128-share_rows))).reshape(model_width,128)
    fold_con=grad_con.astype(BF).reshape(count,per,share_rows,model_width).transpose(0,2,1,3).reshape(model_width,per*model_width)
    sums=scatter(jnp.concatenate([grad_out.astype(BF),grad_exp.astype(BF),fold_con,grad_norm.astype(BF)],1))
    sum_out=sums[:,0:at1]
    sum_exp=sums[:,at1:at2]
    sum_con=unfold_rows(sums[:,at2:at3],per,share_rows)
    sum_norm=sums[0:4,at3:at3+share_rows]
    g_own,g_oth=attend_bwd(ctl,own,recv,d_own,d_recv,o_own,o_oth,lse,cos,sin)
    grad_mixed=join_parts(pos,unpair(g_own),unpair(swap_cores(g_oth)))
    grad_mix=inner_rows(tokens,grad_mixed)
    token_grads=grad_first+inner_cols(grad_mixed,w_mix)
    sum_mix=scatter(grad_mix.astype(BF))
    total_rows=group_rows*lax.axis_size("dp")
    matrix_rate=1.0/math.sqrt(total_rows)
    norm_rate=0.3/math.sqrt(total_rows)
    grads=[g[None] for g in (sum_mix,sum_out,sum_exp,sum_con,sum_norm)]
    weights=(mixer_in,mixer_out,expand,contract,norm_params)
    moments=(mixer_in_moment,mixer_out_moment,expand_moment,contract_moment,norm_moment)
    averages=(mixer_in_average,mixer_out_average,expand_average,contract_average,norm_average)
    rates=(matrix_rate,matrix_rate,matrix_rate,matrix_rate,norm_rate)
    results=[advance(weights[k],moments[k],averages[k],grads[k],rates[k]) for k in range(5)]
    return (embeddings,token_grads,*grads,*[results[k][f] for f in range(4) for k in range(5)])

def unpair(g):
    rows,width=g.shape
    pairs=width//384
    return jnp.concatenate([g[:,p*384+s*128:p*384+(s+1)*128] for s in range(3) for p in range(pairs)],1)


def solution(mesh):
    placed = (
        P(("dp", "dim"), None),
        P("dp", None),
        P("dp"),
        P(None, "dim"),
        P(None, ("dp", "dim"), None),
        P(None, ("dp", "dim"), None),
        P(None, ("dp", "dim"), None),
        P(None, ("dp", "dim"), None),
        P(None, None, ("dp", "dim")),
        P(None, ("dp", "dim"), None),
        P(None, ("dp", "dim"), None),
        P(None, ("dp", "dim"), None),
        P(None, ("dp", "dim"), None),
        P(None, None, ("dp", "dim")),
        P(None, ("dp", "dim"), None),
        P(None, ("dp", "dim"), None),
        P(None, ("dp", "dim"), None),
        P(None, ("dp", "dim"), None),
        P(None, None, ("dp", "dim")),
    )
    return jax.shard_map(
        body,
        mesh=mesh,
        in_specs=placed,
        out_specs=(
            P("dp", "dim"),
            P(("dp", "dim"), None),
            P(None, ("dp", "dim"), None),
            P(None, ("dp", "dim"), None),
            P(None, ("dp", "dim"), None),
            P(None, ("dp", "dim"), None),
            P(None, None, ("dp", "dim")),
            P(None, ("dp", "dim"), None),
            P(None, ("dp", "dim"), None),
            P(None, ("dp", "dim"), None),
            P(None, ("dp", "dim"), None),
            P(None, None, ("dp", "dim")),
            P(None, ("dp", "dim"), None),
            P(None, ("dp", "dim"), None),
            P(None, ("dp", "dim"), None),
            P(None, ("dp", "dim"), None),
            P(None, None, ("dp", "dim")),
            P(None, ("dp", "dim"), None),
            P(None, ("dp", "dim"), None),
            P(None, ("dp", "dim"), None),
            P(None, ("dp", "dim"), None),
            P(None, None, ("dp", "dim")),
            P(None, ("dp", "dim"), None),
            P(None, ("dp", "dim"), None),
            P(None, ("dp", "dim"), None),
            P(None, ("dp", "dim"), None),
            P(None, None, ("dp", "dim")),
        ),
        check_vma=False,
    )
```

```python
import math

import jax
import jax.numpy as jnp
from jax import lax
from jax.experimental import pallas as pl
from jax.experimental.pallas import tpu as pltpu
from jax.sharding import PartitionSpec as P

HEAD = 64


NORM_EPSILON = 1e-05
COSINE_EPSILON = 1e-06
MOMENTUM = 0.5
AVERAGE_DECAY = 0.5
PRECISE = lax.Precision.HIGHEST
MASKED = -1e30


def matmul(left_op, right_op):
    return jnp.dot(left_op, right_op, preferred_element_type=jnp.float32)


def matmul_exact(left_op, right_op):
    return jnp.dot(left_op, right_op, precision=PRECISE, preferred_element_type=jnp.float32)


def inner_rows(left_op, right_op):
    return lax.dot_general(
        left_op, right_op, (((0,), (0,)), ((), ())), preferred_element_type=jnp.float32
    )


def inner_cols(left_op, right_op):
    return lax.dot_general(
        left_op, right_op, (((1,), (1,)), ((), ())), preferred_element_type=jnp.float32
    )


def rotate(values, cosines, sines):
    row_count = values.shape[0]
    shaped = values.reshape(row_count, -1, 2, HEAD // 2)
    former = shaped[:, :, 0, :]
    latter = shaped[:, :, 1, :]
    cosine_b = cosines[:, None, :]
    sine_b = sines[:, None, :]
    turned = jnp.stack(
        [former * cosine_b - latter * sine_b, latter * cosine_b + former * sine_b], axis=2
    )
    return turned.reshape(values.shape)


def rotate_back(grads_in, cosines, sines):
    row_count = grads_in.shape[0]
    shaped = grads_in.reshape(row_count, -1, 2, HEAD // 2)
    former = shaped[:, :, 0, :]
    latter = shaped[:, :, 1, :]
    cosine_b = cosines[:, None, :]
    sine_b = sines[:, None, :]
    turned = jnp.stack(
        [former * cosine_b + latter * sine_b, latter * cosine_b - former * sine_b], axis=2
    )
    return turned.reshape(grads_in.shape)


def normalize(summed, gain_vec, bias_vec):
    centred = summed - jnp.mean(summed, axis=1, keepdims=True)
    scaling = lax.rsqrt(jnp.mean(centred * centred, axis=1, keepdims=True) + NORM_EPSILON)
    return centred * scaling * gain_vec + bias_vec


def normalize_back(grad_in, summed, gain_vec):
    centred = summed - jnp.mean(summed, axis=1, keepdims=True)
    scaling = lax.rsqrt(jnp.mean(centred * centred, axis=1, keepdims=True) + NORM_EPSILON)
    unit = centred * scaling
    grad_unit = grad_in * gain_vec
    grad_sum = scaling * (
        grad_unit
        - jnp.mean(grad_unit, axis=1, keepdims=True)
        - unit * jnp.mean(grad_unit * unit, axis=1, keepdims=True)
    )
    return (grad_sum, jnp.sum(grad_in * unit, axis=0), jnp.sum(grad_in, axis=0))


def flatten(stacked):
    return stacked.transpose(1, 0, 2).reshape(stacked.shape[1], -1)


def attend(q_rot, all_keys, all_values, same_doc):
    head_count = q_rot.shape[1] // HEAD

    def one_head(head_pos):
        offset = head_pos * HEAD
        query_part = lax.dynamic_slice_in_dim(q_rot, offset, HEAD, 1)
        key_part = lax.dynamic_slice_in_dim(all_keys, offset, HEAD, 1)
        value_part = lax.dynamic_slice_in_dim(all_values, offset, HEAD, 1)
        scores = jnp.where(same_doc, inner_cols(query_part, key_part) * 0.125, MASKED)
        row_max = jnp.max(scores, axis=1, keepdims=True)
        exponent = jnp.exp(scores - row_max)
        row_total = jnp.sum(exponent, axis=1, keepdims=True)
        attn_probs = (exponent / row_total).astype(jnp.bfloat16)
        return (matmul(attn_probs, value_part), (row_max + jnp.log(row_total))[:, 0])

    outputs, log_totals = lax.map(one_head, jnp.arange(head_count, dtype=jnp.int32))
    return (flatten(outputs), log_totals)


def attend_back(q_rot, all_keys, all_values, same_doc, grad_out, log_totals):
    head_count = q_rot.shape[1] // HEAD

    def one_head(pack):
        head_pos, log_total = pack
        offset = head_pos * HEAD
        query_part = lax.dynamic_slice_in_dim(q_rot, offset, HEAD, 1)
        key_part = lax.dynamic_slice_in_dim(all_keys, offset, HEAD, 1)
        value_part = lax.dynamic_slice_in_dim(all_values, offset, HEAD, 1)
        grad_part = lax.dynamic_slice_in_dim(grad_out, offset, HEAD, 1)
        scores = jnp.where(same_doc, inner_cols(query_part, key_part) * 0.125, MASKED)
        attn_probs = jnp.exp(scores - log_total[:, None])
        grad_probs = inner_cols(grad_part, value_part)
        row_dot = jnp.sum(attn_probs * grad_probs, axis=1, keepdims=True)
        grad_scores = (attn_probs * (grad_probs - row_dot)).astype(jnp.bfloat16)
        grad_query = matmul(grad_scores, key_part) * 0.125
        grad_key = inner_rows(grad_scores, query_part) * 0.125
        grad_value = inner_rows(attn_probs.astype(jnp.bfloat16), grad_part)
        return (grad_query, grad_key, grad_value)

    mapped = lax.map(one_head, (jnp.arange(head_count, dtype=jnp.int32), log_totals))
    return (flatten(mapped[0]), flatten(mapped[1]), flatten(mapped[2]))


def advance(weight, moment, average, grad_in, rate):
    moment_next = MOMENTUM * moment + grad_in
    weight_next = weight - rate * (grad_in + MOMENTUM * moment_next)
    average_next = AVERAGE_DECAY * average + (1.0 - AVERAGE_DECAY) * weight_next
    return (weight_next, moment_next, average_next, weight_next.astype(jnp.bfloat16))


def body_general(
    tokens,
    doc_lengths,
    pair_index,
    target_bank,
    mixer_in,
    mixer_out,
    expand,
    contract,
    norm_params,
    mixer_in_moment,
    mixer_out_moment,
    expand_moment,
    contract_moment,
    norm_moment,
    mixer_in_average,
    mixer_out_average,
    expand_average,
    contract_average,
    norm_average,
):
    local_rows, model_width = tokens.shape
    slices = lax.axis_size("dim")
    group_rows = local_rows * slices
    position = lax.axis_index("dim")
    layer_count = mixer_in.shape[0]
    doc_count = doc_lengths.shape[1]
    lengths = doc_lengths[0]
    doc_ends = jnp.cumsum(lengths)
    doc_starts = doc_ends - lengths
    row_ids = position * local_rows + jnp.arange(local_rows, dtype=jnp.int32)
    key_ids = jnp.arange(group_rows, dtype=jnp.int32)
    seg_rows = jnp.sum((row_ids[:, None] >= doc_ends[None, :]).astype(jnp.int32), axis=1)
    seg_keys = jnp.sum((key_ids[:, None] >= doc_ends[None, :]).astype(jnp.int32), axis=1)
    first_rows = jnp.concatenate([doc_starts, doc_ends[-1:]])
    segment_ids = jnp.arange(doc_count + 1, dtype=jnp.int32)
    row_begin = jnp.sum(
        jnp.where(seg_rows[:, None] == segment_ids[None, :], first_rows[None, :], 0), axis=1
    )
    frequency = jnp.power(1000.0, -jnp.arange(0, HEAD, 2).astype(jnp.float32) / HEAD)
    angles = (row_ids - row_begin).astype(jnp.float32)[:, None] * frequency[None, :]
    cosines = jnp.cos(angles)
    sines = jnp.sin(angles)
    same_doc = seg_rows[:, None] == seg_keys[None, :]
    stream = tokens.astype(jnp.float32)
    layer_pos = 0
    layer_weights = (
        lax.all_gather(mixer_in[layer_pos].astype(jnp.bfloat16), ("dp", "dim"), axis=0, tiled=True),
        lax.all_gather(
            mixer_out[layer_pos].astype(jnp.bfloat16), ("dp", "dim"), axis=0, tiled=True
        ),
        lax.all_gather(expand[layer_pos].astype(jnp.bfloat16), ("dp", "dim"), axis=0, tiled=True),
        lax.all_gather(contract[layer_pos].astype(jnp.bfloat16), ("dp", "dim"), axis=0, tiled=True),
        lax.all_gather(
            norm_params[layer_pos].astype(jnp.bfloat16), ("dp", "dim"), axis=1, tiled=True
        ),
    )
    w_mix, w_out, w_exp, w_con, w_norm = layer_weights
    norm_gains = w_norm.astype(jnp.float32)
    x_low = stream.astype(jnp.bfloat16)
    mixed = matmul(x_low, w_mix)
    q_rot = rotate(mixed[:, 0:model_width], cosines, sines).astype(jnp.bfloat16)
    k_rot = rotate(mixed[:, model_width : 2 * model_width], cosines, sines).astype(jnp.bfloat16)
    v_low = mixed[:, 2 * model_width : 3 * model_width].astype(jnp.bfloat16)
    all_keys = lax.all_gather(k_rot, "dim", axis=0, tiled=True)
    all_values = lax.all_gather(v_low, "dim", axis=0, tiled=True)
    attended, log_totals = attend(q_rot, all_keys, all_values, same_doc)
    att_low = attended.astype(jnp.bfloat16)
    first_sum = stream + matmul(att_low, w_out)
    normed = normalize(first_sum, norm_gains[0], norm_gains[1])
    y_low = normed.astype(jnp.bfloat16)
    gate_up = matmul(y_low, w_exp)
    half = gate_up.shape[1] // 2
    hidden = (jax.nn.silu(gate_up[:, 0:half]) * gate_up[:, half : 2 * half]).astype(jnp.bfloat16)
    second_sum = normed + matmul(hidden, w_con)
    saved = [
        (
            stream,
            layer_weights,
            q_rot,
            k_rot,
            v_low,
            all_keys,
            all_values,
            log_totals,
            attended,
            att_low,
            first_sum,
            normed,
            y_low,
            gate_up,
            hidden,
            second_sum,
        )
    ]
    stream = normalize(second_sum, norm_gains[2], norm_gains[3])
    member = (seg_rows[None, :] == jnp.arange(doc_count, dtype=jnp.int32)[:, None]).astype(
        jnp.float32
    )
    partial_value = matmul_exact(member, stream)
    pooled = lax.psum_scatter(partial_value, "dim", scatter_dimension=1, tiled=True)
    length_f = lengths.astype(jnp.float32)
    embeddings = pooled / length_f[:, None]
    share = embeddings.shape[1]
    pick = (
        pair_index[:, None] == jnp.arange(target_bank.shape[0], dtype=jnp.int32)[None, :]
    ).astype(jnp.bfloat16)
    targets = matmul(pick, target_bank)
    feature_ids = position * share + jnp.arange(share, dtype=jnp.int32)
    cuts = jnp.array(
        [model_width // 12, model_width // 6, model_width // 3, 2 * model_width // 3, model_width],
        dtype=jnp.int32,
    )
    masks = (feature_ids[None, :] < cuts[:, None]).astype(jnp.float32)
    cross = matmul_exact(embeddings * targets, masks.T)
    own = matmul_exact(embeddings * embeddings, masks.T)
    other = matmul_exact(targets * targets, masks.T)
    cross, own, other = lax.psum((cross, own, other), "dim")
    own_root = lax.rsqrt(own + COSINE_EPSILON)
    other_root = lax.rsqrt(other + COSINE_EPSILON)
    cosine = cross * own_root * other_root
    coef_target = -length_f[:, None] * own_root * other_root
    coef_self = length_f[:, None] * cosine * own_root * own_root
    grad_emb = (
        matmul_exact(coef_target, masks) * targets + matmul_exact(coef_self, masks) * embeddings
    )
    grad_full = lax.all_gather(grad_emb, "dim", axis=1, tiled=True)
    spread_rows = member / length_f[:, None]
    grad_stream = lax.dot_general(
        spread_rows,
        grad_full,
        (((0,), (0,)), ((), ())),
        precision=PRECISE,
        preferred_element_type=jnp.float32,
    )
    grad_list = [None] * layer_count
    for layer_pos in reversed(range(layer_count)):
        (
            layer_input,
            layer_weights,
            q_rot,
            k_rot,
            v_low,
            all_keys,
            all_values,
            log_totals,
            attended,
            att_low,
            first_sum,
            normed,
            y_low,
            gate_up,
            hidden,
            second_sum,
        ) = saved[layer_pos]
        w_mix = lax.all_gather(
            mixer_in[layer_pos].astype(jnp.bfloat16), ("dp", "dim"), axis=0, tiled=True
        )
        w_out = lax.all_gather(
            mixer_out[layer_pos].astype(jnp.bfloat16), ("dp", "dim"), axis=0, tiled=True
        )
        w_exp = lax.all_gather(
            expand[layer_pos].astype(jnp.bfloat16), ("dp", "dim"), axis=0, tiled=True
        )
        w_con = lax.all_gather(
            contract[layer_pos].astype(jnp.bfloat16), ("dp", "dim"), axis=0, tiled=True
        )
        w_norm = lax.all_gather(
            norm_params[layer_pos].astype(jnp.bfloat16), ("dp", "dim"), axis=1, tiled=True
        )
        norm_gains = w_norm.astype(jnp.float32)
        grad_second, grad_gain2, grad_bias2 = normalize_back(grad_stream, second_sum, norm_gains[2])
        grad_m_low = grad_second.astype(jnp.bfloat16)
        grad_con = inner_rows(hidden, grad_m_low)
        grad_hidden = inner_cols(grad_m_low, w_con)
        half = gate_up.shape[1] // 2
        gate_part = gate_up[:, 0:half]
        up_part = gate_up[:, half : 2 * half]
        sigmoid_gate = jax.nn.sigmoid(gate_part)
        activated = gate_part * sigmoid_gate
        grad_gate = grad_hidden * up_part * sigmoid_gate * (1.0 + gate_part * (1.0 - sigmoid_gate))
        grad_up = grad_hidden * activated
        grad_both = jnp.concatenate([grad_gate, grad_up], axis=1).astype(jnp.bfloat16)
        grad_exp = inner_rows(y_low, grad_both)
        grad_normed = grad_second + inner_cols(grad_both, w_exp)
        grad_first, grad_gain1, grad_bias1 = normalize_back(grad_normed, first_sum, norm_gains[0])
        grad_a_low = grad_first.astype(jnp.bfloat16)
        grad_out = inner_rows(att_low, grad_a_low)
        grad_attended = inner_cols(grad_a_low, w_out).astype(jnp.bfloat16)
        keys_back, values_back = (
            lax.all_gather(k_rot, "dim", axis=0, tiled=True),
            lax.all_gather(v_low, "dim", axis=0, tiled=True),
        )
        grad_query, grad_key_all, grad_value_all = attend_back(
            q_rot, keys_back, values_back, same_doc, grad_attended, log_totals
        )
        grad_kv = lax.psum_scatter(
            jnp.concatenate([grad_key_all, grad_value_all], axis=1).astype(jnp.bfloat16),
            "dim",
            scatter_dimension=0,
            tiled=True,
        ).astype(jnp.float32)
        grad_mixed = jnp.concatenate(
            [
                rotate_back(grad_query, cosines, sines),
                rotate_back(grad_kv[:, 0:model_width], cosines, sines),
                grad_kv[:, model_width : 2 * model_width],
            ],
            axis=1,
        ).astype(jnp.bfloat16)
        x_low = layer_input.astype(jnp.bfloat16)
        grad_mix = inner_rows(x_low, grad_mixed)
        grad_stream = grad_first + inner_cols(grad_mixed, w_mix)
        grad_norm = jnp.stack([grad_gain1, grad_bias1, grad_gain2, grad_bias2])
        grad_list[layer_pos] = (
            lax.psum_scatter(grad_mix, ("dp", "dim"), scatter_dimension=0, tiled=True),
            lax.psum_scatter(grad_out, ("dp", "dim"), scatter_dimension=0, tiled=True),
            lax.psum_scatter(grad_exp, ("dp", "dim"), scatter_dimension=0, tiled=True),
            lax.psum_scatter(grad_con, ("dp", "dim"), scatter_dimension=0, tiled=True),
            lax.psum_scatter(grad_norm, ("dp", "dim"), scatter_dimension=1, tiled=True),
        )
    total_rows = group_rows * lax.axis_size("dp")
    matrix_rate = 1.0 / math.sqrt(total_rows)
    norm_rate = 0.3 / math.sqrt(total_rows)
    grads = [jnp.stack([grad_list[0][kind]]) for kind in range(5)]
    weights = (mixer_in, mixer_out, expand, contract, norm_params)
    moments = (mixer_in_moment, mixer_out_moment, expand_moment, contract_moment, norm_moment)
    averages = (mixer_in_average, mixer_out_average, expand_average, contract_average, norm_average)
    rates = (matrix_rate, matrix_rate, matrix_rate, matrix_rate, norm_rate)
    results = [
        advance(weights[kind], moments[kind], averages[kind], grads[kind], rates[kind])
        for kind in range(5)
    ]
    return (
        embeddings,
        grad_stream,
        grads[0],
        grads[1],
        grads[2],
        grads[3],
        grads[4],
        results[0][0],
        results[1][0],
        results[2][0],
        results[3][0],
        results[4][0],
        results[0][1],
        results[1][1],
        results[2][1],
        results[3][1],
        results[4][1],
        results[0][2],
        results[1][2],
        results[2][2],
        results[3][2],
        results[4][2],
        results[0][3],
        results[1][3],
        results[2][3],
        results[3][3],
        results[4][3],
    )


NEG=-1e30
BQ=512
ROWS=256
BK=512
F32=jnp.float32
BF=jnp.bfloat16

def nt(a,b): return lax.dot_general(a,b,(((1,),(1,)),((),())),preferred_element_type=F32)
def nn(a,b): return jnp.dot(a,b,preferred_element_type=F32)

def fill_masks(e0,e1,kaug,q0,q1,rows,pad):
    r=lax.broadcasted_iota(jnp.int32,(rows+pad,128),0)
    l=lax.broadcasted_iota(jnp.int32,(rows+pad,128),1)
    seg=(r>=e0).astype(jnp.int32)+(r>=e1).astype(jnp.int32)
    kaug[:,128:256]=jnp.where((l<3)&(l!=seg),NEG,0.0).astype(BF)
    qm=jnp.where(l==seg,1.0,0.0).astype(BF)[0:rows]
    q0[:,128:256]=qm
    q1[:,128:256]=qm

def key_range(i,e0,e1):
    first=i*BQ
    last=jnp.minimum(first+BQ,e1)-1
    lo=jnp.where(first>=e0,e0,0)
    hi=jnp.where(last>=e0,e1,e0)
    base=(lo//128)*128
    return pl.multiple_of(base,128),(hi-base+BK-1)//BK

def fwd_kernel(ctl,qo,ko,vo,qr,kr,vr,oo,ox,lse,kaug,q0,q1,vt):
    rows=kaug.shape[0]-BK
    half=rows//2
    pos,e0,e1=ctl[0],ctl[1],ctl[2]
    p=pl.program_id(0)
    @pl.when(p==0)
    def _():
        fill_masks(e0,e1,kaug,q0,q1,rows,BK)
        kaug[rows:,0:128]=jnp.zeros((BK,128),BF)
        vt[:,:]=jnp.where(lax.broadcasted_iota(jnp.int32,vt.shape,0)%80>=64,1.0,0.0).astype(BF)
    lane=lax.broadcasted_iota(jnp.int32,(half,128),1)
    for own,(q,k,v) in ((True,(qo,ko,vo)),(False,(qr,kr,vr))):
        at=pl.multiple_of((pos if own else 1-pos)*half,half)
        scaled=q[...]*jnp.asarray(0.125,BF)
        zero=jnp.zeros_like(scaled)
        q0[pl.ds(at,half),0:128]=jnp.where(lane<64,scaled,zero)
        q1[pl.ds(at,half),0:128]=jnp.where(lane<64,zero,scaled)
        kaug[pl.ds(at,half),0:128]=k[...]
        turned=v[...].T
        vt[0:64,pl.ds(at,half)]=turned[0:64]
        vt[80:144,pl.ds(at,half)]=turned[64:128]
    def qblock(i,_):
        r0=pl.multiple_of(i*BQ,BQ)
        base,count=key_range(i,e0,e1)
        qs=(q0[pl.ds(r0,BQ),:],q1[pl.ds(r0,BQ),:])
        def step(j,carry):
            k0=pl.multiple_of(base+j*BK,128)
            kb=kaug[pl.ds(k0,BK),:]
            scores=[nt(kb,qs[h]) for h in range(2)]
            out=[]
            for h in range(2):
                m,acc=carry[h]
                mn=jnp.maximum(m,jnp.max(scores[h],axis=0,keepdims=True))
                pt=jnp.exp(scores[h]-mn).astype(BF)
                acc=acc*jnp.exp(m-mn)+nn(vt[80*h:80*h+80,pl.ds(k0,BK)],pt)
                out.append((mn,acc))
            return tuple(out)
        init=(jnp.full((1,BQ),-jnp.inf,F32),jnp.zeros((80,BQ),F32))
        res=lax.fori_loop(0,count,step,(init,init))
        outs=[]
        for h in range(2):
            m,acc=res[h]
            l=acc[64:65]
            outs.append(acc[0:64]/l)
            lse[0,h:h+1,pl.ds(r0,BQ)]=m+jnp.log(l)
        ob=jnp.concatenate(outs,axis=0).T.astype(BF)
        put(i,ob)
        return 0
    def put(i,ob):
        local=i*BQ-pos*half
        @pl.when((local>=0)&(local<half))
        def _(): oo[pl.ds(pl.multiple_of(local,BQ),BQ),:]=ob
        @pl.when((local<0)|(local>=half))
        def _(): ox[pl.ds(pl.multiple_of(i*BQ-(1-pos)*half,BQ),BQ),:]=ob
    used=(e1+BQ-1)//BQ
    lax.fori_loop(0,used,qblock,0)
    def blank(i,_):
        r0=pl.multiple_of(i*BQ,BQ)
        lse[0,:,pl.ds(r0,BQ)]=jnp.zeros((8,BQ),F32)
        put(i,jnp.zeros((BQ,128),BF))
        return 0
    lax.fori_loop(used,rows//BQ,blank,0)

def attend_fwd(ctl,own,recv):
    half,width=own.shape
    pairs=width//384
    rows=2*half
    sp=[pl.BlockSpec((half,128),(lambda p,c,s=s:(0,s*pairs+p))) for s in range(3)]
    outw=pairs*128
    return pl.pallas_call(fwd_kernel,
        grid_spec=pltpu.PrefetchScalarGridSpec(num_scalar_prefetch=1,grid=(pairs,),
          in_specs=sp+sp,
          out_specs=[pl.BlockSpec((half,128),lambda p,c:(0,p))]*2+[pl.BlockSpec((1,8,rows),lambda p,c:(p,0,0))],
          scratch_shapes=[pltpu.VMEM((rows+BK,256),BF),pltpu.VMEM((rows,256),BF),pltpu.VMEM((rows,256),BF),pltpu.VMEM((160,rows+BK),BF)]),
        out_shape=[jax.ShapeDtypeStruct((half,outw),BF)]*2+[jax.ShapeDtypeStruct((pairs,8,rows),F32)],
        compiler_params=pltpu.CompilerParams(vmem_limit_bytes=56<<20,dimension_semantics=("arbitrary",)),
        cost_estimate=pl.CostEstimate(flops=4*rows*rows*64*2*pairs//2,bytes_accessed=10*half*width,transcendentals=rows*rows*pairs),
        name="attend_fwd",
    )(ctl,own,own,own,recv,recv,recv)

def bwd_kernel(ctl,qo,ko,vo,qr,kr,vr,do_o,do_r,oo,ox,lse,cos,sin,go,gx,kaug,q0,q1,vs,d0,d1,kt,delta,dk,dv):
    rows=kaug.shape[0]-BK
    half=rows//2
    pos,e0,e1=ctl[0],ctl[1],ctl[2]
    p=pl.program_id(0)
    @pl.when(p==0)
    def _():
        fill_masks(e0,e1,kaug,q0,q1,rows,BK)
        kaug[rows:,0:128]=jnp.zeros((BK,128),BF)
        vs[rows:,:]=jnp.zeros((BK,128),BF)
        kt[:,rows:]=jnp.zeros((128,BK),BF)
    lane=lax.broadcasted_iota(jnp.int32,(half,128),1)
    pick_r=lax.broadcasted_iota(jnp.int32,(16,128),0)
    pick_l=lax.broadcasted_iota(jnp.int32,(16,128),1)
    pick=jnp.where(pick_l//64==pick_r,1.0,0.0).astype(BF)
    for own,(q,k,v,d,o) in ((True,(qo,ko,vo,do_o,oo)),(False,(qr,kr,vr,do_r,ox))):
        at=pl.multiple_of((pos if own else 1-pos)*half,half)
        scaled=q[...]*jnp.asarray(0.125,BF)
        zero=jnp.zeros_like(scaled)
        q0[pl.ds(at,half),0:128]=jnp.where(lane<64,scaled,zero)
        q1[pl.ds(at,half),0:128]=jnp.where(lane<64,zero,scaled)
        kb=k[...]
        kaug[pl.ds(at,half),0:128]=kb
        kt[:,pl.ds(at,half)]=kb.T
        vs[pl.ds(at,half),:]=v[...]
        db=d[...]
        d0[pl.ds(at,half),:]=jnp.where(lane<64,db,zero)
        d1[pl.ds(at,half),:]=jnp.where(lane<64,zero,db)
        prod=db.astype(F32)*o[...].astype(F32)
        hi=prod.astype(BF)
        lo=(prod-hi.astype(F32)).astype(BF)
        delta[:,pl.ds(at,half)]=nt(pick,hi)+nt(pick,lo)
    dk[...]=jnp.zeros_like(dk)
    dv[...]=jnp.zeros_like(dv)
    def spread(i,col,val):
        local=i*ROWS-pos*half
        @pl.when((local>=0)&(local<half))
        def _(): go[pl.ds(pl.multiple_of(local,ROWS),ROWS),col*128:(col+1)*128]=val
        @pl.when((local<0)|(local>=half))
        def _(): gx[pl.ds(pl.multiple_of(i*ROWS-(1-pos)*half,ROWS),ROWS),col*128:(col+1)*128]=val
    def unturn(x,r0):
        ln=lax.broadcasted_iota(jnp.int32,x.shape,1)
        swapped=jnp.where((ln%64)<32,pltpu.roll(x,96,1),pltpu.roll(x,32,1))
        return x*cos[pl.ds(r0,ROWS),:]-swapped*sin[pl.ds(r0,ROWS),:]
    def qblock(i,_):
        r0=pl.multiple_of(i*BQ,BQ)
        base,count=key_range(i,e0,e1)
        qs=(q0[pl.ds(r0,BQ),:],q1[pl.ds(r0,BQ),:])
        ds_=(d0[pl.ds(r0,BQ),:],d1[pl.ds(r0,BQ),:])
        ls=[lse[0,h:h+1,pl.ds(r0,BQ)] for h in range(2)]
        de=[delta[h:h+1,pl.ds(r0,BQ)] for h in range(2)]
        def step(j,carry):
            k0=pl.multiple_of(base+j*BK,128)
            kb=kaug[pl.ds(k0,BK),:]
            vb=vs[pl.ds(k0,BK),:]
            both=range(2)
            st=[nt(kb,qs[h]) for h in both]
            dpt=[nt(vb,ds_[h]) for h in both]
            pt=[jnp.exp(st[h]-ls[h]) for h in both]
            dst=[(pt[h]*(dpt[h]-de[h])).astype(BF) for h in both]
            pb=[pt[h].astype(BF) for h in both]
            dv[pl.ds(k0,BK),:]+=nn(pb[0],ds_[0])+nn(pb[1],ds_[1])
            dk[pl.ds(k0,BK),:]+=nn(dst[0],qs[0][:,0:128])+nn(dst[1],qs[1][:,0:128])
            out=[carry[h]+nn(kt[64*h:64*h+64,pl.ds(k0,BK)],dst[h]) for h in both]
            return tuple(out)
        init=jnp.zeros((64,BQ),F32)
        res=lax.fori_loop(0,count,step,(init,init))
        dq=jnp.concatenate(res,axis=0).T*0.125
        for t in range(BQ//ROWS):
            at=pl.multiple_of(r0+t*ROWS,ROWS)
            spread(i*(BQ//ROWS)+t,0,unturn(dq[t*ROWS:(t+1)*ROWS],at).astype(BF))
        return 0
    used=(e1+BQ-1)//BQ
    lax.fori_loop(0,used,qblock,0)
    def blank(i,_):
        spread(i,0,jnp.zeros((ROWS,128),BF))
        return 0
    lax.fori_loop(used*(BQ//ROWS),rows//ROWS,blank,0)
    def last(i,_):
        r0=pl.multiple_of(i*ROWS,ROWS)
        spread(i,1,unturn(dk[pl.ds(r0,ROWS),:],r0).astype(BF))
        spread(i,2,dv[pl.ds(r0,ROWS),:].astype(BF))
        return 0
    lax.fori_loop(0,rows//ROWS,last,0)

def attend_bwd(ctl,own,recv,d_own,d_recv,o_own,o_oth,lse,cos,sin):
    half,width=own.shape
    pairs=width//384
    rows=2*half
    sp=[pl.BlockSpec((half,128),(lambda p,c,s=s:(0,s*pairs+p))) for s in range(3)]
    one=pl.BlockSpec((half,128),lambda p,c:(0,p))
    full=pl.BlockSpec((rows,128),lambda p,c:(0,0))
    return pl.pallas_call(bwd_kernel,
        grid_spec=pltpu.PrefetchScalarGridSpec(num_scalar_prefetch=1,grid=(pairs,),
          in_specs=sp+sp+[one]*4+[pl.BlockSpec((1,8,rows),lambda p,c:(p,0,0)),full,full],
          out_specs=[pl.BlockSpec((half,384),lambda p,c:(0,p))]*2,
          scratch_shapes=[pltpu.VMEM((rows+BK,256),BF),pltpu.VMEM((rows,256),BF),pltpu.VMEM((rows,256),BF),
             pltpu.VMEM((rows+BK,128),BF),pltpu.VMEM((rows,128),BF),pltpu.VMEM((rows,128),BF),
             pltpu.VMEM((128,rows+BK),BF),pltpu.VMEM((16,rows),F32),pltpu.VMEM((rows+BK,128),F32),pltpu.VMEM((rows+BK,128),F32)]),
        out_shape=[jax.ShapeDtypeStruct((half,width),BF)]*2,
        compiler_params=pltpu.CompilerParams(vmem_limit_bytes=56<<20,dimension_semantics=("arbitrary",)),
        cost_estimate=pl.CostEstimate(flops=10*rows*rows*64*2*pairs//2,bytes_accessed=20*half*width,transcendentals=rows*rows*pairs),
        name="attend_bwd",
    )(ctl,own,own,own,recv,recv,recv,d_own,d_recv,o_own,o_oth,lse,cos,sin)

def mix_kernel(ctl,x,w,cos,sin,own,oth):
    pos=ctl[0]
    width=x.shape[1]
    share=width//2
    xb=x[...]
    c=cos[...]
    s=sin[...]
    lane=lax.broadcasted_iota(jnp.int32,c.shape,1)
    first=(lane%64)<32
    for out,side in ((own,pos),(oth,1-pos)):
        for part in range(3):
            cols=pl.ds(pl.multiple_of(part*width+side*share,128),share)
            y=nn(xb,w[:,cols])
            for t in range(share//128):
                z=y[:,t*128:(t+1)*128]
                if part<2:
                    swapped=jnp.where(first,pltpu.roll(z,96,1),pltpu.roll(z,32,1))
                    z=z*c+swapped*s
                out[:,part*share+t*128:part*share+(t+1)*128]=z.astype(BF)

def mix(ctl,x,w,cos,sin):
    rows,width=x.shape
    cols=w.shape[1]
    block=256
    row=lambda n: pl.BlockSpec((block,n),lambda i,c:(i,0))
    return pl.pallas_call(mix_kernel,
        grid_spec=pltpu.PrefetchScalarGridSpec(num_scalar_prefetch=1,grid=(rows//block,),
          in_specs=[row(width),pl.BlockSpec((width,cols),lambda i,c:(0,0)),row(128),row(128)],
          out_specs=[row(cols//2)]*2),
        out_shape=[jax.ShapeDtypeStruct((rows,cols//2),BF)]*2,
        compiler_params=pltpu.CompilerParams(vmem_limit_bytes=40<<20,dimension_semantics=("arbitrary",)),
        cost_estimate=pl.CostEstimate(flops=2*rows*width*cols,bytes_accessed=2*(rows*width+width*cols+rows*cols),transcendentals=0),
        name="mix",
    )(ctl,x,w,cos,sin)

def shuffle(x,count,per,share):
    rows=x.shape[0]
    return x.reshape(rows,2,count,per,share).transpose(0,1,3,2,4).reshape(x.shape)

def unshuffle(x,count,per,share):
    rows=x.shape[0]
    return x.reshape(rows,2,per,count,share).transpose(0,1,3,2,4).reshape(x.shape)

def fold_rows(x,per):
    rows,cols=x.shape
    return x.reshape(per,rows//per,cols).transpose(1,0,2).reshape(rows//per,per*cols)

def unfold_rows(x,per,share):
    count=x.shape[0]//share
    cols=x.shape[1]//per
    return x.reshape(count,share,per,cols).transpose(0,2,1,3).reshape(count*per*share,cols)

def swap_cores(x):
    return lax.ppermute(x,"dim",[(0,1),(1,0)])

def join(pos,own,recv,axis=1):
    return jnp.where(pos==0,jnp.concatenate([own,recv],axis),jnp.concatenate([recv,own],axis))

def join_parts(pos,own,recv):
    share=own.shape[1]//3
    pieces=[]
    for s in range(3):
        pieces.append(own[:,s*share:(s+1)*share])
        pieces.append(recv[:,s*share:(s+1)*share])
    flip=[pieces[i^1] for i in range(6)]
    return jnp.where(pos==0,jnp.concatenate(pieces,1),jnp.concatenate(flip,1))

def body(tokens,doc_lengths,pair_index,target_bank,mixer_in,mixer_out,expand,contract,norm_params,*rest):
    slices=lax.axis_size("dim")
    if slices!=2 or doc_lengths.shape[1]!=2:
        return body_general(tokens,doc_lengths,pair_index,target_bank,mixer_in,mixer_out,expand,contract,norm_params,*rest)
    (mixer_in_moment,mixer_out_moment,expand_moment,contract_moment,norm_moment,
     mixer_in_average,mixer_out_average,expand_average,contract_average,norm_average)=rest
    local_rows,model_width=tokens.shape
    group_rows=local_rows*slices
    pos=lax.axis_index("dim")
    doc_count=2
    gather=lambda w,axis=0: lax.all_gather(w[0].astype(BF),("dp","dim"),axis=axis,tiled=True)
    w_mix=gather(mixer_in)
    share_rows=mixer_out.shape[1]
    per=contract.shape[1]//share_rows
    count=model_width//share_rows
    hidden_width=contract.shape[1]*count
    exp_cols=shuffle(expand[0].astype(BF),count,per,share_rows)
    con_cols=fold_rows(contract[0].astype(BF),per)
    norm_cols=jnp.pad(norm_params[0].astype(BF),((0,share_rows-4),(0,128-share_rows)))
    bundle=jnp.concatenate([exp_cols,con_cols,mixer_out[0].astype(BF),norm_cols],1)
    bundle=lax.all_gather(bundle,("dp","dim"),axis=0,tiled=True)
    at1=2*hidden_width
    at2=at1+per*model_width
    at3=at2+model_width
    w_exp=bundle[:,0:at1]
    w_con=[bundle[:,at1+j*model_width:at1+(j+1)*model_width] for j in range(per)]
    w_out=bundle[:,at2:at3]
    w_norm=bundle[:,at3:].reshape(count,share_rows,128)[:,0:4,0:share_rows].transpose(1,0,2).reshape(4,model_width)
    lengths=doc_lengths[0]
    e0=lengths[0]
    e1=lengths[0]+lengths[1]
    ctl=jnp.stack([pos.astype(jnp.int32),e0,e1])
    ids=jnp.arange(group_rows,dtype=jnp.int32)
    seg=(ids>=e0).astype(jnp.int32)+(ids>=e1).astype(jnp.int32)
    begin=jnp.where(seg==0,0,jnp.where(seg==1,e0,e1))
    lane=jnp.arange(128,dtype=jnp.int32)
    frequency=jnp.power(1000.0,-(2*(lane%32)).astype(F32)/HEAD)
    angles=(ids-begin).astype(F32)[:,None]*frequency[None,:]
    cos=jnp.cos(angles)
    sin=jnp.sin(angles)*jnp.where((lane%64)<32,-1.0,1.0)[None,:]
    cos_own=lax.dynamic_slice_in_dim(cos,pos*local_rows,local_rows,0)
    sin_own=lax.dynamic_slice_in_dim(sin,pos*local_rows,local_rows,0)
    seg_rows=lax.dynamic_slice_in_dim(seg,pos*local_rows,local_rows,0)
    stream=tokens.astype(F32)
    own,oth=mix(ctl,tokens,w_mix,cos_own,sin_own)
    recv=swap_cores(oth)
    o_own,o_oth,lse=attend_fwd(ctl,own,recv)
    att_low=join(pos,o_own,swap_cores(o_oth))
    norm_gains=w_norm.astype(F32)
    first_sum=stream+matmul(att_low,w_out)
    normed=normalize(first_sum,norm_gains[0],norm_gains[1])
    y_low=normed.astype(BF)
    gate_up=matmul(y_low,w_exp)
    half=gate_up.shape[1]//2
    hidden=(jax.nn.silu(gate_up[:,0:half])*gate_up[:,half:2*half]).astype(BF)
    w_con=jnp.concatenate(w_con,0)
    second_sum=normed+matmul(hidden,w_con)
    final=normalize(second_sum,norm_gains[2],norm_gains[3])
    member=(seg_rows[None,:]==jnp.arange(doc_count,dtype=jnp.int32)[:,None]).astype(F32)
    partial_value=matmul_exact(member,final)
    pooled=lax.psum_scatter(partial_value,"dim",scatter_dimension=1,tiled=True)
    length_f=lengths.astype(F32)
    embeddings=pooled/length_f[:,None]
    share=embeddings.shape[1]
    pick=(pair_index[:,None]==jnp.arange(target_bank.shape[0],dtype=jnp.int32)[None,:]).astype(BF)
    targets=matmul(pick,target_bank)
    feature_ids=pos*share+jnp.arange(share,dtype=jnp.int32)
    cuts=jnp.array([model_width//12,model_width//6,model_width//3,2*model_width//3,model_width],dtype=jnp.int32)
    masks=(feature_ids[None,:]<cuts[:,None]).astype(F32)
    cross=matmul_exact(embeddings*targets,masks.T)
    own_sq=matmul_exact(embeddings*embeddings,masks.T)
    other=matmul_exact(targets*targets,masks.T)
    cross,own_sq,other=lax.psum((cross,own_sq,other),"dim")
    own_root=lax.rsqrt(own_sq+COSINE_EPSILON)
    other_root=lax.rsqrt(other+COSINE_EPSILON)
    cosine=cross*own_root*other_root
    coef_target=-length_f[:,None]*own_root*other_root
    coef_self=length_f[:,None]*cosine*own_root*own_root
    grad_emb=matmul_exact(coef_target,masks)*targets+matmul_exact(coef_self,masks)*embeddings
    grad_full=lax.all_gather(grad_emb,"dim",axis=1,tiled=True)
    spread_rows=member/length_f[:,None]
    grad_stream=lax.dot_general(spread_rows,grad_full,(((0,),(0,)),((),())),precision=PRECISE,preferred_element_type=F32)
    grad_second,grad_gain2,grad_bias2=normalize_back(grad_stream,second_sum,norm_gains[2])
    grad_m_low=grad_second.astype(BF)
    grad_con=inner_rows(hidden,grad_m_low)
    grad_hidden=inner_cols(grad_m_low,w_con)
    gate_part=gate_up[:,0:half]
    up_part=gate_up[:,half:2*half]
    sigmoid_gate=jax.nn.sigmoid(gate_part)
    activated=gate_part*sigmoid_gate
    grad_gate=grad_hidden*up_part*sigmoid_gate*(1.0+gate_part*(1.0-sigmoid_gate))
    grad_up=grad_hidden*activated
    grad_both=jnp.concatenate([grad_gate,grad_up],axis=1).astype(BF)
    grad_exp=inner_rows(y_low,grad_both)
    grad_normed=grad_second+inner_cols(grad_both,w_exp)
    grad_first,grad_gain1,grad_bias1=normalize_back(grad_normed,first_sum,norm_gains[0])
    grad_a_low=grad_first.astype(BF)
    grad_out=inner_rows(att_low,grad_a_low)
    grad_attended=inner_cols(grad_a_low,w_out).astype(BF)
    width=model_width//2
    d_own=lax.dynamic_slice_in_dim(grad_attended,pos*width,width,1)
    d_oth=lax.dynamic_slice_in_dim(grad_attended,(1-pos)*width,width,1)
    d_recv=swap_cores(d_oth)
    scatter=lambda g: lax.psum_scatter(g,("dp","dim"),scatter_dimension=0,tiled=True).astype(F32)
    grad_norm=jnp.stack([grad_gain1,grad_bias1,grad_gain2,grad_bias2]).reshape(4,count,share_rows).transpose(1,0,2)
    grad_norm=jnp.pad(grad_norm,((0,0),(0,share_rows-4),(0,128-share_rows))).reshape(model_width,128)
    fold_con=[grad_con[j*model_width:(j+1)*model_width].astype(BF) for j in range(per)]
    terms=jnp.concatenate([grad_exp.astype(BF),*fold_con,grad_out.astype(BF),grad_norm.astype(BF)],1)
    terms,d_own,d_recv=lax.optimization_barrier((terms,d_own,d_recv))
    sums=scatter(terms)
    g_own,g_oth=attend_bwd(ctl,own,recv,d_own,d_recv,o_own,o_oth,lse,cos,sin)
    grad_mixed=join_parts(pos,unpair(g_own),unpair(swap_cores(g_oth)))
    grad_mix=inner_rows(tokens,grad_mixed)
    token_grads=grad_first+inner_cols(grad_mixed,w_mix)
    grad_mix=grad_mix.astype(BF)
    grad_mix,sums=lax.optimization_barrier((grad_mix,sums))
    sum_mix=scatter(grad_mix)
    sum_exp=unshuffle(sums[:,0:at1],count,per,share_rows)
    sum_con=unfold_rows(sums[:,at1:at2],per,share_rows)
    sum_out=sums[:,at2:at3]
    sum_norm=sums[0:4,at3:at3+share_rows]
    total_rows=group_rows*lax.axis_size("dp")
    matrix_rate=1.0/math.sqrt(total_rows)
    norm_rate=0.3/math.sqrt(total_rows)
    grads=[g[None] for g in (sum_mix,sum_out,sum_exp,sum_con,sum_norm)]
    weights=(mixer_in,mixer_out,expand,contract,norm_params)
    moments=(mixer_in_moment,mixer_out_moment,expand_moment,contract_moment,norm_moment)
    averages=(mixer_in_average,mixer_out_average,expand_average,contract_average,norm_average)
    rates=(matrix_rate,matrix_rate,matrix_rate,matrix_rate,norm_rate)
    results=[advance(weights[k],moments[k],averages[k],grads[k],rates[k]) for k in range(5)]
    return (embeddings,token_grads,*grads,*[results[k][f] for f in range(4) for k in range(5)])

def unpair(g):
    rows,width=g.shape
    pairs=width//384
    return jnp.concatenate([g[:,p*384+s*128:p*384+(s+1)*128] for s in range(3) for p in range(pairs)],1)


def solution(mesh):
    placed = (
        P(("dp", "dim"), None),
        P("dp", None),
        P("dp"),
        P(None, "dim"),
        P(None, ("dp", "dim"), None),
        P(None, ("dp", "dim"), None),
        P(None, ("dp", "dim"), None),
        P(None, ("dp", "dim"), None),
        P(None, None, ("dp", "dim")),
        P(None, ("dp", "dim"), None),
        P(None, ("dp", "dim"), None),
        P(None, ("dp", "dim"), None),
        P(None, ("dp", "dim"), None),
        P(None, None, ("dp", "dim")),
        P(None, ("dp", "dim"), None),
        P(None, ("dp", "dim"), None),
        P(None, ("dp", "dim"), None),
        P(None, ("dp", "dim"), None),
        P(None, None, ("dp", "dim")),
    )
    return jax.shard_map(
        body,
        mesh=mesh,
        in_specs=placed,
        out_specs=(
            P("dp", "dim"),
            P(("dp", "dim"), None),
            P(None, ("dp", "dim"), None),
            P(None, ("dp", "dim"), None),
            P(None, ("dp", "dim"), None),
            P(None, ("dp", "dim"), None),
            P(None, None, ("dp", "dim")),
            P(None, ("dp", "dim"), None),
            P(None, ("dp", "dim"), None),
            P(None, ("dp", "dim"), None),
            P(None, ("dp", "dim"), None),
            P(None, None, ("dp", "dim")),
            P(None, ("dp", "dim"), None),
            P(None, ("dp", "dim"), None),
            P(None, ("dp", "dim"), None),
            P(None, ("dp", "dim"), None),
            P(None, None, ("dp", "dim")),
            P(None, ("dp", "dim"), None),
            P(None, ("dp", "dim"), None),
            P(None, ("dp", "dim"), None),
            P(None, ("dp", "dim"), None),
            P(None, None, ("dp", "dim")),
            P(None, ("dp", "dim"), None),
            P(None, ("dp", "dim"), None),
            P(None, ("dp", "dim"), None),
            P(None, ("dp", "dim"), None),
            P(None, None, ("dp", "dim")),
        ),
        check_vma=False,
    )
```

```python
import math

import jax
import jax.numpy as jnp
from jax import lax
from jax.experimental import pallas as pl
from jax.experimental.pallas import tpu as pltpu
from jax.sharding import PartitionSpec as P

HEAD = 64


NORM_EPSILON = 1e-05
COSINE_EPSILON = 1e-06
MOMENTUM = 0.5
AVERAGE_DECAY = 0.5
PRECISE = lax.Precision.HIGHEST
MASKED = -1e30


def matmul(left_op, right_op):
    return jnp.dot(left_op, right_op, preferred_element_type=jnp.float32)


def matmul_exact(left_op, right_op):
    return jnp.dot(left_op, right_op, precision=PRECISE, preferred_element_type=jnp.float32)


def inner_rows(left_op, right_op):
    return lax.dot_general(
        left_op, right_op, (((0,), (0,)), ((), ())), preferred_element_type=jnp.float32
    )


def inner_cols(left_op, right_op):
    return lax.dot_general(
        left_op, right_op, (((1,), (1,)), ((), ())), preferred_element_type=jnp.float32
    )


def rotate(values, cosines, sines):
    row_count = values.shape[0]
    shaped = values.reshape(row_count, -1, 2, HEAD // 2)
    former = shaped[:, :, 0, :]
    latter = shaped[:, :, 1, :]
    cosine_b = cosines[:, None, :]
    sine_b = sines[:, None, :]
    turned = jnp.stack(
        [former * cosine_b - latter * sine_b, latter * cosine_b + former * sine_b], axis=2
    )
    return turned.reshape(values.shape)


def rotate_back(grads_in, cosines, sines):
    row_count = grads_in.shape[0]
    shaped = grads_in.reshape(row_count, -1, 2, HEAD // 2)
    former = shaped[:, :, 0, :]
    latter = shaped[:, :, 1, :]
    cosine_b = cosines[:, None, :]
    sine_b = sines[:, None, :]
    turned = jnp.stack(
        [former * cosine_b + latter * sine_b, latter * cosine_b - former * sine_b], axis=2
    )
    return turned.reshape(grads_in.shape)


def normalize(summed, gain_vec, bias_vec):
    centred = summed - jnp.mean(summed, axis=1, keepdims=True)
    scaling = lax.rsqrt(jnp.mean(centred * centred, axis=1, keepdims=True) + NORM_EPSILON)
    return centred * scaling * gain_vec + bias_vec


def normalize_back(grad_in, summed, gain_vec):
    centred = summed - jnp.mean(summed, axis=1, keepdims=True)
    scaling = lax.rsqrt(jnp.mean(centred * centred, axis=1, keepdims=True) + NORM_EPSILON)
    unit = centred * scaling
    grad_unit = grad_in * gain_vec
    grad_sum = scaling * (
        grad_unit
        - jnp.mean(grad_unit, axis=1, keepdims=True)
        - unit * jnp.mean(grad_unit * unit, axis=1, keepdims=True)
    )
    return (grad_sum, jnp.sum(grad_in * unit, axis=0), jnp.sum(grad_in, axis=0))


def flatten(stacked):
    return stacked.transpose(1, 0, 2).reshape(stacked.shape[1], -1)


def attend(q_rot, all_keys, all_values, same_doc):
    head_count = q_rot.shape[1] // HEAD

    def one_head(head_pos):
        offset = head_pos * HEAD
        query_part = lax.dynamic_slice_in_dim(q_rot, offset, HEAD, 1)
        key_part = lax.dynamic_slice_in_dim(all_keys, offset, HEAD, 1)
        value_part = lax.dynamic_slice_in_dim(all_values, offset, HEAD, 1)
        scores = jnp.where(same_doc, inner_cols(query_part, key_part) * 0.125, MASKED)
        row_max = jnp.max(scores, axis=1, keepdims=True)
        exponent = jnp.exp(scores - row_max)
        row_total = jnp.sum(exponent, axis=1, keepdims=True)
        attn_probs = (exponent / row_total).astype(jnp.bfloat16)
        return (matmul(attn_probs, value_part), (row_max + jnp.log(row_total))[:, 0])

    outputs, log_totals = lax.map(one_head, jnp.arange(head_count, dtype=jnp.int32))
    return (flatten(outputs), log_totals)


def attend_back(q_rot, all_keys, all_values, same_doc, grad_out, log_totals):
    head_count = q_rot.shape[1] // HEAD

    def one_head(pack):
        head_pos, log_total = pack
        offset = head_pos * HEAD
        query_part = lax.dynamic_slice_in_dim(q_rot, offset, HEAD, 1)
        key_part = lax.dynamic_slice_in_dim(all_keys, offset, HEAD, 1)
        value_part = lax.dynamic_slice_in_dim(all_values, offset, HEAD, 1)
        grad_part = lax.dynamic_slice_in_dim(grad_out, offset, HEAD, 1)
        scores = jnp.where(same_doc, inner_cols(query_part, key_part) * 0.125, MASKED)
        attn_probs = jnp.exp(scores - log_total[:, None])
        grad_probs = inner_cols(grad_part, value_part)
        row_dot = jnp.sum(attn_probs * grad_probs, axis=1, keepdims=True)
        grad_scores = (attn_probs * (grad_probs - row_dot)).astype(jnp.bfloat16)
        grad_query = matmul(grad_scores, key_part) * 0.125
        grad_key = inner_rows(grad_scores, query_part) * 0.125
        grad_value = inner_rows(attn_probs.astype(jnp.bfloat16), grad_part)
        return (grad_query, grad_key, grad_value)

    mapped = lax.map(one_head, (jnp.arange(head_count, dtype=jnp.int32), log_totals))
    return (flatten(mapped[0]), flatten(mapped[1]), flatten(mapped[2]))


def advance(weight, moment, average, grad_in, rate):
    moment_next = MOMENTUM * moment + grad_in
    weight_next = weight - rate * (grad_in + MOMENTUM * moment_next)
    average_next = AVERAGE_DECAY * average + (1.0 - AVERAGE_DECAY) * weight_next
    return (weight_next, moment_next, average_next, weight_next.astype(jnp.bfloat16))


def body_general(
    tokens,
    doc_lengths,
    pair_index,
    target_bank,
    mixer_in,
    mixer_out,
    expand,
    contract,
    norm_params,
    mixer_in_moment,
    mixer_out_moment,
    expand_moment,
    contract_moment,
    norm_moment,
    mixer_in_average,
    mixer_out_average,
    expand_average,
    contract_average,
    norm_average,
):
    local_rows, model_width = tokens.shape
    slices = lax.axis_size("dim")
    group_rows = local_rows * slices
    position = lax.axis_index("dim")
    layer_count = mixer_in.shape[0]
    doc_count = doc_lengths.shape[1]
    lengths = doc_lengths[0]
    doc_ends = jnp.cumsum(lengths)
    doc_starts = doc_ends - lengths
    row_ids = position * local_rows + jnp.arange(local_rows, dtype=jnp.int32)
    key_ids = jnp.arange(group_rows, dtype=jnp.int32)
    seg_rows = jnp.sum((row_ids[:, None] >= doc_ends[None, :]).astype(jnp.int32), axis=1)
    seg_keys = jnp.sum((key_ids[:, None] >= doc_ends[None, :]).astype(jnp.int32), axis=1)
    first_rows = jnp.concatenate([doc_starts, doc_ends[-1:]])
    segment_ids = jnp.arange(doc_count + 1, dtype=jnp.int32)
    row_begin = jnp.sum(
        jnp.where(seg_rows[:, None] == segment_ids[None, :], first_rows[None, :], 0), axis=1
    )
    frequency = jnp.power(1000.0, -jnp.arange(0, HEAD, 2).astype(jnp.float32) / HEAD)
    angles = (row_ids - row_begin).astype(jnp.float32)[:, None] * frequency[None, :]
    cosines = jnp.cos(angles)
    sines = jnp.sin(angles)
    same_doc = seg_rows[:, None] == seg_keys[None, :]
    stream = tokens.astype(jnp.float32)
    layer_pos = 0
    layer_weights = (
        lax.all_gather(mixer_in[layer_pos].astype(jnp.bfloat16), ("dp", "dim"), axis=0, tiled=True),
        lax.all_gather(
            mixer_out[layer_pos].astype(jnp.bfloat16), ("dp", "dim"), axis=0, tiled=True
        ),
        lax.all_gather(expand[layer_pos].astype(jnp.bfloat16), ("dp", "dim"), axis=0, tiled=True),
        lax.all_gather(contract[layer_pos].astype(jnp.bfloat16), ("dp", "dim"), axis=0, tiled=True),
        lax.all_gather(
            norm_params[layer_pos].astype(jnp.bfloat16), ("dp", "dim"), axis=1, tiled=True
        ),
    )
    w_mix, w_out, w_exp, w_con, w_norm = layer_weights
    norm_gains = w_norm.astype(jnp.float32)
    x_low = stream.astype(jnp.bfloat16)
    mixed = matmul(x_low, w_mix)
    q_rot = rotate(mixed[:, 0:model_width], cosines, sines).astype(jnp.bfloat16)
    k_rot = rotate(mixed[:, model_width : 2 * model_width], cosines, sines).astype(jnp.bfloat16)
    v_low = mixed[:, 2 * model_width : 3 * model_width].astype(jnp.bfloat16)
    all_keys = lax.all_gather(k_rot, "dim", axis=0, tiled=True)
    all_values = lax.all_gather(v_low, "dim", axis=0, tiled=True)
    attended, log_totals = attend(q_rot, all_keys, all_values, same_doc)
    att_low = attended.astype(jnp.bfloat16)
    first_sum = stream + matmul(att_low, w_out)
    normed = normalize(first_sum, norm_gains[0], norm_gains[1])
    y_low = normed.astype(jnp.bfloat16)
    gate_up = matmul(y_low, w_exp)
    half = gate_up.shape[1] // 2
    hidden = (jax.nn.silu(gate_up[:, 0:half]) * gate_up[:, half : 2 * half]).astype(jnp.bfloat16)
    second_sum = normed + matmul(hidden, w_con)
    saved = [
        (
            stream,
            layer_weights,
            q_rot,
            k_rot,
            v_low,
            all_keys,
            all_values,
            log_totals,
            attended,
            att_low,
            first_sum,
            normed,
            y_low,
            gate_up,
            hidden,
            second_sum,
        )
    ]
    stream = normalize(second_sum, norm_gains[2], norm_gains[3])
    member = (seg_rows[None, :] == jnp.arange(doc_count, dtype=jnp.int32)[:, None]).astype(
        jnp.float32
    )
    partial_value = matmul_exact(member, stream)
    pooled = lax.psum_scatter(partial_value, "dim", scatter_dimension=1, tiled=True)
    length_f = lengths.astype(jnp.float32)
    embeddings = pooled / length_f[:, None]
    share = embeddings.shape[1]
    pick = (
        pair_index[:, None] == jnp.arange(target_bank.shape[0], dtype=jnp.int32)[None, :]
    ).astype(jnp.bfloat16)
    targets = matmul(pick, target_bank)
    feature_ids = position * share + jnp.arange(share, dtype=jnp.int32)
    cuts = jnp.array(
        [model_width // 12, model_width // 6, model_width // 3, 2 * model_width // 3, model_width],
        dtype=jnp.int32,
    )
    masks = (feature_ids[None, :] < cuts[:, None]).astype(jnp.float32)
    cross = matmul_exact(embeddings * targets, masks.T)
    own = matmul_exact(embeddings * embeddings, masks.T)
    other = matmul_exact(targets * targets, masks.T)
    cross, own, other = lax.psum((cross, own, other), "dim")
    own_root = lax.rsqrt(own + COSINE_EPSILON)
    other_root = lax.rsqrt(other + COSINE_EPSILON)
    cosine = cross * own_root * other_root
    coef_target = -length_f[:, None] * own_root * other_root
    coef_self = length_f[:, None] * cosine * own_root * own_root
    grad_emb = (
        matmul_exact(coef_target, masks) * targets + matmul_exact(coef_self, masks) * embeddings
    )
    grad_full = lax.all_gather(grad_emb, "dim", axis=1, tiled=True)
    spread_rows = member / length_f[:, None]
    grad_stream = lax.dot_general(
        spread_rows,
        grad_full,
        (((0,), (0,)), ((), ())),
        precision=PRECISE,
        preferred_element_type=jnp.float32,
    )
    grad_list = [None] * layer_count
    for layer_pos in reversed(range(layer_count)):
        (
            layer_input,
            layer_weights,
            q_rot,
            k_rot,
            v_low,
            all_keys,
            all_values,
            log_totals,
            attended,
            att_low,
            first_sum,
            normed,
            y_low,
            gate_up,
            hidden,
            second_sum,
        ) = saved[layer_pos]
        w_mix = lax.all_gather(
            mixer_in[layer_pos].astype(jnp.bfloat16), ("dp", "dim"), axis=0, tiled=True
        )
        w_out = lax.all_gather(
            mixer_out[layer_pos].astype(jnp.bfloat16), ("dp", "dim"), axis=0, tiled=True
        )
        w_exp = lax.all_gather(
            expand[layer_pos].astype(jnp.bfloat16), ("dp", "dim"), axis=0, tiled=True
        )
        w_con = lax.all_gather(
            contract[layer_pos].astype(jnp.bfloat16), ("dp", "dim"), axis=0, tiled=True
        )
        w_norm = lax.all_gather(
            norm_params[layer_pos].astype(jnp.bfloat16), ("dp", "dim"), axis=1, tiled=True
        )
        norm_gains = w_norm.astype(jnp.float32)
        grad_second, grad_gain2, grad_bias2 = normalize_back(grad_stream, second_sum, norm_gains[2])
        grad_m_low = grad_second.astype(jnp.bfloat16)
        grad_con = inner_rows(hidden, grad_m_low)
        grad_hidden = inner_cols(grad_m_low, w_con)
        half = gate_up.shape[1] // 2
        gate_part = gate_up[:, 0:half]
        up_part = gate_up[:, half : 2 * half]
        sigmoid_gate = jax.nn.sigmoid(gate_part)
        activated = gate_part * sigmoid_gate
        grad_gate = grad_hidden * up_part * sigmoid_gate * (1.0 + gate_part * (1.0 - sigmoid_gate))
        grad_up = grad_hidden * activated
        grad_both = jnp.concatenate([grad_gate, grad_up], axis=1).astype(jnp.bfloat16)
        grad_exp = inner_rows(y_low, grad_both)
        grad_normed = grad_second + inner_cols(grad_both, w_exp)
        grad_first, grad_gain1, grad_bias1 = normalize_back(grad_normed, first_sum, norm_gains[0])
        grad_a_low = grad_first.astype(jnp.bfloat16)
        grad_out = inner_rows(att_low, grad_a_low)
        grad_attended = inner_cols(grad_a_low, w_out).astype(jnp.bfloat16)
        keys_back, values_back = (
            lax.all_gather(k_rot, "dim", axis=0, tiled=True),
            lax.all_gather(v_low, "dim", axis=0, tiled=True),
        )
        grad_query, grad_key_all, grad_value_all = attend_back(
            q_rot, keys_back, values_back, same_doc, grad_attended, log_totals
        )
        grad_kv = lax.psum_scatter(
            jnp.concatenate([grad_key_all, grad_value_all], axis=1).astype(jnp.bfloat16),
            "dim",
            scatter_dimension=0,
            tiled=True,
        ).astype(jnp.float32)
        grad_mixed = jnp.concatenate(
            [
                rotate_back(grad_query, cosines, sines),
                rotate_back(grad_kv[:, 0:model_width], cosines, sines),
                grad_kv[:, model_width : 2 * model_width],
            ],
            axis=1,
        ).astype(jnp.bfloat16)
        x_low = layer_input.astype(jnp.bfloat16)
        grad_mix = inner_rows(x_low, grad_mixed)
        grad_stream = grad_first + inner_cols(grad_mixed, w_mix)
        grad_norm = jnp.stack([grad_gain1, grad_bias1, grad_gain2, grad_bias2])
        grad_list[layer_pos] = (
            lax.psum_scatter(grad_mix, ("dp", "dim"), scatter_dimension=0, tiled=True),
            lax.psum_scatter(grad_out, ("dp", "dim"), scatter_dimension=0, tiled=True),
            lax.psum_scatter(grad_exp, ("dp", "dim"), scatter_dimension=0, tiled=True),
            lax.psum_scatter(grad_con, ("dp", "dim"), scatter_dimension=0, tiled=True),
            lax.psum_scatter(grad_norm, ("dp", "dim"), scatter_dimension=1, tiled=True),
        )
    total_rows = group_rows * lax.axis_size("dp")
    matrix_rate = 1.0 / math.sqrt(total_rows)
    norm_rate = 0.3 / math.sqrt(total_rows)
    grads = [jnp.stack([grad_list[0][kind]]) for kind in range(5)]
    weights = (mixer_in, mixer_out, expand, contract, norm_params)
    moments = (mixer_in_moment, mixer_out_moment, expand_moment, contract_moment, norm_moment)
    averages = (mixer_in_average, mixer_out_average, expand_average, contract_average, norm_average)
    rates = (matrix_rate, matrix_rate, matrix_rate, matrix_rate, norm_rate)
    results = [
        advance(weights[kind], moments[kind], averages[kind], grads[kind], rates[kind])
        for kind in range(5)
    ]
    return (
        embeddings,
        grad_stream,
        grads[0],
        grads[1],
        grads[2],
        grads[3],
        grads[4],
        results[0][0],
        results[1][0],
        results[2][0],
        results[3][0],
        results[4][0],
        results[0][1],
        results[1][1],
        results[2][1],
        results[3][1],
        results[4][1],
        results[0][2],
        results[1][2],
        results[2][2],
        results[3][2],
        results[4][2],
        results[0][3],
        results[1][3],
        results[2][3],
        results[3][3],
        results[4][3],
    )


NEG=-1e30
BQ=512
ROWS=256
BK=512
F32=jnp.float32
BF=jnp.bfloat16

def nt(a,b): return lax.dot_general(a,b,(((1,),(1,)),((),())),preferred_element_type=F32)
def nn(a,b): return jnp.dot(a,b,preferred_element_type=F32)

def fill_masks(e0,e1,kaug,q0,q1,rows,pad):
    r=lax.broadcasted_iota(jnp.int32,(rows+pad,128),0)
    l=lax.broadcasted_iota(jnp.int32,(rows+pad,128),1)
    seg=(r>=e0).astype(jnp.int32)+(r>=e1).astype(jnp.int32)
    kaug[:,128:256]=jnp.where((l<3)&(l!=seg),NEG,0.0).astype(BF)
    qm=jnp.where(l==seg,1.0,0.0).astype(BF)[0:rows]
    q0[:,128:256]=qm
    q1[:,128:256]=qm

def key_range(i,e0,e1):
    first=i*BQ
    last=jnp.minimum(first+BQ,e1)-1
    lo=jnp.where(first>=e0,e0,0)
    hi=jnp.where(last>=e0,e1,e0)
    base=(lo//128)*128
    return pl.multiple_of(base,128),(hi-base+BK-1)//BK

def fwd_kernel(ctl,qo,ko,vo,qr,kr,vr,oo,ox,lse,kaug,q0,q1,vt):
    rows=kaug.shape[0]-BK
    half=rows//2
    pos,e0,e1=ctl[0],ctl[1],ctl[2]
    p=pl.program_id(0)
    @pl.when(p==0)
    def _():
        fill_masks(e0,e1,kaug,q0,q1,rows,BK)
        kaug[rows:,0:128]=jnp.zeros((BK,128),BF)
        vt[:,:]=jnp.where(lax.broadcasted_iota(jnp.int32,vt.shape,0)%80>=64,1.0,0.0).astype(BF)
    lane=lax.broadcasted_iota(jnp.int32,(half,128),1)
    for own,(q,k,v) in ((True,(qo,ko,vo)),(False,(qr,kr,vr))):
        at=pl.multiple_of((pos if own else 1-pos)*half,half)
        scaled=q[...]*jnp.asarray(0.125,BF)
        zero=jnp.zeros_like(scaled)
        q0[pl.ds(at,half),0:128]=jnp.where(lane<64,scaled,zero)
        q1[pl.ds(at,half),0:128]=jnp.where(lane<64,zero,scaled)
        kaug[pl.ds(at,half),0:128]=k[...]
        turned=v[...].T
        vt[0:64,pl.ds(at,half)]=turned[0:64]
        vt[80:144,pl.ds(at,half)]=turned[64:128]
    def qblock(i,_):
        r0=pl.multiple_of(i*BQ,BQ)
        base,count=key_range(i,e0,e1)
        qs=(q0[pl.ds(r0,BQ),:],q1[pl.ds(r0,BQ),:])
        def step(j,carry):
            k0=pl.multiple_of(base+j*BK,128)
            kb=kaug[pl.ds(k0,BK),:]
            scores=[nt(kb,qs[h]) for h in range(2)]
            out=[]
            for h in range(2):
                m,acc=carry[h]
                mn=jnp.maximum(m,jnp.max(scores[h],axis=0,keepdims=True))
                pt=jnp.exp(scores[h]-mn).astype(BF)
                acc=acc*jnp.exp(m-mn)+nn(vt[80*h:80*h+80,pl.ds(k0,BK)],pt)
                out.append((mn,acc))
            return tuple(out)
        init=(jnp.full((1,BQ),-jnp.inf,F32),jnp.zeros((80,BQ),F32))
        res=lax.fori_loop(0,count,step,(init,init))
        outs=[]
        for h in range(2):
            m,acc=res[h]
            l=acc[64:65]
            outs.append(acc[0:64]/l)
            lse[0,h:h+1,pl.ds(r0,BQ)]=m+jnp.log(l)
        ob=jnp.concatenate(outs,axis=0).T.astype(BF)
        put(i,ob)
        return 0
    def put(i,ob):
        local=i*BQ-pos*half
        @pl.when((local>=0)&(local<half))
        def _(): oo[pl.ds(pl.multiple_of(local,BQ),BQ),:]=ob
        @pl.when((local<0)|(local>=half))
        def _(): ox[pl.ds(pl.multiple_of(i*BQ-(1-pos)*half,BQ),BQ),:]=ob
    used=(e1+BQ-1)//BQ
    lax.fori_loop(0,used,qblock,0)
    def blank(i,_):
        r0=pl.multiple_of(i*BQ,BQ)
        lse[0,:,pl.ds(r0,BQ)]=jnp.zeros((8,BQ),F32)
        put(i,jnp.zeros((BQ,128),BF))
        return 0
    lax.fori_loop(used,rows//BQ,blank,0)

def attend_fwd(ctl,own,recv):
    half,width=own.shape
    pairs=width//384
    rows=2*half
    sp=[pl.BlockSpec((half,128),(lambda p,c,s=s:(0,s*pairs+p))) for s in range(3)]
    outw=pairs*128
    return pl.pallas_call(fwd_kernel,
        grid_spec=pltpu.PrefetchScalarGridSpec(num_scalar_prefetch=1,grid=(pairs,),
          in_specs=sp+sp,
          out_specs=[pl.BlockSpec((half,128),lambda p,c:(0,p))]*2+[pl.BlockSpec((1,8,rows),lambda p,c:(p,0,0))],
          scratch_shapes=[pltpu.VMEM((rows+BK,256),BF),pltpu.VMEM((rows,256),BF),pltpu.VMEM((rows,256),BF),pltpu.VMEM((160,rows+BK),BF)]),
        out_shape=[jax.ShapeDtypeStruct((half,outw),BF)]*2+[jax.ShapeDtypeStruct((pairs,8,rows),F32)],
        compiler_params=pltpu.CompilerParams(vmem_limit_bytes=56<<20,dimension_semantics=("arbitrary",)),
        cost_estimate=pl.CostEstimate(flops=4*rows*rows*64*2*pairs//2,bytes_accessed=10*half*width,transcendentals=rows*rows*pairs),
        name="attend_fwd",
    )(ctl,own,own,own,recv,recv,recv)

def bwd_kernel(ctl,qo,ko,vo,qr,kr,vr,do_o,do_r,oo,ox,lse,cos,sin,go,gx,kaug,q0,q1,vs,d0,d1,kt,delta,dk,dv):
    rows=kaug.shape[0]-BK
    half=rows//2
    pos,e0,e1=ctl[0],ctl[1],ctl[2]
    p=pl.program_id(0)
    @pl.when(p==0)
    def _():
        fill_masks(e0,e1,kaug,q0,q1,rows,BK)
        kaug[rows:,0:128]=jnp.zeros((BK,128),BF)
        vs[rows:,:]=jnp.zeros((BK,128),BF)
        kt[:,rows:]=jnp.zeros((128,BK),BF)
    lane=lax.broadcasted_iota(jnp.int32,(half,128),1)
    pick_r=lax.broadcasted_iota(jnp.int32,(16,128),0)
    pick_l=lax.broadcasted_iota(jnp.int32,(16,128),1)
    pick=jnp.where(pick_l//64==pick_r,1.0,0.0).astype(BF)
    for own,(q,k,v,d,o) in ((True,(qo,ko,vo,do_o,oo)),(False,(qr,kr,vr,do_r,ox))):
        at=pl.multiple_of((pos if own else 1-pos)*half,half)
        scaled=q[...]*jnp.asarray(0.125,BF)
        zero=jnp.zeros_like(scaled)
        q0[pl.ds(at,half),0:128]=jnp.where(lane<64,scaled,zero)
        q1[pl.ds(at,half),0:128]=jnp.where(lane<64,zero,scaled)
        kb=k[...]
        kaug[pl.ds(at,half),0:128]=kb
        kt[:,pl.ds(at,half)]=kb.T
        vs[pl.ds(at,half),:]=v[...]
        db=d[...]
        d0[pl.ds(at,half),:]=jnp.where(lane<64,db,zero)
        d1[pl.ds(at,half),:]=jnp.where(lane<64,zero,db)
        prod=db.astype(F32)*o[...].astype(F32)
        hi=prod.astype(BF)
        lo=(prod-hi.astype(F32)).astype(BF)
        delta[:,pl.ds(at,half)]=nt(pick,hi)+nt(pick,lo)
    dk[...]=jnp.zeros_like(dk)
    dv[...]=jnp.zeros_like(dv)
    def spread(i,col,val):
        local=i*ROWS-pos*half
        @pl.when((local>=0)&(local<half))
        def _(): go[pl.ds(pl.multiple_of(local,ROWS),ROWS),col*128:(col+1)*128]=val
        @pl.when((local<0)|(local>=half))
        def _(): gx[pl.ds(pl.multiple_of(i*ROWS-(1-pos)*half,ROWS),ROWS),col*128:(col+1)*128]=val
    def unturn(x,r0):
        ln=lax.broadcasted_iota(jnp.int32,x.shape,1)
        swapped=jnp.where((ln%64)<32,pltpu.roll(x,96,1),pltpu.roll(x,32,1))
        return x*cos[pl.ds(r0,ROWS),:]-swapped*sin[pl.ds(r0,ROWS),:]
    def qblock(i,_):
        r0=pl.multiple_of(i*BQ,BQ)
        base,count=key_range(i,e0,e1)
        qs=(q0[pl.ds(r0,BQ),:],q1[pl.ds(r0,BQ),:])
        ds_=(d0[pl.ds(r0,BQ),:],d1[pl.ds(r0,BQ),:])
        ls=[lse[0,h:h+1,pl.ds(r0,BQ)] for h in range(2)]
        de=[delta[h:h+1,pl.ds(r0,BQ)] for h in range(2)]
        def step(j,carry):
            k0=pl.multiple_of(base+j*BK,128)
            kb=kaug[pl.ds(k0,BK),:]
            vb=vs[pl.ds(k0,BK),:]
            both=range(2)
            st=[nt(kb,qs[h]) for h in both]
            dpt=[nt(vb,ds_[h]) for h in both]
            pt=[jnp.exp(st[h]-ls[h]) for h in both]
            dst=[(pt[h]*(dpt[h]-de[h])).astype(BF) for h in both]
            pb=[pt[h].astype(BF) for h in both]
            dv[pl.ds(k0,BK),:]+=nn(pb[0],ds_[0])+nn(pb[1],ds_[1])
            dk[pl.ds(k0,BK),:]+=nn(dst[0],qs[0][:,0:128])+nn(dst[1],qs[1][:,0:128])
            out=[carry[h]+nn(kt[64*h:64*h+64,pl.ds(k0,BK)],dst[h]) for h in both]
            return tuple(out)
        init=jnp.zeros((64,BQ),F32)
        res=lax.fori_loop(0,count,step,(init,init))
        dq=jnp.concatenate(res,axis=0).T*0.125
        for t in range(BQ//ROWS):
            at=pl.multiple_of(r0+t*ROWS,ROWS)
            spread(i*(BQ//ROWS)+t,0,unturn(dq[t*ROWS:(t+1)*ROWS],at).astype(BF))
        return 0
    used=(e1+BQ-1)//BQ
    lax.fori_loop(0,used,qblock,0)
    def blank(i,_):
        spread(i,0,jnp.zeros((ROWS,128),BF))
        return 0
    lax.fori_loop(used*(BQ//ROWS),rows//ROWS,blank,0)
    def last(i,_):
        r0=pl.multiple_of(i*ROWS,ROWS)
        spread(i,1,unturn(dk[pl.ds(r0,ROWS),:],r0).astype(BF))
        spread(i,2,dv[pl.ds(r0,ROWS),:].astype(BF))
        return 0
    lax.fori_loop(0,rows//ROWS,last,0)

def attend_bwd(ctl,own,recv,d_own,d_recv,o_own,o_oth,lse,cos,sin):
    half,width=own.shape
    pairs=width//384
    rows=2*half
    sp=[pl.BlockSpec((half,128),(lambda p,c,s=s:(0,s*pairs+p))) for s in range(3)]
    one=pl.BlockSpec((half,128),lambda p,c:(0,p))
    full=pl.BlockSpec((rows,128),lambda p,c:(0,0))
    return pl.pallas_call(bwd_kernel,
        grid_spec=pltpu.PrefetchScalarGridSpec(num_scalar_prefetch=1,grid=(pairs,),
          in_specs=sp+sp+[one]*4+[pl.BlockSpec((1,8,rows),lambda p,c:(p,0,0)),full,full],
          out_specs=[pl.BlockSpec((half,384),lambda p,c:(0,p))]*2,
          scratch_shapes=[pltpu.VMEM((rows+BK,256),BF),pltpu.VMEM((rows,256),BF),pltpu.VMEM((rows,256),BF),
             pltpu.VMEM((rows+BK,128),BF),pltpu.VMEM((rows,128),BF),pltpu.VMEM((rows,128),BF),
             pltpu.VMEM((128,rows+BK),BF),pltpu.VMEM((16,rows),F32),pltpu.VMEM((rows+BK,128),F32),pltpu.VMEM((rows+BK,128),F32)]),
        out_shape=[jax.ShapeDtypeStruct((half,width),BF)]*2,
        compiler_params=pltpu.CompilerParams(vmem_limit_bytes=56<<20,dimension_semantics=("arbitrary",)),
        cost_estimate=pl.CostEstimate(flops=10*rows*rows*64*2*pairs//2,bytes_accessed=20*half*width,transcendentals=rows*rows*pairs),
        name="attend_bwd",
    )(ctl,own,own,own,recv,recv,recv,d_own,d_recv,o_own,o_oth,lse,cos,sin)

BLOCK=512

def spread_mean(x):
    return jnp.mean(x,axis=1,keepdims=True)

def row_docs(ctl,block):
    i=pl.program_id(0)
    r=ctl[0]*(block*pl.num_programs(0))+i*block+lax.broadcasted_iota(jnp.int32,(block,1),0)
    return (r>=ctl[1]).astype(jnp.int32)+(r>=ctl[2]).astype(jnp.int32)

def ffn_fwd_kernel(ctl,ao,ax,tok,w_exp,w_con,w_out,norm,u1,u2,rs,yb,hb,pf,pooled):
    block,width=tok.shape
    hidden=hb.shape[1]
    share=width//2
    pos=ctl[0]
    mine=pl.multiple_of(pos*share,share)
    other=pl.multiple_of((1-pos)*share,share)
    f=tok[...].astype(F32)+nn(ao[...],w_out[pl.ds(mine,share),:])+nn(ax[...],w_out[pl.ds(other,share),:])
    cent=f-spread_mean(f)
    scale=lax.rsqrt(spread_mean(cent*cent)+NORM_EPSILON)
    unit=cent*scale
    u1[...]=unit
    rs[:,0:128]=jnp.broadcast_to(scale,(block,128))
    y=unit*norm[0:1,:]+norm[1:2,:]
    ylow=y.astype(BF)
    yb[...]=ylow
    acc=y
    for c in range(hidden//width):
        gc=slice(c*width,(c+1)*width)
        uc=slice(hidden+c*width,hidden+(c+1)*width)
        gate=nn(ylow,w_exp[:,gc])
        up=nn(ylow,w_exp[:,uc])
        sig=jax.nn.sigmoid(gate)
        act=gate*sig
        low=(act*up).astype(BF)
        hb[:,gc]=low
        pf[:,gc]=(up*sig*(1.0+gate*(1.0-sig))).astype(BF)
        pf[:,uc]=act.astype(BF)
        acc=acc+nn(low,w_con[:,gc])
    cent=acc-spread_mean(acc)
    scale=lax.rsqrt(spread_mean(cent*cent)+NORM_EPSILON)
    unit=cent*scale
    u2[...]=unit
    rs[:,128:256]=jnp.broadcast_to(scale,(block,128))
    out=unit*norm[2:3,:]+norm[3:4,:]
    docs=row_docs(ctl,block)
    @pl.when(pl.program_id(0)==0)
    def _(): pooled[...]=jnp.zeros_like(pooled)
    for d in range(2):
        pooled[d:d+1,:]+=jnp.sum(jnp.where(docs==d,out,0.0),axis=0,keepdims=True)

def ffn_fwd(ctl,ao,ax,tok,bundle,norm,hidden):
    rows,width=tok.shape
    row=lambda n: pl.BlockSpec((BLOCK,n),lambda i,c:(i,0))
    held=lambda n,at: pl.BlockSpec((width,n),lambda i,c:(0,at//n),pipeline_mode=pl.Buffered(1))
    flat=pl.BlockSpec((8,width),lambda i,c:(0,0))
    return pl.pallas_call(ffn_fwd_kernel,
        grid_spec=pltpu.PrefetchScalarGridSpec(num_scalar_prefetch=1,grid=(rows//BLOCK,),
          in_specs=[row(width//2),row(width//2),row(width),held(2*hidden,0),held(hidden,2*hidden),held(width,3*hidden),flat],
          out_specs=[row(width),row(width),row(256),row(width),row(hidden),row(2*hidden),flat]),
        out_shape=[jax.ShapeDtypeStruct((rows,width),F32),jax.ShapeDtypeStruct((rows,width),F32),jax.ShapeDtypeStruct((rows,256),F32),
          jax.ShapeDtypeStruct((rows,width),BF),jax.ShapeDtypeStruct((rows,hidden),BF),jax.ShapeDtypeStruct((rows,2*hidden),BF),
          jax.ShapeDtypeStruct((8,width),F32)],
        compiler_params=pltpu.CompilerParams(vmem_limit_bytes=60<<20,dimension_semantics=("arbitrary",)),
        cost_estimate=pl.CostEstimate(flops=2*rows*width*(width+3*hidden),bytes_accessed=rows*(width*14+hidden*6)+2*width*(width+3*hidden),transcendentals=rows*hidden),
        name="ffn_fwd",
    )(ctl,ao,ax,tok,bundle,bundle,bundle,norm)

def loss_grad(pool,targets,len0,len1):
    width=pool.shape[1]
    docs=lax.broadcasted_iota(jnp.int32,pool.shape,0)
    length=jnp.where(docs==0,len0,len1)
    emb=pool/length
    lane=lax.broadcasted_iota(jnp.int32,pool.shape,1)
    d_target=jnp.zeros_like(pool)
    d_self=jnp.zeros_like(pool)
    for cut in (width//12,width//6,width//3,2*width//3,width):
        keep=lane<cut
        total=lambda v: jnp.sum(jnp.where(keep,v,0.0),axis=1,keepdims=True)
        own_root=lax.rsqrt(total(emb*emb)+COSINE_EPSILON)
        other_root=lax.rsqrt(total(targets*targets)+COSINE_EPSILON)
        cosine=total(emb*targets)*own_root*other_root
        d_target=d_target+jnp.where(keep,own_root*other_root,0.0)
        d_self=d_self+jnp.where(keep,cosine*own_root*own_root,0.0)
    d_emb=length*(d_self*emb-d_target*targets)
    return emb,d_emb/length

def ffn_bwd_kernel(ctl,flen,pool_a,pool_b,targets,u1,u2,rs,pf,w_exp,w_con,w_out,norm,
                   emb,mb,ub,df,ab,do,dx,gn,de):
    block,width=u1.shape
    hidden=pf.shape[1]//2
    share=width//2
    pos=ctl[0]
    @pl.when(pl.program_id(0)==0)
    def _():
        e,d=loss_grad(pool_a[...]+pool_b[...],targets[...],flen[0],flen[1])
        emb[...]=e
        de[...]=d
        gn[...]=jnp.zeros_like(gn)
    docs=row_docs(ctl,block)
    dout=jnp.where(docs==0,de[0:1,:],jnp.where(docs==1,de[1:2,:],0.0))
    unit=u2[...]
    gn[2:3,:]+=jnp.sum(dout*unit,axis=0,keepdims=True)
    gn[3:4,:]+=jnp.sum(dout,axis=0,keepdims=True)
    gu=dout*norm[2:3,:]
    dg=rs[:,128:129]*(gu-spread_mean(gu)-unit*spread_mean(gu*unit))
    mlow=dg.astype(BF)
    mb[...]=mlow
    acc=dg
    for c in range(hidden//width):
        gc=slice(c*width,(c+1)*width)
        uc=slice(hidden+c*width,hidden+(c+1)*width)
        dh=nt(mlow,w_con[:,gc])
        dgate=(dh*pf[:,gc].astype(F32)).astype(BF)
        dup=(dh*pf[:,uc].astype(F32)).astype(BF)
        ub[:,gc]=dgate
        ub[:,uc]=dup
        acc=acc+nt(dgate,w_exp[:,gc])+nt(dup,w_exp[:,uc])
    unit=u1[...]
    gn[0:1,:]+=jnp.sum(acc*unit,axis=0,keepdims=True)
    gn[1:2,:]+=jnp.sum(acc,axis=0,keepdims=True)
    gu=acc*norm[0:1,:]
    dfirst=rs[:,0:1]*(gu-spread_mean(gu)-unit*spread_mean(gu*unit))
    df[...]=dfirst
    alow=dfirst.astype(BF)
    ab[...]=alow
    do[...]=nt(alow,w_out[pl.ds(pl.multiple_of(pos*share,share),share),:]).astype(BF)
    dx[...]=nt(alow,w_out[pl.ds(pl.multiple_of((1-pos)*share,share),share),:]).astype(BF)

def ffn_bwd(ctl,flen,pool_a,pool_b,targets,u1,u2,rs,pf,bundle,norm):
    rows,width=u1.shape
    hidden=pf.shape[1]//2
    row=lambda n: pl.BlockSpec((BLOCK,n),lambda i,c,l:(i,0))
    held=lambda n,at: pl.BlockSpec((width,n),lambda i,c,l:(0,at//n),pipeline_mode=pl.Buffered(1))
    flat=pl.BlockSpec((8,width),lambda i,c,l:(0,0))
    sds=jax.ShapeDtypeStruct
    return pl.pallas_call(ffn_bwd_kernel,
        grid_spec=pltpu.PrefetchScalarGridSpec(num_scalar_prefetch=2,grid=(rows//BLOCK,),
          in_specs=[flat,flat,flat,row(width),row(width),row(256),row(2*hidden),held(2*hidden,0),held(hidden,2*hidden),held(width,3*hidden),flat],
          out_specs=[flat,row(width),row(2*hidden),row(width),row(width),row(width//2),row(width//2),flat],
          scratch_shapes=[pltpu.VMEM((8,width),F32)]),
        out_shape=[sds((8,width),F32),sds((rows,width),BF),sds((rows,2*hidden),BF),sds((rows,width),F32),sds((rows,width),BF),
          sds((rows,width//2),BF),sds((rows,width//2),BF),sds((8,width),F32)],
        compiler_params=pltpu.CompilerParams(vmem_limit_bytes=60<<20,dimension_semantics=("arbitrary",)),
        cost_estimate=pl.CostEstimate(flops=2*rows*width*(width+3*hidden),bytes_accessed=rows*(width*18+hidden*8)+2*width*(width+3*hidden),transcendentals=0),
        name="ffn_bwd",
    )(ctl,flen,pool_a,pool_b,targets,u1,u2,rs,pf,bundle,bundle,bundle,norm)

def mix_kernel(ctl,x,w,cos,sin,own,oth):
    pos=ctl[0]
    width=x.shape[1]
    share=width//2
    xb=x[...]
    c=cos[...]
    s=sin[...]
    lane=lax.broadcasted_iota(jnp.int32,c.shape,1)
    first=(lane%64)<32
    for out,side in ((own,pos),(oth,1-pos)):
        for part in range(3):
            cols=pl.ds(pl.multiple_of(part*width+side*share,128),share)
            y=nn(xb,w[:,cols])
            for t in range(share//128):
                z=y[:,t*128:(t+1)*128]
                if part<2:
                    swapped=jnp.where(first,pltpu.roll(z,96,1),pltpu.roll(z,32,1))
                    z=z*c+swapped*s
                out[:,part*share+t*128:part*share+(t+1)*128]=z.astype(BF)

def mix(ctl,x,w,cos,sin):
    rows,width=x.shape
    cols=w.shape[1]
    block=256
    row=lambda n: pl.BlockSpec((block,n),lambda i,c:(i,0))
    return pl.pallas_call(mix_kernel,
        grid_spec=pltpu.PrefetchScalarGridSpec(num_scalar_prefetch=1,grid=(rows//block,),
          in_specs=[row(width),pl.BlockSpec((width,cols),lambda i,c:(0,0)),row(128),row(128)],
          out_specs=[row(cols//2)]*2),
        out_shape=[jax.ShapeDtypeStruct((rows,cols//2),BF)]*2,
        compiler_params=pltpu.CompilerParams(vmem_limit_bytes=40<<20,dimension_semantics=("arbitrary",)),
        cost_estimate=pl.CostEstimate(flops=2*rows*width*cols,bytes_accessed=2*(rows*width+width*cols+rows*cols),transcendentals=0),
        name="mix",
    )(ctl,x,w,cos,sin)

def shuffle(x,count,per,share):
    rows=x.shape[0]
    return x.reshape(rows,2,count,per,share).transpose(0,1,3,2,4).reshape(x.shape)

def unshuffle(x,count,per,share):
    rows=x.shape[0]
    return x.reshape(rows,2,per,count,share).transpose(0,1,3,2,4).reshape(x.shape)

def fold_rows(x,per):
    rows,cols=x.shape
    return x.reshape(per,rows//per,cols).transpose(1,0,2).reshape(rows//per,per*cols)

def unfold_rows(x,per,share):
    count=x.shape[0]//share
    cols=x.shape[1]//per
    return x.reshape(count,share,per,cols).transpose(0,2,1,3).reshape(count*per*share,cols)

def swap_cores(x):
    return lax.ppermute(x,"dim",[(0,1),(1,0)])

def join(pos,own,recv,axis=1):
    return jnp.where(pos==0,jnp.concatenate([own,recv],axis),jnp.concatenate([recv,own],axis))

def join_parts(pos,own,recv):
    share=own.shape[1]//3
    pieces=[]
    for s in range(3):
        pieces.append(own[:,s*share:(s+1)*share])
        pieces.append(recv[:,s*share:(s+1)*share])
    flip=[pieces[i^1] for i in range(6)]
    return jnp.where(pos==0,jnp.concatenate(pieces,1),jnp.concatenate(flip,1))

def body(tokens,doc_lengths,pair_index,target_bank,mixer_in,mixer_out,expand,contract,norm_params,*rest):
    slices=lax.axis_size("dim")
    if slices!=2 or doc_lengths.shape[1]!=2:
        return body_general(tokens,doc_lengths,pair_index,target_bank,mixer_in,mixer_out,expand,contract,norm_params,*rest)
    (mixer_in_moment,mixer_out_moment,expand_moment,contract_moment,norm_moment,
     mixer_in_average,mixer_out_average,expand_average,contract_average,norm_average)=rest
    local_rows,model_width=tokens.shape
    group_rows=local_rows*slices
    pos=lax.axis_index("dim")
    doc_count=2
    gather=lambda w,axis=0: lax.all_gather(w[0].astype(BF),("dp","dim"),axis=axis,tiled=True)
    w_mix=gather(mixer_in)
    share_rows=mixer_out.shape[1]
    per=contract.shape[1]//share_rows
    count=model_width//share_rows
    hidden_width=contract.shape[1]*count
    exp_cols=shuffle(expand[0].astype(BF),count,per,share_rows)
    con_cols=fold_rows(contract[0].astype(BF),per)
    norm_cols=jnp.pad(norm_params[0].astype(BF),((0,share_rows-4),(0,128-share_rows)))
    bundle=jnp.concatenate([exp_cols,con_cols,mixer_out[0].astype(BF),norm_cols],1)
    bundle=lax.all_gather(bundle,("dp","dim"),axis=0,tiled=True)
    at1=2*hidden_width
    at2=at1+per*model_width
    at3=at2+model_width
    w_norm=bundle[:,at3:].reshape(count,share_rows,128)[:,0:4,0:share_rows].transpose(1,0,2).reshape(4,model_width)
    lengths=doc_lengths[0]
    e0=lengths[0]
    e1=lengths[0]+lengths[1]
    ctl=jnp.stack([pos.astype(jnp.int32),e0,e1])
    ids=jnp.arange(group_rows,dtype=jnp.int32)
    seg=(ids>=e0).astype(jnp.int32)+(ids>=e1).astype(jnp.int32)
    begin=jnp.where(seg==0,0,jnp.where(seg==1,e0,e1))
    lane=jnp.arange(128,dtype=jnp.int32)
    frequency=jnp.power(1000.0,-(2*(lane%32)).astype(F32)/HEAD)
    angles=(ids-begin).astype(F32)[:,None]*frequency[None,:]
    cos=jnp.cos(angles)
    sin=jnp.sin(angles)*jnp.where((lane%64)<32,-1.0,1.0)[None,:]
    cos_own=lax.dynamic_slice_in_dim(cos,pos*local_rows,local_rows,0)
    sin_own=lax.dynamic_slice_in_dim(sin,pos*local_rows,local_rows,0)
    own,oth=mix(ctl,tokens,w_mix,cos_own,sin_own)
    recv=swap_cores(oth)
    pick=(pair_index[:,None]==jnp.arange(target_bank.shape[0],dtype=jnp.int32)[None,:]).astype(BF)
    some=matmul(pick,target_bank)
    targets=jnp.pad(join(pos,some,swap_cores(some)),((0,6),(0,0)))
    o_own,o_oth,lse=attend_fwd(ctl,own,recv)
    o_recv=swap_cores(o_oth)
    norm_gains=jnp.pad(w_norm.astype(F32),((0,4),(0,0)))
    u1,u2,rs,y_low,hidden,factors,pooled=ffn_fwd(ctl,o_own,o_recv,tokens,bundle,norm_gains,hidden_width)
    embeds,grad_m_low,grad_both,grad_first,grad_a_low,d_own,d_oth,grad_norm=ffn_bwd(
        ctl,lengths.astype(F32),pooled,swap_cores(pooled),targets,u1,u2,rs,factors,bundle,norm_gains)
    share=model_width//2
    embeddings=lax.dynamic_slice(embeds,(0,pos*share),(doc_count,share))
    d_recv=swap_cores(d_oth)
    grad_exp=inner_rows(y_low,grad_both)
    grad_con=inner_rows(hidden,grad_m_low)
    grad_out=join(pos,inner_rows(o_own,grad_a_low),inner_rows(o_recv,grad_a_low),0)
    scatter=lambda g: lax.psum_scatter(g,("dp","dim"),scatter_dimension=0,tiled=True).astype(F32)
    grad_norm=grad_norm[0:4].reshape(4,count,share_rows).transpose(1,0,2)
    grad_norm=jnp.pad(grad_norm,((0,0),(0,share_rows-4),(0,128-share_rows))).reshape(model_width,128)
    fold_con=[grad_con[j*model_width:(j+1)*model_width].astype(BF) for j in range(per)]
    terms=jnp.concatenate([grad_exp.astype(BF),*fold_con,grad_out.astype(BF),grad_norm.astype(BF)],1)
    terms,d_own,d_recv=lax.optimization_barrier((terms,d_own,d_recv))
    sums=scatter(terms)
    g_own,g_oth=attend_bwd(ctl,own,recv,d_own,d_recv,o_own,o_oth,lse,cos,sin)
    grad_mixed=join_parts(pos,unpair(g_own),unpair(swap_cores(g_oth)))
    grad_mix=inner_rows(tokens,grad_mixed)
    token_grads=grad_first+inner_cols(grad_mixed,w_mix)
    grad_mix=grad_mix.astype(BF)
    grad_mix,sums=lax.optimization_barrier((grad_mix,sums))
    sum_mix=scatter(grad_mix)
    sum_exp=unshuffle(sums[:,0:at1],count,per,share_rows)
    sum_con=unfold_rows(sums[:,at1:at2],per,share_rows)
    sum_out=sums[:,at2:at3]
    sum_norm=sums[0:4,at3:at3+share_rows]
    total_rows=group_rows*lax.axis_size("dp")
    matrix_rate=1.0/math.sqrt(total_rows)
    norm_rate=0.3/math.sqrt(total_rows)
    grads=[g[None] for g in (sum_mix,sum_out,sum_exp,sum_con,sum_norm)]
    weights=(mixer_in,mixer_out,expand,contract,norm_params)
    moments=(mixer_in_moment,mixer_out_moment,expand_moment,contract_moment,norm_moment)
    averages=(mixer_in_average,mixer_out_average,expand_average,contract_average,norm_average)
    rates=(matrix_rate,matrix_rate,matrix_rate,matrix_rate,norm_rate)
    results=[advance(weights[k],moments[k],averages[k],grads[k],rates[k]) for k in range(5)]
    return (embeddings,token_grads,*grads,*[results[k][f] for f in range(4) for k in range(5)])

def unpair(g):
    rows,width=g.shape
    pairs=width//384
    return jnp.concatenate([g[:,p*384+s*128:p*384+(s+1)*128] for s in range(3) for p in range(pairs)],1)


def solution(mesh):
    placed = (
        P(("dp", "dim"), None),
        P("dp", None),
        P("dp"),
        P(None, "dim"),
        P(None, ("dp", "dim"), None),
        P(None, ("dp", "dim"), None),
        P(None, ("dp", "dim"), None),
        P(None, ("dp", "dim"), None),
        P(None, None, ("dp", "dim")),
        P(None, ("dp", "dim"), None),
        P(None, ("dp", "dim"), None),
        P(None, ("dp", "dim"), None),
        P(None, ("dp", "dim"), None),
        P(None, None, ("dp", "dim")),
        P(None, ("dp", "dim"), None),
        P(None, ("dp", "dim"), None),
        P(None, ("dp", "dim"), None),
        P(None, ("dp", "dim"), None),
        P(None, None, ("dp", "dim")),
    )
    return jax.shard_map(
        body,
        mesh=mesh,
        in_specs=placed,
        out_specs=(
            P("dp", "dim"),
            P(("dp", "dim"), None),
            P(None, ("dp", "dim"), None),
            P(None, ("dp", "dim"), None),
            P(None, ("dp", "dim"), None),
            P(None, ("dp", "dim"), None),
            P(None, None, ("dp", "dim")),
            P(None, ("dp", "dim"), None),
            P(None, ("dp", "dim"), None),
            P(None, ("dp", "dim"), None),
            P(None, ("dp", "dim"), None),
            P(None, None, ("dp", "dim")),
            P(None, ("dp", "dim"), None),
            P(None, ("dp", "dim"), None),
            P(None, ("dp", "dim"), None),
            P(None, ("dp", "dim"), None),
            P(None, None, ("dp", "dim")),
            P(None, ("dp", "dim"), None),
            P(None, ("dp", "dim"), None),
            P(None, ("dp", "dim"), None),
            P(None, ("dp", "dim"), None),
            P(None, None, ("dp", "dim")),
            P(None, ("dp", "dim"), None),
            P(None, ("dp", "dim"), None),
            P(None, ("dp", "dim"), None),
            P(None, ("dp", "dim"), None),
            P(None, None, ("dp", "dim")),
        ),
        check_vma=False,
    )
```

```python
import math

import jax
import jax.numpy as jnp
from jax import lax
from jax.experimental import pallas as pl
from jax.experimental.pallas import tpu as pltpu
from jax.sharding import PartitionSpec as P

HEAD = 64


NORM_EPSILON = 1e-05
COSINE_EPSILON = 1e-06
MOMENTUM = 0.5
AVERAGE_DECAY = 0.5
PRECISE = lax.Precision.HIGHEST
MASKED = -1e30


def matmul(left_op, right_op):
    return jnp.dot(left_op, right_op, preferred_element_type=jnp.float32)


def matmul_exact(left_op, right_op):
    return jnp.dot(left_op, right_op, precision=PRECISE, preferred_element_type=jnp.float32)


def inner_rows(left_op, right_op):
    return lax.dot_general(
        left_op, right_op, (((0,), (0,)), ((), ())), preferred_element_type=jnp.float32
    )


def inner_cols(left_op, right_op):
    return lax.dot_general(
        left_op, right_op, (((1,), (1,)), ((), ())), preferred_element_type=jnp.float32
    )


def rotate(values, cosines, sines):
    row_count = values.shape[0]
    shaped = values.reshape(row_count, -1, 2, HEAD // 2)
    former = shaped[:, :, 0, :]
    latter = shaped[:, :, 1, :]
    cosine_b = cosines[:, None, :]
    sine_b = sines[:, None, :]
    turned = jnp.stack(
        [former * cosine_b - latter * sine_b, latter * cosine_b + former * sine_b], axis=2
    )
    return turned.reshape(values.shape)


def rotate_back(grads_in, cosines, sines):
    row_count = grads_in.shape[0]
    shaped = grads_in.reshape(row_count, -1, 2, HEAD // 2)
    former = shaped[:, :, 0, :]
    latter = shaped[:, :, 1, :]
    cosine_b = cosines[:, None, :]
    sine_b = sines[:, None, :]
    turned = jnp.stack(
        [former * cosine_b + latter * sine_b, latter * cosine_b - former * sine_b], axis=2
    )
    return turned.reshape(grads_in.shape)


def normalize(summed, gain_vec, bias_vec):
    centred = summed - jnp.mean(summed, axis=1, keepdims=True)
    scaling = lax.rsqrt(jnp.mean(centred * centred, axis=1, keepdims=True) + NORM_EPSILON)
    return centred * scaling * gain_vec + bias_vec


def normalize_back(grad_in, summed, gain_vec):
    centred = summed - jnp.mean(summed, axis=1, keepdims=True)
    scaling = lax.rsqrt(jnp.mean(centred * centred, axis=1, keepdims=True) + NORM_EPSILON)
    unit = centred * scaling
    grad_unit = grad_in * gain_vec
    grad_sum = scaling * (
        grad_unit
        - jnp.mean(grad_unit, axis=1, keepdims=True)
        - unit * jnp.mean(grad_unit * unit, axis=1, keepdims=True)
    )
    return (grad_sum, jnp.sum(grad_in * unit, axis=0), jnp.sum(grad_in, axis=0))


def flatten(stacked):
    return stacked.transpose(1, 0, 2).reshape(stacked.shape[1], -1)


def attend(q_rot, all_keys, all_values, same_doc):
    head_count = q_rot.shape[1] // HEAD

    def one_head(head_pos):
        offset = head_pos * HEAD
        query_part = lax.dynamic_slice_in_dim(q_rot, offset, HEAD, 1)
        key_part = lax.dynamic_slice_in_dim(all_keys, offset, HEAD, 1)
        value_part = lax.dynamic_slice_in_dim(all_values, offset, HEAD, 1)
        scores = jnp.where(same_doc, inner_cols(query_part, key_part) * 0.125, MASKED)
        row_max = jnp.max(scores, axis=1, keepdims=True)
        exponent = jnp.exp(scores - row_max)
        row_total = jnp.sum(exponent, axis=1, keepdims=True)
        attn_probs = (exponent / row_total).astype(jnp.bfloat16)
        return (matmul(attn_probs, value_part), (row_max + jnp.log(row_total))[:, 0])

    outputs, log_totals = lax.map(one_head, jnp.arange(head_count, dtype=jnp.int32))
    return (flatten(outputs), log_totals)


def attend_back(q_rot, all_keys, all_values, same_doc, grad_out, log_totals):
    head_count = q_rot.shape[1] // HEAD

    def one_head(pack):
        head_pos, log_total = pack
        offset = head_pos * HEAD
        query_part = lax.dynamic_slice_in_dim(q_rot, offset, HEAD, 1)
        key_part = lax.dynamic_slice_in_dim(all_keys, offset, HEAD, 1)
        value_part = lax.dynamic_slice_in_dim(all_values, offset, HEAD, 1)
        grad_part = lax.dynamic_slice_in_dim(grad_out, offset, HEAD, 1)
        scores = jnp.where(same_doc, inner_cols(query_part, key_part) * 0.125, MASKED)
        attn_probs = jnp.exp(scores - log_total[:, None])
        grad_probs = inner_cols(grad_part, value_part)
        row_dot = jnp.sum(attn_probs * grad_probs, axis=1, keepdims=True)
        grad_scores = (attn_probs * (grad_probs - row_dot)).astype(jnp.bfloat16)
        grad_query = matmul(grad_scores, key_part) * 0.125
        grad_key = inner_rows(grad_scores, query_part) * 0.125
        grad_value = inner_rows(attn_probs.astype(jnp.bfloat16), grad_part)
        return (grad_query, grad_key, grad_value)

    mapped = lax.map(one_head, (jnp.arange(head_count, dtype=jnp.int32), log_totals))
    return (flatten(mapped[0]), flatten(mapped[1]), flatten(mapped[2]))


def advance(weight, moment, average, grad_in, rate):
    moment_next = MOMENTUM * moment + grad_in
    weight_next = weight - rate * (grad_in + MOMENTUM * moment_next)
    average_next = AVERAGE_DECAY * average + (1.0 - AVERAGE_DECAY) * weight_next
    return (weight_next, moment_next, average_next, weight_next.astype(jnp.bfloat16))


def body_general(
    tokens,
    doc_lengths,
    pair_index,
    target_bank,
    mixer_in,
    mixer_out,
    expand,
    contract,
    norm_params,
    mixer_in_moment,
    mixer_out_moment,
    expand_moment,
    contract_moment,
    norm_moment,
    mixer_in_average,
    mixer_out_average,
    expand_average,
    contract_average,
    norm_average,
):
    local_rows, model_width = tokens.shape
    slices = lax.axis_size("dim")
    group_rows = local_rows * slices
    position = lax.axis_index("dim")
    layer_count = mixer_in.shape[0]
    doc_count = doc_lengths.shape[1]
    lengths = doc_lengths[0]
    doc_ends = jnp.cumsum(lengths)
    doc_starts = doc_ends - lengths
    row_ids = position * local_rows + jnp.arange(local_rows, dtype=jnp.int32)
    key_ids = jnp.arange(group_rows, dtype=jnp.int32)
    seg_rows = jnp.sum((row_ids[:, None] >= doc_ends[None, :]).astype(jnp.int32), axis=1)
    seg_keys = jnp.sum((key_ids[:, None] >= doc_ends[None, :]).astype(jnp.int32), axis=1)
    first_rows = jnp.concatenate([doc_starts, doc_ends[-1:]])
    segment_ids = jnp.arange(doc_count + 1, dtype=jnp.int32)
    row_begin = jnp.sum(
        jnp.where(seg_rows[:, None] == segment_ids[None, :], first_rows[None, :], 0), axis=1
    )
    frequency = jnp.power(1000.0, -jnp.arange(0, HEAD, 2).astype(jnp.float32) / HEAD)
    angles = (row_ids - row_begin).astype(jnp.float32)[:, None] * frequency[None, :]
    cosines = jnp.cos(angles)
    sines = jnp.sin(angles)
    same_doc = seg_rows[:, None] == seg_keys[None, :]
    stream = tokens.astype(jnp.float32)
    layer_pos = 0
    layer_weights = (
        lax.all_gather(mixer_in[layer_pos].astype(jnp.bfloat16), ("dp", "dim"), axis=0, tiled=True),
        lax.all_gather(
            mixer_out[layer_pos].astype(jnp.bfloat16), ("dp", "dim"), axis=0, tiled=True
        ),
        lax.all_gather(expand[layer_pos].astype(jnp.bfloat16), ("dp", "dim"), axis=0, tiled=True),
        lax.all_gather(contract[layer_pos].astype(jnp.bfloat16), ("dp", "dim"), axis=0, tiled=True),
        lax.all_gather(
            norm_params[layer_pos].astype(jnp.bfloat16), ("dp", "dim"), axis=1, tiled=True
        ),
    )
    w_mix, w_out, w_exp, w_con, w_norm = layer_weights
    norm_gains = w_norm.astype(jnp.float32)
    x_low = stream.astype(jnp.bfloat16)
    mixed = matmul(x_low, w_mix)
    q_rot = rotate(mixed[:, 0:model_width], cosines, sines).astype(jnp.bfloat16)
    k_rot = rotate(mixed[:, model_width : 2 * model_width], cosines, sines).astype(jnp.bfloat16)
    v_low = mixed[:, 2 * model_width : 3 * model_width].astype(jnp.bfloat16)
    all_keys = lax.all_gather(k_rot, "dim", axis=0, tiled=True)
    all_values = lax.all_gather(v_low, "dim", axis=0, tiled=True)
    attended, log_totals = attend(q_rot, all_keys, all_values, same_doc)
    att_low = attended.astype(jnp.bfloat16)
    first_sum = stream + matmul(att_low, w_out)
    normed = normalize(first_sum, norm_gains[0], norm_gains[1])
    y_low = normed.astype(jnp.bfloat16)
    gate_up = matmul(y_low, w_exp)
    half = gate_up.shape[1] // 2
    hidden = (jax.nn.silu(gate_up[:, 0:half]) * gate_up[:, half : 2 * half]).astype(jnp.bfloat16)
    second_sum = normed + matmul(hidden, w_con)
    saved = [
        (
            stream,
            layer_weights,
            q_rot,
            k_rot,
            v_low,
            all_keys,
            all_values,
            log_totals,
            attended,
            att_low,
            first_sum,
            normed,
            y_low,
            gate_up,
            hidden,
            second_sum,
        )
    ]
    stream = normalize(second_sum, norm_gains[2], norm_gains[3])
    member = (seg_rows[None, :] == jnp.arange(doc_count, dtype=jnp.int32)[:, None]).astype(
        jnp.float32
    )
    partial_value = matmul_exact(member, stream)
    pooled = lax.psum_scatter(partial_value, "dim", scatter_dimension=1, tiled=True)
    length_f = lengths.astype(jnp.float32)
    embeddings = pooled / length_f[:, None]
    share = embeddings.shape[1]
    pick = (
        pair_index[:, None] == jnp.arange(target_bank.shape[0], dtype=jnp.int32)[None, :]
    ).astype(jnp.bfloat16)
    targets = matmul(pick, target_bank)
    feature_ids = position * share + jnp.arange(share, dtype=jnp.int32)
    cuts = jnp.array(
        [model_width // 12, model_width // 6, model_width // 3, 2 * model_width // 3, model_width],
        dtype=jnp.int32,
    )
    masks = (feature_ids[None, :] < cuts[:, None]).astype(jnp.float32)
    cross = matmul_exact(embeddings * targets, masks.T)
    own = matmul_exact(embeddings * embeddings, masks.T)
    other = matmul_exact(targets * targets, masks.T)
    cross, own, other = lax.psum((cross, own, other), "dim")
    own_root = lax.rsqrt(own + COSINE_EPSILON)
    other_root = lax.rsqrt(other + COSINE_EPSILON)
    cosine = cross * own_root * other_root
    coef_target = -length_f[:, None] * own_root * other_root
    coef_self = length_f[:, None] * cosine * own_root * own_root
    grad_emb = (
        matmul_exact(coef_target, masks) * targets + matmul_exact(coef_self, masks) * embeddings
    )
    grad_full = lax.all_gather(grad_emb, "dim", axis=1, tiled=True)
    spread_rows = member / length_f[:, None]
    grad_stream = lax.dot_general(
        spread_rows,
        grad_full,
        (((0,), (0,)), ((), ())),
        precision=PRECISE,
        preferred_element_type=jnp.float32,
    )
    grad_list = [None] * layer_count
    for layer_pos in reversed(range(layer_count)):
        (
            layer_input,
            layer_weights,
            q_rot,
            k_rot,
            v_low,
            all_keys,
            all_values,
            log_totals,
            attended,
            att_low,
            first_sum,
            normed,
            y_low,
            gate_up,
            hidden,
            second_sum,
        ) = saved[layer_pos]
        w_mix = lax.all_gather(
            mixer_in[layer_pos].astype(jnp.bfloat16), ("dp", "dim"), axis=0, tiled=True
        )
        w_out = lax.all_gather(
            mixer_out[layer_pos].astype(jnp.bfloat16), ("dp", "dim"), axis=0, tiled=True
        )
        w_exp = lax.all_gather(
            expand[layer_pos].astype(jnp.bfloat16), ("dp", "dim"), axis=0, tiled=True
        )
        w_con = lax.all_gather(
            contract[layer_pos].astype(jnp.bfloat16), ("dp", "dim"), axis=0, tiled=True
        )
        w_norm = lax.all_gather(
            norm_params[layer_pos].astype(jnp.bfloat16), ("dp", "dim"), axis=1, tiled=True
        )
        norm_gains = w_norm.astype(jnp.float32)
        grad_second, grad_gain2, grad_bias2 = normalize_back(grad_stream, second_sum, norm_gains[2])
        grad_m_low = grad_second.astype(jnp.bfloat16)
        grad_con = inner_rows(hidden, grad_m_low)
        grad_hidden = inner_cols(grad_m_low, w_con)
        half = gate_up.shape[1] // 2
        gate_part = gate_up[:, 0:half]
        up_part = gate_up[:, half : 2 * half]
        sigmoid_gate = jax.nn.sigmoid(gate_part)
        activated = gate_part * sigmoid_gate
        grad_gate = grad_hidden * up_part * sigmoid_gate * (1.0 + gate_part * (1.0 - sigmoid_gate))
        grad_up = grad_hidden * activated
        grad_both = jnp.concatenate([grad_gate, grad_up], axis=1).astype(jnp.bfloat16)
        grad_exp = inner_rows(y_low, grad_both)
        grad_normed = grad_second + inner_cols(grad_both, w_exp)
        grad_first, grad_gain1, grad_bias1 = normalize_back(grad_normed, first_sum, norm_gains[0])
        grad_a_low = grad_first.astype(jnp.bfloat16)
        grad_out = inner_rows(att_low, grad_a_low)
        grad_attended = inner_cols(grad_a_low, w_out).astype(jnp.bfloat16)
        keys_back, values_back = (
            lax.all_gather(k_rot, "dim", axis=0, tiled=True),
            lax.all_gather(v_low, "dim", axis=0, tiled=True),
        )
        grad_query, grad_key_all, grad_value_all = attend_back(
            q_rot, keys_back, values_back, same_doc, grad_attended, log_totals
        )
        grad_kv = lax.psum_scatter(
            jnp.concatenate([grad_key_all, grad_value_all], axis=1).astype(jnp.bfloat16),
            "dim",
            scatter_dimension=0,
            tiled=True,
        ).astype(jnp.float32)
        grad_mixed = jnp.concatenate(
            [
                rotate_back(grad_query, cosines, sines),
                rotate_back(grad_kv[:, 0:model_width], cosines, sines),
                grad_kv[:, model_width : 2 * model_width],
            ],
            axis=1,
        ).astype(jnp.bfloat16)
        x_low = layer_input.astype(jnp.bfloat16)
        grad_mix = inner_rows(x_low, grad_mixed)
        grad_stream = grad_first + inner_cols(grad_mixed, w_mix)
        grad_norm = jnp.stack([grad_gain1, grad_bias1, grad_gain2, grad_bias2])
        grad_list[layer_pos] = (
            lax.psum_scatter(grad_mix, ("dp", "dim"), scatter_dimension=0, tiled=True),
            lax.psum_scatter(grad_out, ("dp", "dim"), scatter_dimension=0, tiled=True),
            lax.psum_scatter(grad_exp, ("dp", "dim"), scatter_dimension=0, tiled=True),
            lax.psum_scatter(grad_con, ("dp", "dim"), scatter_dimension=0, tiled=True),
            lax.psum_scatter(grad_norm, ("dp", "dim"), scatter_dimension=1, tiled=True),
        )
    total_rows = group_rows * lax.axis_size("dp")
    matrix_rate = 1.0 / math.sqrt(total_rows)
    norm_rate = 0.3 / math.sqrt(total_rows)
    grads = [jnp.stack([grad_list[0][kind]]) for kind in range(5)]
    weights = (mixer_in, mixer_out, expand, contract, norm_params)
    moments = (mixer_in_moment, mixer_out_moment, expand_moment, contract_moment, norm_moment)
    averages = (mixer_in_average, mixer_out_average, expand_average, contract_average, norm_average)
    rates = (matrix_rate, matrix_rate, matrix_rate, matrix_rate, norm_rate)
    results = [
        advance(weights[kind], moments[kind], averages[kind], grads[kind], rates[kind])
        for kind in range(5)
    ]
    return (
        embeddings,
        grad_stream,
        grads[0],
        grads[1],
        grads[2],
        grads[3],
        grads[4],
        results[0][0],
        results[1][0],
        results[2][0],
        results[3][0],
        results[4][0],
        results[0][1],
        results[1][1],
        results[2][1],
        results[3][1],
        results[4][1],
        results[0][2],
        results[1][2],
        results[2][2],
        results[3][2],
        results[4][2],
        results[0][3],
        results[1][3],
        results[2][3],
        results[3][3],
        results[4][3],
    )


NEG=-1e30
BQ=512
ROWS=256
BK=512
F32=jnp.float32
BF=jnp.bfloat16

def nt(a,b): return lax.dot_general(a,b,(((1,),(1,)),((),())),preferred_element_type=F32)
def nn(a,b): return jnp.dot(a,b,preferred_element_type=F32)

def fill_masks(e0,e1,kaug,q0,q1,rows,pad):
    r=lax.broadcasted_iota(jnp.int32,(rows+pad,128),0)
    l=lax.broadcasted_iota(jnp.int32,(rows+pad,128),1)
    seg=(r>=e0).astype(jnp.int32)+(r>=e1).astype(jnp.int32)
    kaug[:,128:256]=jnp.where((l<3)&(l!=seg),NEG,0.0).astype(BF)
    qm=jnp.where(l==seg,1.0,0.0).astype(BF)[0:rows]
    q0[:,128:256]=qm
    q1[:,128:256]=qm

def key_range(i,e0,e1):
    first=i*BQ
    last=jnp.minimum(first+BQ,e1)-1
    lo=jnp.where(first>=e0,e0,0)
    hi=jnp.where(last>=e0,e1,e0)
    base=(lo//128)*128
    return pl.multiple_of(base,128),(hi-base+BK-1)//BK

def fwd_kernel(ctl,qo,ko,vo,qr,kr,vr,oo,ox,lse,kaug,q0,q1,vt):
    rows=kaug.shape[0]-BK
    half=rows//2
    pos,e0,e1=ctl[0],ctl[1],ctl[2]
    p=pl.program_id(0)
    @pl.when(p==0)
    def _():
        fill_masks(e0,e1,kaug,q0,q1,rows,BK)
        kaug[rows:,0:128]=jnp.zeros((BK,128),BF)
        vt[:,:]=jnp.where(lax.broadcasted_iota(jnp.int32,vt.shape,0)%80>=64,1.0,0.0).astype(BF)
    lane=lax.broadcasted_iota(jnp.int32,(half,128),1)
    for own,(q,k,v) in ((True,(qo,ko,vo)),(False,(qr,kr,vr))):
        at=pl.multiple_of((pos if own else 1-pos)*half,half)
        scaled=q[...]*jnp.asarray(0.125,BF)
        zero=jnp.zeros_like(scaled)
        q0[pl.ds(at,half),0:128]=jnp.where(lane<64,scaled,zero)
        q1[pl.ds(at,half),0:128]=jnp.where(lane<64,zero,scaled)
        kaug[pl.ds(at,half),0:128]=k[...]
        turned=v[...].T
        vt[0:64,pl.ds(at,half)]=turned[0:64]
        vt[80:144,pl.ds(at,half)]=turned[64:128]
    def qblock(i,_):
        r0=pl.multiple_of(i*BQ,BQ)
        base,count=key_range(i,e0,e1)
        qs=(q0[pl.ds(r0,BQ),:],q1[pl.ds(r0,BQ),:])
        def step(j,carry):
            k0=pl.multiple_of(base+j*BK,128)
            kb=kaug[pl.ds(k0,BK),:]
            scores=[nt(kb,qs[h]) for h in range(2)]
            out=[]
            for h in range(2):
                m,acc=carry[h]
                mn=jnp.maximum(m,jnp.max(scores[h],axis=0,keepdims=True))
                pt=jnp.exp(scores[h]-mn).astype(BF)
                acc=acc*jnp.exp(m-mn)+nn(vt[80*h:80*h+80,pl.ds(k0,BK)],pt)
                out.append((mn,acc))
            return tuple(out)
        init=(jnp.full((1,BQ),-jnp.inf,F32),jnp.zeros((80,BQ),F32))
        res=lax.fori_loop(0,count,step,(init,init))
        outs=[]
        for h in range(2):
            m,acc=res[h]
            l=acc[64:65]
            outs.append(acc[0:64]/l)
            lse[0,h:h+1,pl.ds(r0,BQ)]=m+jnp.log(l)
        ob=jnp.concatenate(outs,axis=0).T.astype(BF)
        put(i,ob)
        return 0
    def put(i,ob):
        local=i*BQ-pos*half
        @pl.when((local>=0)&(local<half))
        def _(): oo[pl.ds(pl.multiple_of(local,BQ),BQ),:]=ob
        @pl.when((local<0)|(local>=half))
        def _(): ox[pl.ds(pl.multiple_of(i*BQ-(1-pos)*half,BQ),BQ),:]=ob
    used=(e1+BQ-1)//BQ
    lax.fori_loop(0,used,qblock,0)
    def blank(i,_):
        r0=pl.multiple_of(i*BQ,BQ)
        lse[0,:,pl.ds(r0,BQ)]=jnp.zeros((8,BQ),F32)
        put(i,jnp.zeros((BQ,128),BF))
        return 0
    lax.fori_loop(used,rows//BQ,blank,0)

def attend_fwd(ctl,own,recv):
    half,width=own.shape
    pairs=width//384
    rows=2*half
    sp=[pl.BlockSpec((half,128),(lambda p,c,s=s:(0,s*pairs+p))) for s in range(3)]
    outw=pairs*128
    return pl.pallas_call(fwd_kernel,
        grid_spec=pltpu.PrefetchScalarGridSpec(num_scalar_prefetch=1,grid=(pairs,),
          in_specs=sp+sp,
          out_specs=[pl.BlockSpec((half,128),lambda p,c:(0,p))]*2+[pl.BlockSpec((1,8,rows),lambda p,c:(p,0,0))],
          scratch_shapes=[pltpu.VMEM((rows+BK,256),BF),pltpu.VMEM((rows,256),BF),pltpu.VMEM((rows,256),BF),pltpu.VMEM((160,rows+BK),BF)]),
        out_shape=[jax.ShapeDtypeStruct((half,outw),BF)]*2+[jax.ShapeDtypeStruct((pairs,8,rows),F32)],
        compiler_params=pltpu.CompilerParams(vmem_limit_bytes=60<<20,dimension_semantics=("arbitrary",)),
        cost_estimate=pl.CostEstimate(flops=4*rows*rows*64*2*pairs//2,bytes_accessed=10*half*width,transcendentals=rows*rows*pairs),
        name="attend_fwd",
    )(ctl,own,own,own,recv,recv,recv)

def bwd_kernel(ctl,qo,ko,vo,qr,kr,vr,do_o,do_r,oo,ox,lse,cos,sin,go,gx,kaug,q0,q1,vs,d0,d1,kt,delta,dk,dv):
    rows=kaug.shape[0]-BK
    half=rows//2
    pos,e0,e1=ctl[0],ctl[1],ctl[2]
    p=pl.program_id(0)
    @pl.when(p==0)
    def _():
        fill_masks(e0,e1,kaug,q0,q1,rows,BK)
        kaug[rows:,0:128]=jnp.zeros((BK,128),BF)
        vs[rows:,:]=jnp.zeros((BK,128),BF)
        kt[:,rows:]=jnp.zeros((128,BK),BF)
    lane=lax.broadcasted_iota(jnp.int32,(half,128),1)
    pick_r=lax.broadcasted_iota(jnp.int32,(16,128),0)
    pick_l=lax.broadcasted_iota(jnp.int32,(16,128),1)
    pick=jnp.where(pick_l//64==pick_r,1.0,0.0).astype(BF)
    for own,(q,k,v,d,o) in ((True,(qo,ko,vo,do_o,oo)),(False,(qr,kr,vr,do_r,ox))):
        at=pl.multiple_of((pos if own else 1-pos)*half,half)
        scaled=q[...]*jnp.asarray(0.125,BF)
        zero=jnp.zeros_like(scaled)
        q0[pl.ds(at,half),0:128]=jnp.where(lane<64,scaled,zero)
        q1[pl.ds(at,half),0:128]=jnp.where(lane<64,zero,scaled)
        kb=k[...]
        kaug[pl.ds(at,half),0:128]=kb
        kt[:,pl.ds(at,half)]=kb.T
        vs[pl.ds(at,half),:]=v[...]
        db=d[...]
        d0[pl.ds(at,half),:]=jnp.where(lane<64,db,zero)
        d1[pl.ds(at,half),:]=jnp.where(lane<64,zero,db)
        prod=db.astype(F32)*o[...].astype(F32)
        hi=prod.astype(BF)
        lo=(prod-hi.astype(F32)).astype(BF)
        delta[:,pl.ds(at,half)]=nt(pick,hi)+nt(pick,lo)
    dk[...]=jnp.zeros_like(dk)
    dv[...]=jnp.zeros_like(dv)
    def spread(i,col,val):
        local=i*ROWS-pos*half
        @pl.when((local>=0)&(local<half))
        def _(): go[pl.ds(pl.multiple_of(local,ROWS),ROWS),col*128:(col+1)*128]=val
        @pl.when((local<0)|(local>=half))
        def _(): gx[pl.ds(pl.multiple_of(i*ROWS-(1-pos)*half,ROWS),ROWS),col*128:(col+1)*128]=val
    def unturn(x,r0):
        ln=lax.broadcasted_iota(jnp.int32,x.shape,1)
        swapped=jnp.where((ln%64)<32,pltpu.roll(x,96,1),pltpu.roll(x,32,1))
        return x*cos[pl.ds(r0,ROWS),:]-swapped*sin[pl.ds(r0,ROWS),:]
    def qblock(i,_):
        r0=pl.multiple_of(i*BQ,BQ)
        base,count=key_range(i,e0,e1)
        qs=(q0[pl.ds(r0,BQ),:],q1[pl.ds(r0,BQ),:])
        ds_=(d0[pl.ds(r0,BQ),:],d1[pl.ds(r0,BQ),:])
        ls=[lse[0,h:h+1,pl.ds(r0,BQ)] for h in range(2)]
        de=[delta[h:h+1,pl.ds(r0,BQ)] for h in range(2)]
        def step(j,carry):
            k0=pl.multiple_of(base+j*BK,128)
            kb=kaug[pl.ds(k0,BK),:]
            vb=vs[pl.ds(k0,BK),:]
            both=range(2)
            st=[nt(kb,qs[h]) for h in both]
            dpt=[nt(vb,ds_[h]) for h in both]
            pt=[jnp.exp(st[h]-ls[h]) for h in both]
            dst=[(pt[h]*(dpt[h]-de[h])).astype(BF) for h in both]
            pb=[pt[h].astype(BF) for h in both]
            dv[pl.ds(k0,BK),:]+=nn(pb[0],ds_[0])+nn(pb[1],ds_[1])
            dk[pl.ds(k0,BK),:]+=nn(dst[0],qs[0][:,0:128])+nn(dst[1],qs[1][:,0:128])
            out=[carry[h]+nn(kt[64*h:64*h+64,pl.ds(k0,BK)],dst[h]) for h in both]
            return tuple(out)
        init=jnp.zeros((64,BQ),F32)
        res=lax.fori_loop(0,count,step,(init,init))
        dq=jnp.concatenate(res,axis=0).T*0.125
        for t in range(BQ//ROWS):
            at=pl.multiple_of(r0+t*ROWS,ROWS)
            spread(i*(BQ//ROWS)+t,0,unturn(dq[t*ROWS:(t+1)*ROWS],at).astype(BF))
        return 0
    used=(e1+BQ-1)//BQ
    lax.fori_loop(0,used,qblock,0)
    def blank(i,_):
        spread(i,0,jnp.zeros((ROWS,128),BF))
        return 0
    lax.fori_loop(used*(BQ//ROWS),rows//ROWS,blank,0)
    def last(i,_):
        r0=pl.multiple_of(i*ROWS,ROWS)
        spread(i,1,unturn(dk[pl.ds(r0,ROWS),:],r0).astype(BF))
        spread(i,2,dv[pl.ds(r0,ROWS),:].astype(BF))
        return 0
    lax.fori_loop(0,rows//ROWS,last,0)

def attend_bwd(ctl,own,recv,d_own,d_recv,o_own,o_oth,lse,cos,sin):
    half,width=own.shape
    pairs=width//384
    rows=2*half
    sp=[pl.BlockSpec((half,128),(lambda p,c,s=s:(0,s*pairs+p))) for s in range(3)]
    one=pl.BlockSpec((half,128),lambda p,c:(0,p))
    full=pl.BlockSpec((rows,128),lambda p,c:(0,0))
    return pl.pallas_call(bwd_kernel,
        grid_spec=pltpu.PrefetchScalarGridSpec(num_scalar_prefetch=1,grid=(pairs,),
          in_specs=sp+sp+[one]*4+[pl.BlockSpec((1,8,rows),lambda p,c:(p,0,0)),full,full],
          out_specs=[pl.BlockSpec((half,384),lambda p,c:(0,p))]*2,
          scratch_shapes=[pltpu.VMEM((rows+BK,256),BF),pltpu.VMEM((rows,256),BF),pltpu.VMEM((rows,256),BF),
             pltpu.VMEM((rows+BK,128),BF),pltpu.VMEM((rows,128),BF),pltpu.VMEM((rows,128),BF),
             pltpu.VMEM((128,rows+BK),BF),pltpu.VMEM((16,rows),F32),pltpu.VMEM((rows+BK,128),F32),pltpu.VMEM((rows+BK,128),F32)]),
        out_shape=[jax.ShapeDtypeStruct((half,width),BF)]*2,
        compiler_params=pltpu.CompilerParams(vmem_limit_bytes=60<<20,dimension_semantics=("arbitrary",)),
        cost_estimate=pl.CostEstimate(flops=10*rows*rows*64*2*pairs//2,bytes_accessed=20*half*width,transcendentals=rows*rows*pairs),
        name="attend_bwd",
    )(ctl,own,own,own,recv,recv,recv,d_own,d_recv,o_own,o_oth,lse,cos,sin)

BLOCK=512

def spread_mean(x):
    return jnp.mean(x,axis=1,keepdims=True)

def row_docs(ctl,block):
    i=pl.program_id(0)
    r=ctl[0]*(block*pl.num_programs(0))+i*block+lax.broadcasted_iota(jnp.int32,(block,1),0)
    return (r>=ctl[1]).astype(jnp.int32)+(r>=ctl[2]).astype(jnp.int32)

def ffn_fwd_kernel(ctl,ao,ax,tok,w_exp,w_con,w_out,norm,u1,u2,rs,yb,hb,pf,pooled):
    block,width=tok.shape
    hidden=hb.shape[1]
    share=width//2
    pos=ctl[0]
    mine=pl.multiple_of(pos*share,share)
    other=pl.multiple_of((1-pos)*share,share)
    f=tok[...].astype(F32)+nn(ao[...],w_out[pl.ds(mine,share),:])+nn(ax[...],w_out[pl.ds(other,share),:])
    cent=f-spread_mean(f)
    scale=lax.rsqrt(spread_mean(cent*cent)+NORM_EPSILON)
    unit=cent*scale
    u1[...]=unit
    rs[:,0:128]=jnp.broadcast_to(scale,(block,128))
    y=unit*norm[0:1,:]+norm[1:2,:]
    ylow=y.astype(BF)
    yb[...]=ylow
    acc=y
    for c in range(hidden//width):
        gc=slice(c*width,(c+1)*width)
        uc=slice(hidden+c*width,hidden+(c+1)*width)
        gate=nn(ylow,w_exp[:,gc])
        up=nn(ylow,w_exp[:,uc])
        sig=jax.nn.sigmoid(gate)
        act=gate*sig
        low=(act*up).astype(BF)
        hb[:,gc]=low
        pf[:,gc]=(up*sig*(1.0+gate*(1.0-sig))).astype(BF)
        pf[:,uc]=act.astype(BF)
        acc=acc+nn(low,w_con[:,gc])
    cent=acc-spread_mean(acc)
    scale=lax.rsqrt(spread_mean(cent*cent)+NORM_EPSILON)
    unit=cent*scale
    u2[...]=unit
    rs[:,128:256]=jnp.broadcast_to(scale,(block,128))
    out=unit*norm[2:3,:]+norm[3:4,:]
    docs=row_docs(ctl,block)
    @pl.when(pl.program_id(0)==0)
    def _(): pooled[...]=jnp.zeros_like(pooled)
    for d in range(2):
        pooled[d:d+1,:]+=jnp.sum(jnp.where(docs==d,out,0.0),axis=0,keepdims=True)

def ffn_fwd(ctl,ao,ax,tok,bundle,norm,hidden):
    rows,width=tok.shape
    row=lambda n: pl.BlockSpec((BLOCK,n),lambda i,c:(i,0))
    held=lambda n,at: pl.BlockSpec((width,n),lambda i,c:(0,at//n),pipeline_mode=pl.Buffered(1))
    flat=pl.BlockSpec((8,width),lambda i,c:(0,0))
    return pl.pallas_call(ffn_fwd_kernel,
        grid_spec=pltpu.PrefetchScalarGridSpec(num_scalar_prefetch=1,grid=(rows//BLOCK,),
          in_specs=[row(width//2),row(width//2),row(width),held(2*hidden,0),held(hidden,2*hidden),held(width,3*hidden),flat],
          out_specs=[row(width),row(width),row(256),row(width),row(hidden),row(2*hidden),flat]),
        out_shape=[jax.ShapeDtypeStruct((rows,width),F32),jax.ShapeDtypeStruct((rows,width),F32),jax.ShapeDtypeStruct((rows,256),F32),
          jax.ShapeDtypeStruct((rows,width),BF),jax.ShapeDtypeStruct((rows,hidden),BF),jax.ShapeDtypeStruct((rows,2*hidden),BF),
          jax.ShapeDtypeStruct((8,width),F32)],
        compiler_params=pltpu.CompilerParams(vmem_limit_bytes=60<<20,dimension_semantics=("arbitrary",)),
        cost_estimate=pl.CostEstimate(flops=2*rows*width*(width+3*hidden),bytes_accessed=rows*(width*14+hidden*6)+2*width*(width+3*hidden),transcendentals=rows*hidden),
        name="ffn_fwd",
    )(ctl,ao,ax,tok,bundle,bundle,bundle,norm)

def loss_grad(pool,targets,len0,len1):
    width=pool.shape[1]
    docs=lax.broadcasted_iota(jnp.int32,pool.shape,0)
    length=jnp.where(docs==0,len0,len1)
    emb=pool/length
    lane=lax.broadcasted_iota(jnp.int32,pool.shape,1)
    d_target=jnp.zeros_like(pool)
    d_self=jnp.zeros_like(pool)
    for cut in (width//12,width//6,width//3,2*width//3,width):
        keep=lane<cut
        total=lambda v: jnp.sum(jnp.where(keep,v,0.0),axis=1,keepdims=True)
        own_root=lax.rsqrt(total(emb*emb)+COSINE_EPSILON)
        other_root=lax.rsqrt(total(targets*targets)+COSINE_EPSILON)
        cosine=total(emb*targets)*own_root*other_root
        d_target=d_target+jnp.where(keep,own_root*other_root,0.0)
        d_self=d_self+jnp.where(keep,cosine*own_root*own_root,0.0)
    d_emb=length*(d_self*emb-d_target*targets)
    return emb,d_emb/length

def ffn_bwd_kernel(ctl,flen,pool_a,pool_b,targets,u1,u2,rs,pf,w_exp,w_con,w_out,norm,
                   emb,mb,ub,df,ab,do,dx,gn,de):
    block,width=u1.shape
    hidden=pf.shape[1]//2
    share=width//2
    pos=ctl[0]
    @pl.when(pl.program_id(0)==0)
    def _():
        e,d=loss_grad(pool_a[...]+pool_b[...],targets[...],flen[0],flen[1])
        emb[...]=e
        de[...]=d
        gn[...]=jnp.zeros_like(gn)
    docs=row_docs(ctl,block)
    dout=jnp.where(docs==0,de[0:1,:],jnp.where(docs==1,de[1:2,:],0.0))
    unit=u2[...]
    gn[2:3,:]+=jnp.sum(dout*unit,axis=0,keepdims=True)
    gn[3:4,:]+=jnp.sum(dout,axis=0,keepdims=True)
    gu=dout*norm[2:3,:]
    dg=rs[:,128:129]*(gu-spread_mean(gu)-unit*spread_mean(gu*unit))
    mlow=dg.astype(BF)
    mb[...]=mlow
    acc=dg
    for c in range(hidden//width):
        gc=slice(c*width,(c+1)*width)
        uc=slice(hidden+c*width,hidden+(c+1)*width)
        dh=nt(mlow,w_con[:,gc])
        dgate=(dh*pf[:,gc].astype(F32)).astype(BF)
        dup=(dh*pf[:,uc].astype(F32)).astype(BF)
        ub[:,gc]=dgate
        ub[:,uc]=dup
        acc=acc+nt(dgate,w_exp[:,gc])+nt(dup,w_exp[:,uc])
    unit=u1[...]
    gn[0:1,:]+=jnp.sum(acc*unit,axis=0,keepdims=True)
    gn[1:2,:]+=jnp.sum(acc,axis=0,keepdims=True)
    gu=acc*norm[0:1,:]
    dfirst=rs[:,0:1]*(gu-spread_mean(gu)-unit*spread_mean(gu*unit))
    df[...]=dfirst
    alow=dfirst.astype(BF)
    ab[...]=alow
    do[...]=nt(alow,w_out[pl.ds(pl.multiple_of(pos*share,share),share),:]).astype(BF)
    dx[...]=nt(alow,w_out[pl.ds(pl.multiple_of((1-pos)*share,share),share),:]).astype(BF)

def ffn_bwd(ctl,flen,pool_a,pool_b,targets,u1,u2,rs,pf,bundle,norm):
    rows,width=u1.shape
    hidden=pf.shape[1]//2
    row=lambda n: pl.BlockSpec((BLOCK,n),lambda i,c,l:(i,0))
    held=lambda n,at: pl.BlockSpec((width,n),lambda i,c,l:(0,at//n),pipeline_mode=pl.Buffered(1))
    flat=pl.BlockSpec((8,width),lambda i,c,l:(0,0))
    sds=jax.ShapeDtypeStruct
    return pl.pallas_call(ffn_bwd_kernel,
        grid_spec=pltpu.PrefetchScalarGridSpec(num_scalar_prefetch=2,grid=(rows//BLOCK,),
          in_specs=[flat,flat,flat,row(width),row(width),row(256),row(2*hidden),held(2*hidden,0),held(hidden,2*hidden),held(width,3*hidden),flat],
          out_specs=[flat,row(width),row(2*hidden),row(width),row(width),row(width//2),row(width//2),flat],
          scratch_shapes=[pltpu.VMEM((8,width),F32)]),
        out_shape=[sds((8,width),F32),sds((rows,width),BF),sds((rows,2*hidden),BF),sds((rows,width),F32),sds((rows,width),BF),
          sds((rows,width//2),BF),sds((rows,width//2),BF),sds((8,width),F32)],
        compiler_params=pltpu.CompilerParams(vmem_limit_bytes=60<<20,dimension_semantics=("arbitrary",)),
        cost_estimate=pl.CostEstimate(flops=2*rows*width*(width+3*hidden),bytes_accessed=rows*(width*18+hidden*8)+2*width*(width+3*hidden),transcendentals=0),
        name="ffn_bwd",
    )(ctl,flen,pool_a,pool_b,targets,u1,u2,rs,pf,bundle,bundle,bundle,norm)

MESH=pl.DeviceIdType.MESH

def place():
    dp=lax.axis_index("dp")
    core=lax.axis_index("dim")
    return dp//4,(dp//2)%2,dp%2,core

def meet(z,y,x,core):
    chip=lambda a,b,c: a*4+b*2+c
    peers=[(chip(z,y,x),1-core),(chip(z,y,1-x),core),(chip(z,1-y,x),core)]
    peers+=[(chip(lax.rem(z+k,4),y,x),core) for k in (1,2,3)]
    barrier=pltpu.get_barrier_semaphore()
    for peer in peers:
        pl.semaphore_signal(barrier,inc=1,device_id=peer,device_id_type=MESH)
    pl.semaphore_wait(barrier,len(peers))
    return peers

def lanes_of(cols):
    tiles=cols//128
    widths=[tiles-tiles//4*3]+[tiles//4]*3
    widths=[widths[0],widths[2],widths[1],widths[3]]
    widths=[5,5,4,4] if tiles==18 else widths
    out=[]
    at=0
    for n,w in enumerate(widths):
        out.append((at*128,w*128,n%2==0))
        at+=w
    return out

def send(src,dst,sems,n,k,peer):
    copy=pltpu.make_async_remote_copy(src_ref=src,dst_ref=dst,send_sem=sems[0].at[n,k],recv_sem=sems[1].at[n,k],device_id=peer,device_id_type=MESH)
    copy.start()
    return copy

def gather_kernel(w,out,low,local,s_sem,r_sem):
    z,y,x,core=place()
    low[...]=w[...].astype(BF)
    keep=pltpu.make_async_copy(low,out.at[z,y,x,core],local)
    keep.start()
    pair,xn,yn,z1,z2,z3=meet(z,y,x,core)
    sems=(s_sem,r_sem)
    lanes=lanes_of(w.shape[1])
    every=[]
    def go(n,k,peer,*index,src=None):
        at,width,_=lanes[n]
        dst=out.at[(*index,slice(None),pl.ds(at,width))]
        if src is None: src=dst
        copy=send(src,dst,sems,n,k,peer)
        every.append(copy)
        return copy
    whole=slice(None)
    first=[]
    for n,(at,width,_) in enumerate(lanes):
        piece=low.at[:,pl.ds(at,width)]
        first.append([go(n,k,peer,z,y,x,core,src=piece) for k,peer in enumerate((z1,z2,z3))])
    keep.wait()
    second=[]
    for n,(_,_,flip) in enumerate(lanes):
        for copy in first[n]: copy.wait_recv()
        second.append(go(n,3,yn if flip else xn,whole,y,x,core))
        go(n,5,pair,whole,y,x,core)
    third=[]
    for n,(_,_,flip) in enumerate(lanes):
        second[n].wait_recv()
        if flip:
            third.append(go(n,4,xn,whole,whole,x,core))
            go(n,6,pair,whole,1-y,x,core)
        else:
            third.append(go(n,4,yn,whole,y,whole,core))
            go(n,6,pair,whole,y,1-x,core)
    for n,(_,_,flip) in enumerate(lanes):
        third[n].wait_recv()
        if flip: go(n,7,pair,whole,whole,1-x,core)
        else: go(n,7,pair,whole,1-y,whole,core)
    done=set(id(c) for c in second+third+[c for f in first for c in f])
    for copy in every:
        copy.wait_send()
        if id(copy) not in done: copy.wait_recv()

def ring_gather(w):
    share,cols=w.shape
    out=pl.pallas_call(gather_kernel,
        in_specs=[pl.BlockSpec(memory_space=pltpu.VMEM)],
        out_specs=pl.BlockSpec(memory_space=pl.ANY),
        scratch_shapes=[pltpu.VMEM((share,cols),BF),pltpu.SemaphoreType.DMA,pltpu.SemaphoreType.DMA((4,8)),pltpu.SemaphoreType.DMA((4,8))],
        out_shape=jax.ShapeDtypeStruct((4,2,2,2,share,cols),BF),
        compiler_params=pltpu.CompilerParams(collective_id=1,has_side_effects=True,vmem_limit_bytes=16<<20),
        cost_estimate=pl.CostEstimate(flops=0,bytes_accessed=64*share*cols*20,transcendentals=0),
        name="comm_gather",
    )(w)
    return out.reshape(32*share,cols)

def scatter_kernel(g,out,r0,b1,k1,r1,b2,k2,r2,b3,k3,r3,s_sem,r_sem):
    z,y,x,core=place()
    pair,xn,yn,z1,z2,z3=meet(z,y,x,core)
    sems=(s_sem,r_sem)
    lanes=lanes_of(out.shape[1])
    span=[pl.ds(at,width) for at,width,_ in lanes]
    every=[]
    def go(n,k,peer,src,dst):
        copy=send(src,dst,sems,n,k,peer)
        every.append(copy)
        return copy
    n_lanes=range(len(lanes))
    zero=[go(n,0,pair,g.at[:,1-core,:,span[n]],r0.at[:,:,span[n]]) for n in n_lanes]
    def split1(n,iz,j,side):
        row=iz*4+(j*2+side if lanes[n][2] else side*2+j)
        c=span[n]
        return g[row,core,:,c].astype(F32)+r0[row,:,c].astype(F32)
    one=[]
    for n in n_lanes:
        flip=lanes[n][2]
        side=x if flip else y
        zero[n].wait_recv()
        for iz in range(4):
            for j in range(2):
                b1[iz,j,:,span[n]]=split1(n,iz,j,1-side).astype(BF)
        one.append(go(n,1,xn if flip else yn,b1.at[:,:,:,span[n]],r1.at[:,:,:,span[n]]))
        for iz in range(4):
            for j in range(2):
                k1[iz,j,:,span[n]]=split1(n,iz,j,side)
    two=[]
    for n in n_lanes:
        flip=lanes[n][2]
        side=y if flip else x
        c=span[n]
        one[n].wait_recv()
        for iz in range(4):
            b2[iz,:,c]=(k1[iz,1-side,:,c]+r1[iz,1-side,:,c].astype(F32)).astype(BF)
        two.append(go(n,2,yn if flip else xn,b2.at[:,:,c],r2.at[:,:,c]))
        for iz in range(4):
            k2[iz,:,c]=k1[iz,side,:,c]+r1[iz,side,:,c].astype(F32)
    three=[]
    for n in n_lanes:
        c=span[n]
        two[n].wait_recv()
        for k in (1,2,3):
            to=lax.rem(z+k,4)
            b3[k-1,:,c]=(k2[to,:,c]+r2[to,:,c].astype(F32)).astype(BF)
        three.append([go(n,2+k,(z1,z2,z3)[k-1],b3.at[k-1,:,c],r3.at[k-1,:,c]) for k in (1,2,3)])
        k3[:,c]=k2[z,:,c]+r2[z,:,c].astype(F32)
    for n in n_lanes:
        c=span[n]
        for copy in three[n]: copy.wait_recv()
        out[:,c]=k3[:,c]+r3[0,:,c].astype(F32)+r3[1,:,c].astype(F32)+r3[2,:,c].astype(F32)
    for copy in every: copy.wait_send()

def ring_scatter(g):
    rows,cols=g.shape
    share=rows//32
    v=lambda *s: pltpu.VMEM((*s,share,cols),BF)
    f=lambda *s: pltpu.VMEM((*s,share,cols),F32)
    return pl.pallas_call(scatter_kernel,
        in_specs=[pl.BlockSpec(memory_space=pltpu.VMEM)],
        out_specs=pl.BlockSpec(memory_space=pltpu.VMEM),
        scratch_shapes=[v(16),v(4,2),f(4,2),v(4,2),v(4),f(4),v(4),v(3),f(),v(3),pltpu.SemaphoreType.DMA((4,6)),pltpu.SemaphoreType.DMA((4,6))],
        out_shape=jax.ShapeDtypeStruct((share,cols),F32),
        compiler_params=pltpu.CompilerParams(collective_id=2,has_side_effects=True,vmem_limit_bytes=40<<20),
        cost_estimate=pl.CostEstimate(flops=0,bytes_accessed=64*share*cols*20,transcendentals=0),
        name="comm_scatter",
    )(g.reshape(16,2,share,cols))

def mix_kernel(ctl,x,w,cos,sin,own,oth):
    pos=ctl[0]
    width=x.shape[1]
    share=width//2
    xb=x[...]
    c=cos[...]
    s=sin[...]
    lane=lax.broadcasted_iota(jnp.int32,c.shape,1)
    first=(lane%64)<32
    for out,side in ((own,pos),(oth,1-pos)):
        for part in range(3):
            cols=pl.ds(pl.multiple_of(part*width+side*share,128),share)
            y=nn(xb,w[:,cols])
            for t in range(share//128):
                z=y[:,t*128:(t+1)*128]
                if part<2:
                    swapped=jnp.where(first,pltpu.roll(z,96,1),pltpu.roll(z,32,1))
                    z=z*c+swapped*s
                out[:,part*share+t*128:part*share+(t+1)*128]=z.astype(BF)

def mix(ctl,x,w,cos,sin):
    rows,width=x.shape
    cols=w.shape[1]
    block=256
    row=lambda n: pl.BlockSpec((block,n),lambda i,c:(i,0))
    return pl.pallas_call(mix_kernel,
        grid_spec=pltpu.PrefetchScalarGridSpec(num_scalar_prefetch=1,grid=(rows//block,),
          in_specs=[row(width),pl.BlockSpec((width,cols),lambda i,c:(0,0)),row(128),row(128)],
          out_specs=[row(cols//2)]*2),
        out_shape=[jax.ShapeDtypeStruct((rows,cols//2),BF)]*2,
        compiler_params=pltpu.CompilerParams(vmem_limit_bytes=60<<20,dimension_semantics=("arbitrary",)),
        cost_estimate=pl.CostEstimate(flops=2*rows*width*cols,bytes_accessed=2*(rows*width+width*cols+rows*cols),transcendentals=0),
        name="mix",
    )(ctl,x,w,cos,sin)

def shuffle(x,count,per,share):
    rows=x.shape[0]
    return x.reshape(rows,2,count,per,share).transpose(0,1,3,2,4).reshape(x.shape)

def unshuffle(x,count,per,share):
    rows=x.shape[0]
    return x.reshape(rows,2,per,count,share).transpose(0,1,3,2,4).reshape(x.shape)

def fold_rows(x,per):
    rows,cols=x.shape
    return x.reshape(per,rows//per,cols).transpose(1,0,2).reshape(rows//per,per*cols)

def unfold_rows(x,per,share):
    count=x.shape[0]//share
    cols=x.shape[1]//per
    return x.reshape(count,share,per,cols).transpose(0,2,1,3).reshape(count*per*share,cols)

def swap_cores(x):
    return lax.ppermute(x,"dim",[(0,1),(1,0)])

def join(pos,own,recv,axis=1):
    return jnp.where(pos==0,jnp.concatenate([own,recv],axis),jnp.concatenate([recv,own],axis))

def join_parts(pos,own,recv):
    share=own.shape[1]//3
    pieces=[]
    for s in range(3):
        pieces.append(own[:,s*share:(s+1)*share])
        pieces.append(recv[:,s*share:(s+1)*share])
    flip=[pieces[i^1] for i in range(6)]
    return jnp.where(pos==0,jnp.concatenate(pieces,1),jnp.concatenate(flip,1))

def body(tokens,doc_lengths,pair_index,target_bank,mixer_in,mixer_out,expand,contract,norm_params,*rest):
    slices=lax.axis_size("dim")
    if slices!=2 or lax.axis_size("dp")!=16 or doc_lengths.shape[1]!=2:
        return body_general(tokens,doc_lengths,pair_index,target_bank,mixer_in,mixer_out,expand,contract,norm_params,*rest)
    (mixer_in_moment,mixer_out_moment,expand_moment,contract_moment,norm_moment,
     mixer_in_average,mixer_out_average,expand_average,contract_average,norm_average)=rest
    local_rows,model_width=tokens.shape
    group_rows=local_rows*slices
    pos=lax.axis_index("dim")
    doc_count=2
    w_mix=ring_gather(mixer_in[0])
    share_rows=mixer_out.shape[1]
    per=contract.shape[1]//share_rows
    count=model_width//share_rows
    hidden_width=contract.shape[1]*count
    exp_cols=shuffle(expand[0].astype(BF),count,per,share_rows)
    con_cols=fold_rows(contract[0].astype(BF),per)
    norm_cols=jnp.pad(norm_params[0].astype(BF),((0,share_rows-4),(0,128-share_rows)))
    bundle=jnp.concatenate([exp_cols,con_cols,mixer_out[0].astype(BF),norm_cols],1)
    bundle=lax.all_gather(bundle,("dp","dim"),axis=0,tiled=True)
    at1=2*hidden_width
    at2=at1+per*model_width
    at3=at2+model_width
    w_norm=bundle[:,at3:].reshape(count,share_rows,128)[:,0:4,0:share_rows].transpose(1,0,2).reshape(4,model_width)
    lengths=doc_lengths[0]
    e0=lengths[0]
    e1=lengths[0]+lengths[1]
    ctl=jnp.stack([pos.astype(jnp.int32),e0,e1])
    ids=jnp.arange(group_rows,dtype=jnp.int32)
    seg=(ids>=e0).astype(jnp.int32)+(ids>=e1).astype(jnp.int32)
    begin=jnp.where(seg==0,0,jnp.where(seg==1,e0,e1))
    lane=jnp.arange(128,dtype=jnp.int32)
    frequency=jnp.power(1000.0,-(2*(lane%32)).astype(F32)/HEAD)
    angles=(ids-begin).astype(F32)[:,None]*frequency[None,:]
    cos=jnp.cos(angles)
    sin=jnp.sin(angles)*jnp.where((lane%64)<32,-1.0,1.0)[None,:]
    cos_own=lax.dynamic_slice_in_dim(cos,pos*local_rows,local_rows,0)
    sin_own=lax.dynamic_slice_in_dim(sin,pos*local_rows,local_rows,0)
    own,oth=mix(ctl,tokens,w_mix,cos_own,sin_own)
    recv=swap_cores(oth)
    pick=(pair_index[:,None]==jnp.arange(target_bank.shape[0],dtype=jnp.int32)[None,:]).astype(BF)
    some=matmul(pick,target_bank)
    targets=jnp.pad(join(pos,some,swap_cores(some)),((0,6),(0,0)))
    o_own,o_oth,lse=attend_fwd(ctl,own,recv)
    o_recv=swap_cores(o_oth)
    norm_gains=jnp.pad(w_norm.astype(F32),((0,4),(0,0)))
    u1,u2,rs,y_low,hidden,factors,pooled=ffn_fwd(ctl,o_own,o_recv,tokens,bundle,norm_gains,hidden_width)
    embeds,grad_m_low,grad_both,grad_first,grad_a_low,d_own,d_oth,grad_norm=ffn_bwd(
        ctl,lengths.astype(F32),pooled,swap_cores(pooled),targets,u1,u2,rs,factors,bundle,norm_gains)
    share=model_width//2
    embeddings=lax.dynamic_slice(embeds,(0,pos*share),(doc_count,share))
    d_recv=swap_cores(d_oth)
    grad_exp=inner_rows(y_low,grad_both)
    grad_con=inner_rows(hidden,grad_m_low)
    grad_out=join(pos,inner_rows(o_own,grad_a_low),inner_rows(o_recv,grad_a_low),0)
    scatter=lambda g: lax.psum_scatter(g,("dp","dim"),scatter_dimension=0,tiled=True).astype(F32)
    grad_norm=grad_norm[0:4].reshape(4,count,share_rows).transpose(1,0,2)
    grad_norm=jnp.pad(grad_norm,((0,0),(0,share_rows-4),(0,128-share_rows))).reshape(model_width,128)
    fold_con=[grad_con[j*model_width:(j+1)*model_width].astype(BF) for j in range(per)]
    terms=jnp.concatenate([grad_exp.astype(BF),*fold_con,grad_out.astype(BF),grad_norm.astype(BF)],1)
    terms,d_own,d_recv=lax.optimization_barrier((terms,d_own,d_recv))
    sums=scatter(terms)
    g_own,g_oth=attend_bwd(ctl,own,recv,d_own,d_recv,o_own,o_oth,lse,cos,sin)
    grad_mixed=join_parts(pos,unpair(g_own),unpair(swap_cores(g_oth)))
    grad_mix=inner_rows(tokens,grad_mixed)
    token_grads=grad_first+inner_cols(grad_mixed,w_mix)
    grad_mix=grad_mix.astype(BF)
    grad_mix,sums=lax.optimization_barrier((grad_mix,sums))
    sum_mix=ring_scatter(grad_mix)
    sum_exp=unshuffle(sums[:,0:at1],count,per,share_rows)
    sum_con=unfold_rows(sums[:,at1:at2],per,share_rows)
    sum_out=sums[:,at2:at3]
    sum_norm=sums[0:4,at3:at3+share_rows]
    total_rows=group_rows*lax.axis_size("dp")
    matrix_rate=1.0/math.sqrt(total_rows)
    norm_rate=0.3/math.sqrt(total_rows)
    grads=[g[None] for g in (sum_mix,sum_out,sum_exp,sum_con,sum_norm)]
    weights=(mixer_in,mixer_out,expand,contract,norm_params)
    moments=(mixer_in_moment,mixer_out_moment,expand_moment,contract_moment,norm_moment)
    averages=(mixer_in_average,mixer_out_average,expand_average,contract_average,norm_average)
    rates=(matrix_rate,matrix_rate,matrix_rate,matrix_rate,norm_rate)
    results=[advance(weights[k],moments[k],averages[k],grads[k],rates[k]) for k in range(5)]
    return (embeddings,token_grads,*grads,*[results[k][f] for f in range(4) for k in range(5)])

def unpair(g):
    rows,width=g.shape
    pairs=width//384
    return jnp.concatenate([g[:,p*384+s*128:p*384+(s+1)*128] for s in range(3) for p in range(pairs)],1)


def solution(mesh):
    placed = (
        P(("dp", "dim"), None),
        P("dp", None),
        P("dp"),
        P(None, "dim"),
        P(None, ("dp", "dim"), None),
        P(None, ("dp", "dim"), None),
        P(None, ("dp", "dim"), None),
        P(None, ("dp", "dim"), None),
        P(None, None, ("dp", "dim")),
        P(None, ("dp", "dim"), None),
        P(None, ("dp", "dim"), None),
        P(None, ("dp", "dim"), None),
        P(None, ("dp", "dim"), None),
        P(None, None, ("dp", "dim")),
        P(None, ("dp", "dim"), None),
        P(None, ("dp", "dim"), None),
        P(None, ("dp", "dim"), None),
        P(None, ("dp", "dim"), None),
        P(None, None, ("dp", "dim")),
    )
    return jax.shard_map(
        body,
        mesh=mesh,
        in_specs=placed,
        out_specs=(
            P("dp", "dim"),
            P(("dp", "dim"), None),
            P(None, ("dp", "dim"), None),
            P(None, ("dp", "dim"), None),
            P(None, ("dp", "dim"), None),
            P(None, ("dp", "dim"), None),
            P(None, None, ("dp", "dim")),
            P(None, ("dp", "dim"), None),
            P(None, ("dp", "dim"), None),
            P(None, ("dp", "dim"), None),
            P(None, ("dp", "dim"), None),
            P(None, None, ("dp", "dim")),
            P(None, ("dp", "dim"), None),
            P(None, ("dp", "dim"), None),
            P(None, ("dp", "dim"), None),
            P(None, ("dp", "dim"), None),
            P(None, None, ("dp", "dim")),
            P(None, ("dp", "dim"), None),
            P(None, ("dp", "dim"), None),
            P(None, ("dp", "dim"), None),
            P(None, ("dp", "dim"), None),
            P(None, None, ("dp", "dim")),
            P(None, ("dp", "dim"), None),
            P(None, ("dp", "dim"), None),
            P(None, ("dp", "dim"), None),
            P(None, ("dp", "dim"), None),
            P(None, None, ("dp", "dim")),
        ),
        check_vma=False,
    )
```

```python
import math

import jax
import jax.numpy as jnp
from jax import lax
from jax.experimental import pallas as pl
from jax.experimental.pallas import tpu as pltpu
from jax.sharding import PartitionSpec as P

HEAD = 64


NORM_EPSILON = 1e-05
COSINE_EPSILON = 1e-06
MOMENTUM = 0.5
AVERAGE_DECAY = 0.5
PRECISE = lax.Precision.HIGHEST
MASKED = -1e30


def matmul(left_op, right_op):
    return jnp.dot(left_op, right_op, preferred_element_type=jnp.float32)


def matmul_exact(left_op, right_op):
    return jnp.dot(left_op, right_op, precision=PRECISE, preferred_element_type=jnp.float32)


def inner_rows(left_op, right_op):
    return lax.dot_general(
        left_op, right_op, (((0,), (0,)), ((), ())), preferred_element_type=jnp.float32
    )


def inner_cols(left_op, right_op):
    return lax.dot_general(
        left_op, right_op, (((1,), (1,)), ((), ())), preferred_element_type=jnp.float32
    )


def rotate(values, cosines, sines):
    row_count = values.shape[0]
    shaped = values.reshape(row_count, -1, 2, HEAD // 2)
    former = shaped[:, :, 0, :]
    latter = shaped[:, :, 1, :]
    cosine_b = cosines[:, None, :]
    sine_b = sines[:, None, :]
    turned = jnp.stack(
        [former * cosine_b - latter * sine_b, latter * cosine_b + former * sine_b], axis=2
    )
    return turned.reshape(values.shape)


def rotate_back(grads_in, cosines, sines):
    row_count = grads_in.shape[0]
    shaped = grads_in.reshape(row_count, -1, 2, HEAD // 2)
    former = shaped[:, :, 0, :]
    latter = shaped[:, :, 1, :]
    cosine_b = cosines[:, None, :]
    sine_b = sines[:, None, :]
    turned = jnp.stack(
        [former * cosine_b + latter * sine_b, latter * cosine_b - former * sine_b], axis=2
    )
    return turned.reshape(grads_in.shape)


def normalize(summed, gain_vec, bias_vec):
    centred = summed - jnp.mean(summed, axis=1, keepdims=True)
    scaling = lax.rsqrt(jnp.mean(centred * centred, axis=1, keepdims=True) + NORM_EPSILON)
    return centred * scaling * gain_vec + bias_vec


def normalize_back(grad_in, summed, gain_vec):
    centred = summed - jnp.mean(summed, axis=1, keepdims=True)
    scaling = lax.rsqrt(jnp.mean(centred * centred, axis=1, keepdims=True) + NORM_EPSILON)
    unit = centred * scaling
    grad_unit = grad_in * gain_vec
    grad_sum = scaling * (
        grad_unit
        - jnp.mean(grad_unit, axis=1, keepdims=True)
        - unit * jnp.mean(grad_unit * unit, axis=1, keepdims=True)
    )
    return (grad_sum, jnp.sum(grad_in * unit, axis=0), jnp.sum(grad_in, axis=0))


def flatten(stacked):
    return stacked.transpose(1, 0, 2).reshape(stacked.shape[1], -1)


def attend(q_rot, all_keys, all_values, same_doc):
    head_count = q_rot.shape[1] // HEAD

    def one_head(head_pos):
        offset = head_pos * HEAD
        query_part = lax.dynamic_slice_in_dim(q_rot, offset, HEAD, 1)
        key_part = lax.dynamic_slice_in_dim(all_keys, offset, HEAD, 1)
        value_part = lax.dynamic_slice_in_dim(all_values, offset, HEAD, 1)
        scores = jnp.where(same_doc, inner_cols(query_part, key_part) * 0.125, MASKED)
        row_max = jnp.max(scores, axis=1, keepdims=True)
        exponent = jnp.exp(scores - row_max)
        row_total = jnp.sum(exponent, axis=1, keepdims=True)
        attn_probs = (exponent / row_total).astype(jnp.bfloat16)
        return (matmul(attn_probs, value_part), (row_max + jnp.log(row_total))[:, 0])

    outputs, log_totals = lax.map(one_head, jnp.arange(head_count, dtype=jnp.int32))
    return (flatten(outputs), log_totals)


def attend_back(q_rot, all_keys, all_values, same_doc, grad_out, log_totals):
    head_count = q_rot.shape[1] // HEAD

    def one_head(pack):
        head_pos, log_total = pack
        offset = head_pos * HEAD
        query_part = lax.dynamic_slice_in_dim(q_rot, offset, HEAD, 1)
        key_part = lax.dynamic_slice_in_dim(all_keys, offset, HEAD, 1)
        value_part = lax.dynamic_slice_in_dim(all_values, offset, HEAD, 1)
        grad_part = lax.dynamic_slice_in_dim(grad_out, offset, HEAD, 1)
        scores = jnp.where(same_doc, inner_cols(query_part, key_part) * 0.125, MASKED)
        attn_probs = jnp.exp(scores - log_total[:, None])
        grad_probs = inner_cols(grad_part, value_part)
        row_dot = jnp.sum(attn_probs * grad_probs, axis=1, keepdims=True)
        grad_scores = (attn_probs * (grad_probs - row_dot)).astype(jnp.bfloat16)
        grad_query = matmul(grad_scores, key_part) * 0.125
        grad_key = inner_rows(grad_scores, query_part) * 0.125
        grad_value = inner_rows(attn_probs.astype(jnp.bfloat16), grad_part)
        return (grad_query, grad_key, grad_value)

    mapped = lax.map(one_head, (jnp.arange(head_count, dtype=jnp.int32), log_totals))
    return (flatten(mapped[0]), flatten(mapped[1]), flatten(mapped[2]))


def advance(weight, moment, average, grad_in, rate):
    moment_next = MOMENTUM * moment + grad_in
    weight_next = weight - rate * (grad_in + MOMENTUM * moment_next)
    average_next = AVERAGE_DECAY * average + (1.0 - AVERAGE_DECAY) * weight_next
    return (weight_next, moment_next, average_next, weight_next.astype(jnp.bfloat16))


def body_general(
    tokens,
    doc_lengths,
    pair_index,
    target_bank,
    mixer_in,
    mixer_out,
    expand,
    contract,
    norm_params,
    mixer_in_moment,
    mixer_out_moment,
    expand_moment,
    contract_moment,
    norm_moment,
    mixer_in_average,
    mixer_out_average,
    expand_average,
    contract_average,
    norm_average,
):
    local_rows, model_width = tokens.shape
    slices = lax.axis_size("dim")
    group_rows = local_rows * slices
    position = lax.axis_index("dim")
    layer_count = mixer_in.shape[0]
    doc_count = doc_lengths.shape[1]
    lengths = doc_lengths[0]
    doc_ends = jnp.cumsum(lengths)
    doc_starts = doc_ends - lengths
    row_ids = position * local_rows + jnp.arange(local_rows, dtype=jnp.int32)
    key_ids = jnp.arange(group_rows, dtype=jnp.int32)
    seg_rows = jnp.sum((row_ids[:, None] >= doc_ends[None, :]).astype(jnp.int32), axis=1)
    seg_keys = jnp.sum((key_ids[:, None] >= doc_ends[None, :]).astype(jnp.int32), axis=1)
    first_rows = jnp.concatenate([doc_starts, doc_ends[-1:]])
    segment_ids = jnp.arange(doc_count + 1, dtype=jnp.int32)
    row_begin = jnp.sum(
        jnp.where(seg_rows[:, None] == segment_ids[None, :], first_rows[None, :], 0), axis=1
    )
    frequency = jnp.power(1000.0, -jnp.arange(0, HEAD, 2).astype(jnp.float32) / HEAD)
    angles = (row_ids - row_begin).astype(jnp.float32)[:, None] * frequency[None, :]
    cosines = jnp.cos(angles)
    sines = jnp.sin(angles)
    same_doc = seg_rows[:, None] == seg_keys[None, :]
    stream = tokens.astype(jnp.float32)
    layer_pos = 0
    layer_weights = (
        lax.all_gather(mixer_in[layer_pos].astype(jnp.bfloat16), ("dp", "dim"), axis=0, tiled=True),
        lax.all_gather(
            mixer_out[layer_pos].astype(jnp.bfloat16), ("dp", "dim"), axis=0, tiled=True
        ),
        lax.all_gather(expand[layer_pos].astype(jnp.bfloat16), ("dp", "dim"), axis=0, tiled=True),
        lax.all_gather(contract[layer_pos].astype(jnp.bfloat16), ("dp", "dim"), axis=0, tiled=True),
        lax.all_gather(
            norm_params[layer_pos].astype(jnp.bfloat16), ("dp", "dim"), axis=1, tiled=True
        ),
    )
    w_mix, w_out, w_exp, w_con, w_norm = layer_weights
    norm_gains = w_norm.astype(jnp.float32)
    x_low = stream.astype(jnp.bfloat16)
    mixed = matmul(x_low, w_mix)
    q_rot = rotate(mixed[:, 0:model_width], cosines, sines).astype(jnp.bfloat16)
    k_rot = rotate(mixed[:, model_width : 2 * model_width], cosines, sines).astype(jnp.bfloat16)
    v_low = mixed[:, 2 * model_width : 3 * model_width].astype(jnp.bfloat16)
    all_keys = lax.all_gather(k_rot, "dim", axis=0, tiled=True)
    all_values = lax.all_gather(v_low, "dim", axis=0, tiled=True)
    attended, log_totals = attend(q_rot, all_keys, all_values, same_doc)
    att_low = attended.astype(jnp.bfloat16)
    first_sum = stream + matmul(att_low, w_out)
    normed = normalize(first_sum, norm_gains[0], norm_gains[1])
    y_low = normed.astype(jnp.bfloat16)
    gate_up = matmul(y_low, w_exp)
    half = gate_up.shape[1] // 2
    hidden = (jax.nn.silu(gate_up[:, 0:half]) * gate_up[:, half : 2 * half]).astype(jnp.bfloat16)
    second_sum = normed + matmul(hidden, w_con)
    saved = [
        (
            stream,
            layer_weights,
            q_rot,
            k_rot,
            v_low,
            all_keys,
            all_values,
            log_totals,
            attended,
            att_low,
            first_sum,
            normed,
            y_low,
            gate_up,
            hidden,
            second_sum,
        )
    ]
    stream = normalize(second_sum, norm_gains[2], norm_gains[3])
    member = (seg_rows[None, :] == jnp.arange(doc_count, dtype=jnp.int32)[:, None]).astype(
        jnp.float32
    )
    partial_value = matmul_exact(member, stream)
    pooled = lax.psum_scatter(partial_value, "dim", scatter_dimension=1, tiled=True)
    length_f = lengths.astype(jnp.float32)
    embeddings = pooled / length_f[:, None]
    share = embeddings.shape[1]
    pick = (
        pair_index[:, None] == jnp.arange(target_bank.shape[0], dtype=jnp.int32)[None, :]
    ).astype(jnp.bfloat16)
    targets = matmul(pick, target_bank)
    feature_ids = position * share + jnp.arange(share, dtype=jnp.int32)
    cuts = jnp.array(
        [model_width // 12, model_width // 6, model_width // 3, 2 * model_width // 3, model_width],
        dtype=jnp.int32,
    )
    masks = (feature_ids[None, :] < cuts[:, None]).astype(jnp.float32)
    cross = matmul_exact(embeddings * targets, masks.T)
    own = matmul_exact(embeddings * embeddings, masks.T)
    other = matmul_exact(targets * targets, masks.T)
    cross, own, other = lax.psum((cross, own, other), "dim")
    own_root = lax.rsqrt(own + COSINE_EPSILON)
    other_root = lax.rsqrt(other + COSINE_EPSILON)
    cosine = cross * own_root * other_root
    coef_target = -length_f[:, None] * own_root * other_root
    coef_self = length_f[:, None] * cosine * own_root * own_root
    grad_emb = (
        matmul_exact(coef_target, masks) * targets + matmul_exact(coef_self, masks) * embeddings
    )
    grad_full = lax.all_gather(grad_emb, "dim", axis=1, tiled=True)
    spread_rows = member / length_f[:, None]
    grad_stream = lax.dot_general(
        spread_rows,
        grad_full,
        (((0,), (0,)), ((), ())),
        precision=PRECISE,
        preferred_element_type=jnp.float32,
    )
    grad_list = [None] * layer_count
    for layer_pos in reversed(range(layer_count)):
        (
            layer_input,
            layer_weights,
            q_rot,
            k_rot,
            v_low,
            all_keys,
            all_values,
            log_totals,
            attended,
            att_low,
            first_sum,
            normed,
            y_low,
            gate_up,
            hidden,
            second_sum,
        ) = saved[layer_pos]
        w_mix = lax.all_gather(
            mixer_in[layer_pos].astype(jnp.bfloat16), ("dp", "dim"), axis=0, tiled=True
        )
        w_out = lax.all_gather(
            mixer_out[layer_pos].astype(jnp.bfloat16), ("dp", "dim"), axis=0, tiled=True
        )
        w_exp = lax.all_gather(
            expand[layer_pos].astype(jnp.bfloat16), ("dp", "dim"), axis=0, tiled=True
        )
        w_con = lax.all_gather(
            contract[layer_pos].astype(jnp.bfloat16), ("dp", "dim"), axis=0, tiled=True
        )
        w_norm = lax.all_gather(
            norm_params[layer_pos].astype(jnp.bfloat16), ("dp", "dim"), axis=1, tiled=True
        )
        norm_gains = w_norm.astype(jnp.float32)
        grad_second, grad_gain2, grad_bias2 = normalize_back(grad_stream, second_sum, norm_gains[2])
        grad_m_low = grad_second.astype(jnp.bfloat16)
        grad_con = inner_rows(hidden, grad_m_low)
        grad_hidden = inner_cols(grad_m_low, w_con)
        half = gate_up.shape[1] // 2
        gate_part = gate_up[:, 0:half]
        up_part = gate_up[:, half : 2 * half]
        sigmoid_gate = jax.nn.sigmoid(gate_part)
        activated = gate_part * sigmoid_gate
        grad_gate = grad_hidden * up_part * sigmoid_gate * (1.0 + gate_part * (1.0 - sigmoid_gate))
        grad_up = grad_hidden * activated
        grad_both = jnp.concatenate([grad_gate, grad_up], axis=1).astype(jnp.bfloat16)
        grad_exp = inner_rows(y_low, grad_both)
        grad_normed = grad_second + inner_cols(grad_both, w_exp)
        grad_first, grad_gain1, grad_bias1 = normalize_back(grad_normed, first_sum, norm_gains[0])
        grad_a_low = grad_first.astype(jnp.bfloat16)
        grad_out = inner_rows(att_low, grad_a_low)
        grad_attended = inner_cols(grad_a_low, w_out).astype(jnp.bfloat16)
        keys_back, values_back = (
            lax.all_gather(k_rot, "dim", axis=0, tiled=True),
            lax.all_gather(v_low, "dim", axis=0, tiled=True),
        )
        grad_query, grad_key_all, grad_value_all = attend_back(
            q_rot, keys_back, values_back, same_doc, grad_attended, log_totals
        )
        grad_kv = lax.psum_scatter(
            jnp.concatenate([grad_key_all, grad_value_all], axis=1).astype(jnp.bfloat16),
            "dim",
            scatter_dimension=0,
            tiled=True,
        ).astype(jnp.float32)
        grad_mixed = jnp.concatenate(
            [
                rotate_back(grad_query, cosines, sines),
                rotate_back(grad_kv[:, 0:model_width], cosines, sines),
                grad_kv[:, model_width : 2 * model_width],
            ],
            axis=1,
        ).astype(jnp.bfloat16)
        x_low = layer_input.astype(jnp.bfloat16)
        grad_mix = inner_rows(x_low, grad_mixed)
        grad_stream = grad_first + inner_cols(grad_mixed, w_mix)
        grad_norm = jnp.stack([grad_gain1, grad_bias1, grad_gain2, grad_bias2])
        grad_list[layer_pos] = (
            lax.psum_scatter(grad_mix, ("dp", "dim"), scatter_dimension=0, tiled=True),
            lax.psum_scatter(grad_out, ("dp", "dim"), scatter_dimension=0, tiled=True),
            lax.psum_scatter(grad_exp, ("dp", "dim"), scatter_dimension=0, tiled=True),
            lax.psum_scatter(grad_con, ("dp", "dim"), scatter_dimension=0, tiled=True),
            lax.psum_scatter(grad_norm, ("dp", "dim"), scatter_dimension=1, tiled=True),
        )
    total_rows = group_rows * lax.axis_size("dp")
    matrix_rate = 1.0 / math.sqrt(total_rows)
    norm_rate = 0.3 / math.sqrt(total_rows)
    grads = [jnp.stack([grad_list[0][kind]]) for kind in range(5)]
    weights = (mixer_in, mixer_out, expand, contract, norm_params)
    moments = (mixer_in_moment, mixer_out_moment, expand_moment, contract_moment, norm_moment)
    averages = (mixer_in_average, mixer_out_average, expand_average, contract_average, norm_average)
    rates = (matrix_rate, matrix_rate, matrix_rate, matrix_rate, norm_rate)
    results = [
        advance(weights[kind], moments[kind], averages[kind], grads[kind], rates[kind])
        for kind in range(5)
    ]
    return (
        embeddings,
        grad_stream,
        grads[0],
        grads[1],
        grads[2],
        grads[3],
        grads[4],
        results[0][0],
        results[1][0],
        results[2][0],
        results[3][0],
        results[4][0],
        results[0][1],
        results[1][1],
        results[2][1],
        results[3][1],
        results[4][1],
        results[0][2],
        results[1][2],
        results[2][2],
        results[3][2],
        results[4][2],
        results[0][3],
        results[1][3],
        results[2][3],
        results[3][3],
        results[4][3],
    )


NEG=-1e30
BQ=512
ROWS=256
BK=512
F32=jnp.float32
BF=jnp.bfloat16

def nt(a,b): return lax.dot_general(a,b,(((1,),(1,)),((),())),preferred_element_type=F32)
def nn(a,b): return jnp.dot(a,b,preferred_element_type=F32)

def fill_masks(e0,e1,kaug,q0,q1,rows,pad):
    r=lax.broadcasted_iota(jnp.int32,(rows+pad,128),0)
    l=lax.broadcasted_iota(jnp.int32,(rows+pad,128),1)
    seg=(r>=e0).astype(jnp.int32)+(r>=e1).astype(jnp.int32)
    kaug[:,128:256]=jnp.where((l<3)&(l!=seg),NEG,0.0).astype(BF)
    qm=jnp.where(l==seg,1.0,0.0).astype(BF)[0:rows]
    q0[:,128:256]=qm
    q1[:,128:256]=qm

def key_range(i,e0,e1):
    first=i*BQ
    last=jnp.minimum(first+BQ,e1)-1
    lo=jnp.where(first>=e0,e0,0)
    hi=jnp.where(last>=e0,e1,e0)
    base=(lo//128)*128
    return pl.multiple_of(base,128),(hi-base+BK-1)//BK

def fwd_kernel(ctl,qo,ko,vo,qr,kr,vr,oo,ox,lse,kaug,q0,q1,vt):
    rows=kaug.shape[0]-BK
    half=rows//2
    pos,e0,e1=ctl[0],ctl[1],ctl[2]
    p=pl.program_id(0)
    @pl.when(p==0)
    def _():
        fill_masks(e0,e1,kaug,q0,q1,rows,BK)
        kaug[rows:,0:128]=jnp.zeros((BK,128),BF)
        vt[:,:]=jnp.where(lax.broadcasted_iota(jnp.int32,vt.shape,0)%80>=64,1.0,0.0).astype(BF)
    lane=lax.broadcasted_iota(jnp.int32,(half,128),1)
    for own,(q,k,v) in ((True,(qo,ko,vo)),(False,(qr,kr,vr))):
        at=pl.multiple_of((pos if own else 1-pos)*half,half)
        scaled=q[...]*jnp.asarray(0.125,BF)
        zero=jnp.zeros_like(scaled)
        q0[pl.ds(at,half),0:128]=jnp.where(lane<64,scaled,zero)
        q1[pl.ds(at,half),0:128]=jnp.where(lane<64,zero,scaled)
        kaug[pl.ds(at,half),0:128]=k[...]
        turned=v[...].T
        vt[0:64,pl.ds(at,half)]=turned[0:64]
        vt[80:144,pl.ds(at,half)]=turned[64:128]
    def qblock(i,_):
        r0=pl.multiple_of(i*BQ,BQ)
        base,count=key_range(i,e0,e1)
        qs=(q0[pl.ds(r0,BQ),:],q1[pl.ds(r0,BQ),:])
        def step(j,carry):
            k0=pl.multiple_of(base+j*BK,128)
            kb=kaug[pl.ds(k0,BK),:]
            scores=[nt(kb,qs[h]) for h in range(2)]
            out=[]
            for h in range(2):
                m,acc=carry[h]
                mn=jnp.maximum(m,jnp.max(scores[h],axis=0,keepdims=True))
                pt=jnp.exp(scores[h]-mn).astype(BF)
                acc=acc*jnp.exp(m-mn)+nn(vt[80*h:80*h+80,pl.ds(k0,BK)],pt)
                out.append((mn,acc))
            return tuple(out)
        init=(jnp.full((1,BQ),-jnp.inf,F32),jnp.zeros((80,BQ),F32))
        res=lax.fori_loop(0,count,step,(init,init))
        outs=[]
        for h in range(2):
            m,acc=res[h]
            l=acc[64:65]
            outs.append(acc[0:64]/l)
            lse[0,h:h+1,pl.ds(r0,BQ)]=m+jnp.log(l)
        ob=jnp.concatenate(outs,axis=0).T.astype(BF)
        put(i,ob)
        return 0
    def put(i,ob):
        local=i*BQ-pos*half
        @pl.when((local>=0)&(local<half))
        def _(): oo[pl.ds(pl.multiple_of(local,BQ),BQ),:]=ob
        @pl.when((local<0)|(local>=half))
        def _(): ox[pl.ds(pl.multiple_of(i*BQ-(1-pos)*half,BQ),BQ),:]=ob
    used=(e1+BQ-1)//BQ
    lax.fori_loop(0,used,qblock,0)
    def blank(i,_):
        r0=pl.multiple_of(i*BQ,BQ)
        lse[0,:,pl.ds(r0,BQ)]=jnp.zeros((8,BQ),F32)
        put(i,jnp.zeros((BQ,128),BF))
        return 0
    lax.fori_loop(used,rows//BQ,blank,0)

def attend_fwd(ctl,own,recv):
    half,width=own.shape
    pairs=width//384
    rows=2*half
    sp=[pl.BlockSpec((half,128),(lambda p,c,s=s:(0,s*pairs+p))) for s in range(3)]
    outw=pairs*128
    return pl.pallas_call(fwd_kernel,
        grid_spec=pltpu.PrefetchScalarGridSpec(num_scalar_prefetch=1,grid=(pairs,),
          in_specs=sp+sp,
          out_specs=[pl.BlockSpec((half,128),lambda p,c:(0,p))]*2+[pl.BlockSpec((1,8,rows),lambda p,c:(p,0,0))],
          scratch_shapes=[pltpu.VMEM((rows+BK,256),BF),pltpu.VMEM((rows,256),BF),pltpu.VMEM((rows,256),BF),pltpu.VMEM((160,rows+BK),BF)]),
        out_shape=[jax.ShapeDtypeStruct((half,outw),BF)]*2+[jax.ShapeDtypeStruct((pairs,8,rows),F32)],
        compiler_params=pltpu.CompilerParams(vmem_limit_bytes=60<<20,dimension_semantics=("arbitrary",)),
        cost_estimate=pl.CostEstimate(flops=4*rows*rows*64*2*pairs//2,bytes_accessed=10*half*width,transcendentals=rows*rows*pairs),
        name="attend_fwd",
    )(ctl,own,own,own,recv,recv,recv)

def bwd_kernel(ctl,qo,ko,vo,qr,kr,vr,do_o,do_r,oo,ox,lse,cos,sin,g0,g1,g2,x0,x1,x2,kaug,q0,q1,vs,d0,d1,kt,delta,dk,dv):
    rows=kaug.shape[0]-BK
    half=rows//2
    pos,e0,e1=ctl[0],ctl[1],ctl[2]
    p=pl.program_id(0)
    @pl.when(p==0)
    def _():
        fill_masks(e0,e1,kaug,q0,q1,rows,BK)
        kaug[rows:,0:128]=jnp.zeros((BK,128),BF)
        vs[rows:,:]=jnp.zeros((BK,128),BF)
        kt[:,rows:]=jnp.zeros((128,BK),BF)
    lane=lax.broadcasted_iota(jnp.int32,(half,128),1)
    pick_r=lax.broadcasted_iota(jnp.int32,(16,128),0)
    pick_l=lax.broadcasted_iota(jnp.int32,(16,128),1)
    pick=jnp.where(pick_l//64==pick_r,1.0,0.0).astype(BF)
    for own,(q,k,v,d,o) in ((True,(qo,ko,vo,do_o,oo)),(False,(qr,kr,vr,do_r,ox))):
        at=pl.multiple_of((pos if own else 1-pos)*half,half)
        scaled=q[...]*jnp.asarray(0.125,BF)
        zero=jnp.zeros_like(scaled)
        q0[pl.ds(at,half),0:128]=jnp.where(lane<64,scaled,zero)
        q1[pl.ds(at,half),0:128]=jnp.where(lane<64,zero,scaled)
        kb=k[...]
        kaug[pl.ds(at,half),0:128]=kb
        kt[:,pl.ds(at,half)]=kb.T
        vs[pl.ds(at,half),:]=v[...]
        db=d[...]
        d0[pl.ds(at,half),:]=jnp.where(lane<64,db,zero)
        d1[pl.ds(at,half),:]=jnp.where(lane<64,zero,db)
        prod=db.astype(F32)*o[...].astype(F32)
        hi=prod.astype(BF)
        lo=(prod-hi.astype(F32)).astype(BF)
        delta[:,pl.ds(at,half)]=nt(pick,hi)+nt(pick,lo)
    dk[...]=jnp.zeros_like(dk)
    dv[...]=jnp.zeros_like(dv)
    def spread(i,col,val):
        local=i*ROWS-pos*half
        @pl.when((local>=0)&(local<half))
        def _(): (g0,g1,g2)[col][pl.ds(pl.multiple_of(local,ROWS),ROWS),:]=val
        @pl.when((local<0)|(local>=half))
        def _(): (x0,x1,x2)[col][pl.ds(pl.multiple_of(i*ROWS-(1-pos)*half,ROWS),ROWS),:]=val
    def unturn(x,r0):
        ln=lax.broadcasted_iota(jnp.int32,x.shape,1)
        swapped=jnp.where((ln%64)<32,pltpu.roll(x,96,1),pltpu.roll(x,32,1))
        return x*cos[pl.ds(r0,ROWS),:]-swapped*sin[pl.ds(r0,ROWS),:]
    def qblock(i,_):
        r0=pl.multiple_of(i*BQ,BQ)
        base,count=key_range(i,e0,e1)
        qs=(q0[pl.ds(r0,BQ),:],q1[pl.ds(r0,BQ),:])
        ds_=(d0[pl.ds(r0,BQ),:],d1[pl.ds(r0,BQ),:])
        ls=[lse[0,h:h+1,pl.ds(r0,BQ)] for h in range(2)]
        de=[delta[h:h+1,pl.ds(r0,BQ)] for h in range(2)]
        def step(j,carry):
            k0=pl.multiple_of(base+j*BK,128)
            kb=kaug[pl.ds(k0,BK),:]
            vb=vs[pl.ds(k0,BK),:]
            both=range(2)
            st=[nt(kb,qs[h]) for h in both]
            dpt=[nt(vb,ds_[h]) for h in both]
            pt=[jnp.exp(st[h]-ls[h]) for h in both]
            dst=[(pt[h]*(dpt[h]-de[h])).astype(BF) for h in both]
            pb=[pt[h].astype(BF) for h in both]
            dv[pl.ds(k0,BK),:]+=nn(pb[0],ds_[0])+nn(pb[1],ds_[1])
            dk[pl.ds(k0,BK),:]+=nn(dst[0],qs[0][:,0:128])+nn(dst[1],qs[1][:,0:128])
            out=[carry[h]+nn(kt[64*h:64*h+64,pl.ds(k0,BK)],dst[h]) for h in both]
            return tuple(out)
        init=jnp.zeros((64,BQ),F32)
        res=lax.fori_loop(0,count,step,(init,init))
        dq=jnp.concatenate(res,axis=0).T*0.125
        for t in range(BQ//ROWS):
            at=pl.multiple_of(r0+t*ROWS,ROWS)
            spread(i*(BQ//ROWS)+t,0,unturn(dq[t*ROWS:(t+1)*ROWS],at).astype(BF))
        return 0
    used=(e1+BQ-1)//BQ
    lax.fori_loop(0,used,qblock,0)
    def blank(i,_):
        spread(i,0,jnp.zeros((ROWS,128),BF))
        return 0
    lax.fori_loop(used*(BQ//ROWS),rows//ROWS,blank,0)
    def last(i,_):
        r0=pl.multiple_of(i*ROWS,ROWS)
        spread(i,1,unturn(dk[pl.ds(r0,ROWS),:],r0).astype(BF))
        spread(i,2,dv[pl.ds(r0,ROWS),:].astype(BF))
        return 0
    lax.fori_loop(0,rows//ROWS,last,0)

def attend_bwd(ctl,own,recv,d_own,d_recv,o_own,o_oth,lse,cos,sin):
    half,width=own.shape
    pairs=width//384
    rows=2*half
    sp=[pl.BlockSpec((half,128),(lambda p,c,s=s:(0,s*pairs+p))) for s in range(3)]
    one=pl.BlockSpec((half,128),lambda p,c:(0,p))
    full=pl.BlockSpec((rows,128),lambda p,c:(0,0))
    return pl.pallas_call(bwd_kernel,
        grid_spec=pltpu.PrefetchScalarGridSpec(num_scalar_prefetch=1,grid=(pairs,),
          in_specs=sp+sp+[one]*4+[pl.BlockSpec((1,8,rows),lambda p,c:(p,0,0)),full,full],
          out_specs=[one]*6,
          scratch_shapes=[pltpu.VMEM((rows+BK,256),BF),pltpu.VMEM((rows,256),BF),pltpu.VMEM((rows,256),BF),
             pltpu.VMEM((rows+BK,128),BF),pltpu.VMEM((rows,128),BF),pltpu.VMEM((rows,128),BF),
             pltpu.VMEM((128,rows+BK),BF),pltpu.VMEM((16,rows),F32),pltpu.VMEM((rows+BK,128),F32),pltpu.VMEM((rows+BK,128),F32)]),
        out_shape=[jax.ShapeDtypeStruct((half,width//3),BF)]*6,
        compiler_params=pltpu.CompilerParams(vmem_limit_bytes=60<<20,dimension_semantics=("arbitrary",)),
        cost_estimate=pl.CostEstimate(flops=10*rows*rows*64*2*pairs//2,bytes_accessed=20*half*width,transcendentals=rows*rows*pairs),
        name="attend_bwd",
    )(ctl,own,own,own,recv,recv,recv,d_own,d_recv,o_own,o_oth,lse,cos,sin)

BLOCK=512

def spread_mean(x):
    return jnp.mean(x,axis=1,keepdims=True)

def row_docs(ctl,block):
    i=pl.program_id(0)
    r=ctl[0]*(block*pl.num_programs(0))+i*block+lax.broadcasted_iota(jnp.int32,(block,1),0)
    return (r>=ctl[1]).astype(jnp.int32)+(r>=ctl[2]).astype(jnp.int32)

def ffn_fwd_kernel(ctl,ao,ax,tok,w_exp,w_con,w_out,norm,u1,u2,rs,yb,hb,pf,pooled):
    block,width=tok.shape
    hidden=hb.shape[1]
    share=width//2
    pos=ctl[0]
    mine=pl.multiple_of(pos*share,share)
    other=pl.multiple_of((1-pos)*share,share)
    f=tok[...].astype(F32)+nn(ao[...],w_out[pl.ds(mine,share),:])+nn(ax[...],w_out[pl.ds(other,share),:])
    cent=f-spread_mean(f)
    scale=lax.rsqrt(spread_mean(cent*cent)+NORM_EPSILON)
    unit=cent*scale
    u1[...]=unit
    rs[:,0:128]=jnp.broadcast_to(scale,(block,128))
    y=unit*norm[0:1,:]+norm[1:2,:]
    ylow=y.astype(BF)
    yb[...]=ylow
    acc=y
    for c in range(hidden//width):
        gc=slice(c*width,(c+1)*width)
        uc=slice(hidden+c*width,hidden+(c+1)*width)
        gate=nn(ylow,w_exp[:,gc])
        up=nn(ylow,w_exp[:,uc])
        sig=jax.nn.sigmoid(gate)
        act=gate*sig
        low=(act*up).astype(BF)
        hb[:,gc]=low
        pf[:,gc]=(up*sig*(1.0+gate*(1.0-sig))).astype(BF)
        pf[:,uc]=act.astype(BF)
        acc=acc+nn(low,w_con[:,gc])
    cent=acc-spread_mean(acc)
    scale=lax.rsqrt(spread_mean(cent*cent)+NORM_EPSILON)
    unit=cent*scale
    u2[...]=unit
    rs[:,128:256]=jnp.broadcast_to(scale,(block,128))
    out=unit*norm[2:3,:]+norm[3:4,:]
    docs=row_docs(ctl,block)
    @pl.when(pl.program_id(0)==0)
    def _(): pooled[...]=jnp.zeros_like(pooled)
    for d in range(2):
        pooled[d:d+1,:]+=jnp.sum(jnp.where(docs==d,out,0.0),axis=0,keepdims=True)

def ffn_fwd(ctl,ao,ax,tok,bundle,norm,hidden):
    rows,width=tok.shape
    row=lambda n: pl.BlockSpec((BLOCK,n),lambda i,c:(i,0))
    held=lambda n,at: pl.BlockSpec((width,n),lambda i,c:(0,at//n),pipeline_mode=pl.Buffered(1))
    flat=pl.BlockSpec((8,width),lambda i,c:(0,0))
    return pl.pallas_call(ffn_fwd_kernel,
        grid_spec=pltpu.PrefetchScalarGridSpec(num_scalar_prefetch=1,grid=(rows//BLOCK,),
          in_specs=[row(width//2),row(width//2),row(width),held(2*hidden,0),held(hidden,2*hidden),held(width,3*hidden),flat],
          out_specs=[row(width),row(width),row(256),row(width),row(hidden),row(2*hidden),flat]),
        out_shape=[jax.ShapeDtypeStruct((rows,width),F32),jax.ShapeDtypeStruct((rows,width),F32),jax.ShapeDtypeStruct((rows,256),F32),
          jax.ShapeDtypeStruct((rows,width),BF),jax.ShapeDtypeStruct((rows,hidden),BF),jax.ShapeDtypeStruct((rows,2*hidden),BF),
          jax.ShapeDtypeStruct((8,width),F32)],
        compiler_params=pltpu.CompilerParams(vmem_limit_bytes=60<<20,dimension_semantics=("arbitrary",)),
        cost_estimate=pl.CostEstimate(flops=2*rows*width*(width+3*hidden),bytes_accessed=rows*(width*14+hidden*6)+2*width*(width+3*hidden),transcendentals=rows*hidden),
        name="ffn_fwd",
    )(ctl,ao,ax,tok,bundle,bundle,bundle,norm)

def loss_grad(pool,targets,len0,len1):
    width=pool.shape[1]
    docs=lax.broadcasted_iota(jnp.int32,pool.shape,0)
    length=jnp.where(docs==0,len0,len1)
    emb=pool/length
    lane=lax.broadcasted_iota(jnp.int32,pool.shape,1)
    d_target=jnp.zeros_like(pool)
    d_self=jnp.zeros_like(pool)
    for cut in (width//12,width//6,width//3,2*width//3,width):
        keep=lane<cut
        total=lambda v: jnp.sum(jnp.where(keep,v,0.0),axis=1,keepdims=True)
        own_root=lax.rsqrt(total(emb*emb)+COSINE_EPSILON)
        other_root=lax.rsqrt(total(targets*targets)+COSINE_EPSILON)
        cosine=total(emb*targets)*own_root*other_root
        d_target=d_target+jnp.where(keep,own_root*other_root,0.0)
        d_self=d_self+jnp.where(keep,cosine*own_root*own_root,0.0)
    d_emb=length*(d_self*emb-d_target*targets)
    return emb,d_emb/length

def ffn_bwd_kernel(ctl,flen,pool_a,pool_b,targets,u1,u2,rs,pf,w_exp,w_con,w_out,norm,
                   emb,mb,ub,df,ab,do,dx,gn,de):
    block,width=u1.shape
    hidden=pf.shape[1]//2
    share=width//2
    pos=ctl[0]
    @pl.when(pl.program_id(0)==0)
    def _():
        e,d=loss_grad(pool_a[...]+pool_b[...],targets[...],flen[0],flen[1])
        emb[...]=e
        de[...]=d
        gn[...]=jnp.zeros_like(gn)
    docs=row_docs(ctl,block)
    dout=jnp.where(docs==0,de[0:1,:],jnp.where(docs==1,de[1:2,:],0.0))
    unit=u2[...]
    gn[2:3,:]+=jnp.sum(dout*unit,axis=0,keepdims=True)
    gn[3:4,:]+=jnp.sum(dout,axis=0,keepdims=True)
    gu=dout*norm[2:3,:]
    dg=rs[:,128:129]*(gu-spread_mean(gu)-unit*spread_mean(gu*unit))
    mlow=dg.astype(BF)
    mb[...]=mlow
    acc=dg
    for c in range(hidden//width):
        gc=slice(c*width,(c+1)*width)
        uc=slice(hidden+c*width,hidden+(c+1)*width)
        dh=nt(mlow,w_con[:,gc])
        dgate=(dh*pf[:,gc].astype(F32)).astype(BF)
        dup=(dh*pf[:,uc].astype(F32)).astype(BF)
        ub[:,gc]=dgate
        ub[:,uc]=dup
        acc=acc+nt(dgate,w_exp[:,gc])+nt(dup,w_exp[:,uc])
    unit=u1[...]
    gn[0:1,:]+=jnp.sum(acc*unit,axis=0,keepdims=True)
    gn[1:2,:]+=jnp.sum(acc,axis=0,keepdims=True)
    gu=acc*norm[0:1,:]
    dfirst=rs[:,0:1]*(gu-spread_mean(gu)-unit*spread_mean(gu*unit))
    df[...]=dfirst
    alow=dfirst.astype(BF)
    ab[...]=alow
    do[...]=nt(alow,w_out[pl.ds(pl.multiple_of(pos*share,share),share),:]).astype(BF)
    dx[...]=nt(alow,w_out[pl.ds(pl.multiple_of((1-pos)*share,share),share),:]).astype(BF)

def ffn_bwd(ctl,flen,pool_a,pool_b,targets,u1,u2,rs,pf,bundle,norm):
    rows,width=u1.shape
    hidden=pf.shape[1]//2
    row=lambda n: pl.BlockSpec((BLOCK,n),lambda i,c,l:(i,0))
    held=lambda n,at: pl.BlockSpec((width,n),lambda i,c,l:(0,at//n),pipeline_mode=pl.Buffered(1))
    flat=pl.BlockSpec((8,width),lambda i,c,l:(0,0))
    sds=jax.ShapeDtypeStruct
    return pl.pallas_call(ffn_bwd_kernel,
        grid_spec=pltpu.PrefetchScalarGridSpec(num_scalar_prefetch=2,grid=(rows//BLOCK,),
          in_specs=[flat,flat,flat,row(width),row(width),row(256),row(2*hidden),held(2*hidden,0),held(hidden,2*hidden),held(width,3*hidden),flat],
          out_specs=[flat,row(width),row(2*hidden),row(width),row(width),row(width//2),row(width//2),flat],
          scratch_shapes=[pltpu.VMEM((8,width),F32)]),
        out_shape=[sds((8,width),F32),sds((rows,width),BF),sds((rows,2*hidden),BF),sds((rows,width),F32),sds((rows,width),BF),
          sds((rows,width//2),BF),sds((rows,width//2),BF),sds((8,width),F32)],
        compiler_params=pltpu.CompilerParams(vmem_limit_bytes=60<<20,dimension_semantics=("arbitrary",)),
        cost_estimate=pl.CostEstimate(flops=2*rows*width*(width+3*hidden),bytes_accessed=rows*(width*18+hidden*8)+2*width*(width+3*hidden),transcendentals=0),
        name="ffn_bwd",
    )(ctl,flen,pool_a,pool_b,targets,u1,u2,rs,pf,bundle,bundle,bundle,norm)

MESH=pl.DeviceIdType.MESH

def place():
    dp=lax.axis_index("dp")
    core=lax.axis_index("dim")
    return dp//4,(dp//2)%2,dp%2,core

def meet(z,y,x,core):
    chip=lambda a,b,c: a*4+b*2+c
    peers=[(chip(z,y,x),1-core),(chip(z,y,1-x),core),(chip(z,1-y,x),core)]
    peers+=[(chip(lax.rem(z+k,4),y,x),core) for k in (1,2,3)]
    barrier=pltpu.get_barrier_semaphore()
    for peer in peers:
        pl.semaphore_signal(barrier,inc=1,device_id=peer,device_id_type=MESH)
    pl.semaphore_wait(barrier,len(peers))
    return peers

def lanes_of(cols):
    tiles=cols//128
    widths=[tiles-tiles//4*3]+[tiles//4]*3
    widths=[widths[0],widths[2],widths[1],widths[3]]
    widths=[5,5,4,4] if tiles==18 else widths
    out=[]
    at=0
    for n,w in enumerate(widths):
        out.append((at*128,w*128,n%2==0))
        at+=w
    return out

def send(src,dst,sems,n,k,peer):
    copy=pltpu.make_async_remote_copy(src_ref=src,dst_ref=dst,send_sem=sems[0].at[n,k],recv_sem=sems[1].at[n,k],device_id=peer,device_id_type=MESH)
    copy.start()
    return copy

def gather_kernel(w,out,low,local,s_sem,r_sem):
    z,y,x,core=place()
    low[...]=w[...].astype(BF)
    keep=pltpu.make_async_copy(low,out.at[z,y,x,core],local)
    keep.start()
    pair,xn,yn,z1,z2,z3=meet(z,y,x,core)
    sems=(s_sem,r_sem)
    lanes=lanes_of(w.shape[1])
    every=[]
    def go(n,k,peer,*index,src=None):
        at,width,_=lanes[n]
        dst=out.at[(*index,slice(None),pl.ds(at,width))]
        if src is None: src=dst
        copy=send(src,dst,sems,n,k,peer)
        every.append(copy)
        return copy
    whole=slice(None)
    first=[]
    for n,(at,width,_) in enumerate(lanes):
        piece=low.at[:,pl.ds(at,width)]
        first.append([go(n,k,peer,z,y,x,core,src=piece) for k,peer in enumerate((z1,z2,z3))])
    keep.wait()
    second=[]
    for n,(_,_,flip) in enumerate(lanes):
        for copy in first[n]: copy.wait_recv()
        second.append(go(n,3,yn if flip else xn,whole,y,x,core))
        go(n,5,pair,whole,y,x,core)
    third=[]
    for n,(_,_,flip) in enumerate(lanes):
        second[n].wait_recv()
        if flip:
            third.append(go(n,4,xn,whole,whole,x,core))
            go(n,6,pair,whole,1-y,x,core)
        else:
            third.append(go(n,4,yn,whole,y,whole,core))
            go(n,6,pair,whole,y,1-x,core)
    for n,(_,_,flip) in enumerate(lanes):
        third[n].wait_recv()
        if flip: go(n,7,pair,whole,whole,1-x,core)
        else: go(n,7,pair,whole,1-y,whole,core)
    done=set(id(c) for c in second+third+[c for f in first for c in f])
    for copy in every:
        copy.wait_send()
        if id(copy) not in done: copy.wait_recv()

def ring_gather(w):
    share,cols=w.shape
    out=pl.pallas_call(gather_kernel,
        in_specs=[pl.BlockSpec(memory_space=pltpu.VMEM)],
        out_specs=pl.BlockSpec(memory_space=pl.ANY),
        scratch_shapes=[pltpu.VMEM((share,cols),BF),pltpu.SemaphoreType.DMA,pltpu.SemaphoreType.DMA((4,8)),pltpu.SemaphoreType.DMA((4,8))],
        out_shape=jax.ShapeDtypeStruct((4,2,2,2,share,cols),BF),
        compiler_params=pltpu.CompilerParams(collective_id=1,has_side_effects=True,vmem_limit_bytes=16<<20),
        cost_estimate=pl.CostEstimate(flops=0,bytes_accessed=64*share*cols*20,transcendentals=0),
        name="comm_gather",
    )(w)
    return out.reshape(32*share,cols)

def scatter_kernel(g,out,gl,r0,b1,k1,r1,b2,k2,r2,b3,k3,r3,local,s_sem,r_sem):
    z,y,x,core=place()
    keep=pltpu.make_async_copy(g.at[:,core],gl,local)
    keep.start()
    pair,xn,yn,z1,z2,z3=meet(z,y,x,core)
    sems=(s_sem,r_sem)
    lanes=lanes_of(out.shape[1])
    span=[pl.ds(at,width) for at,width,_ in lanes]
    every=[]
    def go(n,k,peer,src,dst):
        copy=send(src,dst,sems,n,k,peer)
        every.append(copy)
        return copy
    n_lanes=range(len(lanes))
    zero=[go(n,0,pair,g.at[:,1-core,:,span[n]],r0.at[:,:,span[n]]) for n in n_lanes]
    def split1(n,iz,j,side):
        row=iz*4+(j*2+side if lanes[n][2] else side*2+j)
        c=span[n]
        return gl[row,:,c].astype(F32)+r0[row,:,c].astype(F32)
    one=[]
    keep.wait()
    for n in n_lanes:
        flip=lanes[n][2]
        side=x if flip else y
        zero[n].wait_recv()
        for iz in range(4):
            for j in range(2):
                b1[iz,j,:,span[n]]=split1(n,iz,j,1-side).astype(BF)
        one.append(go(n,1,xn if flip else yn,b1.at[:,:,:,span[n]],r1.at[:,:,:,span[n]]))
        for iz in range(4):
            for j in range(2):
                k1[iz,j,:,span[n]]=split1(n,iz,j,side)
    two=[]
    for n in n_lanes:
        flip=lanes[n][2]
        side=y if flip else x
        c=span[n]
        one[n].wait_recv()
        for iz in range(4):
            b2[iz,:,c]=(k1[iz,1-side,:,c]+r1[iz,1-side,:,c].astype(F32)).astype(BF)
        two.append(go(n,2,yn if flip else xn,b2.at[:,:,c],r2.at[:,:,c]))
        for iz in range(4):
            k2[iz,:,c]=k1[iz,side,:,c]+r1[iz,side,:,c].astype(F32)
    three=[]
    for n in n_lanes:
        c=span[n]
        two[n].wait_recv()
        for k in (1,2,3):
            to=lax.rem(z+k,4)
            b3[k-1,:,c]=(k2[to,:,c]+r2[to,:,c].astype(F32)).astype(BF)
        three.append([go(n,2+k,(z1,z2,z3)[k-1],b3.at[k-1,:,c],r3.at[k-1,:,c]) for k in (1,2,3)])
        k3[:,c]=k2[z,:,c]+r2[z,:,c].astype(F32)
    for n in n_lanes:
        c=span[n]
        for copy in three[n]: copy.wait_recv()
        out[:,c]=k3[:,c]+r3[0,:,c].astype(F32)+r3[1,:,c].astype(F32)+r3[2,:,c].astype(F32)
    for copy in every: copy.wait_send()

def ring_scatter(g):
    rows,cols=g.shape
    share=rows//32
    v=lambda *s: pltpu.VMEM((*s,share,cols),BF)
    f=lambda *s: pltpu.VMEM((*s,share,cols),F32)
    return pl.pallas_call(scatter_kernel,
        in_specs=[pl.BlockSpec(memory_space=pl.ANY)],
        out_specs=pl.BlockSpec(memory_space=pltpu.VMEM),
        scratch_shapes=[v(16),v(16),v(4,2),f(4,2),v(4,2),v(4),f(4),v(4),v(3),f(),v(3),pltpu.SemaphoreType.DMA,pltpu.SemaphoreType.DMA((4,6)),pltpu.SemaphoreType.DMA((4,6))],
        out_shape=jax.ShapeDtypeStruct((share,cols),F32),
        compiler_params=pltpu.CompilerParams(collective_id=2,has_side_effects=True,vmem_limit_bytes=40<<20),
        cost_estimate=pl.CostEstimate(flops=0,bytes_accessed=64*share*cols*20,transcendentals=0),
        name="comm_scatter",
    )(g.reshape(16,2,share,cols))

def selector(forward):
    r=lax.broadcasted_iota(jnp.int32,(512,512),0)
    c=lax.broadcasted_iota(jnp.int32,(512,512),1)
    a,b=(r,c) if forward else (c,r)
    return jnp.where(a==4*(b%128)+b//128,1.0,0.0).astype(BF)

def bundle_kernel(exp,con,out,norm,bundle,tiles):
    share,width=out.shape
    hidden=exp.shape[1]//2
    pick=selector(True)
    for b in range(exp.shape[1]//512):
        half,at=divmod(b*512,hidden)
        y=nn(exp[:,b*512:(b+1)*512].astype(BF),pick).astype(BF)
        for j in range(4):
            to=half*hidden+j*width+at//4
            bundle[:,to:to+128]=y[:,j*128:(j+1)*128]
    for t in range(width//128):
        tiles[t]=con[:,t*128:(t+1)*128]
        for j in range(4):
            to=2*hidden+j*width+t*128
            bundle[:,to:to+128]=tiles[t,pl.ds(j,share,stride=4),:].astype(BF)
    bundle[:,3*hidden:3*hidden+width]=out[...].astype(BF)
    flat=jnp.concatenate([norm[...],jnp.zeros((4,128-share),F32)],1)
    bundle[:,3*hidden+width:]=jnp.concatenate([flat,jnp.zeros((share-4,128),F32)],0).astype(BF)

def make_bundle(exp,con,out,norm):
    share,width=out.shape
    total=exp.shape[1]+4*width+width+128
    return pl.pallas_call(bundle_kernel,
        out_shape=jax.ShapeDtypeStruct((share,total),BF),
        scratch_shapes=[pltpu.VMEM((width//128,4*share,128),F32)],
        compiler_params=pltpu.CompilerParams(vmem_limit_bytes=24<<20),
        cost_estimate=pl.CostEstimate(flops=2*share*512*exp.shape[1],bytes_accessed=6*share*total,transcendentals=0),
        name="make_bundle",
    )(exp,con,out,norm)

def update_kernel(rates,sums,*refs):
    ins,outs,tiles=refs[:12],refs[12:32],refs[32]
    exp_w,con_w,out_w,norm_w=(ins[3*k:3*k+3] for k in range(4))
    share,width=out_w[0].shape
    hidden=exp_w[0].shape[1]//2
    def step(kind,index,g,rate):
        w,m,a=(ref[index] for ref in ins[3*kind:3*kind+3])
        grad,nxt,mom,avg,low=outs[5*kind:5*kind+5]
        mn=MOMENTUM*m+g
        wn=w-rate*(g+MOMENTUM*mn)
        grad[index]=g
        nxt[index]=wn
        mom[index]=mn
        avg[index]=AVERAGE_DECAY*a+(1.0-AVERAGE_DECAY)*wn
        low[index]=wn.astype(BF)
    pick=selector(False)
    for b in range(2*hidden//512):
        half,at=divmod(b*512,hidden)
        z=jnp.concatenate([sums[:,half*hidden+j*width+at//4:half*hidden+j*width+at//4+128] for j in range(4)],1)
        step(0,(slice(None),slice(b*512,(b+1)*512)),nn(z,pick),rates[0])
    for t in range(width//128):
        for j in range(4):
            at=2*hidden+j*width+t*128
            tiles[t,pl.ds(j,share,stride=4),:]=sums[:,at:at+128].astype(F32)
        step(1,(slice(None),slice(t*128,(t+1)*128)),tiles[t],rates[0])
    step(2,(slice(None),slice(None)),sums[:,3*hidden:3*hidden+width].astype(F32),rates[0])
    step(3,(slice(None),slice(None)),sums[0:8,3*hidden+width:].astype(F32)[0:4,0:share],rates[1])

def update(sums,rates,params):
    sds=jax.ShapeDtypeStruct
    shapes=[]
    for w,_,_ in params:
        shapes+=[sds(w.shape,F32)]*4+[sds(w.shape,BF)]
    flat=[x for p in params for x in p]
    import_vmem=pl.BlockSpec(memory_space=pltpu.VMEM)
    outs=pl.pallas_call(lambda *refs: update_kernel(rates,*refs),
        in_specs=[import_vmem]*13,
        out_specs=[import_vmem]*20,
        out_shape=shapes,
        scratch_shapes=[pltpu.VMEM((params[2][0].shape[1]//128,params[1][0].shape[0],128),F32)],
        compiler_params=pltpu.CompilerParams(vmem_limit_bytes=40<<20),
        cost_estimate=pl.CostEstimate(flops=2*24*512*6144,bytes_accessed=12<<20,transcendentals=0),
        name="update",
    )(sums,*flat)
    return [outs[5*k:5*k+5] for k in range(4)]

def tail_kernel(ctl,x,qo,ko,vo,qr,kr,vr,w,df,tok,gm,acc):
    pos=ctl[0]
    i=pl.program_id(0)
    width=x.shape[1]
    share=width//2
    turned=x[...].T
    total=df[...]
    @pl.when(i==0)
    def _(): acc[...]=jnp.zeros_like(acc)
    for side,parts in ((pos,(qo,ko,vo)),(1-pos,(qr,kr,vr))):
        for s,d in enumerate(parts):
            cols=pl.ds(pl.multiple_of(s*width+side*share,128),share)
            grad=d[...]
            total=total+nt(grad,w[:,cols])
            acc[:,cols]+=nn(turned,grad)
    tok[...]=total
    @pl.when(i==pl.num_programs(0)-1)
    def _(): gm[...]=acc[...].astype(BF)

def tail(ctl,x,own,recv,w,df):
    rows,width=x.shape
    cols=w.shape[1]
    row=lambda n: pl.BlockSpec((BLOCK,n),lambda i,c:(i,0))
    held=pl.BlockSpec((width,cols),lambda i,c:(0,0),pipeline_mode=pl.Buffered(1))
    return pl.pallas_call(tail_kernel,
        grid_spec=pltpu.PrefetchScalarGridSpec(num_scalar_prefetch=1,grid=(rows//BLOCK,),
          in_specs=[row(width)]+[row(width//2)]*6+[held,row(width)],
          out_specs=[row(width),pl.BlockSpec((width,cols),lambda i,c:(0,0))],
          scratch_shapes=[pltpu.VMEM((width,cols),F32)]),
        out_shape=[jax.ShapeDtypeStruct((rows,width),F32),jax.ShapeDtypeStruct((width,cols),BF)],
        compiler_params=pltpu.CompilerParams(vmem_limit_bytes=60<<20,dimension_semantics=("arbitrary",)),
        cost_estimate=pl.CostEstimate(flops=4*rows*width*cols,bytes_accessed=rows*width*16+8*width*cols,transcendentals=0),
        name="tail",
    )(ctl,x,*own,*recv,w,df)

def mix_kernel(ctl,x,w,cos,sin,own,oth):
    pos=ctl[0]
    width=x.shape[1]
    share=width//2
    xb=x[...]
    c=cos[...]
    s=sin[...]
    lane=lax.broadcasted_iota(jnp.int32,c.shape,1)
    first=(lane%64)<32
    for out,side in ((own,pos),(oth,1-pos)):
        for part in range(3):
            cols=pl.ds(pl.multiple_of(part*width+side*share,128),share)
            y=nn(xb,w[:,cols])
            for t in range(share//128):
                z=y[:,t*128:(t+1)*128]
                if part<2:
                    swapped=jnp.where(first,pltpu.roll(z,96,1),pltpu.roll(z,32,1))
                    z=z*c+swapped*s
                out[:,part*share+t*128:part*share+(t+1)*128]=z.astype(BF)

def mix(ctl,x,w,cos,sin):
    rows,width=x.shape
    cols=w.shape[1]
    block=256
    row=lambda n: pl.BlockSpec((block,n),lambda i,c:(i,0))
    return pl.pallas_call(mix_kernel,
        grid_spec=pltpu.PrefetchScalarGridSpec(num_scalar_prefetch=1,grid=(rows//block,),
          in_specs=[row(width),pl.BlockSpec((width,cols),lambda i,c:(0,0)),row(128),row(128)],
          out_specs=[row(cols//2)]*2),
        out_shape=[jax.ShapeDtypeStruct((rows,cols//2),BF)]*2,
        compiler_params=pltpu.CompilerParams(vmem_limit_bytes=60<<20,dimension_semantics=("arbitrary",)),
        cost_estimate=pl.CostEstimate(flops=2*rows*width*cols,bytes_accessed=2*(rows*width+width*cols+rows*cols),transcendentals=0),
        name="mix",
    )(ctl,x,w,cos,sin)

def swap_cores(x):
    return lax.ppermute(x,"dim",[(0,1),(1,0)])

def join(pos,own,recv,axis=1):
    return jnp.where(pos==0,jnp.concatenate([own,recv],axis),jnp.concatenate([recv,own],axis))

def body(tokens,doc_lengths,pair_index,target_bank,mixer_in,mixer_out,expand,contract,norm_params,*rest):
    slices=lax.axis_size("dim")
    if slices!=2 or lax.axis_size("dp")!=16 or doc_lengths.shape[1]!=2:
        return body_general(tokens,doc_lengths,pair_index,target_bank,mixer_in,mixer_out,expand,contract,norm_params,*rest)
    (mixer_in_moment,mixer_out_moment,expand_moment,contract_moment,norm_moment,
     mixer_in_average,mixer_out_average,expand_average,contract_average,norm_average)=rest
    local_rows,model_width=tokens.shape
    group_rows=local_rows*slices
    pos=lax.axis_index("dim")
    doc_count=2
    w_mix=ring_gather(mixer_in[0])
    share_rows=mixer_out.shape[1]
    per=contract.shape[1]//share_rows
    count=model_width//share_rows
    hidden_width=contract.shape[1]*count
    bundle=make_bundle(expand[0],contract[0],mixer_out[0],norm_params[0])
    bundle=lax.all_gather(bundle,("dp","dim"),axis=0,tiled=True)
    at1=2*hidden_width
    at2=at1+per*model_width
    at3=at2+model_width
    w_norm=bundle[:,at3:].reshape(count,share_rows,128)[:,0:4,0:share_rows].transpose(1,0,2).reshape(4,model_width)
    lengths=doc_lengths[0]
    e0=lengths[0]
    e1=lengths[0]+lengths[1]
    ctl=jnp.stack([pos.astype(jnp.int32),e0,e1])
    ids=jnp.arange(group_rows,dtype=jnp.int32)
    seg=(ids>=e0).astype(jnp.int32)+(ids>=e1).astype(jnp.int32)
    begin=jnp.where(seg==0,0,jnp.where(seg==1,e0,e1))
    lane=jnp.arange(128,dtype=jnp.int32)
    frequency=jnp.power(1000.0,-(2*(lane%32)).astype(F32)/HEAD)
    angles=(ids-begin).astype(F32)[:,None]*frequency[None,:]
    cos=jnp.cos(angles)
    sin=jnp.sin(angles)*jnp.where((lane%64)<32,-1.0,1.0)[None,:]
    cos_own=lax.dynamic_slice_in_dim(cos,pos*local_rows,local_rows,0)
    sin_own=lax.dynamic_slice_in_dim(sin,pos*local_rows,local_rows,0)
    own,oth=mix(ctl,tokens,w_mix,cos_own,sin_own)
    recv=swap_cores(oth)
    pick=(pair_index[:,None]==jnp.arange(target_bank.shape[0],dtype=jnp.int32)[None,:]).astype(BF)
    some=matmul(pick,target_bank)
    targets=jnp.pad(join(pos,some,swap_cores(some)),((0,6),(0,0)))
    o_own,o_oth,lse=attend_fwd(ctl,own,recv)
    o_recv=swap_cores(o_oth)
    norm_gains=jnp.pad(w_norm.astype(F32),((0,4),(0,0)))
    u1,u2,rs,y_low,hidden,factors,pooled=ffn_fwd(ctl,o_own,o_recv,tokens,bundle,norm_gains,hidden_width)
    embeds,grad_m_low,grad_both,grad_first,grad_a_low,d_own,d_oth,grad_norm=ffn_bwd(
        ctl,lengths.astype(F32),pooled,swap_cores(pooled),targets,u1,u2,rs,factors,bundle,norm_gains)
    share=model_width//2
    embeddings=lax.dynamic_slice(embeds,(0,pos*share),(doc_count,share))
    d_recv=swap_cores(d_oth)
    grad_exp=inner_rows(y_low,grad_both)
    grad_con=inner_rows(hidden,grad_m_low)
    grad_out=join(pos,inner_rows(o_own,grad_a_low),inner_rows(o_recv,grad_a_low),0)
    grad_norm=grad_norm[0:4].reshape(4,count,share_rows).transpose(1,0,2)
    grad_norm=jnp.pad(grad_norm,((0,0),(0,share_rows-4),(0,128-share_rows))).reshape(model_width,128)
    fold_con=[grad_con[j*model_width:(j+1)*model_width].astype(BF) for j in range(per)]
    terms=jnp.concatenate([grad_exp.astype(BF),*fold_con,grad_out.astype(BF),grad_norm.astype(BF)],1)
    terms,d_own,d_recv=lax.optimization_barrier((terms,d_own,d_recv))
    sums=lax.psum_scatter(terms,("dp","dim"),scatter_dimension=0,tiled=True)
    backs=attend_bwd(ctl,own,recv,d_own,d_recv,o_own,o_oth,lse,cos,sin)
    token_grads,grad_mix=tail(ctl,tokens,backs[0:3],[swap_cores(g) for g in backs[3:6]],w_mix,grad_first)
    grad_mix,sums=lax.optimization_barrier((grad_mix,sums))
    total_rows=group_rows*lax.axis_size("dp")
    matrix_rate=1.0/math.sqrt(total_rows)
    norm_rate=0.3/math.sqrt(total_rows)
    new_exp,new_con,new_out,new_norm=update(sums,(matrix_rate,norm_rate),[
        (expand[0],expand_moment[0],expand_average[0]),(contract[0],contract_moment[0],contract_average[0]),
        (mixer_out[0],mixer_out_moment[0],mixer_out_average[0]),(norm_params[0],norm_moment[0],norm_average[0])])
    sum_mix=ring_scatter(grad_mix)
    nxt,mom,avg,low=advance(mixer_in[0],mixer_in_moment[0],mixer_in_average[0],sum_mix,matrix_rate)
    results=[[sum_mix,nxt,mom,avg,low],new_out,new_exp,new_con,new_norm]
    return (embeddings,token_grads,*[results[k][f][None] for f in range(5) for k in range(5)])

def solution(mesh):
    placed = (
        P(("dp", "dim"), None),
        P("dp", None),
        P("dp"),
        P(None, "dim"),
        P(None, ("dp", "dim"), None),
        P(None, ("dp", "dim"), None),
        P(None, ("dp", "dim"), None),
        P(None, ("dp", "dim"), None),
        P(None, None, ("dp", "dim")),
        P(None, ("dp", "dim"), None),
        P(None, ("dp", "dim"), None),
        P(None, ("dp", "dim"), None),
        P(None, ("dp", "dim"), None),
        P(None, None, ("dp", "dim")),
        P(None, ("dp", "dim"), None),
        P(None, ("dp", "dim"), None),
        P(None, ("dp", "dim"), None),
        P(None, ("dp", "dim"), None),
        P(None, None, ("dp", "dim")),
    )
    return jax.shard_map(
        body,
        mesh=mesh,
        in_specs=placed,
        out_specs=(
            P("dp", "dim"),
            P(("dp", "dim"), None),
            P(None, ("dp", "dim"), None),
            P(None, ("dp", "dim"), None),
            P(None, ("dp", "dim"), None),
            P(None, ("dp", "dim"), None),
            P(None, None, ("dp", "dim")),
            P(None, ("dp", "dim"), None),
            P(None, ("dp", "dim"), None),
            P(None, ("dp", "dim"), None),
            P(None, ("dp", "dim"), None),
            P(None, None, ("dp", "dim")),
            P(None, ("dp", "dim"), None),
            P(None, ("dp", "dim"), None),
            P(None, ("dp", "dim"), None),
            P(None, ("dp", "dim"), None),
            P(None, None, ("dp", "dim")),
            P(None, ("dp", "dim"), None),
            P(None, ("dp", "dim"), None),
            P(None, ("dp", "dim"), None),
            P(None, ("dp", "dim"), None),
            P(None, None, ("dp", "dim")),
            P(None, ("dp", "dim"), None),
            P(None, ("dp", "dim"), None),
            P(None, ("dp", "dim"), None),
            P(None, ("dp", "dim"), None),
            P(None, None, ("dp", "dim")),
        ),
        check_vma=False,
    )
```

```python
import math

import jax
import jax.numpy as jnp
from jax import lax
from jax.experimental import pallas as pl
from jax.experimental.pallas import tpu as pltpu
from jax.sharding import PartitionSpec as P

HEAD = 64


NORM_EPSILON = 1e-05
COSINE_EPSILON = 1e-06
MOMENTUM = 0.5
AVERAGE_DECAY = 0.5
PRECISE = lax.Precision.HIGHEST
MASKED = -1e30


def matmul(left_op, right_op):
    return jnp.dot(left_op, right_op, preferred_element_type=jnp.float32)


def matmul_exact(left_op, right_op):
    return jnp.dot(left_op, right_op, precision=PRECISE, preferred_element_type=jnp.float32)


def inner_rows(left_op, right_op):
    return lax.dot_general(
        left_op, right_op, (((0,), (0,)), ((), ())), preferred_element_type=jnp.float32
    )


def inner_cols(left_op, right_op):
    return lax.dot_general(
        left_op, right_op, (((1,), (1,)), ((), ())), preferred_element_type=jnp.float32
    )


def rotate(values, cosines, sines):
    row_count = values.shape[0]
    shaped = values.reshape(row_count, -1, 2, HEAD // 2)
    former = shaped[:, :, 0, :]
    latter = shaped[:, :, 1, :]
    cosine_b = cosines[:, None, :]
    sine_b = sines[:, None, :]
    turned = jnp.stack(
        [former * cosine_b - latter * sine_b, latter * cosine_b + former * sine_b], axis=2
    )
    return turned.reshape(values.shape)


def rotate_back(grads_in, cosines, sines):
    row_count = grads_in.shape[0]
    shaped = grads_in.reshape(row_count, -1, 2, HEAD // 2)
    former = shaped[:, :, 0, :]
    latter = shaped[:, :, 1, :]
    cosine_b = cosines[:, None, :]
    sine_b = sines[:, None, :]
    turned = jnp.stack(
        [former * cosine_b + latter * sine_b, latter * cosine_b - former * sine_b], axis=2
    )
    return turned.reshape(grads_in.shape)


def normalize(summed, gain_vec, bias_vec):
    centred = summed - jnp.mean(summed, axis=1, keepdims=True)
    scaling = lax.rsqrt(jnp.mean(centred * centred, axis=1, keepdims=True) + NORM_EPSILON)
    return centred * scaling * gain_vec + bias_vec


def normalize_back(grad_in, summed, gain_vec):
    centred = summed - jnp.mean(summed, axis=1, keepdims=True)
    scaling = lax.rsqrt(jnp.mean(centred * centred, axis=1, keepdims=True) + NORM_EPSILON)
    unit = centred * scaling
    grad_unit = grad_in * gain_vec
    grad_sum = scaling * (
        grad_unit
        - jnp.mean(grad_unit, axis=1, keepdims=True)
        - unit * jnp.mean(grad_unit * unit, axis=1, keepdims=True)
    )
    return (grad_sum, jnp.sum(grad_in * unit, axis=0), jnp.sum(grad_in, axis=0))


def flatten(stacked):
    return stacked.transpose(1, 0, 2).reshape(stacked.shape[1], -1)


def attend(q_rot, all_keys, all_values, same_doc):
    head_count = q_rot.shape[1] // HEAD

    def one_head(head_pos):
        offset = head_pos * HEAD
        query_part = lax.dynamic_slice_in_dim(q_rot, offset, HEAD, 1)
        key_part = lax.dynamic_slice_in_dim(all_keys, offset, HEAD, 1)
        value_part = lax.dynamic_slice_in_dim(all_values, offset, HEAD, 1)
        scores = jnp.where(same_doc, inner_cols(query_part, key_part) * 0.125, MASKED)
        row_max = jnp.max(scores, axis=1, keepdims=True)
        exponent = jnp.exp(scores - row_max)
        row_total = jnp.sum(exponent, axis=1, keepdims=True)
        attn_probs = (exponent / row_total).astype(jnp.bfloat16)
        return (matmul(attn_probs, value_part), (row_max + jnp.log(row_total))[:, 0])

    outputs, log_totals = lax.map(one_head, jnp.arange(head_count, dtype=jnp.int32))
    return (flatten(outputs), log_totals)


def attend_back(q_rot, all_keys, all_values, same_doc, grad_out, log_totals):
    head_count = q_rot.shape[1] // HEAD

    def one_head(pack):
        head_pos, log_total = pack
        offset = head_pos * HEAD
        query_part = lax.dynamic_slice_in_dim(q_rot, offset, HEAD, 1)
        key_part = lax.dynamic_slice_in_dim(all_keys, offset, HEAD, 1)
        value_part = lax.dynamic_slice_in_dim(all_values, offset, HEAD, 1)
        grad_part = lax.dynamic_slice_in_dim(grad_out, offset, HEAD, 1)
        scores = jnp.where(same_doc, inner_cols(query_part, key_part) * 0.125, MASKED)
        attn_probs = jnp.exp(scores - log_total[:, None])
        grad_probs = inner_cols(grad_part, value_part)
        row_dot = jnp.sum(attn_probs * grad_probs, axis=1, keepdims=True)
        grad_scores = (attn_probs * (grad_probs - row_dot)).astype(jnp.bfloat16)
        grad_query = matmul(grad_scores, key_part) * 0.125
        grad_key = inner_rows(grad_scores, query_part) * 0.125
        grad_value = inner_rows(attn_probs.astype(jnp.bfloat16), grad_part)
        return (grad_query, grad_key, grad_value)

    mapped = lax.map(one_head, (jnp.arange(head_count, dtype=jnp.int32), log_totals))
    return (flatten(mapped[0]), flatten(mapped[1]), flatten(mapped[2]))


def advance(weight, moment, average, grad_in, rate):
    moment_next = MOMENTUM * moment + grad_in
    weight_next = weight - rate * (grad_in + MOMENTUM * moment_next)
    average_next = AVERAGE_DECAY * average + (1.0 - AVERAGE_DECAY) * weight_next
    return (weight_next, moment_next, average_next, weight_next.astype(jnp.bfloat16))


def body_general(
    tokens,
    doc_lengths,
    pair_index,
    target_bank,
    mixer_in,
    mixer_out,
    expand,
    contract,
    norm_params,
    mixer_in_moment,
    mixer_out_moment,
    expand_moment,
    contract_moment,
    norm_moment,
    mixer_in_average,
    mixer_out_average,
    expand_average,
    contract_average,
    norm_average,
):
    local_rows, model_width = tokens.shape
    slices = lax.axis_size("dim")
    group_rows = local_rows * slices
    position = lax.axis_index("dim")
    layer_count = mixer_in.shape[0]
    doc_count = doc_lengths.shape[1]
    lengths = doc_lengths[0]
    doc_ends = jnp.cumsum(lengths)
    doc_starts = doc_ends - lengths
    row_ids = position * local_rows + jnp.arange(local_rows, dtype=jnp.int32)
    key_ids = jnp.arange(group_rows, dtype=jnp.int32)
    seg_rows = jnp.sum((row_ids[:, None] >= doc_ends[None, :]).astype(jnp.int32), axis=1)
    seg_keys = jnp.sum((key_ids[:, None] >= doc_ends[None, :]).astype(jnp.int32), axis=1)
    first_rows = jnp.concatenate([doc_starts, doc_ends[-1:]])
    segment_ids = jnp.arange(doc_count + 1, dtype=jnp.int32)
    row_begin = jnp.sum(
        jnp.where(seg_rows[:, None] == segment_ids[None, :], first_rows[None, :], 0), axis=1
    )
    frequency = jnp.power(1000.0, -jnp.arange(0, HEAD, 2).astype(jnp.float32) / HEAD)
    angles = (row_ids - row_begin).astype(jnp.float32)[:, None] * frequency[None, :]
    cosines = jnp.cos(angles)
    sines = jnp.sin(angles)
    same_doc = seg_rows[:, None] == seg_keys[None, :]
    stream = tokens.astype(jnp.float32)
    layer_pos = 0
    layer_weights = (
        lax.all_gather(mixer_in[layer_pos].astype(jnp.bfloat16), ("dp", "dim"), axis=0, tiled=True),
        lax.all_gather(
            mixer_out[layer_pos].astype(jnp.bfloat16), ("dp", "dim"), axis=0, tiled=True
        ),
        lax.all_gather(expand[layer_pos].astype(jnp.bfloat16), ("dp", "dim"), axis=0, tiled=True),
        lax.all_gather(contract[layer_pos].astype(jnp.bfloat16), ("dp", "dim"), axis=0, tiled=True),
        lax.all_gather(
            norm_params[layer_pos].astype(jnp.bfloat16), ("dp", "dim"), axis=1, tiled=True
        ),
    )
    w_mix, w_out, w_exp, w_con, w_norm = layer_weights
    norm_gains = w_norm.astype(jnp.float32)
    x_low = stream.astype(jnp.bfloat16)
    mixed = matmul(x_low, w_mix)
    q_rot = rotate(mixed[:, 0:model_width], cosines, sines).astype(jnp.bfloat16)
    k_rot = rotate(mixed[:, model_width : 2 * model_width], cosines, sines).astype(jnp.bfloat16)
    v_low = mixed[:, 2 * model_width : 3 * model_width].astype(jnp.bfloat16)
    all_keys = lax.all_gather(k_rot, "dim", axis=0, tiled=True)
    all_values = lax.all_gather(v_low, "dim", axis=0, tiled=True)
    attended, log_totals = attend(q_rot, all_keys, all_values, same_doc)
    att_low = attended.astype(jnp.bfloat16)
    first_sum = stream + matmul(att_low, w_out)
    normed = normalize(first_sum, norm_gains[0], norm_gains[1])
    y_low = normed.astype(jnp.bfloat16)
    gate_up = matmul(y_low, w_exp)
    half = gate_up.shape[1] // 2
    hidden = (jax.nn.silu(gate_up[:, 0:half]) * gate_up[:, half : 2 * half]).astype(jnp.bfloat16)
    second_sum = normed + matmul(hidden, w_con)
    saved = [
        (
            stream,
            layer_weights,
            q_rot,
            k_rot,
            v_low,
            all_keys,
            all_values,
            log_totals,
            attended,
            att_low,
            first_sum,
            normed,
            y_low,
            gate_up,
            hidden,
            second_sum,
        )
    ]
    stream = normalize(second_sum, norm_gains[2], norm_gains[3])
    member = (seg_rows[None, :] == jnp.arange(doc_count, dtype=jnp.int32)[:, None]).astype(
        jnp.float32
    )
    partial_value = matmul_exact(member, stream)
    pooled = lax.psum_scatter(partial_value, "dim", scatter_dimension=1, tiled=True)
    length_f = lengths.astype(jnp.float32)
    embeddings = pooled / length_f[:, None]
    share = embeddings.shape[1]
    pick = (
        pair_index[:, None] == jnp.arange(target_bank.shape[0], dtype=jnp.int32)[None, :]
    ).astype(jnp.bfloat16)
    targets = matmul(pick, target_bank)
    feature_ids = position * share + jnp.arange(share, dtype=jnp.int32)
    cuts = jnp.array(
        [model_width // 12, model_width // 6, model_width // 3, 2 * model_width // 3, model_width],
        dtype=jnp.int32,
    )
    masks = (feature_ids[None, :] < cuts[:, None]).astype(jnp.float32)
    cross = matmul_exact(embeddings * targets, masks.T)
    own = matmul_exact(embeddings * embeddings, masks.T)
    other = matmul_exact(targets * targets, masks.T)
    cross, own, other = lax.psum((cross, own, other), "dim")
    own_root = lax.rsqrt(own + COSINE_EPSILON)
    other_root = lax.rsqrt(other + COSINE_EPSILON)
    cosine = cross * own_root * other_root
    coef_target = -length_f[:, None] * own_root * other_root
    coef_self = length_f[:, None] * cosine * own_root * own_root
    grad_emb = (
        matmul_exact(coef_target, masks) * targets + matmul_exact(coef_self, masks) * embeddings
    )
    grad_full = lax.all_gather(grad_emb, "dim", axis=1, tiled=True)
    spread_rows = member / length_f[:, None]
    grad_stream = lax.dot_general(
        spread_rows,
        grad_full,
        (((0,), (0,)), ((), ())),
        precision=PRECISE,
        preferred_element_type=jnp.float32,
    )
    grad_list = [None] * layer_count
    for layer_pos in reversed(range(layer_count)):
        (
            layer_input,
            layer_weights,
            q_rot,
            k_rot,
            v_low,
            all_keys,
            all_values,
            log_totals,
            attended,
            att_low,
            first_sum,
            normed,
            y_low,
            gate_up,
            hidden,
            second_sum,
        ) = saved[layer_pos]
        w_mix = lax.all_gather(
            mixer_in[layer_pos].astype(jnp.bfloat16), ("dp", "dim"), axis=0, tiled=True
        )
        w_out = lax.all_gather(
            mixer_out[layer_pos].astype(jnp.bfloat16), ("dp", "dim"), axis=0, tiled=True
        )
        w_exp = lax.all_gather(
            expand[layer_pos].astype(jnp.bfloat16), ("dp", "dim"), axis=0, tiled=True
        )
        w_con = lax.all_gather(
            contract[layer_pos].astype(jnp.bfloat16), ("dp", "dim"), axis=0, tiled=True
        )
        w_norm = lax.all_gather(
            norm_params[layer_pos].astype(jnp.bfloat16), ("dp", "dim"), axis=1, tiled=True
        )
        norm_gains = w_norm.astype(jnp.float32)
        grad_second, grad_gain2, grad_bias2 = normalize_back(grad_stream, second_sum, norm_gains[2])
        grad_m_low = grad_second.astype(jnp.bfloat16)
        grad_con = inner_rows(hidden, grad_m_low)
        grad_hidden = inner_cols(grad_m_low, w_con)
        half = gate_up.shape[1] // 2
        gate_part = gate_up[:, 0:half]
        up_part = gate_up[:, half : 2 * half]
        sigmoid_gate = jax.nn.sigmoid(gate_part)
        activated = gate_part * sigmoid_gate
        grad_gate = grad_hidden * up_part * sigmoid_gate * (1.0 + gate_part * (1.0 - sigmoid_gate))
        grad_up = grad_hidden * activated
        grad_both = jnp.concatenate([grad_gate, grad_up], axis=1).astype(jnp.bfloat16)
        grad_exp = inner_rows(y_low, grad_both)
        grad_normed = grad_second + inner_cols(grad_both, w_exp)
        grad_first, grad_gain1, grad_bias1 = normalize_back(grad_normed, first_sum, norm_gains[0])
        grad_a_low = grad_first.astype(jnp.bfloat16)
        grad_out = inner_rows(att_low, grad_a_low)
        grad_attended = inner_cols(grad_a_low, w_out).astype(jnp.bfloat16)
        keys_back, values_back = (
            lax.all_gather(k_rot, "dim", axis=0, tiled=True),
            lax.all_gather(v_low, "dim", axis=0, tiled=True),
        )
        grad_query, grad_key_all, grad_value_all = attend_back(
            q_rot, keys_back, values_back, same_doc, grad_attended, log_totals
        )
        grad_kv = lax.psum_scatter(
            jnp.concatenate([grad_key_all, grad_value_all], axis=1).astype(jnp.bfloat16),
            "dim",
            scatter_dimension=0,
            tiled=True,
        ).astype(jnp.float32)
        grad_mixed = jnp.concatenate(
            [
                rotate_back(grad_query, cosines, sines),
                rotate_back(grad_kv[:, 0:model_width], cosines, sines),
                grad_kv[:, model_width : 2 * model_width],
            ],
            axis=1,
        ).astype(jnp.bfloat16)
        x_low = layer_input.astype(jnp.bfloat16)
        grad_mix = inner_rows(x_low, grad_mixed)
        grad_stream = grad_first + inner_cols(grad_mixed, w_mix)
        grad_norm = jnp.stack([grad_gain1, grad_bias1, grad_gain2, grad_bias2])
        grad_list[layer_pos] = (
            lax.psum_scatter(grad_mix, ("dp", "dim"), scatter_dimension=0, tiled=True),
            lax.psum_scatter(grad_out, ("dp", "dim"), scatter_dimension=0, tiled=True),
            lax.psum_scatter(grad_exp, ("dp", "dim"), scatter_dimension=0, tiled=True),
            lax.psum_scatter(grad_con, ("dp", "dim"), scatter_dimension=0, tiled=True),
            lax.psum_scatter(grad_norm, ("dp", "dim"), scatter_dimension=1, tiled=True),
        )
    total_rows = group_rows * lax.axis_size("dp")
    matrix_rate = 1.0 / math.sqrt(total_rows)
    norm_rate = 0.3 / math.sqrt(total_rows)
    grads = [jnp.stack([grad_list[0][kind]]) for kind in range(5)]
    weights = (mixer_in, mixer_out, expand, contract, norm_params)
    moments = (mixer_in_moment, mixer_out_moment, expand_moment, contract_moment, norm_moment)
    averages = (mixer_in_average, mixer_out_average, expand_average, contract_average, norm_average)
    rates = (matrix_rate, matrix_rate, matrix_rate, matrix_rate, norm_rate)
    results = [
        advance(weights[kind], moments[kind], averages[kind], grads[kind], rates[kind])
        for kind in range(5)
    ]
    return (
        embeddings,
        grad_stream,
        grads[0],
        grads[1],
        grads[2],
        grads[3],
        grads[4],
        results[0][0],
        results[1][0],
        results[2][0],
        results[3][0],
        results[4][0],
        results[0][1],
        results[1][1],
        results[2][1],
        results[3][1],
        results[4][1],
        results[0][2],
        results[1][2],
        results[2][2],
        results[3][2],
        results[4][2],
        results[0][3],
        results[1][3],
        results[2][3],
        results[3][3],
        results[4][3],
    )


NEG=-1e30
BQ=512
ROWS=256
BK=384
F32=jnp.float32
BF=jnp.bfloat16

def nt(a,b): return lax.dot_general(a,b,(((1,),(1,)),((),())),preferred_element_type=F32)
def nn(a,b): return jnp.dot(a,b,preferred_element_type=F32)

def fill_masks(e0,e1,kaug,q0,q1,rows,pad):
    r=lax.broadcasted_iota(jnp.int32,(rows+pad,128),0)
    l=lax.broadcasted_iota(jnp.int32,(rows+pad,128),1)
    seg=(r>=e0).astype(jnp.int32)+(r>=e1).astype(jnp.int32)
    kaug[:,128:256]=jnp.where((l<3)&(l!=seg),NEG,0.0).astype(BF)
    qm=jnp.where(l==seg,1.0,0.0).astype(BF)[0:rows]
    q0[:,128:256]=qm
    q1[:,128:256]=qm

def key_range(i,e0,e1):
    first=i*BQ
    last=jnp.minimum(first+BQ,e1)-1
    lo=jnp.where(first>=e0,e0,0)
    hi=jnp.where(last>=e0,e1,e0)
    base=(lo//128)*128
    return pl.multiple_of(base,128),(hi-base+BK-1)//BK

def fwd_kernel(ctl,qo,ko,vo,qr,kr,vr,oo,ox,lse,kaug,q0,q1,vt):
    rows=kaug.shape[0]-BK
    half=rows//2
    pos,e0,e1=ctl[0],ctl[1],ctl[2]
    p=pl.program_id(0)
    @pl.when(p==0)
    def _():
        fill_masks(e0,e1,kaug,q0,q1,rows,BK)
        kaug[rows:,0:128]=jnp.zeros((BK,128),BF)
        vt[:,:]=jnp.where(lax.broadcasted_iota(jnp.int32,vt.shape,0)%80>=64,1.0,0.0).astype(BF)
    lane=lax.broadcasted_iota(jnp.int32,(half,128),1)
    for own,(q,k,v) in ((True,(qo,ko,vo)),(False,(qr,kr,vr))):
        at=pl.multiple_of((pos if own else 1-pos)*half,half)
        scaled=q[...]*jnp.asarray(0.125,BF)
        zero=jnp.zeros_like(scaled)
        q0[pl.ds(at,half),0:128]=jnp.where(lane<64,scaled,zero)
        q1[pl.ds(at,half),0:128]=jnp.where(lane<64,zero,scaled)
        kaug[pl.ds(at,half),0:128]=k[...]
        turned=v[...].T
        vt[0:64,pl.ds(at,half)]=turned[0:64]
        vt[80:144,pl.ds(at,half)]=turned[64:128]
    def qblock(i,_):
        r0=pl.multiple_of(i*BQ,BQ)
        base,count=key_range(i,e0,e1)
        qs=(q0[pl.ds(r0,BQ),:],q1[pl.ds(r0,BQ),:])
        def step(j,carry):
            k0=pl.multiple_of(base+j*BK,128)
            kb=kaug[pl.ds(k0,BK),:]
            scores=[nt(kb,qs[h]) for h in range(2)]
            out=[]
            for h in range(2):
                m,acc=carry[h]
                mn=jnp.maximum(m,jnp.max(scores[h],axis=0,keepdims=True))
                pt=jnp.exp(scores[h]-mn).astype(BF)
                acc=acc*jnp.exp(m-mn)+nn(vt[80*h:80*h+80,pl.ds(k0,BK)],pt)
                out.append((mn,acc))
            return tuple(out)
        init=(jnp.full((1,BQ),-jnp.inf,F32),jnp.zeros((80,BQ),F32))
        res=lax.fori_loop(0,count,step,(init,init))
        outs=[]
        for h in range(2):
            m,acc=res[h]
            l=acc[64:65]
            outs.append(acc[0:64]/l)
            lse[0,h:h+1,pl.ds(r0,BQ)]=m+jnp.log(l)
        ob=jnp.concatenate(outs,axis=0).T.astype(BF)
        put(i,ob)
        return 0
    def put(i,ob):
        local=i*BQ-pos*half
        @pl.when((local>=0)&(local<half))
        def _(): oo[pl.ds(pl.multiple_of(local,BQ),BQ),:]=ob
        @pl.when((local<0)|(local>=half))
        def _(): ox[pl.ds(pl.multiple_of(i*BQ-(1-pos)*half,BQ),BQ),:]=ob
    used=(e1+BQ-1)//BQ
    lax.fori_loop(0,used,qblock,0)
    def blank(i,_):
        r0=pl.multiple_of(i*BQ,BQ)
        lse[0,:,pl.ds(r0,BQ)]=jnp.zeros((8,BQ),F32)
        put(i,jnp.zeros((BQ,128),BF))
        return 0
    lax.fori_loop(used,rows//BQ,blank,0)

def attend_fwd(ctl,own,recv):
    half,width=own.shape
    pairs=width//384
    rows=2*half
    sp=[pl.BlockSpec((half,128),(lambda p,c,s=s:(0,s*pairs+p))) for s in range(3)]
    outw=pairs*128
    return pl.pallas_call(fwd_kernel,
        grid_spec=pltpu.PrefetchScalarGridSpec(num_scalar_prefetch=1,grid=(pairs,),
          in_specs=sp+sp,
          out_specs=[pl.BlockSpec((half,128),lambda p,c:(0,p))]*2+[pl.BlockSpec((1,8,rows),lambda p,c:(p,0,0))],
          scratch_shapes=[pltpu.VMEM((rows+BK,256),BF),pltpu.VMEM((rows,256),BF),pltpu.VMEM((rows,256),BF),pltpu.VMEM((160,rows+BK),BF)]),
        out_shape=[jax.ShapeDtypeStruct((half,outw),BF)]*2+[jax.ShapeDtypeStruct((pairs,8,rows),F32)],
        compiler_params=pltpu.CompilerParams(vmem_limit_bytes=60<<20,dimension_semantics=("arbitrary",)),
        cost_estimate=pl.CostEstimate(flops=4*rows*rows*64*2*pairs//2,bytes_accessed=10*half*width,transcendentals=rows*rows*pairs),
        name="attend_fwd",
    )(ctl,own,own,own,recv,recv,recv)

def bwd_kernel(ctl,qo,ko,vo,qr,kr,vr,do_o,do_r,oo,ox,lse,cos,sin,g0,g1,g2,x0,x1,x2,kaug,q0,q1,vs,d0,d1,kt,delta,dk,dv):
    rows=kaug.shape[0]-BK
    half=rows//2
    pos,e0,e1=ctl[0],ctl[1],ctl[2]
    p=pl.program_id(0)
    @pl.when(p==0)
    def _():
        fill_masks(e0,e1,kaug,q0,q1,rows,BK)
        kaug[rows:,0:128]=jnp.zeros((BK,128),BF)
        vs[rows:,:]=jnp.zeros((BK,128),BF)
        kt[:,rows:]=jnp.zeros((128,BK),BF)
    lane=lax.broadcasted_iota(jnp.int32,(half,128),1)
    pick_r=lax.broadcasted_iota(jnp.int32,(16,128),0)
    pick_l=lax.broadcasted_iota(jnp.int32,(16,128),1)
    pick=jnp.where(pick_l//64==pick_r,1.0,0.0).astype(BF)
    for own,(q,k,v,d,o) in ((True,(qo,ko,vo,do_o,oo)),(False,(qr,kr,vr,do_r,ox))):
        at=pl.multiple_of((pos if own else 1-pos)*half,half)
        scaled=q[...]*jnp.asarray(0.125,BF)
        zero=jnp.zeros_like(scaled)
        q0[pl.ds(at,half),0:128]=jnp.where(lane<64,scaled,zero)
        q1[pl.ds(at,half),0:128]=jnp.where(lane<64,zero,scaled)
        kb=k[...]
        kaug[pl.ds(at,half),0:128]=kb
        kt[:,pl.ds(at,half)]=kb.T
        vs[pl.ds(at,half),:]=v[...]
        db=d[...]
        d0[pl.ds(at,half),:]=jnp.where(lane<64,db,zero)
        d1[pl.ds(at,half),:]=jnp.where(lane<64,zero,db)
        prod=db.astype(F32)*o[...].astype(F32)
        hi=prod.astype(BF)
        lo=(prod-hi.astype(F32)).astype(BF)
        delta[:,pl.ds(at,half)]=nt(pick,hi)+nt(pick,lo)
    dk[...]=jnp.zeros_like(dk)
    dv[...]=jnp.zeros_like(dv)
    def spread(i,col,val):
        local=i*ROWS-pos*half
        @pl.when((local>=0)&(local<half))
        def _(): (g0,g1,g2)[col][pl.ds(pl.multiple_of(local,ROWS),ROWS),:]=val
        @pl.when((local<0)|(local>=half))
        def _(): (x0,x1,x2)[col][pl.ds(pl.multiple_of(i*ROWS-(1-pos)*half,ROWS),ROWS),:]=val
    def unturn(x,r0):
        ln=lax.broadcasted_iota(jnp.int32,x.shape,1)
        swapped=jnp.where((ln%64)<32,pltpu.roll(x,96,1),pltpu.roll(x,32,1))
        return x*cos[pl.ds(r0,ROWS),:]-swapped*sin[pl.ds(r0,ROWS),:]
    def qblock(i,_):
        r0=pl.multiple_of(i*BQ,BQ)
        base,count=key_range(i,e0,e1)
        qs=(q0[pl.ds(r0,BQ),:],q1[pl.ds(r0,BQ),:])
        ds_=(d0[pl.ds(r0,BQ),:],d1[pl.ds(r0,BQ),:])
        ls=[lse[0,h:h+1,pl.ds(r0,BQ)] for h in range(2)]
        de=[delta[h:h+1,pl.ds(r0,BQ)] for h in range(2)]
        def step(j,carry):
            k0=pl.multiple_of(base+j*BK,128)
            kb=kaug[pl.ds(k0,BK),:]
            vb=vs[pl.ds(k0,BK),:]
            both=range(2)
            st=[nt(kb,qs[h]) for h in both]
            dpt=[nt(vb,ds_[h]) for h in both]
            pt=[jnp.exp(st[h]-ls[h]) for h in both]
            dst=[(pt[h]*(dpt[h]-de[h])).astype(BF) for h in both]
            pb=[pt[h].astype(BF) for h in both]
            dv[pl.ds(k0,BK),:]+=nn(pb[0],ds_[0])+nn(pb[1],ds_[1])
            dk[pl.ds(k0,BK),:]+=nn(dst[0],qs[0][:,0:128])+nn(dst[1],qs[1][:,0:128])
            out=[carry[h]+nn(kt[64*h:64*h+64,pl.ds(k0,BK)],dst[h]) for h in both]
            return tuple(out)
        init=jnp.zeros((64,BQ),F32)
        res=lax.fori_loop(0,count,step,(init,init))
        dq=jnp.concatenate(res,axis=0).T*0.125
        for t in range(BQ//ROWS):
            at=pl.multiple_of(r0+t*ROWS,ROWS)
            spread(i*(BQ//ROWS)+t,0,unturn(dq[t*ROWS:(t+1)*ROWS],at).astype(BF))
        return 0
    used=(e1+BQ-1)//BQ
    lax.fori_loop(0,used,qblock,0)
    def blank(i,_):
        spread(i,0,jnp.zeros((ROWS,128),BF))
        return 0
    lax.fori_loop(used*(BQ//ROWS),rows//ROWS,blank,0)
    def last(i,_):
        r0=pl.multiple_of(i*ROWS,ROWS)
        spread(i,1,unturn(dk[pl.ds(r0,ROWS),:],r0).astype(BF))
        spread(i,2,dv[pl.ds(r0,ROWS),:].astype(BF))
        return 0
    lax.fori_loop(0,rows//ROWS,last,0)

def attend_bwd(ctl,own,recv,d_own,d_recv,o_own,o_oth,lse,cos,sin):
    half,width=own.shape
    pairs=width//384
    rows=2*half
    sp=[pl.BlockSpec((half,128),(lambda p,c,s=s:(0,s*pairs+p))) for s in range(3)]
    one=pl.BlockSpec((half,128),lambda p,c:(0,p))
    full=pl.BlockSpec((rows,128),lambda p,c:(0,0))
    return pl.pallas_call(bwd_kernel,
        grid_spec=pltpu.PrefetchScalarGridSpec(num_scalar_prefetch=1,grid=(pairs,),
          in_specs=sp+sp+[one]*4+[pl.BlockSpec((1,8,rows),lambda p,c:(p,0,0)),full,full],
          out_specs=[one]*6,
          scratch_shapes=[pltpu.VMEM((rows+BK,256),BF),pltpu.VMEM((rows,256),BF),pltpu.VMEM((rows,256),BF),
             pltpu.VMEM((rows+BK,128),BF),pltpu.VMEM((rows,128),BF),pltpu.VMEM((rows,128),BF),
             pltpu.VMEM((128,rows+BK),BF),pltpu.VMEM((16,rows),F32),pltpu.VMEM((rows+BK,128),F32),pltpu.VMEM((rows+BK,128),F32)]),
        out_shape=[jax.ShapeDtypeStruct((half,width//3),BF)]*6,
        compiler_params=pltpu.CompilerParams(vmem_limit_bytes=60<<20,dimension_semantics=("arbitrary",)),
        cost_estimate=pl.CostEstimate(flops=10*rows*rows*64*2*pairs//2,bytes_accessed=20*half*width,transcendentals=rows*rows*pairs),
        name="attend_bwd",
    )(ctl,own,own,own,recv,recv,recv,d_own,d_recv,o_own,o_oth,lse,cos,sin)

BLOCK=256

def spread_mean(x):
    return jnp.mean(x,axis=1,keepdims=True)

def row_docs(ctl,block):
    i=pl.program_id(0)
    r=ctl[0]*(block*pl.num_programs(0))+i*block+lax.broadcasted_iota(jnp.int32,(block,1),0)
    return (r>=ctl[1]).astype(jnp.int32)+(r>=ctl[2]).astype(jnp.int32)

def ffn_fwd_kernel(ctl,ao,ax,tok,w_exp,w_con,w_out,norm,u1,u2,rs,yb,h0,h1,h2,h3,pf,pooled):
    block,width=tok.shape
    hidden=pf.shape[1]//2
    kept=(h0,h1,h2,h3)
    share=width//2
    pos=ctl[0]
    mine=pl.multiple_of(pos*share,share)
    other=pl.multiple_of((1-pos)*share,share)
    f=tok[...].astype(F32)+nn(ao[...],w_out[pl.ds(mine,share),:])+nn(ax[...],w_out[pl.ds(other,share),:])
    cent=f-spread_mean(f)
    scale=lax.rsqrt(spread_mean(cent*cent)+NORM_EPSILON)
    unit=cent*scale
    u1[...]=unit
    rs[:,0:128]=jnp.broadcast_to(scale,(block,128))
    y=unit*norm[0:1,:]+norm[1:2,:]
    ylow=y.astype(BF)
    yb[...]=ylow
    acc=y
    count=hidden//width
    spans=[(slice(c*width,(c+1)*width),slice(hidden+c*width,hidden+(c+1)*width)) for c in range(count)]
    pre=lambda c: (nn(ylow,w_exp[:,spans[c][0]]),nn(ylow,w_exp[:,spans[c][1]]))
    ahead=pre(0)
    for c in range(count):
        gate,up=ahead
        if c+1<count: ahead=pre(c+1)
        gc,uc=spans[c]
        sig=jax.nn.sigmoid(gate)
        act=gate*sig
        low=(act*up).astype(BF)
        kept[c][...]=low
        pf[:,gc]=(up*(sig+act*(1.0-sig))).astype(BF)
        pf[:,uc]=act.astype(BF)
        acc=acc+nn(low,w_con[:,gc])
    cent=acc-spread_mean(acc)
    scale=lax.rsqrt(spread_mean(cent*cent)+NORM_EPSILON)
    unit=cent*scale
    u2[...]=unit
    rs[:,128:256]=jnp.broadcast_to(scale,(block,128))
    out=unit*norm[2:3,:]+norm[3:4,:]
    docs=row_docs(ctl,block)
    @pl.when(pl.program_id(0)==0)
    def _(): pooled[...]=jnp.zeros_like(pooled)
    for d in range(2):
        pooled[d:d+1,:]+=jnp.sum(jnp.where(docs==d,out,0.0),axis=0,keepdims=True)

def ffn_fwd(ctl,ao,ax,tok,bundle,norm,hidden):
    rows,width=tok.shape
    row=lambda n: pl.BlockSpec((BLOCK,n),lambda i,c:(i,0))
    held=lambda n,at: pl.BlockSpec((width,n),lambda i,c:(0,at//n),pipeline_mode=pl.Buffered(1))
    flat=pl.BlockSpec((8,width),lambda i,c:(0,0))
    return pl.pallas_call(ffn_fwd_kernel,
        grid_spec=pltpu.PrefetchScalarGridSpec(num_scalar_prefetch=1,grid=(rows//BLOCK,),
          in_specs=[row(width//2),row(width//2),row(width),held(2*hidden,0),held(hidden,2*hidden),held(width,3*hidden),flat],
          out_specs=[row(width),row(width),row(256),*[row(width)]*5,row(2*hidden),flat]),
        out_shape=[jax.ShapeDtypeStruct((rows,width),F32),jax.ShapeDtypeStruct((rows,width),F32),jax.ShapeDtypeStruct((rows,256),F32),
          *[jax.ShapeDtypeStruct((rows,width),BF)]*5,jax.ShapeDtypeStruct((rows,2*hidden),BF),
          jax.ShapeDtypeStruct((8,width),F32)],
        compiler_params=pltpu.CompilerParams(vmem_limit_bytes=60<<20,dimension_semantics=("arbitrary",)),
        cost_estimate=pl.CostEstimate(flops=2*rows*width*(width+3*hidden),bytes_accessed=rows*(width*14+hidden*6)+2*width*(width+3*hidden),transcendentals=rows*hidden),
        name="ffn_fwd",
    )(ctl,ao,ax,tok,bundle,bundle,bundle,norm)

def loss_grad(pool,targets,len0,len1):
    width=pool.shape[1]
    docs=lax.broadcasted_iota(jnp.int32,pool.shape,0)
    length=jnp.where(docs==0,len0,len1)
    emb=pool/length
    lane=lax.broadcasted_iota(jnp.int32,pool.shape,1)
    d_target=jnp.zeros_like(pool)
    d_self=jnp.zeros_like(pool)
    for cut in (width//12,width//6,width//3,2*width//3,width):
        keep=lane<cut
        total=lambda v: jnp.sum(jnp.where(keep,v,0.0),axis=1,keepdims=True)
        own_root=lax.rsqrt(total(emb*emb)+COSINE_EPSILON)
        other_root=lax.rsqrt(total(targets*targets)+COSINE_EPSILON)
        cosine=total(emb*targets)*own_root*other_root
        d_target=d_target+jnp.where(keep,own_root*other_root,0.0)
        d_self=d_self+jnp.where(keep,cosine*own_root*own_root,0.0)
    d_emb=length*(d_self*emb-d_target*targets)
    return emb,d_emb/length

def ffn_bwd_kernel(ctl,flen,pool_a,pool_b,targets,u1,u2,rs,pf,w_exp,w_con,w_out,norm,
                   emb,mb,ub,df,ab,do,dx,gn,de):
    block,width=u1.shape
    hidden=pf.shape[1]//2
    share=width//2
    pos=ctl[0]
    @pl.when(pl.program_id(0)==0)
    def _():
        e,d=loss_grad(pool_a[...]+pool_b[...],targets[...],flen[0],flen[1])
        emb[...]=e
        de[...]=d
        gn[...]=jnp.zeros_like(gn)
    docs=row_docs(ctl,block)
    dout=jnp.where(docs==0,de[0:1,:],jnp.where(docs==1,de[1:2,:],0.0))
    unit=u2[...]
    gn[2:3,:]+=jnp.sum(dout*unit,axis=0,keepdims=True)
    gn[3:4,:]+=jnp.sum(dout,axis=0,keepdims=True)
    gu=dout*norm[2:3,:]
    dg=rs[:,128:129]*(gu-spread_mean(gu)-unit*spread_mean(gu*unit))
    mlow=dg.astype(BF)
    mb[...]=mlow
    acc=dg
    for c in range(hidden//width):
        gc=slice(c*width,(c+1)*width)
        uc=slice(hidden+c*width,hidden+(c+1)*width)
        dh=nt(mlow,w_con[:,gc])
        dgate=(dh*pf[:,gc].astype(F32)).astype(BF)
        dup=(dh*pf[:,uc].astype(F32)).astype(BF)
        ub[:,gc]=dgate
        ub[:,uc]=dup
        acc=acc+nt(dgate,w_exp[:,gc])+nt(dup,w_exp[:,uc])
    unit=u1[...]
    gn[0:1,:]+=jnp.sum(acc*unit,axis=0,keepdims=True)
    gn[1:2,:]+=jnp.sum(acc,axis=0,keepdims=True)
    gu=acc*norm[0:1,:]
    dfirst=rs[:,0:1]*(gu-spread_mean(gu)-unit*spread_mean(gu*unit))
    df[...]=dfirst
    alow=dfirst.astype(BF)
    ab[...]=alow
    do[...]=nt(alow,w_out[pl.ds(pl.multiple_of(pos*share,share),share),:]).astype(BF)
    dx[...]=nt(alow,w_out[pl.ds(pl.multiple_of((1-pos)*share,share),share),:]).astype(BF)

def ffn_bwd(ctl,flen,pool_a,pool_b,targets,u1,u2,rs,pf,bundle,norm):
    rows,width=u1.shape
    hidden=pf.shape[1]//2
    row=lambda n: pl.BlockSpec((BLOCK,n),lambda i,c,l:(i,0))
    held=lambda n,at: pl.BlockSpec((width,n),lambda i,c,l:(0,at//n),pipeline_mode=pl.Buffered(1))
    flat=pl.BlockSpec((8,width),lambda i,c,l:(0,0))
    sds=jax.ShapeDtypeStruct
    return pl.pallas_call(ffn_bwd_kernel,
        grid_spec=pltpu.PrefetchScalarGridSpec(num_scalar_prefetch=2,grid=(rows//BLOCK,),
          in_specs=[flat,flat,flat,row(width),row(width),row(256),row(2*hidden),held(2*hidden,0),held(hidden,2*hidden),held(width,3*hidden),flat],
          out_specs=[flat,row(width),row(2*hidden),row(width),row(width),row(width//2),row(width//2),flat],
          scratch_shapes=[pltpu.VMEM((8,width),F32)]),
        out_shape=[sds((8,width),F32),sds((rows,width),BF),sds((rows,2*hidden),BF),sds((rows,width),F32),sds((rows,width),BF),
          sds((rows,width//2),BF),sds((rows,width//2),BF),sds((8,width),F32)],
        compiler_params=pltpu.CompilerParams(vmem_limit_bytes=60<<20,dimension_semantics=("arbitrary",)),
        cost_estimate=pl.CostEstimate(flops=2*rows*width*(width+3*hidden),bytes_accessed=rows*(width*18+hidden*8)+2*width*(width+3*hidden),transcendentals=0),
        name="ffn_bwd",
    )(ctl,flen,pool_a,pool_b,targets,u1,u2,rs,pf,bundle,bundle,bundle,norm)

MESH=pl.DeviceIdType.MESH

def place():
    dp=lax.axis_index("dp")
    core=lax.axis_index("dim")
    return dp//4,(dp//2)%2,dp%2,core

def meet(z,y,x,core):
    chip=lambda a,b,c: a*4+b*2+c
    peers=[(chip(z,y,x),1-core),(chip(z,y,1-x),core),(chip(z,1-y,x),core)]
    peers+=[(chip(lax.rem(z+k,4),y,x),core) for k in (1,2,3)]
    barrier=pltpu.get_barrier_semaphore()
    for peer in peers:
        pl.semaphore_signal(barrier,inc=1,device_id=peer,device_id_type=MESH)
    pl.semaphore_wait(barrier,len(peers))
    return peers

def lanes_of(cols):
    tiles=cols//128
    widths=[tiles-tiles//4*3]+[tiles//4]*3
    widths=[widths[0],widths[2],widths[1],widths[3]]
    widths=[5,5,4,4] if tiles==18 else widths
    out=[]
    at=0
    for n,w in enumerate(widths):
        out.append((at*128,w*128,n%2==0))
        at+=w
    return out

def send(src,dst,sems,n,k,peer):
    copy=pltpu.make_async_remote_copy(src_ref=src,dst_ref=dst,send_sem=sems[0].at[n,k],recv_sem=sems[1].at[n,k],device_id=peer,device_id_type=MESH)
    copy.start()
    return copy

def gather_kernel(w,out,low,local,s_sem,r_sem):
    z,y,x,core=place()
    low[...]=w[...].astype(BF)
    keep=pltpu.make_async_copy(low,out.at[z,y,x,core],local)
    keep.start()
    pair,xn,yn,z1,z2,z3=meet(z,y,x,core)
    sems=(s_sem,r_sem)
    lanes=lanes_of(w.shape[1])
    every=[]
    def go(n,k,peer,*index,src=None):
        at,width,_=lanes[n]
        dst=out.at[(*index,slice(None),pl.ds(at,width))]
        if src is None: src=dst
        copy=send(src,dst,sems,n,k,peer)
        every.append(copy)
        return copy
    whole=slice(None)
    first=[]
    for n,(at,width,_) in enumerate(lanes):
        piece=low.at[:,pl.ds(at,width)]
        first.append([go(n,k,peer,z,y,x,core,src=piece) for k,peer in enumerate((z1,z2,z3))])
    keep.wait()
    second=[]
    for n,(_,_,flip) in enumerate(lanes):
        for copy in first[n]: copy.wait_recv()
        second.append(go(n,3,yn if flip else xn,whole,y,x,core))
        go(n,5,pair,whole,y,x,core)
    third=[]
    for n,(_,_,flip) in enumerate(lanes):
        second[n].wait_recv()
        if flip:
            third.append(go(n,4,xn,whole,whole,x,core))
            go(n,6,pair,whole,1-y,x,core)
        else:
            third.append(go(n,4,yn,whole,y,whole,core))
            go(n,6,pair,whole,y,1-x,core)
    for n,(_,_,flip) in enumerate(lanes):
        third[n].wait_recv()
        if flip: go(n,7,pair,whole,whole,1-x,core)
        else: go(n,7,pair,whole,1-y,whole,core)
    done=set(id(c) for c in second+third+[c for f in first for c in f])
    for copy in every:
        copy.wait_send()
        if id(copy) not in done: copy.wait_recv()

def ring_gather(w):
    share,cols=w.shape
    out=pl.pallas_call(gather_kernel,
        in_specs=[pl.BlockSpec(memory_space=pltpu.VMEM)],
        out_specs=pl.BlockSpec(memory_space=pl.ANY),
        scratch_shapes=[pltpu.VMEM((share,cols),BF),pltpu.SemaphoreType.DMA,pltpu.SemaphoreType.DMA((4,8)),pltpu.SemaphoreType.DMA((4,8))],
        out_shape=jax.ShapeDtypeStruct((4,2,2,2,share,cols),BF),
        compiler_params=pltpu.CompilerParams(collective_id=1,has_side_effects=True,vmem_limit_bytes=60<<20),
        cost_estimate=pl.CostEstimate(flops=0,bytes_accessed=64*share*cols*20,transcendentals=0),
        name="comm_gather",
    )(w)
    return out.reshape(32*share,cols)

def scatter_kernel(g,out,gl,r0,b1,k1,r1,b2,k2,r2,b3,k3,r3,local,s_sem,r_sem):
    z,y,x,core=place()
    keep=pltpu.make_async_copy(g.at[:,core],gl,local)
    keep.start()
    pair,xn,yn,z1,z2,z3=meet(z,y,x,core)
    sems=(s_sem,r_sem)
    lanes=lanes_of(out.shape[1])
    span=[pl.ds(at,width) for at,width,_ in lanes]
    every=[]
    def go(n,k,peer,src,dst):
        copy=send(src,dst,sems,n,k,peer)
        every.append(copy)
        return copy
    n_lanes=range(len(lanes))
    zero=[go(n,0,pair,g.at[:,1-core,:,span[n]],r0.at[:,:,span[n]]) for n in n_lanes]
    def split1(n,iz,j,side):
        row=iz*4+(j*2+side if lanes[n][2] else side*2+j)
        c=span[n]
        return gl[row,:,c].astype(F32)+r0[row,:,c].astype(F32)
    one=[]
    keep.wait()
    for n in n_lanes:
        flip=lanes[n][2]
        side=x if flip else y
        zero[n].wait_recv()
        for iz in range(4):
            for j in range(2):
                b1[iz,j,:,span[n]]=split1(n,iz,j,1-side).astype(BF)
        one.append(go(n,1,xn if flip else yn,b1.at[:,:,:,span[n]],r1.at[:,:,:,span[n]]))
        for iz in range(4):
            for j in range(2):
                k1[iz,j,:,span[n]]=split1(n,iz,j,side)
    two=[]
    for n in n_lanes:
        flip=lanes[n][2]
        side=y if flip else x
        c=span[n]
        one[n].wait_recv()
        for iz in range(4):
            b2[iz,:,c]=(k1[iz,1-side,:,c]+r1[iz,1-side,:,c].astype(F32)).astype(BF)
        two.append(go(n,2,yn if flip else xn,b2.at[:,:,c],r2.at[:,:,c]))
        for iz in range(4):
            k2[iz,:,c]=k1[iz,side,:,c]+r1[iz,side,:,c].astype(F32)
    three=[]
    for n in n_lanes:
        c=span[n]
        two[n].wait_recv()
        for k in (1,2,3):
            to=lax.rem(z+k,4)
            b3[k-1,:,c]=(k2[to,:,c]+r2[to,:,c].astype(F32)).astype(BF)
        three.append([go(n,2+k,(z1,z2,z3)[k-1],b3.at[k-1,:,c],r3.at[k-1,:,c]) for k in (1,2,3)])
        k3[:,c]=k2[z,:,c]+r2[z,:,c].astype(F32)
    for n in n_lanes:
        c=span[n]
        for copy in three[n]: copy.wait_recv()
        out[:,c]=k3[:,c]+r3[0,:,c].astype(F32)+r3[1,:,c].astype(F32)+r3[2,:,c].astype(F32)
    for copy in every: copy.wait_send()

def ring_scatter(g):
    rows,cols=g.shape
    share=rows//32
    v=lambda *s: pltpu.VMEM((*s,share,cols),BF)
    f=lambda *s: pltpu.VMEM((*s,share,cols),F32)
    return pl.pallas_call(scatter_kernel,
        in_specs=[pl.BlockSpec(memory_space=pl.ANY)],
        out_specs=pl.BlockSpec(memory_space=pltpu.VMEM),
        scratch_shapes=[v(16),v(16),v(4,2),f(4,2),v(4,2),v(4),f(4),v(4),v(3),f(),v(3),pltpu.SemaphoreType.DMA,pltpu.SemaphoreType.DMA((4,6)),pltpu.SemaphoreType.DMA((4,6))],
        out_shape=jax.ShapeDtypeStruct((share,cols),F32),
        compiler_params=pltpu.CompilerParams(collective_id=2,has_side_effects=True,vmem_limit_bytes=60<<20),
        cost_estimate=pl.CostEstimate(flops=0,bytes_accessed=64*share*cols*20,transcendentals=0),
        name="comm_scatter",
    )(g.reshape(16,2,share,cols))

def selector(forward):
    r=lax.broadcasted_iota(jnp.int32,(512,512),0)
    c=lax.broadcasted_iota(jnp.int32,(512,512),1)
    a,b=(r,c) if forward else (c,r)
    return jnp.where(a==4*(b%128)+b//128,1.0,0.0).astype(BF)

def bundle_kernel(exp,con,out,norm,bundle,tiles):
    share,width=out.shape
    hidden=exp.shape[1]//2
    pick=selector(True)
    for b in range(exp.shape[1]//512):
        half,at=divmod(b*512,hidden)
        y=nn(exp[:,b*512:(b+1)*512].astype(BF),pick).astype(BF)
        for j in range(4):
            to=half*hidden+j*width+at//4
            bundle[:,to:to+128]=y[:,j*128:(j+1)*128]
    for t in range(width//128):
        tiles[t]=con[:,t*128:(t+1)*128]
        for j in range(4):
            to=2*hidden+j*width+t*128
            bundle[:,to:to+128]=tiles[t,pl.ds(j,share,stride=4),:].astype(BF)
    bundle[:,3*hidden:3*hidden+width]=out[...].astype(BF)
    flat=jnp.concatenate([norm[...],jnp.zeros((4,128-share),F32)],1)
    bundle[:,3*hidden+width:]=jnp.concatenate([flat,jnp.zeros((share-4,128),F32)],0).astype(BF)

def make_bundle(exp,con,out,norm):
    share,width=out.shape
    total=exp.shape[1]+4*width+width+128
    return pl.pallas_call(bundle_kernel,
        out_shape=jax.ShapeDtypeStruct((share,total),BF),
        scratch_shapes=[pltpu.VMEM((width//128,4*share,128),F32)],
        compiler_params=pltpu.CompilerParams(vmem_limit_bytes=60<<20),
        cost_estimate=pl.CostEstimate(flops=2*share*512*exp.shape[1],bytes_accessed=6*share*total,transcendentals=0),
        name="make_bundle",
    )(exp,con,out,norm)

def update_kernel(rates,sums,*refs):
    ins,outs,tiles=refs[:12],refs[12:32],refs[32]
    exp_w,con_w,out_w,norm_w=(ins[3*k:3*k+3] for k in range(4))
    share,width=out_w[0].shape
    hidden=exp_w[0].shape[1]//2
    def step(kind,index,g,rate):
        w,m,a=(ref[index] for ref in ins[3*kind:3*kind+3])
        grad,nxt,mom,avg,low=outs[5*kind:5*kind+5]
        mn=MOMENTUM*m+g
        wn=w-rate*(g+MOMENTUM*mn)
        grad[index]=g
        nxt[index]=wn
        mom[index]=mn
        avg[index]=AVERAGE_DECAY*a+(1.0-AVERAGE_DECAY)*wn
        low[index]=wn.astype(BF)
    pick=selector(False)
    for b in range(2*hidden//512):
        half,at=divmod(b*512,hidden)
        z=jnp.concatenate([sums[:,half*hidden+j*width+at//4:half*hidden+j*width+at//4+128] for j in range(4)],1)
        step(0,(slice(None),slice(b*512,(b+1)*512)),nn(z,pick),rates[0])
    for t in range(width//128):
        for j in range(4):
            at=2*hidden+j*width+t*128
            tiles[t,pl.ds(j,share,stride=4),:]=sums[:,at:at+128].astype(F32)
        step(1,(slice(None),slice(t*128,(t+1)*128)),tiles[t],rates[0])
    step(2,(slice(None),slice(None)),sums[:,3*hidden:3*hidden+width].astype(F32),rates[0])
    step(3,(slice(None),slice(None)),sums[0:8,3*hidden+width:].astype(F32)[0:4,0:share],rates[1])

def update(sums,rates,params):
    sds=jax.ShapeDtypeStruct
    shapes=[]
    for w,_,_ in params:
        shapes+=[sds(w.shape,F32)]*4+[sds(w.shape,BF)]
    flat=[x for p in params for x in p]
    import_vmem=pl.BlockSpec(memory_space=pltpu.VMEM)
    outs=pl.pallas_call(lambda *refs: update_kernel(rates,*refs),
        in_specs=[import_vmem]*13,
        out_specs=[import_vmem]*20,
        out_shape=shapes,
        scratch_shapes=[pltpu.VMEM((params[2][0].shape[1]//128,params[1][0].shape[0],128),F32)],
        compiler_params=pltpu.CompilerParams(vmem_limit_bytes=60<<20),
        cost_estimate=pl.CostEstimate(flops=2*24*512*6144,bytes_accessed=12<<20,transcendentals=0),
        name="update",
    )(sums,*flat)
    return [outs[5*k:5*k+5] for k in range(4)]

def tail_kernel(ctl,x,qo,ko,vo,qr,kr,vr,w,df,tok,gm,acc):
    pos=ctl[0]
    i=pl.program_id(0)
    width=x.shape[1]
    turned=x[...].T
    total=df[...]
    @pl.when(i==0)
    def _(): acc[...]=jnp.zeros_like(acc)
    for s,(mine,theirs) in enumerate(((qo,qr),(ko,kr),(vo,vr))):
        a=mine[...]
        b=theirs[...]
        grad=jnp.concatenate([jnp.where(pos==0,a,b),jnp.where(pos==0,b,a)],1)
        cols=slice(s*width,(s+1)*width)
        total=total+nt(grad,w[:,cols])
        acc[:,cols]+=nn(turned,grad)
    tok[...]=total
    @pl.when(i==pl.num_programs(0)-1)
    def _(): gm[...]=acc[...].astype(BF)

def tail(ctl,x,own,recv,w,df):
    rows,width=x.shape
    cols=w.shape[1]
    row=lambda n: pl.BlockSpec((512,n),lambda i,c:(i,0))
    held=pl.BlockSpec((width,cols),lambda i,c:(0,0),pipeline_mode=pl.Buffered(1))
    return pl.pallas_call(tail_kernel,
        grid_spec=pltpu.PrefetchScalarGridSpec(num_scalar_prefetch=1,grid=(rows//512,),
          in_specs=[row(width)]+[row(width//2)]*6+[held,row(width)],
          out_specs=[row(width),pl.BlockSpec((width,cols),lambda i,c:(0,0))],
          scratch_shapes=[pltpu.VMEM((width,cols),F32)]),
        out_shape=[jax.ShapeDtypeStruct((rows,width),F32),jax.ShapeDtypeStruct((width,cols),BF)],
        compiler_params=pltpu.CompilerParams(vmem_limit_bytes=60<<20,dimension_semantics=("arbitrary",)),
        cost_estimate=pl.CostEstimate(flops=4*rows*width*cols,bytes_accessed=rows*width*16+8*width*cols,transcendentals=0),
        name="tail",
    )(ctl,x,*own,*recv,w,df)

def mix_kernel(ctl,x,w,cos,sin,own,oth):
    pos=ctl[0]
    width=x.shape[1]
    share=width//2
    xb=x[...]
    c=cos[...]
    s=sin[...]
    lane=lax.broadcasted_iota(jnp.int32,c.shape,1)
    first=(lane%64)<32
    for part in range(3):
        y=nn(xb,w[:,part*width:(part+1)*width])
        tiles=[]
        for t in range(width//128):
            z=y[:,t*128:(t+1)*128]
            if part<2:
                swapped=jnp.where(first,pltpu.roll(z,96,1),pltpu.roll(z,32,1))
                z=z*c+swapped*s
            tiles.append(z.astype(BF))
        count=share//128
        for t in range(count):
            cols=slice(part*share+t*128,part*share+(t+1)*128)
            own[:,cols]=jnp.where(pos==0,tiles[t],tiles[count+t])
            oth[:,cols]=jnp.where(pos==0,tiles[count+t],tiles[t])

def mix(ctl,x,w,cos,sin):
    rows,width=x.shape
    cols=w.shape[1]
    block=256
    row=lambda n: pl.BlockSpec((block,n),lambda i,c:(i,0))
    angle=pl.BlockSpec((block,128),lambda i,c:(c[0]*(rows//block)+i,0))
    return pl.pallas_call(mix_kernel,
        grid_spec=pltpu.PrefetchScalarGridSpec(num_scalar_prefetch=1,grid=(rows//block,),
          in_specs=[row(width),pl.BlockSpec((width,cols),lambda i,c:(0,0)),angle,angle],
          out_specs=[row(cols//2)]*2),
        out_shape=[jax.ShapeDtypeStruct((rows,cols//2),BF)]*2,
        compiler_params=pltpu.CompilerParams(vmem_limit_bytes=60<<20,dimension_semantics=("arbitrary",)),
        cost_estimate=pl.CostEstimate(flops=2*rows*width*cols,bytes_accessed=2*(rows*width+width*cols+rows*cols),transcendentals=0),
        name="mix",
    )(ctl,x,w,cos,sin)

def swap_cores(x):
    return lax.ppermute(x,"dim",[(0,1),(1,0)])

def join(pos,own,recv,axis=1):
    return jnp.where(pos==0,jnp.concatenate([own,recv],axis),jnp.concatenate([recv,own],axis))

def body(tokens,doc_lengths,pair_index,target_bank,mixer_in,mixer_out,expand,contract,norm_params,*rest):
    slices=lax.axis_size("dim")
    if slices!=2 or lax.axis_size("dp")!=16 or doc_lengths.shape[1]!=2:
        return body_general(tokens,doc_lengths,pair_index,target_bank,mixer_in,mixer_out,expand,contract,norm_params,*rest)
    (mixer_in_moment,mixer_out_moment,expand_moment,contract_moment,norm_moment,
     mixer_in_average,mixer_out_average,expand_average,contract_average,norm_average)=rest
    local_rows,model_width=tokens.shape
    group_rows=local_rows*slices
    pos=lax.axis_index("dim")
    doc_count=2
    w_mix=ring_gather(mixer_in[0])
    share_rows=mixer_out.shape[1]
    per=contract.shape[1]//share_rows
    count=model_width//share_rows
    hidden_width=contract.shape[1]*count
    bundle=make_bundle(expand[0],contract[0],mixer_out[0],norm_params[0])
    bundle=lax.all_gather(bundle,("dp","dim"),axis=0,tiled=True)
    at1=2*hidden_width
    at2=at1+per*model_width
    at3=at2+model_width
    w_norm=bundle[:,at3:].reshape(count,share_rows,128)[:,0:4,0:share_rows].transpose(1,0,2).reshape(4,model_width)
    lengths=doc_lengths[0]
    e0=lengths[0]
    e1=lengths[0]+lengths[1]
    ctl=jnp.stack([pos.astype(jnp.int32),e0,e1])
    ids=jnp.arange(group_rows,dtype=jnp.int32)
    seg=(ids>=e0).astype(jnp.int32)+(ids>=e1).astype(jnp.int32)
    begin=jnp.where(seg==0,0,jnp.where(seg==1,e0,e1))
    lane=jnp.arange(128,dtype=jnp.int32)
    frequency=jnp.power(1000.0,-(2*(lane%32)).astype(F32)/HEAD)
    angles=(ids-begin).astype(F32)[:,None]*frequency[None,:]
    cos=jnp.cos(angles)
    sin=jnp.sin(angles)*jnp.where((lane%64)<32,-1.0,1.0)[None,:]
    own,oth=mix(ctl,tokens,w_mix,cos,sin)
    recv=swap_cores(oth)
    pick=(pair_index[:,None]==jnp.arange(target_bank.shape[0],dtype=jnp.int32)[None,:]).astype(BF)
    some=matmul(pick,target_bank)
    targets=jnp.pad(join(pos,some,swap_cores(some)),((0,6),(0,0)))
    o_own,o_oth,lse=attend_fwd(ctl,own,recv)
    o_recv=swap_cores(o_oth)
    norm_gains=jnp.pad(w_norm.astype(F32),((0,4),(0,0)))
    u1,u2,rs,y_low,*hidden,factors,pooled=ffn_fwd(ctl,o_own,o_recv,tokens,bundle,norm_gains,hidden_width)
    embeds,grad_m_low,grad_both,grad_first,grad_a_low,d_own,d_oth,grad_norm=ffn_bwd(
        ctl,lengths.astype(F32),pooled,swap_cores(pooled),targets,u1,u2,rs,factors,bundle,norm_gains)
    share=model_width//2
    embeddings=lax.dynamic_slice(embeds,(0,pos*share),(doc_count,share))
    d_recv=swap_cores(d_oth)
    grad_exp=inner_rows(y_low,grad_both)
    grad_con=[inner_rows(h,grad_m_low).astype(BF) for h in hidden]
    grad_out=join(pos,inner_rows(o_own,grad_a_low),inner_rows(o_recv,grad_a_low),0)
    grad_norm=grad_norm[0:4].reshape(4,count,share_rows).transpose(1,0,2)
    grad_norm=jnp.pad(grad_norm,((0,0),(0,share_rows-4),(0,128-share_rows))).reshape(model_width,128)
    terms=jnp.concatenate([grad_exp.astype(BF),*grad_con,grad_out.astype(BF),grad_norm.astype(BF)],1)
    terms,d_own,d_recv=lax.optimization_barrier((terms,d_own,d_recv))
    sums=lax.psum_scatter(terms,("dp","dim"),scatter_dimension=0,tiled=True)
    backs=attend_bwd(ctl,own,recv,d_own,d_recv,o_own,o_oth,lse,cos,sin)
    token_grads,grad_mix=tail(ctl,tokens,backs[0:3],[swap_cores(g) for g in backs[3:6]],w_mix,grad_first)
    grad_mix,sums=lax.optimization_barrier((grad_mix,sums))
    total_rows=group_rows*lax.axis_size("dp")
    matrix_rate=1.0/math.sqrt(total_rows)
    norm_rate=0.3/math.sqrt(total_rows)
    new_exp,new_con,new_out,new_norm=update(sums,(matrix_rate,norm_rate),[
        (expand[0],expand_moment[0],expand_average[0]),(contract[0],contract_moment[0],contract_average[0]),
        (mixer_out[0],mixer_out_moment[0],mixer_out_average[0]),(norm_params[0],norm_moment[0],norm_average[0])])
    sum_mix=ring_scatter(grad_mix)
    nxt,mom,avg,low=advance(mixer_in[0],mixer_in_moment[0],mixer_in_average[0],sum_mix,matrix_rate)
    results=[[sum_mix,nxt,mom,avg,low],new_out,new_exp,new_con,new_norm]
    return (embeddings,token_grads,*[results[k][f][None] for f in range(5) for k in range(5)])

def solution(mesh):
    placed = (
        P(("dp", "dim"), None),
        P("dp", None),
        P("dp"),
        P(None, "dim"),
        P(None, ("dp", "dim"), None),
        P(None, ("dp", "dim"), None),
        P(None, ("dp", "dim"), None),
        P(None, ("dp", "dim"), None),
        P(None, None, ("dp", "dim")),
        P(None, ("dp", "dim"), None),
        P(None, ("dp", "dim"), None),
        P(None, ("dp", "dim"), None),
        P(None, ("dp", "dim"), None),
        P(None, None, ("dp", "dim")),
        P(None, ("dp", "dim"), None),
        P(None, ("dp", "dim"), None),
        P(None, ("dp", "dim"), None),
        P(None, ("dp", "dim"), None),
        P(None, None, ("dp", "dim")),
    )
    return jax.shard_map(
        body,
        mesh=mesh,
        in_specs=placed,
        out_specs=(
            P("dp", "dim"),
            P(("dp", "dim"), None),
            P(None, ("dp", "dim"), None),
            P(None, ("dp", "dim"), None),
            P(None, ("dp", "dim"), None),
            P(None, ("dp", "dim"), None),
            P(None, None, ("dp", "dim")),
            P(None, ("dp", "dim"), None),
            P(None, ("dp", "dim"), None),
            P(None, ("dp", "dim"), None),
            P(None, ("dp", "dim"), None),
            P(None, None, ("dp", "dim")),
            P(None, ("dp", "dim"), None),
            P(None, ("dp", "dim"), None),
            P(None, ("dp", "dim"), None),
            P(None, ("dp", "dim"), None),
            P(None, None, ("dp", "dim")),
            P(None, ("dp", "dim"), None),
            P(None, ("dp", "dim"), None),
            P(None, ("dp", "dim"), None),
            P(None, ("dp", "dim"), None),
            P(None, None, ("dp", "dim")),
            P(None, ("dp", "dim"), None),
            P(None, ("dp", "dim"), None),
            P(None, ("dp", "dim"), None),
            P(None, ("dp", "dim"), None),
            P(None, None, ("dp", "dim")),
        ),
        check_vma=False,
    )
```

```python
import math

import jax
import jax.numpy as jnp
from jax import lax
from jax.experimental import pallas as pl
from jax.experimental.pallas import tpu as pltpu
from jax.sharding import PartitionSpec as P

HEAD = 64


NORM_EPSILON = 1e-05
COSINE_EPSILON = 1e-06
MOMENTUM = 0.5
AVERAGE_DECAY = 0.5
PRECISE = lax.Precision.HIGHEST
MASKED = -1e30


def matmul(left_op, right_op):
    return jnp.dot(left_op, right_op, preferred_element_type=jnp.float32)


def matmul_exact(left_op, right_op):
    return jnp.dot(left_op, right_op, precision=PRECISE, preferred_element_type=jnp.float32)


def inner_rows(left_op, right_op):
    return lax.dot_general(
        left_op, right_op, (((0,), (0,)), ((), ())), preferred_element_type=jnp.float32
    )


def inner_cols(left_op, right_op):
    return lax.dot_general(
        left_op, right_op, (((1,), (1,)), ((), ())), preferred_element_type=jnp.float32
    )


def rotate(values, cosines, sines):
    row_count = values.shape[0]
    shaped = values.reshape(row_count, -1, 2, HEAD // 2)
    former = shaped[:, :, 0, :]
    latter = shaped[:, :, 1, :]
    cosine_b = cosines[:, None, :]
    sine_b = sines[:, None, :]
    turned = jnp.stack(
        [former * cosine_b - latter * sine_b, latter * cosine_b + former * sine_b], axis=2
    )
    return turned.reshape(values.shape)


def rotate_back(grads_in, cosines, sines):
    row_count = grads_in.shape[0]
    shaped = grads_in.reshape(row_count, -1, 2, HEAD // 2)
    former = shaped[:, :, 0, :]
    latter = shaped[:, :, 1, :]
    cosine_b = cosines[:, None, :]
    sine_b = sines[:, None, :]
    turned = jnp.stack(
        [former * cosine_b + latter * sine_b, latter * cosine_b - former * sine_b], axis=2
    )
    return turned.reshape(grads_in.shape)


def normalize(summed, gain_vec, bias_vec):
    centred = summed - jnp.mean(summed, axis=1, keepdims=True)
    scaling = lax.rsqrt(jnp.mean(centred * centred, axis=1, keepdims=True) + NORM_EPSILON)
    return centred * scaling * gain_vec + bias_vec


def normalize_back(grad_in, summed, gain_vec):
    centred = summed - jnp.mean(summed, axis=1, keepdims=True)
    scaling = lax.rsqrt(jnp.mean(centred * centred, axis=1, keepdims=True) + NORM_EPSILON)
    unit = centred * scaling
    grad_unit = grad_in * gain_vec
    grad_sum = scaling * (
        grad_unit
        - jnp.mean(grad_unit, axis=1, keepdims=True)
        - unit * jnp.mean(grad_unit * unit, axis=1, keepdims=True)
    )
    return (grad_sum, jnp.sum(grad_in * unit, axis=0), jnp.sum(grad_in, axis=0))


def flatten(stacked):
    return stacked.transpose(1, 0, 2).reshape(stacked.shape[1], -1)


def attend(q_rot, all_keys, all_values, same_doc):
    head_count = q_rot.shape[1] // HEAD

    def one_head(head_pos):
        offset = head_pos * HEAD
        query_part = lax.dynamic_slice_in_dim(q_rot, offset, HEAD, 1)
        key_part = lax.dynamic_slice_in_dim(all_keys, offset, HEAD, 1)
        value_part = lax.dynamic_slice_in_dim(all_values, offset, HEAD, 1)
        scores = jnp.where(same_doc, inner_cols(query_part, key_part) * 0.125, MASKED)
        row_max = jnp.max(scores, axis=1, keepdims=True)
        exponent = jnp.exp(scores - row_max)
        row_total = jnp.sum(exponent, axis=1, keepdims=True)
        attn_probs = (exponent / row_total).astype(jnp.bfloat16)
        return (matmul(attn_probs, value_part), (row_max + jnp.log(row_total))[:, 0])

    outputs, log_totals = lax.map(one_head, jnp.arange(head_count, dtype=jnp.int32))
    return (flatten(outputs), log_totals)


def attend_back(q_rot, all_keys, all_values, same_doc, grad_out, log_totals):
    head_count = q_rot.shape[1] // HEAD

    def one_head(pack):
        head_pos, log_total = pack
        offset = head_pos * HEAD
        query_part = lax.dynamic_slice_in_dim(q_rot, offset, HEAD, 1)
        key_part = lax.dynamic_slice_in_dim(all_keys, offset, HEAD, 1)
        value_part = lax.dynamic_slice_in_dim(all_values, offset, HEAD, 1)
        grad_part = lax.dynamic_slice_in_dim(grad_out, offset, HEAD, 1)
        scores = jnp.where(same_doc, inner_cols(query_part, key_part) * 0.125, MASKED)
        attn_probs = jnp.exp(scores - log_total[:, None])
        grad_probs = inner_cols(grad_part, value_part)
        row_dot = jnp.sum(attn_probs * grad_probs, axis=1, keepdims=True)
        grad_scores = (attn_probs * (grad_probs - row_dot)).astype(jnp.bfloat16)
        grad_query = matmul(grad_scores, key_part) * 0.125
        grad_key = inner_rows(grad_scores, query_part) * 0.125
        grad_value = inner_rows(attn_probs.astype(jnp.bfloat16), grad_part)
        return (grad_query, grad_key, grad_value)

    mapped = lax.map(one_head, (jnp.arange(head_count, dtype=jnp.int32), log_totals))
    return (flatten(mapped[0]), flatten(mapped[1]), flatten(mapped[2]))


def advance(weight, moment, average, grad_in, rate):
    moment_next = MOMENTUM * moment + grad_in
    weight_next = weight - rate * (grad_in + MOMENTUM * moment_next)
    average_next = AVERAGE_DECAY * average + (1.0 - AVERAGE_DECAY) * weight_next
    return (weight_next, moment_next, average_next, weight_next.astype(jnp.bfloat16))


def body_general(
    tokens,
    doc_lengths,
    pair_index,
    target_bank,
    mixer_in,
    mixer_out,
    expand,
    contract,
    norm_params,
    mixer_in_moment,
    mixer_out_moment,
    expand_moment,
    contract_moment,
    norm_moment,
    mixer_in_average,
    mixer_out_average,
    expand_average,
    contract_average,
    norm_average,
):
    local_rows, model_width = tokens.shape
    slices = lax.axis_size("dim")
    group_rows = local_rows * slices
    position = lax.axis_index("dim")
    layer_count = mixer_in.shape[0]
    doc_count = doc_lengths.shape[1]
    lengths = doc_lengths[0]
    doc_ends = jnp.cumsum(lengths)
    doc_starts = doc_ends - lengths
    row_ids = position * local_rows + jnp.arange(local_rows, dtype=jnp.int32)
    key_ids = jnp.arange(group_rows, dtype=jnp.int32)
    seg_rows = jnp.sum((row_ids[:, None] >= doc_ends[None, :]).astype(jnp.int32), axis=1)
    seg_keys = jnp.sum((key_ids[:, None] >= doc_ends[None, :]).astype(jnp.int32), axis=1)
    first_rows = jnp.concatenate([doc_starts, doc_ends[-1:]])
    segment_ids = jnp.arange(doc_count + 1, dtype=jnp.int32)
    row_begin = jnp.sum(
        jnp.where(seg_rows[:, None] == segment_ids[None, :], first_rows[None, :], 0), axis=1
    )
    frequency = jnp.power(1000.0, -jnp.arange(0, HEAD, 2).astype(jnp.float32) / HEAD)
    angles = (row_ids - row_begin).astype(jnp.float32)[:, None] * frequency[None, :]
    cosines = jnp.cos(angles)
    sines = jnp.sin(angles)
    same_doc = seg_rows[:, None] == seg_keys[None, :]
    stream = tokens.astype(jnp.float32)
    layer_pos = 0
    layer_weights = (
        lax.all_gather(mixer_in[layer_pos].astype(jnp.bfloat16), ("dp", "dim"), axis=0, tiled=True),
        lax.all_gather(
            mixer_out[layer_pos].astype(jnp.bfloat16), ("dp", "dim"), axis=0, tiled=True
        ),
        lax.all_gather(expand[layer_pos].astype(jnp.bfloat16), ("dp", "dim"), axis=0, tiled=True),
        lax.all_gather(contract[layer_pos].astype(jnp.bfloat16), ("dp", "dim"), axis=0, tiled=True),
        lax.all_gather(
            norm_params[layer_pos].astype(jnp.bfloat16), ("dp", "dim"), axis=1, tiled=True
        ),
    )
    w_mix, w_out, w_exp, w_con, w_norm = layer_weights
    norm_gains = w_norm.astype(jnp.float32)
    x_low = stream.astype(jnp.bfloat16)
    mixed = matmul(x_low, w_mix)
    q_rot = rotate(mixed[:, 0:model_width], cosines, sines).astype(jnp.bfloat16)
    k_rot = rotate(mixed[:, model_width : 2 * model_width], cosines, sines).astype(jnp.bfloat16)
    v_low = mixed[:, 2 * model_width : 3 * model_width].astype(jnp.bfloat16)
    all_keys = lax.all_gather(k_rot, "dim", axis=0, tiled=True)
    all_values = lax.all_gather(v_low, "dim", axis=0, tiled=True)
    attended, log_totals = attend(q_rot, all_keys, all_values, same_doc)
    att_low = attended.astype(jnp.bfloat16)
    first_sum = stream + matmul(att_low, w_out)
    normed = normalize(first_sum, norm_gains[0], norm_gains[1])
    y_low = normed.astype(jnp.bfloat16)
    gate_up = matmul(y_low, w_exp)
    half = gate_up.shape[1] // 2
    hidden = (jax.nn.silu(gate_up[:, 0:half]) * gate_up[:, half : 2 * half]).astype(jnp.bfloat16)
    second_sum = normed + matmul(hidden, w_con)
    saved = [
        (
            stream,
            layer_weights,
            q_rot,
            k_rot,
            v_low,
            all_keys,
            all_values,
            log_totals,
            attended,
            att_low,
            first_sum,
            normed,
            y_low,
            gate_up,
            hidden,
            second_sum,
        )
    ]
    stream = normalize(second_sum, norm_gains[2], norm_gains[3])
    member = (seg_rows[None, :] == jnp.arange(doc_count, dtype=jnp.int32)[:, None]).astype(
        jnp.float32
    )
    partial_value = matmul_exact(member, stream)
    pooled = lax.psum_scatter(partial_value, "dim", scatter_dimension=1, tiled=True)
    length_f = lengths.astype(jnp.float32)
    embeddings = pooled / length_f[:, None]
    share = embeddings.shape[1]
    pick = (
        pair_index[:, None] == jnp.arange(target_bank.shape[0], dtype=jnp.int32)[None, :]
    ).astype(jnp.bfloat16)
    targets = matmul(pick, target_bank)
    feature_ids = position * share + jnp.arange(share, dtype=jnp.int32)
    cuts = jnp.array(
        [model_width // 12, model_width // 6, model_width // 3, 2 * model_width // 3, model_width],
        dtype=jnp.int32,
    )
    masks = (feature_ids[None, :] < cuts[:, None]).astype(jnp.float32)
    cross = matmul_exact(embeddings * targets, masks.T)
    own = matmul_exact(embeddings * embeddings, masks.T)
    other = matmul_exact(targets * targets, masks.T)
    cross, own, other = lax.psum((cross, own, other), "dim")
    own_root = lax.rsqrt(own + COSINE_EPSILON)
    other_root = lax.rsqrt(other + COSINE_EPSILON)
    cosine = cross * own_root * other_root
    coef_target = -length_f[:, None] * own_root * other_root
    coef_self = length_f[:, None] * cosine * own_root * own_root
    grad_emb = (
        matmul_exact(coef_target, masks) * targets + matmul_exact(coef_self, masks) * embeddings
    )
    grad_full = lax.all_gather(grad_emb, "dim", axis=1, tiled=True)
    spread_rows = member / length_f[:, None]
    grad_stream = lax.dot_general(
        spread_rows,
        grad_full,
        (((0,), (0,)), ((), ())),
        precision=PRECISE,
        preferred_element_type=jnp.float32,
    )
    grad_list = [None] * layer_count
    for layer_pos in reversed(range(layer_count)):
        (
            layer_input,
            layer_weights,
            q_rot,
            k_rot,
            v_low,
            all_keys,
            all_values,
            log_totals,
            attended,
            att_low,
            first_sum,
            normed,
            y_low,
            gate_up,
            hidden,
            second_sum,
        ) = saved[layer_pos]
        w_mix = lax.all_gather(
            mixer_in[layer_pos].astype(jnp.bfloat16), ("dp", "dim"), axis=0, tiled=True
        )
        w_out = lax.all_gather(
            mixer_out[layer_pos].astype(jnp.bfloat16), ("dp", "dim"), axis=0, tiled=True
        )
        w_exp = lax.all_gather(
            expand[layer_pos].astype(jnp.bfloat16), ("dp", "dim"), axis=0, tiled=True
        )
        w_con = lax.all_gather(
            contract[layer_pos].astype(jnp.bfloat16), ("dp", "dim"), axis=0, tiled=True
        )
        w_norm = lax.all_gather(
            norm_params[layer_pos].astype(jnp.bfloat16), ("dp", "dim"), axis=1, tiled=True
        )
        norm_gains = w_norm.astype(jnp.float32)
        grad_second, grad_gain2, grad_bias2 = normalize_back(grad_stream, second_sum, norm_gains[2])
        grad_m_low = grad_second.astype(jnp.bfloat16)
        grad_con = inner_rows(hidden, grad_m_low)
        grad_hidden = inner_cols(grad_m_low, w_con)
        half = gate_up.shape[1] // 2
        gate_part = gate_up[:, 0:half]
        up_part = gate_up[:, half : 2 * half]
        sigmoid_gate = jax.nn.sigmoid(gate_part)
        activated = gate_part * sigmoid_gate
        grad_gate = grad_hidden * up_part * sigmoid_gate * (1.0 + gate_part * (1.0 - sigmoid_gate))
        grad_up = grad_hidden * activated
        grad_both = jnp.concatenate([grad_gate, grad_up], axis=1).astype(jnp.bfloat16)
        grad_exp = inner_rows(y_low, grad_both)
        grad_normed = grad_second + inner_cols(grad_both, w_exp)
        grad_first, grad_gain1, grad_bias1 = normalize_back(grad_normed, first_sum, norm_gains[0])
        grad_a_low = grad_first.astype(jnp.bfloat16)
        grad_out = inner_rows(att_low, grad_a_low)
        grad_attended = inner_cols(grad_a_low, w_out).astype(jnp.bfloat16)
        keys_back, values_back = (
            lax.all_gather(k_rot, "dim", axis=0, tiled=True),
            lax.all_gather(v_low, "dim", axis=0, tiled=True),
        )
        grad_query, grad_key_all, grad_value_all = attend_back(
            q_rot, keys_back, values_back, same_doc, grad_attended, log_totals
        )
        grad_kv = lax.psum_scatter(
            jnp.concatenate([grad_key_all, grad_value_all], axis=1).astype(jnp.bfloat16),
            "dim",
            scatter_dimension=0,
            tiled=True,
        ).astype(jnp.float32)
        grad_mixed = jnp.concatenate(
            [
                rotate_back(grad_query, cosines, sines),
                rotate_back(grad_kv[:, 0:model_width], cosines, sines),
                grad_kv[:, model_width : 2 * model_width],
            ],
            axis=1,
        ).astype(jnp.bfloat16)
        x_low = layer_input.astype(jnp.bfloat16)
        grad_mix = inner_rows(x_low, grad_mixed)
        grad_stream = grad_first + inner_cols(grad_mixed, w_mix)
        grad_norm = jnp.stack([grad_gain1, grad_bias1, grad_gain2, grad_bias2])
        grad_list[layer_pos] = (
            lax.psum_scatter(grad_mix, ("dp", "dim"), scatter_dimension=0, tiled=True),
            lax.psum_scatter(grad_out, ("dp", "dim"), scatter_dimension=0, tiled=True),
            lax.psum_scatter(grad_exp, ("dp", "dim"), scatter_dimension=0, tiled=True),
            lax.psum_scatter(grad_con, ("dp", "dim"), scatter_dimension=0, tiled=True),
            lax.psum_scatter(grad_norm, ("dp", "dim"), scatter_dimension=1, tiled=True),
        )
    total_rows = group_rows * lax.axis_size("dp")
    matrix_rate = 1.0 / math.sqrt(total_rows)
    norm_rate = 0.3 / math.sqrt(total_rows)
    grads = [jnp.stack([grad_list[0][kind]]) for kind in range(5)]
    weights = (mixer_in, mixer_out, expand, contract, norm_params)
    moments = (mixer_in_moment, mixer_out_moment, expand_moment, contract_moment, norm_moment)
    averages = (mixer_in_average, mixer_out_average, expand_average, contract_average, norm_average)
    rates = (matrix_rate, matrix_rate, matrix_rate, matrix_rate, norm_rate)
    results = [
        advance(weights[kind], moments[kind], averages[kind], grads[kind], rates[kind])
        for kind in range(5)
    ]
    return (
        embeddings,
        grad_stream,
        grads[0],
        grads[1],
        grads[2],
        grads[3],
        grads[4],
        results[0][0],
        results[1][0],
        results[2][0],
        results[3][0],
        results[4][0],
        results[0][1],
        results[1][1],
        results[2][1],
        results[3][1],
        results[4][1],
        results[0][2],
        results[1][2],
        results[2][2],
        results[3][2],
        results[4][2],
        results[0][3],
        results[1][3],
        results[2][3],
        results[3][3],
        results[4][3],
    )


NEG=-1e30
BQ=512
ROWS=256
BK=384
F32=jnp.float32
BF=jnp.bfloat16

def nt(a,b): return lax.dot_general(a,b,(((1,),(1,)),((),())),preferred_element_type=F32)
def nn(a,b): return jnp.dot(a,b,preferred_element_type=F32)

def fill_masks(e0,e1,kaug,q0,q1,rows,pad):
    r=lax.broadcasted_iota(jnp.int32,(rows+pad,128),0)
    l=lax.broadcasted_iota(jnp.int32,(rows+pad,128),1)
    seg=(r>=e0).astype(jnp.int32)+(r>=e1).astype(jnp.int32)
    kaug[:,128:256]=jnp.where((l<3)&(l!=seg),NEG,0.0).astype(BF)
    qm=jnp.where(l==seg,1.0,0.0).astype(BF)[0:rows]
    q0[:,128:256]=qm
    q1[:,128:256]=qm

def key_range(i,e0,e1):
    first=i*BQ
    last=jnp.minimum(first+BQ,e1)-1
    lo=jnp.where(first>=e0,e0,0)
    hi=jnp.where(last>=e0,e1,e0)
    base=(lo//128)*128
    return pl.multiple_of(base,128),(hi-base+BK-1)//BK

def fwd_kernel(ctl,qo,ko,vo,qr,kr,vr,oo,ox,lse,kaug,q0,q1,vt):
    rows=kaug.shape[0]-BK
    half=rows//2
    pos,e0,e1=ctl[0],ctl[1],ctl[2]
    p=pl.program_id(0)
    @pl.when(p==0)
    def _():
        fill_masks(e0,e1,kaug,q0,q1,rows,BK)
        kaug[rows:,0:128]=jnp.zeros((BK,128),BF)
        vt[:,:]=jnp.where(lax.broadcasted_iota(jnp.int32,vt.shape,0)%80>=64,1.0,0.0).astype(BF)
    pick_r=lax.broadcasted_iota(jnp.int32,(16,128),0)
    pick_l=lax.broadcasted_iota(jnp.int32,(16,128),1)
    pick=jnp.where(pick_l//64==pick_r,1.0,0.0).astype(BF)
    q_top=jnp.zeros((16,1),F32)
    k_top=jnp.zeros((16,1),F32)
    lane=lax.broadcasted_iota(jnp.int32,(half,128),1)
    for own,(q,k,v) in ((True,(qo,ko,vo)),(False,(qr,kr,vr))):
        at=pl.multiple_of((pos if own else 1-pos)*half,half)
        scaled=q[...]*jnp.asarray(0.125,BF)
        zero=jnp.zeros_like(scaled)
        q0[pl.ds(at,half),0:128]=jnp.where(lane<64,scaled,zero)
        q1[pl.ds(at,half),0:128]=jnp.where(lane<64,zero,scaled)
        kb=k[...]
        kaug[pl.ds(at,half),0:128]=kb
        q_top=jnp.maximum(q_top,jnp.max(nt(pick,scaled*scaled),axis=1,keepdims=True))
        k_top=jnp.maximum(k_top,jnp.max(nt(pick,kb*kb),axis=1,keepdims=True))
        turned=v[...].T
        vt[0:64,pl.ds(at,half)]=turned[0:64]
        vt[80:144,pl.ds(at,half)]=turned[64:128]
    narrow=jnp.max(q_top*k_top)*1.05<=1600.0
    def qnarrow(i,_):
        r0=pl.multiple_of(i*BQ,BQ)
        base,count=key_range(i,e0,e1)
        qs=(q0[pl.ds(r0,BQ),:],q1[pl.ds(r0,BQ),:])
        def step(j,carry):
            k0=pl.multiple_of(base+j*BK,128)
            kb=kaug[pl.ds(k0,BK),:]
            pt=[jnp.exp(nt(kb,qs[h])).astype(BF) for h in range(2)]
            return tuple(carry[h]+nn(vt[80*h:80*h+80,pl.ds(k0,BK)],pt[h]) for h in range(2))
        init=jnp.zeros((80,BQ),F32)
        res=lax.fori_loop(0,count,step,(init,init))
        outs=[]
        for h in range(2):
            l=jnp.maximum(res[h][64:65],1e-30)
            outs.append(res[h][0:64]/l)
            lse[0,h:h+1,pl.ds(r0,BQ)]=jnp.log(l)
        put(i,jnp.concatenate(outs,axis=0).T.astype(BF))
        return 0
    def qblock(i,_):
        r0=pl.multiple_of(i*BQ,BQ)
        base,count=key_range(i,e0,e1)
        qs=(q0[pl.ds(r0,BQ),:],q1[pl.ds(r0,BQ),:])
        def step(j,carry):
            k0=pl.multiple_of(base+j*BK,128)
            kb=kaug[pl.ds(k0,BK),:]
            scores=[nt(kb,qs[h]) for h in range(2)]
            out=[]
            for h in range(2):
                m,acc=carry[h]
                mn=jnp.maximum(m,jnp.max(scores[h],axis=0,keepdims=True))
                pt=jnp.exp(scores[h]-mn).astype(BF)
                acc=acc*jnp.exp(m-mn)+nn(vt[80*h:80*h+80,pl.ds(k0,BK)],pt)
                out.append((mn,acc))
            return tuple(out)
        init=(jnp.full((1,BQ),-jnp.inf,F32),jnp.zeros((80,BQ),F32))
        res=lax.fori_loop(0,count,step,(init,init))
        outs=[]
        for h in range(2):
            m,acc=res[h]
            l=acc[64:65]
            outs.append(acc[0:64]/l)
            lse[0,h:h+1,pl.ds(r0,BQ)]=m+jnp.log(l)
        ob=jnp.concatenate(outs,axis=0).T.astype(BF)
        put(i,ob)
        return 0
    def put(i,ob):
        local=i*BQ-pos*half
        @pl.when((local>=0)&(local<half))
        def _(): oo[pl.ds(pl.multiple_of(local,BQ),BQ),:]=ob
        @pl.when((local<0)|(local>=half))
        def _(): ox[pl.ds(pl.multiple_of(i*BQ-(1-pos)*half,BQ),BQ),:]=ob
    used=(e1+BQ-1)//BQ
    @pl.when(narrow)
    def _(): lax.fori_loop(0,used,qnarrow,0)
    @pl.when(jnp.logical_not(narrow))
    def _(): lax.fori_loop(0,used,qblock,0)
    def blank(i,_):
        r0=pl.multiple_of(i*BQ,BQ)
        lse[0,:,pl.ds(r0,BQ)]=jnp.zeros((8,BQ),F32)
        put(i,jnp.zeros((BQ,128),BF))
        return 0
    lax.fori_loop(used,rows//BQ,blank,0)

def attend_fwd(ctl,own,recv):
    half,width=own.shape
    pairs=width//384
    rows=2*half
    sp=[pl.BlockSpec((half,128),(lambda p,c,s=s:(0,s*pairs+p))) for s in range(3)]
    outw=pairs*128
    return pl.pallas_call(fwd_kernel,
        grid_spec=pltpu.PrefetchScalarGridSpec(num_scalar_prefetch=1,grid=(pairs,),
          in_specs=sp+sp,
          out_specs=[pl.BlockSpec((half,128),lambda p,c:(0,p))]*2+[pl.BlockSpec((1,8,rows),lambda p,c:(p,0,0))],
          scratch_shapes=[pltpu.VMEM((rows+BK,256),BF),pltpu.VMEM((rows,256),BF),pltpu.VMEM((rows,256),BF),pltpu.VMEM((160,rows+BK),BF)]),
        out_shape=[jax.ShapeDtypeStruct((half,outw),BF)]*2+[jax.ShapeDtypeStruct((pairs,8,rows),F32)],
        compiler_params=pltpu.CompilerParams(vmem_limit_bytes=60<<20,dimension_semantics=("arbitrary",)),
        cost_estimate=pl.CostEstimate(flops=4*rows*rows*64*2*pairs//2,bytes_accessed=10*half*width,transcendentals=rows*rows*pairs),
        name="attend_fwd",
    )(ctl,own,own,own,recv,recv,recv)

def bwd_kernel(ctl,qo,ko,vo,qr,kr,vr,do_o,do_r,oo,ox,lse,cos,sin,g0,g1,g2,x0,x1,x2,kaug,q0,q1,vs,d0,d1,kt,delta,dk,dv):
    rows=kaug.shape[0]-BK
    half=rows//2
    pos,e0,e1=ctl[0],ctl[1],ctl[2]
    p=pl.program_id(0)
    @pl.when(p==0)
    def _():
        fill_masks(e0,e1,kaug,q0,q1,rows,BK)
        kaug[rows:,0:128]=jnp.zeros((BK,128),BF)
        vs[rows:,:]=jnp.zeros((BK,128),BF)
        kt[:,rows:]=jnp.zeros((128,BK),BF)
    lane=lax.broadcasted_iota(jnp.int32,(half,128),1)
    pick_r=lax.broadcasted_iota(jnp.int32,(16,128),0)
    pick_l=lax.broadcasted_iota(jnp.int32,(16,128),1)
    pick=jnp.where(pick_l//64==pick_r,1.0,0.0).astype(BF)
    for own,(q,k,v,d,o) in ((True,(qo,ko,vo,do_o,oo)),(False,(qr,kr,vr,do_r,ox))):
        at=pl.multiple_of((pos if own else 1-pos)*half,half)
        scaled=q[...]*jnp.asarray(0.125,BF)
        zero=jnp.zeros_like(scaled)
        q0[pl.ds(at,half),0:128]=jnp.where(lane<64,scaled,zero)
        q1[pl.ds(at,half),0:128]=jnp.where(lane<64,zero,scaled)
        kb=k[...]
        kaug[pl.ds(at,half),0:128]=kb
        kt[:,pl.ds(at,half)]=kb.T
        vs[pl.ds(at,half),:]=v[...]
        db=d[...]
        d0[pl.ds(at,half),:]=jnp.where(lane<64,db,zero)
        d1[pl.ds(at,half),:]=jnp.where(lane<64,zero,db)
        prod=db.astype(F32)*o[...].astype(F32)
        hi=prod.astype(BF)
        lo=(prod-hi.astype(F32)).astype(BF)
        delta[:,pl.ds(at,half)]=nt(pick,hi)+nt(pick,lo)
    dk[...]=jnp.zeros_like(dk)
    dv[...]=jnp.zeros_like(dv)
    def spread(i,col,val):
        local=i*ROWS-pos*half
        @pl.when((local>=0)&(local<half))
        def _(): (g0,g1,g2)[col][pl.ds(pl.multiple_of(local,ROWS),ROWS),:]=val
        @pl.when((local<0)|(local>=half))
        def _(): (x0,x1,x2)[col][pl.ds(pl.multiple_of(i*ROWS-(1-pos)*half,ROWS),ROWS),:]=val
    def unturn(x,r0):
        ln=lax.broadcasted_iota(jnp.int32,x.shape,1)
        swapped=jnp.where((ln%64)<32,pltpu.roll(x,96,1),pltpu.roll(x,32,1))
        return x*cos[pl.ds(r0,ROWS),:]-swapped*sin[pl.ds(r0,ROWS),:]
    def qblock(i,_):
        r0=pl.multiple_of(i*BQ,BQ)
        base,count=key_range(i,e0,e1)
        qs=(q0[pl.ds(r0,BQ),:],q1[pl.ds(r0,BQ),:])
        ds_=(d0[pl.ds(r0,BQ),:],d1[pl.ds(r0,BQ),:])
        ls=[lse[0,h:h+1,pl.ds(r0,BQ)] for h in range(2)]
        de=[delta[h:h+1,pl.ds(r0,BQ)] for h in range(2)]
        def step(j,carry):
            k0=pl.multiple_of(base+j*BK,128)
            kb=kaug[pl.ds(k0,BK),:]
            vb=vs[pl.ds(k0,BK),:]
            both=range(2)
            st=[nt(kb,qs[h]) for h in both]
            dpt=[nt(vb,ds_[h]) for h in both]
            pt=[jnp.exp(st[h]-ls[h]) for h in both]
            dst=[(pt[h]*(dpt[h]-de[h])).astype(BF) for h in both]
            pb=[pt[h].astype(BF) for h in both]
            dv[pl.ds(k0,BK),:]+=nn(pb[0],ds_[0])+nn(pb[1],ds_[1])
            dk[pl.ds(k0,BK),:]+=nn(dst[0],qs[0][:,0:128])+nn(dst[1],qs[1][:,0:128])
            out=[carry[h]+nn(kt[64*h:64*h+64,pl.ds(k0,BK)],dst[h]) for h in both]
            return tuple(out)
        init=jnp.zeros((64,BQ),F32)
        res=lax.fori_loop(0,count,step,(init,init))
        dq=jnp.concatenate(res,axis=0).T*0.125
        for t in range(BQ//ROWS):
            at=pl.multiple_of(r0+t*ROWS,ROWS)
            spread(i*(BQ//ROWS)+t,0,unturn(dq[t*ROWS:(t+1)*ROWS],at).astype(BF))
        return 0
    used=(e1+BQ-1)//BQ
    lax.fori_loop(0,used,qblock,0)
    def blank(i,_):
        spread(i,0,jnp.zeros((ROWS,128),BF))
        return 0
    lax.fori_loop(used*(BQ//ROWS),rows//ROWS,blank,0)
    def last(i,_):
        r0=pl.multiple_of(i*ROWS,ROWS)
        spread(i,1,unturn(dk[pl.ds(r0,ROWS),:],r0).astype(BF))
        spread(i,2,dv[pl.ds(r0,ROWS),:].astype(BF))
        return 0
    lax.fori_loop(0,rows//ROWS,last,0)

def attend_bwd(ctl,own,recv,d_own,d_recv,o_own,o_oth,lse,cos,sin):
    half,width=own.shape
    pairs=width//384
    rows=2*half
    sp=[pl.BlockSpec((half,128),(lambda p,c,s=s:(0,s*pairs+p))) for s in range(3)]
    one=pl.BlockSpec((half,128),lambda p,c:(0,p))
    full=pl.BlockSpec((rows,128),lambda p,c:(0,0))
    return pl.pallas_call(bwd_kernel,
        grid_spec=pltpu.PrefetchScalarGridSpec(num_scalar_prefetch=1,grid=(pairs,),
          in_specs=sp+sp+[one]*4+[pl.BlockSpec((1,8,rows),lambda p,c:(p,0,0)),full,full],
          out_specs=[one]*6,
          scratch_shapes=[pltpu.VMEM((rows+BK,256),BF),pltpu.VMEM((rows,256),BF),pltpu.VMEM((rows,256),BF),
             pltpu.VMEM((rows+BK,128),BF),pltpu.VMEM((rows,128),BF),pltpu.VMEM((rows,128),BF),
             pltpu.VMEM((128,rows+BK),BF),pltpu.VMEM((16,rows),F32),pltpu.VMEM((rows+BK,128),F32),pltpu.VMEM((rows+BK,128),F32)]),
        out_shape=[jax.ShapeDtypeStruct((half,width//3),BF)]*6,
        compiler_params=pltpu.CompilerParams(vmem_limit_bytes=60<<20,dimension_semantics=("arbitrary",)),
        cost_estimate=pl.CostEstimate(flops=10*rows*rows*64*2*pairs//2,bytes_accessed=20*half*width,transcendentals=rows*rows*pairs),
        name="attend_bwd",
    )(ctl,own,own,own,recv,recv,recv,d_own,d_recv,o_own,o_oth,lse,cos,sin)

BLOCK=256

def spread_mean(x):
    return jnp.mean(x,axis=1,keepdims=True)

def row_docs(ctl,block):
    i=pl.program_id(0)
    r=ctl[0]*(block*pl.num_programs(0))+i*block+lax.broadcasted_iota(jnp.int32,(block,1),0)
    return (r>=ctl[1]).astype(jnp.int32)+(r>=ctl[2]).astype(jnp.int32)

def ffn_fwd_kernel(ctl,ao,ax,tok,w_exp,w_con,w_out,norm,u1,u2,rs,yb,h0,h1,h2,h3,pf,pooled):
    block,width=tok.shape
    hidden=pf.shape[1]//2
    kept=(h0,h1,h2,h3)
    share=width//2
    pos=ctl[0]
    mine=pl.multiple_of(pos*share,share)
    other=pl.multiple_of((1-pos)*share,share)
    f=tok[...].astype(F32)+nn(ao[...],w_out[pl.ds(mine,share),:])+nn(ax[...],w_out[pl.ds(other,share),:])
    cent=f-spread_mean(f)
    scale=lax.rsqrt(spread_mean(cent*cent)+NORM_EPSILON)
    unit=cent*scale
    u1[...]=unit
    rs[:,0:128]=jnp.broadcast_to(scale,(block,128))
    y=unit*norm[0:1,:]+norm[1:2,:]
    ylow=y.astype(BF)
    yb[...]=ylow
    acc=y
    count=hidden//width
    spans=[(slice(c*width,(c+1)*width),slice(hidden+c*width,hidden+(c+1)*width)) for c in range(count)]
    pre=lambda c: (nn(ylow,w_exp[:,spans[c][0]]),nn(ylow,w_exp[:,spans[c][1]]))
    ahead=pre(0)
    for c in range(count):
        gate,up=ahead
        if c+1<count: ahead=pre(c+1)
        gc,uc=spans[c]
        sig=jax.nn.sigmoid(gate)
        act=gate*sig
        low=(act*up).astype(BF)
        kept[c][...]=low
        pf[:,gc]=(up*(sig+act*(1.0-sig))).astype(BF)
        pf[:,uc]=act.astype(BF)
        acc=acc+nn(low,w_con[:,gc])
    cent=acc-spread_mean(acc)
    scale=lax.rsqrt(spread_mean(cent*cent)+NORM_EPSILON)
    unit=cent*scale
    u2[...]=unit
    rs[:,128:256]=jnp.broadcast_to(scale,(block,128))
    out=unit*norm[2:3,:]+norm[3:4,:]
    docs=row_docs(ctl,block)
    @pl.when(pl.program_id(0)==0)
    def _(): pooled[...]=jnp.zeros_like(pooled)
    for d in range(2):
        pooled[d:d+1,:]+=jnp.sum(jnp.where(docs==d,out,0.0),axis=0,keepdims=True)

def ffn_fwd(ctl,ao,ax,tok,bundle,norm,hidden):
    rows,width=tok.shape
    row=lambda n: pl.BlockSpec((BLOCK,n),lambda i,c:(i,0))
    held=lambda n,at: pl.BlockSpec((width,n),lambda i,c:(0,at//n),pipeline_mode=pl.Buffered(1))
    flat=pl.BlockSpec((8,width),lambda i,c:(0,0))
    return pl.pallas_call(ffn_fwd_kernel,
        grid_spec=pltpu.PrefetchScalarGridSpec(num_scalar_prefetch=1,grid=(rows//BLOCK,),
          in_specs=[row(width//2),row(width//2),row(width),held(2*hidden,0),held(hidden,2*hidden),held(width,3*hidden),flat],
          out_specs=[row(width),row(width),row(256),*[row(width)]*5,row(2*hidden),flat]),
        out_shape=[jax.ShapeDtypeStruct((rows,width),F32),jax.ShapeDtypeStruct((rows,width),F32),jax.ShapeDtypeStruct((rows,256),F32),
          *[jax.ShapeDtypeStruct((rows,width),BF)]*5,jax.ShapeDtypeStruct((rows,2*hidden),BF),
          jax.ShapeDtypeStruct((8,width),F32)],
        compiler_params=pltpu.CompilerParams(vmem_limit_bytes=60<<20,dimension_semantics=("arbitrary",)),
        cost_estimate=pl.CostEstimate(flops=2*rows*width*(width+3*hidden),bytes_accessed=rows*(width*14+hidden*6)+2*width*(width+3*hidden),transcendentals=rows*hidden),
        name="ffn_fwd",
    )(ctl,ao,ax,tok,bundle,bundle,bundle,norm)

def loss_grad(pool,targets,len0,len1):
    width=pool.shape[1]
    docs=lax.broadcasted_iota(jnp.int32,pool.shape,0)
    length=jnp.where(docs==0,len0,len1)
    emb=pool/length
    lane=lax.broadcasted_iota(jnp.int32,pool.shape,1)
    d_target=jnp.zeros_like(pool)
    d_self=jnp.zeros_like(pool)
    for cut in (width//12,width//6,width//3,2*width//3,width):
        keep=lane<cut
        total=lambda v: jnp.sum(jnp.where(keep,v,0.0),axis=1,keepdims=True)
        own_root=lax.rsqrt(total(emb*emb)+COSINE_EPSILON)
        other_root=lax.rsqrt(total(targets*targets)+COSINE_EPSILON)
        cosine=total(emb*targets)*own_root*other_root
        d_target=d_target+jnp.where(keep,own_root*other_root,0.0)
        d_self=d_self+jnp.where(keep,cosine*own_root*own_root,0.0)
    d_emb=length*(d_self*emb-d_target*targets)
    return emb,d_emb/length

def ffn_bwd_kernel(ctl,flen,pool_a,pool_b,targets,u1,u2,rs,pf,w_exp,w_con,w_out,norm,
                   emb,mb,ub,df,ab,do,dx,gn,de):
    block,width=u1.shape
    hidden=pf.shape[1]//2
    share=width//2
    pos=ctl[0]
    @pl.when(pl.program_id(0)==0)
    def _():
        e,d=loss_grad(pool_a[...]+pool_b[...],targets[...],flen[0],flen[1])
        emb[...]=e
        de[...]=d
        gn[...]=jnp.zeros_like(gn)
    docs=row_docs(ctl,block)
    dout=jnp.where(docs==0,de[0:1,:],jnp.where(docs==1,de[1:2,:],0.0))
    unit=u2[...]
    gn[2:3,:]+=jnp.sum(dout*unit,axis=0,keepdims=True)
    gn[3:4,:]+=jnp.sum(dout,axis=0,keepdims=True)
    gu=dout*norm[2:3,:]
    dg=rs[:,128:129]*(gu-spread_mean(gu)-unit*spread_mean(gu*unit))
    mlow=dg.astype(BF)
    mb[...]=mlow
    acc=dg
    for c in range(hidden//width):
        gc=slice(c*width,(c+1)*width)
        uc=slice(hidden+c*width,hidden+(c+1)*width)
        dh=nt(mlow,w_con[:,gc])
        dgate=(dh*pf[:,gc].astype(F32)).astype(BF)
        dup=(dh*pf[:,uc].astype(F32)).astype(BF)
        ub[:,gc]=dgate
        ub[:,uc]=dup
        acc=acc+nt(dgate,w_exp[:,gc])+nt(dup,w_exp[:,uc])
    unit=u1[...]
    gn[0:1,:]+=jnp.sum(acc*unit,axis=0,keepdims=True)
    gn[1:2,:]+=jnp.sum(acc,axis=0,keepdims=True)
    gu=acc*norm[0:1,:]
    dfirst=rs[:,0:1]*(gu-spread_mean(gu)-unit*spread_mean(gu*unit))
    df[...]=dfirst
    alow=dfirst.astype(BF)
    ab[...]=alow
    do[...]=nt(alow,w_out[pl.ds(pl.multiple_of(pos*share,share),share),:]).astype(BF)
    dx[...]=nt(alow,w_out[pl.ds(pl.multiple_of((1-pos)*share,share),share),:]).astype(BF)

def ffn_bwd(ctl,flen,pool_a,pool_b,targets,u1,u2,rs,pf,bundle,norm):
    rows,width=u1.shape
    hidden=pf.shape[1]//2
    row=lambda n: pl.BlockSpec((BLOCK,n),lambda i,c,l:(i,0))
    held=lambda n,at: pl.BlockSpec((width,n),lambda i,c,l:(0,at//n),pipeline_mode=pl.Buffered(1))
    flat=pl.BlockSpec((8,width),lambda i,c,l:(0,0))
    sds=jax.ShapeDtypeStruct
    return pl.pallas_call(ffn_bwd_kernel,
        grid_spec=pltpu.PrefetchScalarGridSpec(num_scalar_prefetch=2,grid=(rows//BLOCK,),
          in_specs=[flat,flat,flat,row(width),row(width),row(256),row(2*hidden),held(2*hidden,0),held(hidden,2*hidden),held(width,3*hidden),flat],
          out_specs=[flat,row(width),row(2*hidden),row(width),row(width),row(width//2),row(width//2),flat],
          scratch_shapes=[pltpu.VMEM((8,width),F32)]),
        out_shape=[sds((8,width),F32),sds((rows,width),BF),sds((rows,2*hidden),BF),sds((rows,width),F32),sds((rows,width),BF),
          sds((rows,width//2),BF),sds((rows,width//2),BF),sds((8,width),F32)],
        compiler_params=pltpu.CompilerParams(vmem_limit_bytes=60<<20,dimension_semantics=("arbitrary",)),
        cost_estimate=pl.CostEstimate(flops=2*rows*width*(width+3*hidden),bytes_accessed=rows*(width*18+hidden*8)+2*width*(width+3*hidden),transcendentals=0),
        name="ffn_bwd",
    )(ctl,flen,pool_a,pool_b,targets,u1,u2,rs,pf,bundle,bundle,bundle,norm)

MESH=pl.DeviceIdType.MESH

def place():
    dp=lax.axis_index("dp")
    core=lax.axis_index("dim")
    return dp//4,(dp//2)%2,dp%2,core

def meet(z,y,x,core):
    chip=lambda a,b,c: a*4+b*2+c
    peers=[(chip(z,y,x),1-core),(chip(z,y,1-x),core),(chip(z,1-y,x),core)]
    peers+=[(chip(lax.rem(z+k,4),y,x),core) for k in (1,2,3)]
    barrier=pltpu.get_barrier_semaphore()
    for peer in peers:
        pl.semaphore_signal(barrier,inc=1,device_id=peer,device_id_type=MESH)
    pl.semaphore_wait(barrier,len(peers))
    return peers

def lanes_of(cols):
    tiles=cols//128
    widths=[tiles-tiles//4*3]+[tiles//4]*3
    widths=[widths[0],widths[2],widths[1],widths[3]]
    widths=[5,5,4,4] if tiles==18 else widths
    out=[]
    at=0
    for n,w in enumerate(widths):
        out.append((at*128,w*128,n%2==0))
        at+=w
    return out

def send(src,dst,sems,n,k,peer):
    copy=pltpu.make_async_remote_copy(src_ref=src,dst_ref=dst,send_sem=sems[0].at[n,k],recv_sem=sems[1].at[n,k],device_id=peer,device_id_type=MESH)
    copy.start()
    return copy

def gather_kernel(w,out,low,local,s_sem,r_sem):
    z,y,x,core=place()
    low[...]=w[...].astype(BF)
    keep=pltpu.make_async_copy(low,out.at[z,y,x,core],local)
    keep.start()
    pair,xn,yn,z1,z2,z3=meet(z,y,x,core)
    sems=(s_sem,r_sem)
    lanes=lanes_of(w.shape[1])
    every=[]
    def go(n,k,peer,*index,src=None):
        at,width,_=lanes[n]
        dst=out.at[(*index,slice(None),pl.ds(at,width))]
        if src is None: src=dst
        copy=send(src,dst,sems,n,k,peer)
        every.append(copy)
        return copy
    whole=slice(None)
    first=[]
    for n,(at,width,_) in enumerate(lanes):
        piece=low.at[:,pl.ds(at,width)]
        first.append([go(n,k,peer,z,y,x,core,src=piece) for k,peer in enumerate((z1,z2,z3))])
    keep.wait()
    second=[]
    for n,(_,_,flip) in enumerate(lanes):
        for copy in first[n]: copy.wait_recv()
        second.append(go(n,3,yn if flip else xn,whole,y,x,core))
        go(n,5,pair,whole,y,x,core)
    third=[]
    for n,(_,_,flip) in enumerate(lanes):
        second[n].wait_recv()
        if flip:
            third.append(go(n,4,xn,whole,whole,x,core))
            go(n,6,pair,whole,1-y,x,core)
        else:
            third.append(go(n,4,yn,whole,y,whole,core))
            go(n,6,pair,whole,y,1-x,core)
    for n,(_,_,flip) in enumerate(lanes):
        third[n].wait_recv()
        if flip: go(n,7,pair,whole,whole,1-x,core)
        else: go(n,7,pair,whole,1-y,whole,core)
    done=set(id(c) for c in second+third+[c for f in first for c in f])
    for copy in every:
        copy.wait_send()
        if id(copy) not in done: copy.wait_recv()

def ring_gather(w):
    share,cols=w.shape
    out=pl.pallas_call(gather_kernel,
        in_specs=[pl.BlockSpec(memory_space=pltpu.VMEM)],
        out_specs=pl.BlockSpec(memory_space=pl.ANY),
        scratch_shapes=[pltpu.VMEM((share,cols),BF),pltpu.SemaphoreType.DMA,pltpu.SemaphoreType.DMA((4,8)),pltpu.SemaphoreType.DMA((4,8))],
        out_shape=jax.ShapeDtypeStruct((4,2,2,2,share,cols),BF),
        compiler_params=pltpu.CompilerParams(collective_id=1,has_side_effects=True,vmem_limit_bytes=60<<20),
        cost_estimate=pl.CostEstimate(flops=0,bytes_accessed=64*share*cols*20,transcendentals=0),
        name="comm_gather",
    )(w)
    return out.reshape(32*share,cols)

def scatter_kernel(g,out,gl,r0,b1,k1,r1,b2,k2,r2,b3,k3,r3,local,s_sem,r_sem):
    z,y,x,core=place()
    keep=pltpu.make_async_copy(g.at[:,core],gl,local)
    keep.start()
    pair,xn,yn,z1,z2,z3=meet(z,y,x,core)
    sems=(s_sem,r_sem)
    lanes=lanes_of(out.shape[1])
    span=[pl.ds(at,width) for at,width,_ in lanes]
    every=[]
    def go(n,k,peer,src,dst):
        copy=send(src,dst,sems,n,k,peer)
        every.append(copy)
        return copy
    n_lanes=range(len(lanes))
    zero=[go(n,0,pair,g.at[:,1-core,:,span[n]],r0.at[:,:,span[n]]) for n in n_lanes]
    def split1(n,iz,j,side):
        row=iz*4+(j*2+side if lanes[n][2] else side*2+j)
        c=span[n]
        return gl[row,:,c].astype(F32)+r0[row,:,c].astype(F32)
    one=[]
    keep.wait()
    for n in n_lanes:
        flip=lanes[n][2]
        side=x if flip else y
        zero[n].wait_recv()
        for iz in range(4):
            for j in range(2):
                b1[iz,j,:,span[n]]=split1(n,iz,j,1-side).astype(BF)
        one.append(go(n,1,xn if flip else yn,b1.at[:,:,:,span[n]],r1.at[:,:,:,span[n]]))
        for iz in range(4):
            for j in range(2):
                k1[iz,j,:,span[n]]=split1(n,iz,j,side)
    two=[]
    for n in n_lanes:
        flip=lanes[n][2]
        side=y if flip else x
        c=span[n]
        one[n].wait_recv()
        for iz in range(4):
            b2[iz,:,c]=(k1[iz,1-side,:,c]+r1[iz,1-side,:,c].astype(F32)).astype(BF)
        two.append(go(n,2,yn if flip else xn,b2.at[:,:,c],r2.at[:,:,c]))
        for iz in range(4):
            k2[iz,:,c]=k1[iz,side,:,c]+r1[iz,side,:,c].astype(F32)
    three=[]
    for n in n_lanes:
        c=span[n]
        two[n].wait_recv()
        for k in (1,2,3):
            to=lax.rem(z+k,4)
            b3[k-1,:,c]=(k2[to,:,c]+r2[to,:,c].astype(F32)).astype(BF)
        three.append([go(n,2+k,(z1,z2,z3)[k-1],b3.at[k-1,:,c],r3.at[k-1,:,c]) for k in (1,2,3)])
        k3[:,c]=k2[z,:,c]+r2[z,:,c].astype(F32)
    for n in n_lanes:
        c=span[n]
        for copy in three[n]: copy.wait_recv()
        out[:,c]=k3[:,c]+r3[0,:,c].astype(F32)+r3[1,:,c].astype(F32)+r3[2,:,c].astype(F32)
    for copy in every: copy.wait_send()

def ring_scatter(g):
    rows,cols=g.shape
    share=rows//32
    v=lambda *s: pltpu.VMEM((*s,share,cols),BF)
    f=lambda *s: pltpu.VMEM((*s,share,cols),F32)
    return pl.pallas_call(scatter_kernel,
        in_specs=[pl.BlockSpec(memory_space=pl.ANY)],
        out_specs=pl.BlockSpec(memory_space=pltpu.VMEM),
        scratch_shapes=[v(16),v(16),v(4,2),f(4,2),v(4,2),v(4),f(4),v(4),v(3),f(),v(3),pltpu.SemaphoreType.DMA,pltpu.SemaphoreType.DMA((4,6)),pltpu.SemaphoreType.DMA((4,6))],
        out_shape=jax.ShapeDtypeStruct((share,cols),F32),
        compiler_params=pltpu.CompilerParams(collective_id=2,has_side_effects=True,vmem_limit_bytes=60<<20),
        cost_estimate=pl.CostEstimate(flops=0,bytes_accessed=64*share*cols*20,transcendentals=0),
        name="comm_scatter",
    )(g.reshape(16,2,share,cols))

def selector(forward):
    r=lax.broadcasted_iota(jnp.int32,(512,512),0)
    c=lax.broadcasted_iota(jnp.int32,(512,512),1)
    a,b=(r,c) if forward else (c,r)
    return jnp.where(a==4*(b%128)+b//128,1.0,0.0).astype(BF)

def bundle_kernel(exp,con,out,norm,bundle,tiles):
    share,width=out.shape
    hidden=exp.shape[1]//2
    pick=selector(True)
    for b in range(exp.shape[1]//512):
        half,at=divmod(b*512,hidden)
        y=nn(exp[:,b*512:(b+1)*512].astype(BF),pick).astype(BF)
        for j in range(4):
            to=half*hidden+j*width+at//4
            bundle[:,to:to+128]=y[:,j*128:(j+1)*128]
    for t in range(width//128):
        tiles[t]=con[:,t*128:(t+1)*128]
        for j in range(4):
            to=2*hidden+j*width+t*128
            bundle[:,to:to+128]=tiles[t,pl.ds(j,share,stride=4),:].astype(BF)
    bundle[:,3*hidden:3*hidden+width]=out[...].astype(BF)
    flat=jnp.concatenate([norm[...],jnp.zeros((4,128-share),F32)],1)
    bundle[:,3*hidden+width:]=jnp.concatenate([flat,jnp.zeros((share-4,128),F32)],0).astype(BF)

def make_bundle(exp,con,out,norm):
    share,width=out.shape
    total=exp.shape[1]+4*width+width+128
    return pl.pallas_call(bundle_kernel,
        out_shape=jax.ShapeDtypeStruct((share,total),BF),
        scratch_shapes=[pltpu.VMEM((width//128,4*share,128),F32)],
        compiler_params=pltpu.CompilerParams(vmem_limit_bytes=60<<20),
        cost_estimate=pl.CostEstimate(flops=2*share*512*exp.shape[1],bytes_accessed=6*share*total,transcendentals=0),
        name="make_bundle",
    )(exp,con,out,norm)

def update_kernel(rates,sums,*refs):
    ins,outs,tiles=refs[:12],refs[12:32],refs[32]
    exp_w,con_w,out_w,norm_w=(ins[3*k:3*k+3] for k in range(4))
    share,width=out_w[0].shape
    hidden=exp_w[0].shape[1]//2
    def step(kind,index,g,rate):
        w,m,a=(ref[index] for ref in ins[3*kind:3*kind+3])
        grad,nxt,mom,avg,low=outs[5*kind:5*kind+5]
        mn=MOMENTUM*m+g
        wn=w-rate*(g+MOMENTUM*mn)
        grad[index]=g
        nxt[index]=wn
        mom[index]=mn
        avg[index]=AVERAGE_DECAY*a+(1.0-AVERAGE_DECAY)*wn
        low[index]=wn.astype(BF)
    pick=selector(False)
    for b in range(2*hidden//512):
        half,at=divmod(b*512,hidden)
        z=jnp.concatenate([sums[:,half*hidden+j*width+at//4:half*hidden+j*width+at//4+128] for j in range(4)],1)
        step(0,(slice(None),slice(b*512,(b+1)*512)),nn(z,pick),rates[0])
    for t in range(width//128):
        for j in range(4):
            at=2*hidden+j*width+t*128
            tiles[t,pl.ds(j,share,stride=4),:]=sums[:,at:at+128].astype(F32)
        step(1,(slice(None),slice(t*128,(t+1)*128)),tiles[t],rates[0])
    step(2,(slice(None),slice(None)),sums[:,3*hidden:3*hidden+width].astype(F32),rates[0])
    step(3,(slice(None),slice(None)),sums[0:8,3*hidden+width:].astype(F32)[0:4,0:share],rates[1])

def update(sums,rates,params):
    sds=jax.ShapeDtypeStruct
    shapes=[]
    for w,_,_ in params:
        shapes+=[sds(w.shape,F32)]*4+[sds(w.shape,BF)]
    flat=[x for p in params for x in p]
    import_vmem=pl.BlockSpec(memory_space=pltpu.VMEM)
    outs=pl.pallas_call(lambda *refs: update_kernel(rates,*refs),
        in_specs=[import_vmem]*13,
        out_specs=[import_vmem]*20,
        out_shape=shapes,
        scratch_shapes=[pltpu.VMEM((params[2][0].shape[1]//128,params[1][0].shape[0],128),F32)],
        compiler_params=pltpu.CompilerParams(vmem_limit_bytes=60<<20),
        cost_estimate=pl.CostEstimate(flops=2*24*512*6144,bytes_accessed=12<<20,transcendentals=0),
        name="update",
    )(sums,*flat)
    return [outs[5*k:5*k+5] for k in range(4)]

def tail_kernel(ctl,x,qo,ko,vo,qr,kr,vr,w,df,tok,gm,acc):
    pos=ctl[0]
    i=pl.program_id(0)
    width=x.shape[1]
    turned=x[...].T
    total=df[...]
    @pl.when(i==0)
    def _(): acc[...]=jnp.zeros_like(acc)
    for s,(mine,theirs) in enumerate(((qo,qr),(ko,kr),(vo,vr))):
        a=mine[...]
        b=theirs[...]
        grad=jnp.concatenate([jnp.where(pos==0,a,b),jnp.where(pos==0,b,a)],1)
        cols=slice(s*width,(s+1)*width)
        total=total+nt(grad,w[:,cols])
        acc[:,cols]+=nn(turned,grad)
    tok[...]=total
    @pl.when(i==pl.num_programs(0)-1)
    def _(): gm[...]=acc[...].astype(BF)

def tail(ctl,x,own,recv,w,df):
    rows,width=x.shape
    cols=w.shape[1]
    row=lambda n: pl.BlockSpec((512,n),lambda i,c:(i,0))
    held=pl.BlockSpec((width,cols),lambda i,c:(0,0),pipeline_mode=pl.Buffered(1))
    return pl.pallas_call(tail_kernel,
        grid_spec=pltpu.PrefetchScalarGridSpec(num_scalar_prefetch=1,grid=(rows//512,),
          in_specs=[row(width)]+[row(width//2)]*6+[held,row(width)],
          out_specs=[row(width),pl.BlockSpec((width,cols),lambda i,c:(0,0))],
          scratch_shapes=[pltpu.VMEM((width,cols),F32)]),
        out_shape=[jax.ShapeDtypeStruct((rows,width),F32),jax.ShapeDtypeStruct((width,cols),BF)],
        compiler_params=pltpu.CompilerParams(vmem_limit_bytes=60<<20,dimension_semantics=("arbitrary",)),
        cost_estimate=pl.CostEstimate(flops=4*rows*width*cols,bytes_accessed=rows*width*16+8*width*cols,transcendentals=0),
        name="tail",
    )(ctl,x,*own,*recv,w,df)

def mix_kernel(ctl,x,w,cos,sin,own,oth):
    pos=ctl[0]
    width=x.shape[1]
    share=width//2
    xb=x[...]
    c=cos[...]
    s=sin[...]
    lane=lax.broadcasted_iota(jnp.int32,c.shape,1)
    first=(lane%64)<32
    for part in range(3):
        y=nn(xb,w[:,part*width:(part+1)*width])
        tiles=[]
        for t in range(width//128):
            z=y[:,t*128:(t+1)*128]
            if part<2:
                swapped=jnp.where(first,pltpu.roll(z,96,1),pltpu.roll(z,32,1))
                z=z*c+swapped*s
            tiles.append(z.astype(BF))
        count=share//128
        for t in range(count):
            cols=slice(part*share+t*128,part*share+(t+1)*128)
            own[:,cols]=jnp.where(pos==0,tiles[t],tiles[count+t])
            oth[:,cols]=jnp.where(pos==0,tiles[count+t],tiles[t])

def mix(ctl,x,w,cos,sin):
    rows,width=x.shape
    cols=w.shape[1]
    block=256
    row=lambda n: pl.BlockSpec((block,n),lambda i,c:(i,0))
    angle=pl.BlockSpec((block,128),lambda i,c:(c[0]*(rows//block)+i,0))
    return pl.pallas_call(mix_kernel,
        grid_spec=pltpu.PrefetchScalarGridSpec(num_scalar_prefetch=1,grid=(rows//block,),
          in_specs=[row(width),pl.BlockSpec((width,cols),lambda i,c:(0,0)),angle,angle],
          out_specs=[row(cols//2)]*2),
        out_shape=[jax.ShapeDtypeStruct((rows,cols//2),BF)]*2,
        compiler_params=pltpu.CompilerParams(vmem_limit_bytes=60<<20,dimension_semantics=("arbitrary",)),
        cost_estimate=pl.CostEstimate(flops=2*rows*width*cols,bytes_accessed=2*(rows*width+width*cols+rows*cols),transcendentals=0),
        name="mix",
    )(ctl,x,w,cos,sin)

def swap_cores(x):
    return lax.ppermute(x,"dim",[(0,1),(1,0)])

def join(pos,own,recv,axis=1):
    return jnp.where(pos==0,jnp.concatenate([own,recv],axis),jnp.concatenate([recv,own],axis))

def body(tokens,doc_lengths,pair_index,target_bank,mixer_in,mixer_out,expand,contract,norm_params,*rest):
    slices=lax.axis_size("dim")
    if slices!=2 or lax.axis_size("dp")!=16 or doc_lengths.shape[1]!=2:
        return body_general(tokens,doc_lengths,pair_index,target_bank,mixer_in,mixer_out,expand,contract,norm_params,*rest)
    (mixer_in_moment,mixer_out_moment,expand_moment,contract_moment,norm_moment,
     mixer_in_average,mixer_out_average,expand_average,contract_average,norm_average)=rest
    local_rows,model_width=tokens.shape
    group_rows=local_rows*slices
    pos=lax.axis_index("dim")
    doc_count=2
    w_mix=ring_gather(mixer_in[0])
    share_rows=mixer_out.shape[1]
    per=contract.shape[1]//share_rows
    count=model_width//share_rows
    hidden_width=contract.shape[1]*count
    bundle=make_bundle(expand[0],contract[0],mixer_out[0],norm_params[0])
    bundle=lax.all_gather(bundle,("dp","dim"),axis=0,tiled=True)
    at1=2*hidden_width
    at2=at1+per*model_width
    at3=at2+model_width
    w_norm=bundle[:,at3:].reshape(count,share_rows,128)[:,0:4,0:share_rows].transpose(1,0,2).reshape(4,model_width)
    lengths=doc_lengths[0]
    e0=lengths[0]
    e1=lengths[0]+lengths[1]
    ctl=jnp.stack([pos.astype(jnp.int32),e0,e1])
    ids=jnp.arange(group_rows,dtype=jnp.int32)
    seg=(ids>=e0).astype(jnp.int32)+(ids>=e1).astype(jnp.int32)
    begin=jnp.where(seg==0,0,jnp.where(seg==1,e0,e1))
    lane=jnp.arange(128,dtype=jnp.int32)
    frequency=jnp.power(1000.0,-(2*(lane%32)).astype(F32)/HEAD)
    angles=(ids-begin).astype(F32)[:,None]*frequency[None,:]
    cos=jnp.cos(angles)
    sin=jnp.sin(angles)*jnp.where((lane%64)<32,-1.0,1.0)[None,:]
    own,oth=mix(ctl,tokens,w_mix,cos,sin)
    recv=swap_cores(oth)
    pick=(pair_index[:,None]==jnp.arange(target_bank.shape[0],dtype=jnp.int32)[None,:]).astype(BF)
    some=matmul(pick,target_bank)
    targets=jnp.pad(join(pos,some,swap_cores(some)),((0,6),(0,0)))
    o_own,o_oth,lse=attend_fwd(ctl,own,recv)
    o_recv=swap_cores(o_oth)
    norm_gains=jnp.pad(w_norm.astype(F32),((0,4),(0,0)))
    u1,u2,rs,y_low,*hidden,factors,pooled=ffn_fwd(ctl,o_own,o_recv,tokens,bundle,norm_gains,hidden_width)
    embeds,grad_m_low,grad_both,grad_first,grad_a_low,d_own,d_oth,grad_norm=ffn_bwd(
        ctl,lengths.astype(F32),pooled,swap_cores(pooled),targets,u1,u2,rs,factors,bundle,norm_gains)
    share=model_width//2
    embeddings=lax.dynamic_slice(embeds,(0,pos*share),(doc_count,share))
    d_recv=swap_cores(d_oth)
    grad_exp=inner_rows(y_low,grad_both)
    grad_con=[inner_rows(h,grad_m_low).astype(BF) for h in hidden]
    grad_out=join(pos,inner_rows(o_own,grad_a_low),inner_rows(o_recv,grad_a_low),0)
    grad_norm=grad_norm[0:4].reshape(4,count,share_rows).transpose(1,0,2)
    grad_norm=jnp.pad(grad_norm,((0,0),(0,share_rows-4),(0,128-share_rows))).reshape(model_width,128)
    terms=jnp.concatenate([grad_exp.astype(BF),*grad_con,grad_out.astype(BF),grad_norm.astype(BF)],1)
    terms,d_own,d_recv=lax.optimization_barrier((terms,d_own,d_recv))
    sums=lax.psum_scatter(terms,("dp","dim"),scatter_dimension=0,tiled=True)
    backs=attend_bwd(ctl,own,recv,d_own,d_recv,o_own,o_oth,lse,cos,sin)
    token_grads,grad_mix=tail(ctl,tokens,backs[0:3],[swap_cores(g) for g in backs[3:6]],w_mix,grad_first)
    total_rows=group_rows*lax.axis_size("dp")
    matrix_rate=1.0/math.sqrt(total_rows)
    norm_rate=0.3/math.sqrt(total_rows)
    new_exp,new_con,new_out,new_norm=update(sums,(matrix_rate,norm_rate),[
        (expand[0],expand_moment[0],expand_average[0]),(contract[0],contract_moment[0],contract_average[0]),
        (mixer_out[0],mixer_out_moment[0],mixer_out_average[0]),(norm_params[0],norm_moment[0],norm_average[0])])
    sum_mix=ring_scatter(grad_mix)
    nxt,mom,avg,low=advance(mixer_in[0],mixer_in_moment[0],mixer_in_average[0],sum_mix,matrix_rate)
    results=[[sum_mix,nxt,mom,avg,low],new_out,new_exp,new_con,new_norm]
    return (embeddings,token_grads,*[results[k][f][None] for f in range(5) for k in range(5)])

def solution(mesh):
    placed = (
        P(("dp", "dim"), None),
        P("dp", None),
        P("dp"),
        P(None, "dim"),
        P(None, ("dp", "dim"), None),
        P(None, ("dp", "dim"), None),
        P(None, ("dp", "dim"), None),
        P(None, ("dp", "dim"), None),
        P(None, None, ("dp", "dim")),
        P(None, ("dp", "dim"), None),
        P(None, ("dp", "dim"), None),
        P(None, ("dp", "dim"), None),
        P(None, ("dp", "dim"), None),
        P(None, None, ("dp", "dim")),
        P(None, ("dp", "dim"), None),
        P(None, ("dp", "dim"), None),
        P(None, ("dp", "dim"), None),
        P(None, ("dp", "dim"), None),
        P(None, None, ("dp", "dim")),
    )
    return jax.shard_map(
        body,
        mesh=mesh,
        in_specs=placed,
        out_specs=(
            P("dp", "dim"),
            P(("dp", "dim"), None),
            P(None, ("dp", "dim"), None),
            P(None, ("dp", "dim"), None),
            P(None, ("dp", "dim"), None),
            P(None, ("dp", "dim"), None),
            P(None, None, ("dp", "dim")),
            P(None, ("dp", "dim"), None),
            P(None, ("dp", "dim"), None),
            P(None, ("dp", "dim"), None),
            P(None, ("dp", "dim"), None),
            P(None, None, ("dp", "dim")),
            P(None, ("dp", "dim"), None),
            P(None, ("dp", "dim"), None),
            P(None, ("dp", "dim"), None),
            P(None, ("dp", "dim"), None),
            P(None, None, ("dp", "dim")),
            P(None, ("dp", "dim"), None),
            P(None, ("dp", "dim"), None),
            P(None, ("dp", "dim"), None),
            P(None, ("dp", "dim"), None),
            P(None, None, ("dp", "dim")),
            P(None, ("dp", "dim"), None),
            P(None, ("dp", "dim"), None),
            P(None, ("dp", "dim"), None),
            P(None, ("dp", "dim"), None),
            P(None, None, ("dp", "dim")),
        ),
        check_vma=False,
    )
```

```python
import functools
import math

import jax
import jax.numpy as jnp
from jax import lax
from jax.experimental import pallas as pl
from jax.experimental.pallas import tpu as pltpu
from jax.sharding import PartitionSpec as P

HEAD = 64


NORM_EPSILON = 1e-05
COSINE_EPSILON = 1e-06
MOMENTUM = 0.5
AVERAGE_DECAY = 0.5
PRECISE = lax.Precision.HIGHEST
MASKED = -1e30


def matmul(left_op, right_op):
    return jnp.dot(left_op, right_op, preferred_element_type=jnp.float32)


def matmul_exact(left_op, right_op):
    return jnp.dot(left_op, right_op, precision=PRECISE, preferred_element_type=jnp.float32)


def inner_rows(left_op, right_op):
    return lax.dot_general(
        left_op, right_op, (((0,), (0,)), ((), ())), preferred_element_type=jnp.float32
    )


def inner_cols(left_op, right_op):
    return lax.dot_general(
        left_op, right_op, (((1,), (1,)), ((), ())), preferred_element_type=jnp.float32
    )


def rotate(values, cosines, sines):
    row_count = values.shape[0]
    shaped = values.reshape(row_count, -1, 2, HEAD // 2)
    former = shaped[:, :, 0, :]
    latter = shaped[:, :, 1, :]
    cosine_b = cosines[:, None, :]
    sine_b = sines[:, None, :]
    turned = jnp.stack(
        [former * cosine_b - latter * sine_b, latter * cosine_b + former * sine_b], axis=2
    )
    return turned.reshape(values.shape)


def rotate_back(grads_in, cosines, sines):
    row_count = grads_in.shape[0]
    shaped = grads_in.reshape(row_count, -1, 2, HEAD // 2)
    former = shaped[:, :, 0, :]
    latter = shaped[:, :, 1, :]
    cosine_b = cosines[:, None, :]
    sine_b = sines[:, None, :]
    turned = jnp.stack(
        [former * cosine_b + latter * sine_b, latter * cosine_b - former * sine_b], axis=2
    )
    return turned.reshape(grads_in.shape)


def normalize(summed, gain_vec, bias_vec):
    centred = summed - jnp.mean(summed, axis=1, keepdims=True)
    scaling = lax.rsqrt(jnp.mean(centred * centred, axis=1, keepdims=True) + NORM_EPSILON)
    return centred * scaling * gain_vec + bias_vec


def normalize_back(grad_in, summed, gain_vec):
    centred = summed - jnp.mean(summed, axis=1, keepdims=True)
    scaling = lax.rsqrt(jnp.mean(centred * centred, axis=1, keepdims=True) + NORM_EPSILON)
    unit = centred * scaling
    grad_unit = grad_in * gain_vec
    grad_sum = scaling * (
        grad_unit
        - jnp.mean(grad_unit, axis=1, keepdims=True)
        - unit * jnp.mean(grad_unit * unit, axis=1, keepdims=True)
    )
    return (grad_sum, jnp.sum(grad_in * unit, axis=0), jnp.sum(grad_in, axis=0))


def flatten(stacked):
    return stacked.transpose(1, 0, 2).reshape(stacked.shape[1], -1)


def attend(q_rot, all_keys, all_values, same_doc):
    head_count = q_rot.shape[1] // HEAD

    def one_head(head_pos):
        offset = head_pos * HEAD
        query_part = lax.dynamic_slice_in_dim(q_rot, offset, HEAD, 1)
        key_part = lax.dynamic_slice_in_dim(all_keys, offset, HEAD, 1)
        value_part = lax.dynamic_slice_in_dim(all_values, offset, HEAD, 1)
        scores = jnp.where(same_doc, inner_cols(query_part, key_part) * 0.125, MASKED)
        row_max = jnp.max(scores, axis=1, keepdims=True)
        exponent = jnp.exp(scores - row_max)
        row_total = jnp.sum(exponent, axis=1, keepdims=True)
        attn_probs = (exponent / row_total).astype(jnp.bfloat16)
        return (matmul(attn_probs, value_part), (row_max + jnp.log(row_total))[:, 0])

    outputs, log_totals = lax.map(one_head, jnp.arange(head_count, dtype=jnp.int32))
    return (flatten(outputs), log_totals)


def attend_back(q_rot, all_keys, all_values, same_doc, grad_out, log_totals):
    head_count = q_rot.shape[1] // HEAD

    def one_head(pack):
        head_pos, log_total = pack
        offset = head_pos * HEAD
        query_part = lax.dynamic_slice_in_dim(q_rot, offset, HEAD, 1)
        key_part = lax.dynamic_slice_in_dim(all_keys, offset, HEAD, 1)
        value_part = lax.dynamic_slice_in_dim(all_values, offset, HEAD, 1)
        grad_part = lax.dynamic_slice_in_dim(grad_out, offset, HEAD, 1)
        scores = jnp.where(same_doc, inner_cols(query_part, key_part) * 0.125, MASKED)
        attn_probs = jnp.exp(scores - log_total[:, None])
        grad_probs = inner_cols(grad_part, value_part)
        row_dot = jnp.sum(attn_probs * grad_probs, axis=1, keepdims=True)
        grad_scores = (attn_probs * (grad_probs - row_dot)).astype(jnp.bfloat16)
        grad_query = matmul(grad_scores, key_part) * 0.125
        grad_key = inner_rows(grad_scores, query_part) * 0.125
        grad_value = inner_rows(attn_probs.astype(jnp.bfloat16), grad_part)
        return (grad_query, grad_key, grad_value)

    mapped = lax.map(one_head, (jnp.arange(head_count, dtype=jnp.int32), log_totals))
    return (flatten(mapped[0]), flatten(mapped[1]), flatten(mapped[2]))


def advance(weight, moment, average, grad_in, rate):
    moment_next = MOMENTUM * moment + grad_in
    weight_next = weight - rate * (grad_in + MOMENTUM * moment_next)
    average_next = AVERAGE_DECAY * average + (1.0 - AVERAGE_DECAY) * weight_next
    return (weight_next, moment_next, average_next, weight_next.astype(jnp.bfloat16))


def body_general(
    tokens,
    doc_lengths,
    pair_index,
    target_bank,
    mixer_in,
    mixer_out,
    expand,
    contract,
    norm_params,
    mixer_in_moment,
    mixer_out_moment,
    expand_moment,
    contract_moment,
    norm_moment,
    mixer_in_average,
    mixer_out_average,
    expand_average,
    contract_average,
    norm_average,
):
    local_rows, model_width = tokens.shape
    slices = lax.axis_size("dim")
    group_rows = local_rows * slices
    position = lax.axis_index("dim")
    layer_count = mixer_in.shape[0]
    doc_count = doc_lengths.shape[1]
    lengths = doc_lengths[0]
    doc_ends = jnp.cumsum(lengths)
    doc_starts = doc_ends - lengths
    row_ids = position * local_rows + jnp.arange(local_rows, dtype=jnp.int32)
    key_ids = jnp.arange(group_rows, dtype=jnp.int32)
    seg_rows = jnp.sum((row_ids[:, None] >= doc_ends[None, :]).astype(jnp.int32), axis=1)
    seg_keys = jnp.sum((key_ids[:, None] >= doc_ends[None, :]).astype(jnp.int32), axis=1)
    first_rows = jnp.concatenate([doc_starts, doc_ends[-1:]])
    segment_ids = jnp.arange(doc_count + 1, dtype=jnp.int32)
    row_begin = jnp.sum(
        jnp.where(seg_rows[:, None] == segment_ids[None, :], first_rows[None, :], 0), axis=1
    )
    frequency = jnp.power(1000.0, -jnp.arange(0, HEAD, 2).astype(jnp.float32) / HEAD)
    angles = (row_ids - row_begin).astype(jnp.float32)[:, None] * frequency[None, :]
    cosines = jnp.cos(angles)
    sines = jnp.sin(angles)
    same_doc = seg_rows[:, None] == seg_keys[None, :]
    stream = tokens.astype(jnp.float32)
    layer_pos = 0
    layer_weights = (
        lax.all_gather(mixer_in[layer_pos].astype(jnp.bfloat16), ("dp", "dim"), axis=0, tiled=True),
        lax.all_gather(
            mixer_out[layer_pos].astype(jnp.bfloat16), ("dp", "dim"), axis=0, tiled=True
        ),
        lax.all_gather(expand[layer_pos].astype(jnp.bfloat16), ("dp", "dim"), axis=0, tiled=True),
        lax.all_gather(contract[layer_pos].astype(jnp.bfloat16), ("dp", "dim"), axis=0, tiled=True),
        lax.all_gather(
            norm_params[layer_pos].astype(jnp.bfloat16), ("dp", "dim"), axis=1, tiled=True
        ),
    )
    w_mix, w_out, w_exp, w_con, w_norm = layer_weights
    norm_gains = w_norm.astype(jnp.float32)
    x_low = stream.astype(jnp.bfloat16)
    mixed = matmul(x_low, w_mix)
    q_rot = rotate(mixed[:, 0:model_width], cosines, sines).astype(jnp.bfloat16)
    k_rot = rotate(mixed[:, model_width : 2 * model_width], cosines, sines).astype(jnp.bfloat16)
    v_low = mixed[:, 2 * model_width : 3 * model_width].astype(jnp.bfloat16)
    all_keys = lax.all_gather(k_rot, "dim", axis=0, tiled=True)
    all_values = lax.all_gather(v_low, "dim", axis=0, tiled=True)
    attended, log_totals = attend(q_rot, all_keys, all_values, same_doc)
    att_low = attended.astype(jnp.bfloat16)
    first_sum = stream + matmul(att_low, w_out)
    normed = normalize(first_sum, norm_gains[0], norm_gains[1])
    y_low = normed.astype(jnp.bfloat16)
    gate_up = matmul(y_low, w_exp)
    half = gate_up.shape[1] // 2
    hidden = (jax.nn.silu(gate_up[:, 0:half]) * gate_up[:, half : 2 * half]).astype(jnp.bfloat16)
    second_sum = normed + matmul(hidden, w_con)
    saved = [
        (
            stream,
            layer_weights,
            q_rot,
            k_rot,
            v_low,
            all_keys,
            all_values,
            log_totals,
            attended,
            att_low,
            first_sum,
            normed,
            y_low,
            gate_up,
            hidden,
            second_sum,
        )
    ]
    stream = normalize(second_sum, norm_gains[2], norm_gains[3])
    member = (seg_rows[None, :] == jnp.arange(doc_count, dtype=jnp.int32)[:, None]).astype(
        jnp.float32
    )
    partial_value = matmul_exact(member, stream)
    pooled = lax.psum_scatter(partial_value, "dim", scatter_dimension=1, tiled=True)
    length_f = lengths.astype(jnp.float32)
    embeddings = pooled / length_f[:, None]
    share = embeddings.shape[1]
    pick = (
        pair_index[:, None] == jnp.arange(target_bank.shape[0], dtype=jnp.int32)[None, :]
    ).astype(jnp.bfloat16)
    targets = matmul(pick, target_bank)
    feature_ids = position * share + jnp.arange(share, dtype=jnp.int32)
    cuts = jnp.array(
        [model_width // 12, model_width // 6, model_width // 3, 2 * model_width // 3, model_width],
        dtype=jnp.int32,
    )
    masks = (feature_ids[None, :] < cuts[:, None]).astype(jnp.float32)
    cross = matmul_exact(embeddings * targets, masks.T)
    own = matmul_exact(embeddings * embeddings, masks.T)
    other = matmul_exact(targets * targets, masks.T)
    cross, own, other = lax.psum((cross, own, other), "dim")
    own_root = lax.rsqrt(own + COSINE_EPSILON)
    other_root = lax.rsqrt(other + COSINE_EPSILON)
    cosine = cross * own_root * other_root
    coef_target = -length_f[:, None] * own_root * other_root
    coef_self = length_f[:, None] * cosine * own_root * own_root
    grad_emb = (
        matmul_exact(coef_target, masks) * targets + matmul_exact(coef_self, masks) * embeddings
    )
    grad_full = lax.all_gather(grad_emb, "dim", axis=1, tiled=True)
    spread_rows = member / length_f[:, None]
    grad_stream = lax.dot_general(
        spread_rows,
        grad_full,
        (((0,), (0,)), ((), ())),
        precision=PRECISE,
        preferred_element_type=jnp.float32,
    )
    grad_list = [None] * layer_count
    for layer_pos in reversed(range(layer_count)):
        (
            layer_input,
            layer_weights,
            q_rot,
            k_rot,
            v_low,
            all_keys,
            all_values,
            log_totals,
            attended,
            att_low,
            first_sum,
            normed,
            y_low,
            gate_up,
            hidden,
            second_sum,
        ) = saved[layer_pos]
        w_mix = lax.all_gather(
            mixer_in[layer_pos].astype(jnp.bfloat16), ("dp", "dim"), axis=0, tiled=True
        )
        w_out = lax.all_gather(
            mixer_out[layer_pos].astype(jnp.bfloat16), ("dp", "dim"), axis=0, tiled=True
        )
        w_exp = lax.all_gather(
            expand[layer_pos].astype(jnp.bfloat16), ("dp", "dim"), axis=0, tiled=True
        )
        w_con = lax.all_gather(
            contract[layer_pos].astype(jnp.bfloat16), ("dp", "dim"), axis=0, tiled=True
        )
        w_norm = lax.all_gather(
            norm_params[layer_pos].astype(jnp.bfloat16), ("dp", "dim"), axis=1, tiled=True
        )
        norm_gains = w_norm.astype(jnp.float32)
        grad_second, grad_gain2, grad_bias2 = normalize_back(grad_stream, second_sum, norm_gains[2])
        grad_m_low = grad_second.astype(jnp.bfloat16)
        grad_con = inner_rows(hidden, grad_m_low)
        grad_hidden = inner_cols(grad_m_low, w_con)
        half = gate_up.shape[1] // 2
        gate_part = gate_up[:, 0:half]
        up_part = gate_up[:, half : 2 * half]
        sigmoid_gate = jax.nn.sigmoid(gate_part)
        activated = gate_part * sigmoid_gate
        grad_gate = grad_hidden * up_part * sigmoid_gate * (1.0 + gate_part * (1.0 - sigmoid_gate))
        grad_up = grad_hidden * activated
        grad_both = jnp.concatenate([grad_gate, grad_up], axis=1).astype(jnp.bfloat16)
        grad_exp = inner_rows(y_low, grad_both)
        grad_normed = grad_second + inner_cols(grad_both, w_exp)
        grad_first, grad_gain1, grad_bias1 = normalize_back(grad_normed, first_sum, norm_gains[0])
        grad_a_low = grad_first.astype(jnp.bfloat16)
        grad_out = inner_rows(att_low, grad_a_low)
        grad_attended = inner_cols(grad_a_low, w_out).astype(jnp.bfloat16)
        keys_back, values_back = (
            lax.all_gather(k_rot, "dim", axis=0, tiled=True),
            lax.all_gather(v_low, "dim", axis=0, tiled=True),
        )
        grad_query, grad_key_all, grad_value_all = attend_back(
            q_rot, keys_back, values_back, same_doc, grad_attended, log_totals
        )
        grad_kv = lax.psum_scatter(
            jnp.concatenate([grad_key_all, grad_value_all], axis=1).astype(jnp.bfloat16),
            "dim",
            scatter_dimension=0,
            tiled=True,
        ).astype(jnp.float32)
        grad_mixed = jnp.concatenate(
            [
                rotate_back(grad_query, cosines, sines),
                rotate_back(grad_kv[:, 0:model_width], cosines, sines),
                grad_kv[:, model_width : 2 * model_width],
            ],
            axis=1,
        ).astype(jnp.bfloat16)
        x_low = layer_input.astype(jnp.bfloat16)
        grad_mix = inner_rows(x_low, grad_mixed)
        grad_stream = grad_first + inner_cols(grad_mixed, w_mix)
        grad_norm = jnp.stack([grad_gain1, grad_bias1, grad_gain2, grad_bias2])
        grad_list[layer_pos] = (
            lax.psum_scatter(grad_mix, ("dp", "dim"), scatter_dimension=0, tiled=True),
            lax.psum_scatter(grad_out, ("dp", "dim"), scatter_dimension=0, tiled=True),
            lax.psum_scatter(grad_exp, ("dp", "dim"), scatter_dimension=0, tiled=True),
            lax.psum_scatter(grad_con, ("dp", "dim"), scatter_dimension=0, tiled=True),
            lax.psum_scatter(grad_norm, ("dp", "dim"), scatter_dimension=1, tiled=True),
        )
    total_rows = group_rows * lax.axis_size("dp")
    matrix_rate = 1.0 / math.sqrt(total_rows)
    norm_rate = 0.3 / math.sqrt(total_rows)
    grads = [jnp.stack([grad_list[0][kind]]) for kind in range(5)]
    weights = (mixer_in, mixer_out, expand, contract, norm_params)
    moments = (mixer_in_moment, mixer_out_moment, expand_moment, contract_moment, norm_moment)
    averages = (mixer_in_average, mixer_out_average, expand_average, contract_average, norm_average)
    rates = (matrix_rate, matrix_rate, matrix_rate, matrix_rate, norm_rate)
    results = [
        advance(weights[kind], moments[kind], averages[kind], grads[kind], rates[kind])
        for kind in range(5)
    ]
    return (
        embeddings,
        grad_stream,
        grads[0],
        grads[1],
        grads[2],
        grads[3],
        grads[4],
        results[0][0],
        results[1][0],
        results[2][0],
        results[3][0],
        results[4][0],
        results[0][1],
        results[1][1],
        results[2][1],
        results[3][1],
        results[4][1],
        results[0][2],
        results[1][2],
        results[2][2],
        results[3][2],
        results[4][2],
        results[0][3],
        results[1][3],
        results[2][3],
        results[3][3],
        results[4][3],
    )


NEG=-1e30
BQ=512
ROWS=256
BK=384
F32=jnp.float32
BF=jnp.bfloat16

def nt(a,b): return lax.dot_general(a,b,(((1,),(1,)),((),())),preferred_element_type=F32)
def nn(a,b): return jnp.dot(a,b,preferred_element_type=F32)

def split_turn(both):
    lane=lax.broadcasted_iota(jnp.int32,both.shape,1)
    moved=pltpu.roll(both,64,1)
    return jnp.where(lane<64,both,moved),jnp.where(lane<64,moved,both)

def fill_masks(e0,e1,kaug,q0,q1,rows,pad):
    r=lax.broadcasted_iota(jnp.int32,(rows+pad,128),0)
    l=lax.broadcasted_iota(jnp.int32,(rows+pad,128),1)
    seg=(r>=e0).astype(jnp.int32)+(r>=e1).astype(jnp.int32)
    kaug[:,128:256]=jnp.where((l<3)&(l!=seg),NEG,0.0).astype(BF)
    qm=jnp.where(l==seg,1.0,0.0).astype(BF)[0:rows]
    q0[:,128:256]=qm
    q1[:,128:256]=qm

def key_range(i,e0,e1):
    first=i*BQ
    last=jnp.minimum(first+BQ,e1)-1
    lo=jnp.where(first>=e0,e0,0)
    hi=jnp.where(last>=e0,e1,e0)
    base=(lo//128)*128
    return pl.multiple_of(base,128),(hi-base+BK-1)//BK

def fwd_kernel(ctl,qo,ko,vo,qr,kr,vr,oo,ox,lse,kaug,q0,q1,vt):
    rows=kaug.shape[0]-BK
    half=rows//2
    pos,e0,e1=ctl[0],ctl[1],ctl[2]
    p=pl.program_id(0)
    @pl.when(p==0)
    def _():
        fill_masks(e0,e1,kaug,q0,q1,rows,BK)
        kaug[rows:,0:128]=jnp.zeros((BK,128),BF)
        vt[:,:]=jnp.where(lax.broadcasted_iota(jnp.int32,vt.shape,0)%80>=64,1.0,0.0).astype(BF)
    pick_r=lax.broadcasted_iota(jnp.int32,(16,128),0)
    pick_l=lax.broadcasted_iota(jnp.int32,(16,128),1)
    pick=jnp.where(pick_l//64==pick_r,1.0,0.0).astype(BF)
    q_top=jnp.zeros((16,1),F32)
    k_top=jnp.zeros((16,1),F32)
    lane=lax.broadcasted_iota(jnp.int32,(half,128),1)
    for own,(q,k,v) in ((True,(qo,ko,vo)),(False,(qr,kr,vr))):
        at=pl.multiple_of((pos if own else 1-pos)*half,half)
        scaled=q[...]*jnp.asarray(0.125,BF)
        zero=jnp.zeros_like(scaled)
        q0[pl.ds(at,half),0:128]=jnp.where(lane<64,scaled,zero)
        q1[pl.ds(at,half),0:128]=jnp.where(lane<64,zero,scaled)
        kb=k[...]
        kaug[pl.ds(at,half),0:128]=kb
        q_top=jnp.maximum(q_top,jnp.max(nt(pick,scaled*scaled),axis=1,keepdims=True))
        k_top=jnp.maximum(k_top,jnp.max(nt(pick,kb*kb),axis=1,keepdims=True))
        turned=v[...].T
        vt[0:64,pl.ds(at,half)]=turned[0:64]
        vt[80:144,pl.ds(at,half)]=turned[64:128]
    narrow=jnp.max(q_top*k_top)*1.05<=1600.0
    def qnarrow(i,_):
        r0=pl.multiple_of(i*BQ,BQ)
        base,count=key_range(i,e0,e1)
        qs=(q0[pl.ds(r0,BQ),:],q1[pl.ds(r0,BQ),:])
        def step(j,carry):
            k0=pl.multiple_of(base+j*BK,128)
            kb=kaug[pl.ds(k0,BK),:]
            pt=[jnp.exp(nt(kb,qs[h])).astype(BF) for h in range(2)]
            return tuple(carry[h]+nn(vt[80*h:80*h+80,pl.ds(k0,BK)],pt[h]) for h in range(2))
        init=jnp.zeros((80,BQ),F32)
        res=lax.fori_loop(0,count,step,(init,init))
        outs=[]
        for h in range(2):
            l=jnp.maximum(res[h][64:65],1e-30)
            outs.append(res[h][0:64]/l)
            lse[0,h:h+1,pl.ds(r0,BQ)]=jnp.log(l)
        put(i,jnp.concatenate(outs,axis=0).T.astype(BF))
        return 0
    def qblock(i,_):
        r0=pl.multiple_of(i*BQ,BQ)
        base,count=key_range(i,e0,e1)
        qs=(q0[pl.ds(r0,BQ),:],q1[pl.ds(r0,BQ),:])
        def step(j,carry):
            k0=pl.multiple_of(base+j*BK,128)
            kb=kaug[pl.ds(k0,BK),:]
            scores=[nt(kb,qs[h]) for h in range(2)]
            out=[]
            for h in range(2):
                m,acc=carry[h]
                mn=jnp.maximum(m,jnp.max(scores[h],axis=0,keepdims=True))
                pt=jnp.exp(scores[h]-mn).astype(BF)
                acc=acc*jnp.exp(m-mn)+nn(vt[80*h:80*h+80,pl.ds(k0,BK)],pt)
                out.append((mn,acc))
            return tuple(out)
        init=(jnp.full((1,BQ),-jnp.inf,F32),jnp.zeros((80,BQ),F32))
        res=lax.fori_loop(0,count,step,(init,init))
        outs=[]
        for h in range(2):
            m,acc=res[h]
            l=acc[64:65]
            outs.append(acc[0:64]/l)
            lse[0,h:h+1,pl.ds(r0,BQ)]=m+jnp.log(l)
        ob=jnp.concatenate(outs,axis=0).T.astype(BF)
        put(i,ob)
        return 0
    def put(i,ob):
        local=i*BQ-pos*half
        @pl.when((local>=0)&(local<half))
        def _(): oo[pl.ds(pl.multiple_of(local,BQ),BQ),:]=ob
        @pl.when((local<0)|(local>=half))
        def _(): ox[pl.ds(pl.multiple_of(i*BQ-(1-pos)*half,BQ),BQ),:]=ob
    used=(e1+BQ-1)//BQ
    @pl.when(narrow)
    def _(): lax.fori_loop(0,used,qnarrow,0)
    @pl.when(jnp.logical_not(narrow))
    def _(): lax.fori_loop(0,used,qblock,0)
    def blank(i,_):
        r0=pl.multiple_of(i*BQ,BQ)
        lse[0,:,pl.ds(r0,BQ)]=jnp.zeros((8,BQ),F32)
        put(i,jnp.zeros((BQ,128),BF))
        return 0
    lax.fori_loop(used,rows//BQ,blank,0)

def attend_fwd(ctl,own,recv):
    half,outw=own[0].shape
    pairs=outw//128
    rows=2*half
    width=3*outw
    sp=[pl.BlockSpec((half,128),lambda p,c:(0,p))]*3
    return pl.pallas_call(fwd_kernel,
        grid_spec=pltpu.PrefetchScalarGridSpec(num_scalar_prefetch=1,grid=(pairs,),
          in_specs=sp+sp,
          out_specs=[pl.BlockSpec((half,128),lambda p,c:(0,p))]*2+[pl.BlockSpec((1,8,rows),lambda p,c:(p,0,0))],
          scratch_shapes=[pltpu.VMEM((rows+BK,256),BF),pltpu.VMEM((rows,256),BF),pltpu.VMEM((rows,256),BF),pltpu.VMEM((160,rows+BK),BF)]),
        out_shape=[jax.ShapeDtypeStruct((half,outw),BF)]*2+[jax.ShapeDtypeStruct((pairs,8,rows),F32)],
        compiler_params=pltpu.CompilerParams(vmem_limit_bytes=60<<20,dimension_semantics=("arbitrary",)),
        cost_estimate=pl.CostEstimate(flops=4*rows*rows*64*2*pairs//2,bytes_accessed=10*half*width,transcendentals=rows*rows*pairs),
        name="attend_fwd",
    )(ctl,*own,*recv)

def bwd_kernel(ctl,qo,ko,vo,qr,kr,vr,do_o,do_r,oo,ox,lse,turn,g0,g1,g2,x0,x1,x2,kaug,q0,q1,vs,d0,d1,kt,delta,dk,dv,cos,sin):
    rows=kaug.shape[0]-BK
    half=rows//2
    pos,e0,e1=ctl[0],ctl[1],ctl[2]
    p=pl.program_id(0)
    @pl.when(p==0)
    def _():
        fill_masks(e0,e1,kaug,q0,q1,rows,BK)
        kaug[rows:,0:128]=jnp.zeros((BK,128),BF)
        vs[rows:,:]=jnp.zeros((BK,128),BF)
        kt[:,rows:]=jnp.zeros((128,BK),BF)
        cos[...],sin[...]=split_turn(turn[...])
    lane=lax.broadcasted_iota(jnp.int32,(half,128),1)
    pick_r=lax.broadcasted_iota(jnp.int32,(16,128),0)
    pick_l=lax.broadcasted_iota(jnp.int32,(16,128),1)
    pick=jnp.where(pick_l//64==pick_r,1.0,0.0).astype(BF)
    for own,(q,k,v,d,o) in ((True,(qo,ko,vo,do_o,oo)),(False,(qr,kr,vr,do_r,ox))):
        at=pl.multiple_of((pos if own else 1-pos)*half,half)
        scaled=q[...]*jnp.asarray(0.125,BF)
        zero=jnp.zeros_like(scaled)
        q0[pl.ds(at,half),0:128]=jnp.where(lane<64,scaled,zero)
        q1[pl.ds(at,half),0:128]=jnp.where(lane<64,zero,scaled)
        kb=k[...]
        kaug[pl.ds(at,half),0:128]=kb
        kt[:,pl.ds(at,half)]=kb.T
        vs[pl.ds(at,half),:]=v[...]
        db=d[...]
        d0[pl.ds(at,half),:]=jnp.where(lane<64,db,zero)
        d1[pl.ds(at,half),:]=jnp.where(lane<64,zero,db)
        prod=db.astype(F32)*o[...].astype(F32)
        hi=prod.astype(BF)
        lo=(prod-hi.astype(F32)).astype(BF)
        delta[:,pl.ds(at,half)]=nt(pick,hi)+nt(pick,lo)
    dk[...]=jnp.zeros_like(dk)
    dv[...]=jnp.zeros_like(dv)
    def spread(i,col,val):
        local=i*ROWS-pos*half
        @pl.when((local>=0)&(local<half))
        def _(): (g0,g1,g2)[col][pl.ds(pl.multiple_of(local,ROWS),ROWS),:]=val
        @pl.when((local<0)|(local>=half))
        def _(): (x0,x1,x2)[col][pl.ds(pl.multiple_of(i*ROWS-(1-pos)*half,ROWS),ROWS),:]=val
    def unturn(x,r0):
        ln=lax.broadcasted_iota(jnp.int32,x.shape,1)
        swapped=jnp.where((ln%64)<32,pltpu.roll(x,96,1),pltpu.roll(x,32,1))
        return x*cos[pl.ds(r0,ROWS),:]-swapped*sin[pl.ds(r0,ROWS),:]
    def qblock(i,_):
        r0=pl.multiple_of(i*BQ,BQ)
        base,count=key_range(i,e0,e1)
        qs=(q0[pl.ds(r0,BQ),:],q1[pl.ds(r0,BQ),:])
        ds_=(d0[pl.ds(r0,BQ),:],d1[pl.ds(r0,BQ),:])
        ls=[lse[0,h:h+1,pl.ds(r0,BQ)] for h in range(2)]
        de=[delta[h:h+1,pl.ds(r0,BQ)] for h in range(2)]
        def step(j,carry):
            k0=pl.multiple_of(base+j*BK,128)
            kb=kaug[pl.ds(k0,BK),:]
            vb=vs[pl.ds(k0,BK),:]
            both=range(2)
            st=[nt(kb,qs[h]) for h in both]
            dpt=[nt(vb,ds_[h]) for h in both]
            pt=[jnp.exp(st[h]-ls[h]) for h in both]
            dst=[(pt[h]*(dpt[h]-de[h])).astype(BF) for h in both]
            pb=[pt[h].astype(BF) for h in both]
            dv[pl.ds(k0,BK),:]+=nn(pb[0],ds_[0])+nn(pb[1],ds_[1])
            dk[pl.ds(k0,BK),:]+=nn(dst[0],qs[0][:,0:128])+nn(dst[1],qs[1][:,0:128])
            out=[carry[h]+nn(kt[64*h:64*h+64,pl.ds(k0,BK)],dst[h]) for h in both]
            return tuple(out)
        init=jnp.zeros((64,BQ),F32)
        res=lax.fori_loop(0,count,step,(init,init))
        dq=jnp.concatenate(res,axis=0).T*0.125
        for t in range(BQ//ROWS):
            at=pl.multiple_of(r0+t*ROWS,ROWS)
            spread(i*(BQ//ROWS)+t,0,unturn(dq[t*ROWS:(t+1)*ROWS],at).astype(BF))
        return 0
    used=(e1+BQ-1)//BQ
    lax.fori_loop(0,used,qblock,0)
    def blank(i,_):
        spread(i,0,jnp.zeros((ROWS,128),BF))
        return 0
    lax.fori_loop(used*(BQ//ROWS),rows//ROWS,blank,0)
    def last(i,_):
        r0=pl.multiple_of(i*ROWS,ROWS)
        spread(i,1,unturn(dk[pl.ds(r0,ROWS),:],r0).astype(BF))
        spread(i,2,dv[pl.ds(r0,ROWS),:].astype(BF))
        return 0
    lax.fori_loop(0,rows//ROWS,last,0)

def attend_bwd(ctl,own,recv,d_own,d_recv,o_own,o_oth,lse,turn):
    half,width=own[0].shape
    pairs=width//128
    width=3*width
    rows=2*half
    sp=[pl.BlockSpec((half,128),lambda p,c:(0,p))]*3
    one=pl.BlockSpec((half,128),lambda p,c:(0,p))
    full=pl.BlockSpec((rows,128),lambda p,c:(0,0))
    return pl.pallas_call(bwd_kernel,
        grid_spec=pltpu.PrefetchScalarGridSpec(num_scalar_prefetch=1,grid=(pairs,),
          in_specs=sp+sp+[one]*4+[pl.BlockSpec((1,8,rows),lambda p,c:(p,0,0)),full],
          out_specs=[one]*6,
          scratch_shapes=[pltpu.VMEM((rows+BK,256),BF),pltpu.VMEM((rows,256),BF),pltpu.VMEM((rows,256),BF),
             pltpu.VMEM((rows+BK,128),BF),pltpu.VMEM((rows,128),BF),pltpu.VMEM((rows,128),BF),
             pltpu.VMEM((128,rows+BK),BF),pltpu.VMEM((16,rows),F32),pltpu.VMEM((rows+BK,128),F32),pltpu.VMEM((rows+BK,128),F32),pltpu.VMEM((rows,128),F32),pltpu.VMEM((rows,128),F32)]),
        out_shape=[jax.ShapeDtypeStruct((half,width//3),BF)]*6,
        compiler_params=pltpu.CompilerParams(vmem_limit_bytes=60<<20,dimension_semantics=("arbitrary",)),
        cost_estimate=pl.CostEstimate(flops=10*rows*rows*64*2*pairs//2,bytes_accessed=20*half*width,transcendentals=rows*rows*pairs),
        name="attend_bwd",
    )(ctl,*own,*recv,d_own,d_recv,o_own,o_oth,lse,turn)

BLOCK=256

def spread_mean(x):
    return jnp.mean(x,axis=1,keepdims=True)

def row_docs(ctl,block):
    i=pl.program_id(0)
    r=ctl[0]*(block*pl.num_programs(0))+i*block+lax.broadcasted_iota(jnp.int32,(block,1),0)
    return (r>=ctl[1]).astype(jnp.int32)+(r>=ctl[2]).astype(jnp.int32)

def ffn_fwd_kernel(ctl,ao,ax,tok,w_exp,w_con,w_out,norm,u1,u2,rs,yb,h0,h1,h2,h3,pf,pooled):
    block,width=tok.shape
    hidden=pf.shape[1]//2
    kept=(h0,h1,h2,h3)
    share=width//2
    pos=ctl[0]
    mine=pl.multiple_of(pos*share,share)
    other=pl.multiple_of((1-pos)*share,share)
    f=tok[...].astype(F32)+nn(ao[...],w_out[pl.ds(mine,share),:])+nn(ax[...],w_out[pl.ds(other,share),:])
    cent=f-spread_mean(f)
    scale=lax.rsqrt(spread_mean(cent*cent)+NORM_EPSILON)
    unit=cent*scale
    u1[...]=unit
    rs[:,0:128]=jnp.broadcast_to(scale,(block,128))
    y=unit*norm[0:1,:]+norm[1:2,:]
    ylow=y.astype(BF)
    yb[...]=ylow
    acc=y
    count=hidden//width
    spans=[(slice(c*width,(c+1)*width),slice(hidden+c*width,hidden+(c+1)*width)) for c in range(count)]
    pre=lambda c: (nn(ylow,w_exp[:,spans[c][0]]),nn(ylow,w_exp[:,spans[c][1]]))
    ahead=pre(0)
    for c in range(count):
        gate,up=ahead
        if c+1<count: ahead=pre(c+1)
        gc,uc=spans[c]
        sig=jax.nn.sigmoid(gate)
        act=gate*sig
        low=(act*up).astype(BF)
        kept[c][...]=low
        pf[:,gc]=(up*(sig+act*(1.0-sig))).astype(BF)
        pf[:,uc]=act.astype(BF)
        acc=acc+nn(low,w_con[:,gc])
    cent=acc-spread_mean(acc)
    scale=lax.rsqrt(spread_mean(cent*cent)+NORM_EPSILON)
    unit=cent*scale
    u2[...]=unit
    rs[:,128:256]=jnp.broadcast_to(scale,(block,128))
    out=unit*norm[2:3,:]+norm[3:4,:]
    docs=row_docs(ctl,block)
    @pl.when(pl.program_id(0)==0)
    def _(): pooled[...]=jnp.zeros_like(pooled)
    for d in range(2):
        pooled[d:d+1,:]+=jnp.sum(jnp.where(docs==d,out,0.0),axis=0,keepdims=True)

def ffn_fwd(ctl,ao,ax,tok,bundle,norm,hidden):
    rows,width=tok.shape
    row=lambda n: pl.BlockSpec((BLOCK,n),lambda i,c:(i,0))
    held=lambda n,at: pl.BlockSpec((width,n),lambda i,c:(0,at//n),pipeline_mode=pl.Buffered(1))
    flat=pl.BlockSpec((8,width),lambda i,c:(0,0))
    return pl.pallas_call(ffn_fwd_kernel,
        grid_spec=pltpu.PrefetchScalarGridSpec(num_scalar_prefetch=1,grid=(rows//BLOCK,),
          in_specs=[row(width//2),row(width//2),row(width),held(2*hidden,0),held(hidden,2*hidden),held(width,3*hidden),flat],
          out_specs=[row(width),row(width),row(256),*[row(width)]*5,row(2*hidden),flat]),
        out_shape=[jax.ShapeDtypeStruct((rows,width),F32),jax.ShapeDtypeStruct((rows,width),F32),jax.ShapeDtypeStruct((rows,256),F32),
          *[jax.ShapeDtypeStruct((rows,width),BF)]*5,jax.ShapeDtypeStruct((rows,2*hidden),BF),
          jax.ShapeDtypeStruct((8,width),F32)],
        compiler_params=pltpu.CompilerParams(vmem_limit_bytes=60<<20,dimension_semantics=("arbitrary",)),
        cost_estimate=pl.CostEstimate(flops=2*rows*width*(width+3*hidden),bytes_accessed=rows*(width*14+hidden*6)+2*width*(width+3*hidden),transcendentals=rows*hidden),
        name="ffn_fwd",
    )(ctl,ao,ax,tok,bundle,bundle,bundle,norm)

def loss_grad(pool,targets,len0,len1):
    width=pool.shape[1]
    docs=lax.broadcasted_iota(jnp.int32,pool.shape,0)
    length=jnp.where(docs==0,len0,len1)
    emb=pool/length
    lane=lax.broadcasted_iota(jnp.int32,pool.shape,1)
    d_target=jnp.zeros_like(pool)
    d_self=jnp.zeros_like(pool)
    for cut in (width//12,width//6,width//3,2*width//3,width):
        keep=lane<cut
        total=lambda v: jnp.sum(jnp.where(keep,v,0.0),axis=1,keepdims=True)
        own_root=lax.rsqrt(total(emb*emb)+COSINE_EPSILON)
        other_root=lax.rsqrt(total(targets*targets)+COSINE_EPSILON)
        cosine=total(emb*targets)*own_root*other_root
        d_target=d_target+jnp.where(keep,own_root*other_root,0.0)
        d_self=d_self+jnp.where(keep,cosine*own_root*own_root,0.0)
    d_emb=length*(d_self*emb-d_target*targets)
    return emb,d_emb/length

def ffn_bwd_kernel(ctl,flen,pool_a,pool_b,targets,u1,u2,rs,pf,w_exp,w_con,w_out,norm,
                   emb,mb,ub,df,ab,do,dx,gn,de):
    block,width=u1.shape
    hidden=pf.shape[1]//2
    share=width//2
    pos=ctl[0]
    @pl.when(pl.program_id(0)==0)
    def _():
        e,d=loss_grad(pool_a[...]+pool_b[...],targets[...],flen[0],flen[1])
        emb[...]=e
        de[...]=d
        gn[...]=jnp.zeros_like(gn)
    docs=row_docs(ctl,block)
    dout=jnp.where(docs==0,de[0:1,:],jnp.where(docs==1,de[1:2,:],0.0))
    unit=u2[...]
    gn[2:3,:]+=jnp.sum(dout*unit,axis=0,keepdims=True)
    gn[3:4,:]+=jnp.sum(dout,axis=0,keepdims=True)
    gu=dout*norm[2:3,:]
    dg=rs[:,128:129]*(gu-spread_mean(gu)-unit*spread_mean(gu*unit))
    mlow=dg.astype(BF)
    mb[...]=mlow
    acc=dg
    for c in range(hidden//width):
        gc=slice(c*width,(c+1)*width)
        uc=slice(hidden+c*width,hidden+(c+1)*width)
        dh=nt(mlow,w_con[:,gc])
        dgate=(dh*pf[:,gc].astype(F32)).astype(BF)
        dup=(dh*pf[:,uc].astype(F32)).astype(BF)
        ub[:,gc]=dgate
        ub[:,uc]=dup
        acc=acc+nt(dgate,w_exp[:,gc])+nt(dup,w_exp[:,uc])
    unit=u1[...]
    gn[0:1,:]+=jnp.sum(acc*unit,axis=0,keepdims=True)
    gn[1:2,:]+=jnp.sum(acc,axis=0,keepdims=True)
    gu=acc*norm[0:1,:]
    dfirst=rs[:,0:1]*(gu-spread_mean(gu)-unit*spread_mean(gu*unit))
    df[...]=dfirst
    alow=dfirst.astype(BF)
    ab[...]=alow
    do[...]=nt(alow,w_out[pl.ds(pl.multiple_of(pos*share,share),share),:]).astype(BF)
    dx[...]=nt(alow,w_out[pl.ds(pl.multiple_of((1-pos)*share,share),share),:]).astype(BF)

def ffn_bwd(ctl,flen,pool_a,pool_b,targets,u1,u2,rs,pf,bundle,norm):
    rows,width=u1.shape
    hidden=pf.shape[1]//2
    row=lambda n: pl.BlockSpec((BLOCK,n),lambda i,c,l:(i,0))
    held=lambda n,at: pl.BlockSpec((width,n),lambda i,c,l:(0,at//n),pipeline_mode=pl.Buffered(1))
    flat=pl.BlockSpec((8,width),lambda i,c,l:(0,0))
    sds=jax.ShapeDtypeStruct
    return pl.pallas_call(ffn_bwd_kernel,
        grid_spec=pltpu.PrefetchScalarGridSpec(num_scalar_prefetch=2,grid=(rows//BLOCK,),
          in_specs=[flat,flat,flat,row(width),row(width),row(256),row(2*hidden),held(2*hidden,0),held(hidden,2*hidden),held(width,3*hidden),flat],
          out_specs=[flat,row(width),row(2*hidden),row(width),row(width),row(width//2),row(width//2),flat],
          scratch_shapes=[pltpu.VMEM((8,width),F32)]),
        out_shape=[sds((8,width),F32),sds((rows,width),BF),sds((rows,2*hidden),BF),sds((rows,width),F32),sds((rows,width),BF),
          sds((rows,width//2),BF),sds((rows,width//2),BF),sds((8,width),F32)],
        compiler_params=pltpu.CompilerParams(vmem_limit_bytes=60<<20,dimension_semantics=("arbitrary",)),
        cost_estimate=pl.CostEstimate(flops=2*rows*width*(width+3*hidden),bytes_accessed=rows*(width*18+hidden*8)+2*width*(width+3*hidden),transcendentals=0),
        name="ffn_bwd",
    )(ctl,flen,pool_a,pool_b,targets,u1,u2,rs,pf,bundle,bundle,bundle,norm)

MESH=pl.DeviceIdType.MESH

def place():
    dp=lax.axis_index("dp")
    core=lax.axis_index("dim")
    return dp//4,(dp//2)%2,dp%2,core

def meet(z,y,x,core):
    chip=lambda a,b,c: a*4+b*2+c
    peers=[(chip(z,y,x),1-core),(chip(z,y,1-x),core),(chip(z,1-y,x),core)]
    peers+=[(chip(lax.rem(z+k,4),y,x),core) for k in (1,2,3)]
    barrier=pltpu.get_barrier_semaphore()
    for peer in peers:
        pl.semaphore_signal(barrier,inc=1,device_id=peer,device_id_type=MESH)
    pl.semaphore_wait(barrier,len(peers))
    return peers

def lanes_of(cols):
    tiles=cols//128
    widths=[tiles-tiles//4*3]+[tiles//4]*3
    widths=[widths[0],widths[2],widths[1],widths[3]]
    widths=[5,5,4,4] if tiles==18 else widths
    out=[]
    at=0
    for n,w in enumerate(widths):
        out.append((at*128,w*128,n%2==0))
        at+=w
    return out

def send(src,dst,sems,n,k,peer):
    copy=pltpu.make_async_remote_copy(src_ref=src,dst_ref=dst,send_sem=sems[0].at[n,k],recv_sem=sems[1].at[n,k],device_id=peer,device_id_type=MESH)
    copy.start()
    return copy

def gather_kernel(w,out,low,local,s_sem,r_sem):
    z,y,x,core=place()
    low[...]=w[...].astype(BF)
    keep=pltpu.make_async_copy(low,out.at[z,y,x,core],local)
    keep.start()
    pair,xn,yn,z1,z2,z3=meet(z,y,x,core)
    sems=(s_sem,r_sem)
    lanes=lanes_of(w.shape[1])
    every=[]
    def go(n,k,peer,*index,src=None):
        at,width,_=lanes[n]
        dst=out.at[(*index,slice(None),pl.ds(at,width))]
        if src is None: src=dst
        copy=send(src,dst,sems,n,k,peer)
        every.append(copy)
        return copy
    whole=slice(None)
    first=[]
    for n,(at,width,_) in enumerate(lanes):
        piece=low.at[:,pl.ds(at,width)]
        first.append([go(n,k,peer,z,y,x,core,src=piece) for k,peer in enumerate((z1,z2,z3))])
    keep.wait()
    second=[]
    for n,(_,_,flip) in enumerate(lanes):
        for copy in first[n]: copy.wait_recv()
        second.append(go(n,3,yn if flip else xn,whole,y,x,core))
        go(n,5,pair,whole,y,x,core)
    third=[]
    for n,(_,_,flip) in enumerate(lanes):
        second[n].wait_recv()
        if flip:
            third.append(go(n,4,xn,whole,whole,x,core))
            go(n,6,pair,whole,1-y,x,core)
        else:
            third.append(go(n,4,yn,whole,y,whole,core))
            go(n,6,pair,whole,y,1-x,core)
    for n,(_,_,flip) in enumerate(lanes):
        third[n].wait_recv()
        if flip: go(n,7,pair,whole,whole,1-x,core)
        else: go(n,7,pair,whole,1-y,whole,core)
    done=set(id(c) for c in second+third+[c for f in first for c in f])
    for copy in every:
        copy.wait_send()
        if id(copy) not in done: copy.wait_recv()

def ring_gather(w):
    share,cols=w.shape
    out=pl.pallas_call(gather_kernel,
        in_specs=[pl.BlockSpec(memory_space=pltpu.VMEM)],
        out_specs=pl.BlockSpec(memory_space=pl.ANY),
        scratch_shapes=[pltpu.VMEM((share,cols),BF),pltpu.SemaphoreType.DMA,pltpu.SemaphoreType.DMA((4,8)),pltpu.SemaphoreType.DMA((4,8))],
        out_shape=jax.ShapeDtypeStruct((4,2,2,2,share,cols),BF),
        compiler_params=pltpu.CompilerParams(collective_id=1,has_side_effects=True,vmem_limit_bytes=60<<20),
        cost_estimate=pl.CostEstimate(flops=0,bytes_accessed=64*share*cols*20,transcendentals=0),
        name="comm_gather",
    )(w)
    return out.reshape(32*share,cols)

def scatter_kernel(g,out,gl,r0,b1,k1,r1,b2,k2,r2,b3,k3,r3,local,s_sem,r_sem):
    z,y,x,core=place()
    keep=pltpu.make_async_copy(g.at[:,core],gl,local)
    keep.start()
    pair,xn,yn,z1,z2,z3=meet(z,y,x,core)
    sems=(s_sem,r_sem)
    lanes=lanes_of(out.shape[1])
    span=[pl.ds(at,width) for at,width,_ in lanes]
    every=[]
    def go(n,k,peer,src,dst):
        copy=send(src,dst,sems,n,k,peer)
        every.append(copy)
        return copy
    n_lanes=range(len(lanes))
    zero=[go(n,0,pair,g.at[:,1-core,:,span[n]],r0.at[:,:,span[n]]) for n in n_lanes]
    def split1(n,iz,j,side):
        row=iz*4+(j*2+side if lanes[n][2] else side*2+j)
        c=span[n]
        return gl[row,:,c].astype(F32)+r0[row,:,c].astype(F32)
    one=[]
    keep.wait()
    for n in n_lanes:
        flip=lanes[n][2]
        side=x if flip else y
        zero[n].wait_recv()
        for iz in range(4):
            for j in range(2):
                b1[iz,j,:,span[n]]=split1(n,iz,j,1-side).astype(BF)
        one.append(go(n,1,xn if flip else yn,b1.at[:,:,:,span[n]],r1.at[:,:,:,span[n]]))
        for iz in range(4):
            for j in range(2):
                k1[iz,j,:,span[n]]=split1(n,iz,j,side)
    two=[]
    for n in n_lanes:
        flip=lanes[n][2]
        side=y if flip else x
        c=span[n]
        one[n].wait_recv()
        for iz in range(4):
            b2[iz,:,c]=(k1[iz,1-side,:,c]+r1[iz,1-side,:,c].astype(F32)).astype(BF)
        two.append(go(n,2,yn if flip else xn,b2.at[:,:,c],r2.at[:,:,c]))
        for iz in range(4):
            k2[iz,:,c]=k1[iz,side,:,c]+r1[iz,side,:,c].astype(F32)
    three=[]
    for n in n_lanes:
        c=span[n]
        two[n].wait_recv()
        for k in (1,2,3):
            to=lax.rem(z+k,4)
            b3[k-1,:,c]=(k2[to,:,c]+r2[to,:,c].astype(F32)).astype(BF)
        three.append([go(n,2+k,(z1,z2,z3)[k-1],b3.at[k-1,:,c],r3.at[k-1,:,c]) for k in (1,2,3)])
        k3[:,c]=k2[z,:,c]+r2[z,:,c].astype(F32)
    for n in n_lanes:
        c=span[n]
        for copy in three[n]: copy.wait_recv()
        out[:,c]=k3[:,c]+r3[0,:,c].astype(F32)+r3[1,:,c].astype(F32)+r3[2,:,c].astype(F32)
    for copy in every: copy.wait_send()

def ring_scatter(g):
    rows,cols=g.shape
    share=rows//32
    v=lambda *s: pltpu.VMEM((*s,share,cols),BF)
    f=lambda *s: pltpu.VMEM((*s,share,cols),F32)
    return pl.pallas_call(scatter_kernel,
        in_specs=[pl.BlockSpec(memory_space=pl.ANY)],
        out_specs=pl.BlockSpec(memory_space=pltpu.VMEM),
        scratch_shapes=[v(16),v(16),v(4,2),f(4,2),v(4,2),v(4),f(4),v(4),v(3),f(),v(3),pltpu.SemaphoreType.DMA,pltpu.SemaphoreType.DMA((4,6)),pltpu.SemaphoreType.DMA((4,6))],
        out_shape=jax.ShapeDtypeStruct((share,cols),F32),
        compiler_params=pltpu.CompilerParams(collective_id=2,has_side_effects=True,vmem_limit_bytes=60<<20),
        cost_estimate=pl.CostEstimate(flops=0,bytes_accessed=64*share*cols*20,transcendentals=0),
        name="comm_scatter",
    )(g.reshape(16,2,share,cols))

def selector(forward):
    r=lax.broadcasted_iota(jnp.int32,(512,512),0)
    c=lax.broadcasted_iota(jnp.int32,(512,512),1)
    a,b=(r,c) if forward else (c,r)
    return jnp.where(a==4*(b%128)+b//128,1.0,0.0).astype(BF)

def bundle_kernel(exp,con,out,norm,bundle,tiles):
    share,width=out.shape
    hidden=exp.shape[1]//2
    pick=selector(True)
    for b in range(exp.shape[1]//512):
        half,at=divmod(b*512,hidden)
        y=nn(exp[:,b*512:(b+1)*512].astype(BF),pick).astype(BF)
        for j in range(4):
            to=half*hidden+j*width+at//4
            bundle[:,to:to+128]=y[:,j*128:(j+1)*128]
    for t in range(width//128):
        tiles[t]=con[:,t*128:(t+1)*128]
        for j in range(4):
            to=2*hidden+j*width+t*128
            bundle[:,to:to+128]=tiles[t,pl.ds(j,share,stride=4),:].astype(BF)
    bundle[:,3*hidden:3*hidden+width]=out[...].astype(BF)
    flat=jnp.concatenate([norm[...],jnp.zeros((4,128-share),F32)],1)
    bundle[:,3*hidden+width:]=jnp.concatenate([flat,jnp.zeros((share-4,128),F32)],0).astype(BF)

def make_bundle(exp,con,out,norm):
    share,width=out.shape
    total=exp.shape[1]+4*width+width+128
    return pl.pallas_call(bundle_kernel,
        out_shape=jax.ShapeDtypeStruct((share,total),BF),
        scratch_shapes=[pltpu.VMEM((width//128,4*share,128),F32)],
        compiler_params=pltpu.CompilerParams(vmem_limit_bytes=60<<20),
        cost_estimate=pl.CostEstimate(flops=2*share*512*exp.shape[1],bytes_accessed=6*share*total,transcendentals=0),
        name="make_bundle",
    )(exp,con,out,norm)

def update_kernel(rates,sums,*refs):
    ins,outs,tiles=refs[:12],refs[12:32],refs[32]
    exp_w,con_w,out_w,norm_w=(ins[3*k:3*k+3] for k in range(4))
    share,width=out_w[0].shape
    hidden=exp_w[0].shape[1]//2
    def step(kind,index,g,rate):
        w,m,a=(ref[index] for ref in ins[3*kind:3*kind+3])
        grad,nxt,mom,avg,low=outs[5*kind:5*kind+5]
        mn=MOMENTUM*m+g
        wn=w-rate*(g+MOMENTUM*mn)
        grad[index]=g
        nxt[index]=wn
        mom[index]=mn
        avg[index]=AVERAGE_DECAY*a+(1.0-AVERAGE_DECAY)*wn
        low[index]=wn.astype(BF)
    pick=selector(False)
    for b in range(2*hidden//512):
        half,at=divmod(b*512,hidden)
        z=jnp.concatenate([sums[:,half*hidden+j*width+at//4:half*hidden+j*width+at//4+128] for j in range(4)],1)
        step(0,(slice(None),slice(b*512,(b+1)*512)),nn(z,pick),rates[0])
    for t in range(width//128):
        for j in range(4):
            at=2*hidden+j*width+t*128
            tiles[t,pl.ds(j,share,stride=4),:]=sums[:,at:at+128].astype(F32)
        step(1,(slice(None),slice(t*128,(t+1)*128)),tiles[t],rates[0])
    step(2,(slice(None),slice(None)),sums[:,3*hidden:3*hidden+width].astype(F32),rates[0])
    step(3,(slice(None),slice(None)),sums[0:8,3*hidden+width:].astype(F32)[0:4,0:share],rates[1])

def update(sums,rates,params):
    sds=jax.ShapeDtypeStruct
    shapes=[]
    for w,_,_ in params:
        shapes+=[sds(w.shape,F32)]*4+[sds(w.shape,BF)]
    flat=[x for p in params for x in p]
    import_vmem=pl.BlockSpec(memory_space=pltpu.VMEM)
    outs=pl.pallas_call(lambda *refs: update_kernel(rates,*refs),
        in_specs=[import_vmem]*13,
        out_specs=[import_vmem]*20,
        out_shape=shapes,
        scratch_shapes=[pltpu.VMEM((params[2][0].shape[1]//128,params[1][0].shape[0],128),F32)],
        compiler_params=pltpu.CompilerParams(vmem_limit_bytes=60<<20),
        cost_estimate=pl.CostEstimate(flops=2*24*512*6144,bytes_accessed=12<<20,transcendentals=0),
        name="update",
    )(sums,*flat)
    return [outs[5*k:5*k+5] for k in range(4)]

def tail_kernel(ctl,x,qo,ko,vo,qr,kr,vr,w,df,tok,gm,acc):
    pos=ctl[0]
    i=pl.program_id(0)
    width=x.shape[1]
    turned=x[...].T
    total=df[...]
    @pl.when(i==0)
    def _(): acc[...]=jnp.zeros_like(acc)
    for s,(mine,theirs) in enumerate(((qo,qr),(ko,kr),(vo,vr))):
        a=mine[...]
        b=theirs[...]
        grad=jnp.concatenate([jnp.where(pos==0,a,b),jnp.where(pos==0,b,a)],1)
        cols=slice(s*width,(s+1)*width)
        total=total+nt(grad,w[:,cols])
        acc[:,cols]+=nn(turned,grad)
    tok[...]=total
    @pl.when(i==pl.num_programs(0)-1)
    def _(): gm[...]=acc[...].astype(BF)

def tail(ctl,x,own,recv,w,df):
    rows,width=x.shape
    cols=w.shape[1]
    row=lambda n: pl.BlockSpec((512,n),lambda i,c:(i,0))
    held=pl.BlockSpec((width,cols),lambda i,c:(0,0),pipeline_mode=pl.Buffered(1))
    return pl.pallas_call(tail_kernel,
        grid_spec=pltpu.PrefetchScalarGridSpec(num_scalar_prefetch=1,grid=(rows//512,),
          in_specs=[row(width)]+[row(width//2)]*6+[held,row(width)],
          out_specs=[row(width),pl.BlockSpec((width,cols),lambda i,c:(0,0))],
          scratch_shapes=[pltpu.VMEM((width,cols),F32)]),
        out_shape=[jax.ShapeDtypeStruct((rows,width),F32),jax.ShapeDtypeStruct((width,cols),BF)],
        compiler_params=pltpu.CompilerParams(vmem_limit_bytes=60<<20,dimension_semantics=("arbitrary",)),
        cost_estimate=pl.CostEstimate(flops=4*rows*width*cols,bytes_accessed=rows*width*16+8*width*cols,transcendentals=0),
        name="tail",
    )(ctl,x,*own,*recv,w,df)

def mix_kernel(rotated,ctl,x,w,turn,own,oth):
    pos=ctl[0]
    width=x.shape[1]
    share=width//2
    c,s=split_turn(turn[...])
    lane=lax.broadcasted_iota(jnp.int32,c.shape,1)
    first=(lane%64)<32
    y=nn(x[...],w[...])
    tiles=[]
    for t in range(width//128):
        z=y[:,t*128:(t+1)*128]
        if rotated:
            swapped=jnp.where(first,pltpu.roll(z,96,1),pltpu.roll(z,32,1))
            z=z*c+swapped*s
        tiles.append(z.astype(BF))
    count=share//128
    for t in range(count):
        cols=slice(t*128,(t+1)*128)
        own[:,cols]=jnp.where(pos==0,tiles[t],tiles[count+t])
        oth[:,cols]=jnp.where(pos==0,tiles[count+t],tiles[t])

def mix(ctl,x,w,turn,part):
    rows,width=x.shape
    block=512
    row=lambda n: pl.BlockSpec((block,n),lambda i,c:(i,0))
    angle=pl.BlockSpec((block,128),lambda i,c:(c[0]*(rows//block)+i,0))
    return pl.pallas_call(functools.partial(mix_kernel,part<2),
        grid_spec=pltpu.PrefetchScalarGridSpec(num_scalar_prefetch=1,grid=(rows//block,),
          in_specs=[row(width),pl.BlockSpec((width,width),lambda i,c:(0,part)),angle],
          out_specs=[row(width//2)]*2),
        out_shape=[jax.ShapeDtypeStruct((rows,width//2),BF)]*2,
        compiler_params=pltpu.CompilerParams(vmem_limit_bytes=60<<20,dimension_semantics=("arbitrary",)),
        cost_estimate=pl.CostEstimate(flops=2*rows*width*width,bytes_accessed=2*(2*rows*width+width*width),transcendentals=0),
        name="mix",
    )(ctl,x,w,turn)

def swap_cores(x):
    return lax.ppermute(x,"dim",[(0,1),(1,0)])

def join(pos,own,recv,axis=1):
    return jnp.where(pos==0,jnp.concatenate([own,recv],axis),jnp.concatenate([recv,own],axis))

def body(tokens,doc_lengths,pair_index,target_bank,mixer_in,mixer_out,expand,contract,norm_params,*rest):
    slices=lax.axis_size("dim")
    if slices!=2 or lax.axis_size("dp")!=16 or doc_lengths.shape[1]!=2:
        return body_general(tokens,doc_lengths,pair_index,target_bank,mixer_in,mixer_out,expand,contract,norm_params,*rest)
    (mixer_in_moment,mixer_out_moment,expand_moment,contract_moment,norm_moment,
     mixer_in_average,mixer_out_average,expand_average,contract_average,norm_average)=rest
    local_rows,model_width=tokens.shape
    group_rows=local_rows*slices
    pos=lax.axis_index("dim")
    doc_count=2
    w_mix=ring_gather(mixer_in[0])
    share_rows=mixer_out.shape[1]
    per=contract.shape[1]//share_rows
    count=model_width//share_rows
    hidden_width=contract.shape[1]*count
    bundle=make_bundle(expand[0],contract[0],mixer_out[0],norm_params[0])
    bundle=lax.all_gather(bundle,("dp","dim"),axis=0,tiled=True)
    at1=2*hidden_width
    at2=at1+per*model_width
    at3=at2+model_width
    w_norm=bundle[:,at3:].reshape(count,share_rows,128)[:,0:4,0:share_rows].transpose(1,0,2).reshape(4,model_width)
    lengths=doc_lengths[0]
    e0=lengths[0]
    e1=lengths[0]+lengths[1]
    ctl=jnp.stack([pos.astype(jnp.int32),e0,e1])
    ids=jnp.arange(group_rows,dtype=jnp.int32)
    seg=(ids>=e0).astype(jnp.int32)+(ids>=e1).astype(jnp.int32)
    begin=jnp.where(seg==0,0,jnp.where(seg==1,e0,e1))
    lane=jnp.arange(128,dtype=jnp.int32)
    frequency=jnp.power(1000.0,-(2*(lane%32)).astype(F32)/HEAD)
    angles=(ids-begin).astype(F32)[:,None]*frequency[None,:]
    shift=jnp.where(lane<64,0.0,jnp.where(lane<96,0.5*math.pi,-0.5*math.pi)).astype(F32)
    turn=jnp.cos(angles+shift[None,:])
    mixed=[mix(ctl,tokens,w_mix,turn,part) for part in range(3)]
    own=[m[0] for m in mixed]
    recv=[swap_cores(m[1]) for m in mixed]
    pick=(pair_index[:,None]==jnp.arange(target_bank.shape[0],dtype=jnp.int32)[None,:]).astype(BF)
    some=matmul(pick,target_bank)
    targets=jnp.pad(join(pos,some,swap_cores(some)),((0,6),(0,0)))
    o_own,o_oth,lse=attend_fwd(ctl,own,recv)
    o_recv=swap_cores(o_oth)
    norm_gains=jnp.pad(w_norm.astype(F32),((0,4),(0,0)))
    u1,u2,rs,y_low,*hidden,factors,pooled=ffn_fwd(ctl,o_own,o_recv,tokens,bundle,norm_gains,hidden_width)
    embeds,grad_m_low,grad_both,grad_first,grad_a_low,d_own,d_oth,grad_norm=ffn_bwd(
        ctl,lengths.astype(F32),pooled,swap_cores(pooled),targets,u1,u2,rs,factors,bundle,norm_gains)
    share=model_width//2
    embeddings=lax.dynamic_slice(embeds,(0,pos*share),(doc_count,share))
    d_recv=swap_cores(d_oth)
    grad_exp=inner_rows(y_low,grad_both)
    grad_con=[inner_rows(h,grad_m_low).astype(BF) for h in hidden]
    grad_out=join(pos,inner_rows(o_own,grad_a_low),inner_rows(o_recv,grad_a_low),0)
    grad_norm=grad_norm[0:4].reshape(4,count,share_rows).transpose(1,0,2)
    grad_norm=jnp.pad(grad_norm,((0,0),(0,share_rows-4),(0,128-share_rows))).reshape(model_width,128)
    terms=jnp.concatenate([grad_exp.astype(BF),*grad_con,grad_out.astype(BF),grad_norm.astype(BF)],1)
    terms,d_own,d_recv=lax.optimization_barrier((terms,d_own,d_recv))
    sums=lax.psum_scatter(terms,("dp","dim"),scatter_dimension=0,tiled=True)
    backs=attend_bwd(ctl,own,recv,d_own,d_recv,o_own,o_oth,lse,turn)
    token_grads,grad_mix=tail(ctl,tokens,backs[0:3],[swap_cores(g) for g in backs[3:6]],w_mix,grad_first)
    total_rows=group_rows*lax.axis_size("dp")
    matrix_rate=1.0/math.sqrt(total_rows)
    norm_rate=0.3/math.sqrt(total_rows)
    new_exp,new_con,new_out,new_norm=update(sums,(matrix_rate,norm_rate),[
        (expand[0],expand_moment[0],expand_average[0]),(contract[0],contract_moment[0],contract_average[0]),
        (mixer_out[0],mixer_out_moment[0],mixer_out_average[0]),(norm_params[0],norm_moment[0],norm_average[0])])
    sum_mix=ring_scatter(grad_mix)
    nxt,mom,avg,low=advance(mixer_in[0],mixer_in_moment[0],mixer_in_average[0],sum_mix,matrix_rate)
    results=[[sum_mix,nxt,mom,avg,low],new_out,new_exp,new_con,new_norm]
    return (embeddings,token_grads,*[results[k][f][None] for f in range(5) for k in range(5)])

def solution(mesh):
    placed = (
        P(("dp", "dim"), None),
        P("dp", None),
        P("dp"),
        P(None, "dim"),
        P(None, ("dp", "dim"), None),
        P(None, ("dp", "dim"), None),
        P(None, ("dp", "dim"), None),
        P(None, ("dp", "dim"), None),
        P(None, None, ("dp", "dim")),
        P(None, ("dp", "dim"), None),
        P(None, ("dp", "dim"), None),
        P(None, ("dp", "dim"), None),
        P(None, ("dp", "dim"), None),
        P(None, None, ("dp", "dim")),
        P(None, ("dp", "dim"), None),
        P(None, ("dp", "dim"), None),
        P(None, ("dp", "dim"), None),
        P(None, ("dp", "dim"), None),
        P(None, None, ("dp", "dim")),
    )
    return jax.shard_map(
        body,
        mesh=mesh,
        in_specs=placed,
        out_specs=(
            P("dp", "dim"),
            P(("dp", "dim"), None),
            P(None, ("dp", "dim"), None),
            P(None, ("dp", "dim"), None),
            P(None, ("dp", "dim"), None),
            P(None, ("dp", "dim"), None),
            P(None, None, ("dp", "dim")),
            P(None, ("dp", "dim"), None),
            P(None, ("dp", "dim"), None),
            P(None, ("dp", "dim"), None),
            P(None, ("dp", "dim"), None),
            P(None, None, ("dp", "dim")),
            P(None, ("dp", "dim"), None),
            P(None, ("dp", "dim"), None),
            P(None, ("dp", "dim"), None),
            P(None, ("dp", "dim"), None),
            P(None, None, ("dp", "dim")),
            P(None, ("dp", "dim"), None),
            P(None, ("dp", "dim"), None),
            P(None, ("dp", "dim"), None),
            P(None, ("dp", "dim"), None),
            P(None, None, ("dp", "dim")),
            P(None, ("dp", "dim"), None),
            P(None, ("dp", "dim"), None),
            P(None, ("dp", "dim"), None),
            P(None, ("dp", "dim"), None),
            P(None, None, ("dp", "dim")),
        ),
        check_vma=False,
    )
```

```python
import functools
import math

import jax
import jax.numpy as jnp
from jax import lax
from jax.experimental import pallas as pl
from jax.experimental.pallas import tpu as pltpu
from jax.sharding import PartitionSpec as P

HEAD = 64


NORM_EPSILON = 1e-05
COSINE_EPSILON = 1e-06
MOMENTUM = 0.5
AVERAGE_DECAY = 0.5
PRECISE = lax.Precision.HIGHEST
MASKED = -1e30


def matmul(left_op, right_op):
    return jnp.dot(left_op, right_op, preferred_element_type=jnp.float32)


def matmul_exact(left_op, right_op):
    return jnp.dot(left_op, right_op, precision=PRECISE, preferred_element_type=jnp.float32)


def inner_rows(left_op, right_op):
    return lax.dot_general(
        left_op, right_op, (((0,), (0,)), ((), ())), preferred_element_type=jnp.float32
    )


def inner_cols(left_op, right_op):
    return lax.dot_general(
        left_op, right_op, (((1,), (1,)), ((), ())), preferred_element_type=jnp.float32
    )


def rotate(values, cosines, sines):
    row_count = values.shape[0]
    shaped = values.reshape(row_count, -1, 2, HEAD // 2)
    former = shaped[:, :, 0, :]
    latter = shaped[:, :, 1, :]
    cosine_b = cosines[:, None, :]
    sine_b = sines[:, None, :]
    turned = jnp.stack(
        [former * cosine_b - latter * sine_b, latter * cosine_b + former * sine_b], axis=2
    )
    return turned.reshape(values.shape)


def rotate_back(grads_in, cosines, sines):
    row_count = grads_in.shape[0]
    shaped = grads_in.reshape(row_count, -1, 2, HEAD // 2)
    former = shaped[:, :, 0, :]
    latter = shaped[:, :, 1, :]
    cosine_b = cosines[:, None, :]
    sine_b = sines[:, None, :]
    turned = jnp.stack(
        [former * cosine_b + latter * sine_b, latter * cosine_b - former * sine_b], axis=2
    )
    return turned.reshape(grads_in.shape)


def normalize(summed, gain_vec, bias_vec):
    centred = summed - jnp.mean(summed, axis=1, keepdims=True)
    scaling = lax.rsqrt(jnp.mean(centred * centred, axis=1, keepdims=True) + NORM_EPSILON)
    return centred * scaling * gain_vec + bias_vec


def normalize_back(grad_in, summed, gain_vec):
    centred = summed - jnp.mean(summed, axis=1, keepdims=True)
    scaling = lax.rsqrt(jnp.mean(centred * centred, axis=1, keepdims=True) + NORM_EPSILON)
    unit = centred * scaling
    grad_unit = grad_in * gain_vec
    grad_sum = scaling * (
        grad_unit
        - jnp.mean(grad_unit, axis=1, keepdims=True)
        - unit * jnp.mean(grad_unit * unit, axis=1, keepdims=True)
    )
    return (grad_sum, jnp.sum(grad_in * unit, axis=0), jnp.sum(grad_in, axis=0))


def flatten(stacked):
    return stacked.transpose(1, 0, 2).reshape(stacked.shape[1], -1)


def attend(q_rot, all_keys, all_values, same_doc):
    head_count = q_rot.shape[1] // HEAD

    def one_head(head_pos):
        offset = head_pos * HEAD
        query_part = lax.dynamic_slice_in_dim(q_rot, offset, HEAD, 1)
        key_part = lax.dynamic_slice_in_dim(all_keys, offset, HEAD, 1)
        value_part = lax.dynamic_slice_in_dim(all_values, offset, HEAD, 1)
        scores = jnp.where(same_doc, inner_cols(query_part, key_part) * 0.125, MASKED)
        row_max = jnp.max(scores, axis=1, keepdims=True)
        exponent = jnp.exp(scores - row_max)
        row_total = jnp.sum(exponent, axis=1, keepdims=True)
        attn_probs = (exponent / row_total).astype(jnp.bfloat16)
        return (matmul(attn_probs, value_part), (row_max + jnp.log(row_total))[:, 0])

    outputs, log_totals = lax.map(one_head, jnp.arange(head_count, dtype=jnp.int32))
    return (flatten(outputs), log_totals)


def attend_back(q_rot, all_keys, all_values, same_doc, grad_out, log_totals):
    head_count = q_rot.shape[1] // HEAD

    def one_head(pack):
        head_pos, log_total = pack
        offset = head_pos * HEAD
        query_part = lax.dynamic_slice_in_dim(q_rot, offset, HEAD, 1)
        key_part = lax.dynamic_slice_in_dim(all_keys, offset, HEAD, 1)
        value_part = lax.dynamic_slice_in_dim(all_values, offset, HEAD, 1)
        grad_part = lax.dynamic_slice_in_dim(grad_out, offset, HEAD, 1)
        scores = jnp.where(same_doc, inner_cols(query_part, key_part) * 0.125, MASKED)
        attn_probs = jnp.exp(scores - log_total[:, None])
        grad_probs = inner_cols(grad_part, value_part)
        row_dot = jnp.sum(attn_probs * grad_probs, axis=1, keepdims=True)
        grad_scores = (attn_probs * (grad_probs - row_dot)).astype(jnp.bfloat16)
        grad_query = matmul(grad_scores, key_part) * 0.125
        grad_key = inner_rows(grad_scores, query_part) * 0.125
        grad_value = inner_rows(attn_probs.astype(jnp.bfloat16), grad_part)
        return (grad_query, grad_key, grad_value)

    mapped = lax.map(one_head, (jnp.arange(head_count, dtype=jnp.int32), log_totals))
    return (flatten(mapped[0]), flatten(mapped[1]), flatten(mapped[2]))


def advance(weight, moment, average, grad_in, rate):
    moment_next = MOMENTUM * moment + grad_in
    weight_next = weight - rate * (grad_in + MOMENTUM * moment_next)
    average_next = AVERAGE_DECAY * average + (1.0 - AVERAGE_DECAY) * weight_next
    return (weight_next, moment_next, average_next, weight_next.astype(jnp.bfloat16))


def body_general(
    tokens,
    doc_lengths,
    pair_index,
    target_bank,
    mixer_in,
    mixer_out,
    expand,
    contract,
    norm_params,
    mixer_in_moment,
    mixer_out_moment,
    expand_moment,
    contract_moment,
    norm_moment,
    mixer_in_average,
    mixer_out_average,
    expand_average,
    contract_average,
    norm_average,
):
    local_rows, model_width = tokens.shape
    slices = lax.axis_size("dim")
    group_rows = local_rows * slices
    position = lax.axis_index("dim")
    layer_count = mixer_in.shape[0]
    doc_count = doc_lengths.shape[1]
    lengths = doc_lengths[0]
    doc_ends = jnp.cumsum(lengths)
    doc_starts = doc_ends - lengths
    row_ids = position * local_rows + jnp.arange(local_rows, dtype=jnp.int32)
    key_ids = jnp.arange(group_rows, dtype=jnp.int32)
    seg_rows = jnp.sum((row_ids[:, None] >= doc_ends[None, :]).astype(jnp.int32), axis=1)
    seg_keys = jnp.sum((key_ids[:, None] >= doc_ends[None, :]).astype(jnp.int32), axis=1)
    first_rows = jnp.concatenate([doc_starts, doc_ends[-1:]])
    segment_ids = jnp.arange(doc_count + 1, dtype=jnp.int32)
    row_begin = jnp.sum(
        jnp.where(seg_rows[:, None] == segment_ids[None, :], first_rows[None, :], 0), axis=1
    )
    frequency = jnp.power(1000.0, -jnp.arange(0, HEAD, 2).astype(jnp.float32) / HEAD)
    angles = (row_ids - row_begin).astype(jnp.float32)[:, None] * frequency[None, :]
    cosines = jnp.cos(angles)
    sines = jnp.sin(angles)
    same_doc = seg_rows[:, None] == seg_keys[None, :]
    stream = tokens.astype(jnp.float32)
    layer_pos = 0
    layer_weights = (
        lax.all_gather(mixer_in[layer_pos].astype(jnp.bfloat16), ("dp", "dim"), axis=0, tiled=True),
        lax.all_gather(
            mixer_out[layer_pos].astype(jnp.bfloat16), ("dp", "dim"), axis=0, tiled=True
        ),
        lax.all_gather(expand[layer_pos].astype(jnp.bfloat16), ("dp", "dim"), axis=0, tiled=True),
        lax.all_gather(contract[layer_pos].astype(jnp.bfloat16), ("dp", "dim"), axis=0, tiled=True),
        lax.all_gather(
            norm_params[layer_pos].astype(jnp.bfloat16), ("dp", "dim"), axis=1, tiled=True
        ),
    )
    w_mix, w_out, w_exp, w_con, w_norm = layer_weights
    norm_gains = w_norm.astype(jnp.float32)
    x_low = stream.astype(jnp.bfloat16)
    mixed = matmul(x_low, w_mix)
    q_rot = rotate(mixed[:, 0:model_width], cosines, sines).astype(jnp.bfloat16)
    k_rot = rotate(mixed[:, model_width : 2 * model_width], cosines, sines).astype(jnp.bfloat16)
    v_low = mixed[:, 2 * model_width : 3 * model_width].astype(jnp.bfloat16)
    all_keys = lax.all_gather(k_rot, "dim", axis=0, tiled=True)
    all_values = lax.all_gather(v_low, "dim", axis=0, tiled=True)
    attended, log_totals = attend(q_rot, all_keys, all_values, same_doc)
    att_low = attended.astype(jnp.bfloat16)
    first_sum = stream + matmul(att_low, w_out)
    normed = normalize(first_sum, norm_gains[0], norm_gains[1])
    y_low = normed.astype(jnp.bfloat16)
    gate_up = matmul(y_low, w_exp)
    half = gate_up.shape[1] // 2
    hidden = (jax.nn.silu(gate_up[:, 0:half]) * gate_up[:, half : 2 * half]).astype(jnp.bfloat16)
    second_sum = normed + matmul(hidden, w_con)
    saved = [
        (
            stream,
            layer_weights,
            q_rot,
            k_rot,
            v_low,
            all_keys,
            all_values,
            log_totals,
            attended,
            att_low,
            first_sum,
            normed,
            y_low,
            gate_up,
            hidden,
            second_sum,
        )
    ]
    stream = normalize(second_sum, norm_gains[2], norm_gains[3])
    member = (seg_rows[None, :] == jnp.arange(doc_count, dtype=jnp.int32)[:, None]).astype(
        jnp.float32
    )
    partial_value = matmul_exact(member, stream)
    pooled = lax.psum_scatter(partial_value, "dim", scatter_dimension=1, tiled=True)
    length_f = lengths.astype(jnp.float32)
    embeddings = pooled / length_f[:, None]
    share = embeddings.shape[1]
    pick = (
        pair_index[:, None] == jnp.arange(target_bank.shape[0], dtype=jnp.int32)[None, :]
    ).astype(jnp.bfloat16)
    targets = matmul(pick, target_bank)
    feature_ids = position * share + jnp.arange(share, dtype=jnp.int32)
    cuts = jnp.array(
        [model_width // 12, model_width // 6, model_width // 3, 2 * model_width // 3, model_width],
        dtype=jnp.int32,
    )
    masks = (feature_ids[None, :] < cuts[:, None]).astype(jnp.float32)
    cross = matmul_exact(embeddings * targets, masks.T)
    own = matmul_exact(embeddings * embeddings, masks.T)
    other = matmul_exact(targets * targets, masks.T)
    cross, own, other = lax.psum((cross, own, other), "dim")
    own_root = lax.rsqrt(own + COSINE_EPSILON)
    other_root = lax.rsqrt(other + COSINE_EPSILON)
    cosine = cross * own_root * other_root
    coef_target = -length_f[:, None] * own_root * other_root
    coef_self = length_f[:, None] * cosine * own_root * own_root
    grad_emb = (
        matmul_exact(coef_target, masks) * targets + matmul_exact(coef_self, masks) * embeddings
    )
    grad_full = lax.all_gather(grad_emb, "dim", axis=1, tiled=True)
    spread_rows = member / length_f[:, None]
    grad_stream = lax.dot_general(
        spread_rows,
        grad_full,
        (((0,), (0,)), ((), ())),
        precision=PRECISE,
        preferred_element_type=jnp.float32,
    )
    grad_list = [None] * layer_count
    for layer_pos in reversed(range(layer_count)):
        (
            layer_input,
            layer_weights,
            q_rot,
            k_rot,
            v_low,
            all_keys,
            all_values,
            log_totals,
            attended,
            att_low,
            first_sum,
            normed,
            y_low,
            gate_up,
            hidden,
            second_sum,
        ) = saved[layer_pos]
        w_mix = lax.all_gather(
            mixer_in[layer_pos].astype(jnp.bfloat16), ("dp", "dim"), axis=0, tiled=True
        )
        w_out = lax.all_gather(
            mixer_out[layer_pos].astype(jnp.bfloat16), ("dp", "dim"), axis=0, tiled=True
        )
        w_exp = lax.all_gather(
            expand[layer_pos].astype(jnp.bfloat16), ("dp", "dim"), axis=0, tiled=True
        )
        w_con = lax.all_gather(
            contract[layer_pos].astype(jnp.bfloat16), ("dp", "dim"), axis=0, tiled=True
        )
        w_norm = lax.all_gather(
            norm_params[layer_pos].astype(jnp.bfloat16), ("dp", "dim"), axis=1, tiled=True
        )
        norm_gains = w_norm.astype(jnp.float32)
        grad_second, grad_gain2, grad_bias2 = normalize_back(grad_stream, second_sum, norm_gains[2])
        grad_m_low = grad_second.astype(jnp.bfloat16)
        grad_con = inner_rows(hidden, grad_m_low)
        grad_hidden = inner_cols(grad_m_low, w_con)
        half = gate_up.shape[1] // 2
        gate_part = gate_up[:, 0:half]
        up_part = gate_up[:, half : 2 * half]
        sigmoid_gate = jax.nn.sigmoid(gate_part)
        activated = gate_part * sigmoid_gate
        grad_gate = grad_hidden * up_part * sigmoid_gate * (1.0 + gate_part * (1.0 - sigmoid_gate))
        grad_up = grad_hidden * activated
        grad_both = jnp.concatenate([grad_gate, grad_up], axis=1).astype(jnp.bfloat16)
        grad_exp = inner_rows(y_low, grad_both)
        grad_normed = grad_second + inner_cols(grad_both, w_exp)
        grad_first, grad_gain1, grad_bias1 = normalize_back(grad_normed, first_sum, norm_gains[0])
        grad_a_low = grad_first.astype(jnp.bfloat16)
        grad_out = inner_rows(att_low, grad_a_low)
        grad_attended = inner_cols(grad_a_low, w_out).astype(jnp.bfloat16)
        keys_back, values_back = (
            lax.all_gather(k_rot, "dim", axis=0, tiled=True),
            lax.all_gather(v_low, "dim", axis=0, tiled=True),
        )
        grad_query, grad_key_all, grad_value_all = attend_back(
            q_rot, keys_back, values_back, same_doc, grad_attended, log_totals
        )
        grad_kv = lax.psum_scatter(
            jnp.concatenate([grad_key_all, grad_value_all], axis=1).astype(jnp.bfloat16),
            "dim",
            scatter_dimension=0,
            tiled=True,
        ).astype(jnp.float32)
        grad_mixed = jnp.concatenate(
            [
                rotate_back(grad_query, cosines, sines),
                rotate_back(grad_kv[:, 0:model_width], cosines, sines),
                grad_kv[:, model_width : 2 * model_width],
            ],
            axis=1,
        ).astype(jnp.bfloat16)
        x_low = layer_input.astype(jnp.bfloat16)
        grad_mix = inner_rows(x_low, grad_mixed)
        grad_stream = grad_first + inner_cols(grad_mixed, w_mix)
        grad_norm = jnp.stack([grad_gain1, grad_bias1, grad_gain2, grad_bias2])
        grad_list[layer_pos] = (
            lax.psum_scatter(grad_mix, ("dp", "dim"), scatter_dimension=0, tiled=True),
            lax.psum_scatter(grad_out, ("dp", "dim"), scatter_dimension=0, tiled=True),
            lax.psum_scatter(grad_exp, ("dp", "dim"), scatter_dimension=0, tiled=True),
            lax.psum_scatter(grad_con, ("dp", "dim"), scatter_dimension=0, tiled=True),
            lax.psum_scatter(grad_norm, ("dp", "dim"), scatter_dimension=1, tiled=True),
        )
    total_rows = group_rows * lax.axis_size("dp")
    matrix_rate = 1.0 / math.sqrt(total_rows)
    norm_rate = 0.3 / math.sqrt(total_rows)
    grads = [jnp.stack([grad_list[0][kind]]) for kind in range(5)]
    weights = (mixer_in, mixer_out, expand, contract, norm_params)
    moments = (mixer_in_moment, mixer_out_moment, expand_moment, contract_moment, norm_moment)
    averages = (mixer_in_average, mixer_out_average, expand_average, contract_average, norm_average)
    rates = (matrix_rate, matrix_rate, matrix_rate, matrix_rate, norm_rate)
    results = [
        advance(weights[kind], moments[kind], averages[kind], grads[kind], rates[kind])
        for kind in range(5)
    ]
    return (
        embeddings,
        grad_stream,
        grads[0],
        grads[1],
        grads[2],
        grads[3],
        grads[4],
        results[0][0],
        results[1][0],
        results[2][0],
        results[3][0],
        results[4][0],
        results[0][1],
        results[1][1],
        results[2][1],
        results[3][1],
        results[4][1],
        results[0][2],
        results[1][2],
        results[2][2],
        results[3][2],
        results[4][2],
        results[0][3],
        results[1][3],
        results[2][3],
        results[3][3],
        results[4][3],
    )


NEG=-1e30
BQ=512
ROWS=256
BK=384
FK=512
F32=jnp.float32
BF=jnp.bfloat16

def nt(a,b): return lax.dot_general(a,b,(((1,),(1,)),((),())),preferred_element_type=F32)
def nn(a,b): return jnp.dot(a,b,preferred_element_type=F32)

def fill_masks(e0,e1,kaug,q0,q1,rows,pad):
    r=lax.broadcasted_iota(jnp.int32,(rows+pad,128),0)
    l=lax.broadcasted_iota(jnp.int32,(rows+pad,128),1)
    seg=(r>=e0).astype(jnp.int32)+(r>=e1).astype(jnp.int32)
    kaug[:,128:256]=jnp.where((l<3)&(l!=seg),NEG,0.0).astype(BF)
    qm=jnp.where(l==seg,1.0,0.0).astype(BF)[0:rows]
    q0[:,128:256]=qm
    q1[:,128:256]=qm

def key_range(i,e0,e1,step):
    first=i*BQ
    last=jnp.minimum(first+BQ,e1)-1
    lo=jnp.where(first>=e0,e0,0)
    hi=jnp.where(last>=e0,e1,e0)
    base=(lo//128)*128
    return pl.multiple_of(base,128),(hi-base+step-1)//step

def fwd_kernel(ctl,qo,ko,vo,qr,kr,vr,oo,ox,lse,kaug,q0,q1,vt):
    rows=kaug.shape[0]-FK
    half=rows//2
    pos,e0,e1=ctl[0],ctl[1],ctl[2]
    p=pl.program_id(0)
    @pl.when(p==0)
    def _():
        fill_masks(e0,e1,kaug,q0,q1,rows,FK)
        kaug[rows:,0:128]=jnp.zeros((FK,128),BF)
        vt[:,:]=jnp.where(lax.broadcasted_iota(jnp.int32,vt.shape,0)%80>=64,1.0,0.0).astype(BF)
    pick_r=lax.broadcasted_iota(jnp.int32,(16,128),0)
    pick_l=lax.broadcasted_iota(jnp.int32,(16,128),1)
    pick=jnp.where(pick_l//64==pick_r,1.0,0.0).astype(BF)
    q_top=jnp.zeros((16,1),F32)
    k_top=jnp.zeros((16,1),F32)
    lane=lax.broadcasted_iota(jnp.int32,(half,128),1)
    for own,(q,k,v) in ((True,(qo,ko,vo)),(False,(qr,kr,vr))):
        at=pl.multiple_of((pos if own else 1-pos)*half,half)
        scaled=q[...]*jnp.asarray(0.125,BF)
        zero=jnp.zeros_like(scaled)
        q0[pl.ds(at,half),0:128]=jnp.where(lane<64,scaled,zero)
        q1[pl.ds(at,half),0:128]=jnp.where(lane<64,zero,scaled)
        kb=k[...]
        kaug[pl.ds(at,half),0:128]=kb
        q_top=jnp.maximum(q_top,jnp.max(nt(pick,scaled*scaled),axis=1,keepdims=True))
        k_top=jnp.maximum(k_top,jnp.max(nt(pick,kb*kb),axis=1,keepdims=True))
        turned=v[...].T
        vt[0:64,pl.ds(at,half)]=turned[0:64]
        vt[80:144,pl.ds(at,half)]=turned[64:128]
    narrow=jnp.max(q_top*k_top)*1.05<=1600.0
    def qnarrow(i,_):
        r0=pl.multiple_of(i*BQ,BQ)
        base,count=key_range(i,e0,e1,FK)
        qs=(q0[pl.ds(r0,BQ),:],q1[pl.ds(r0,BQ),:])
        def step(j,carry):
            k0=pl.multiple_of(base+j*FK,128)
            kb=kaug[pl.ds(k0,FK),:]
            pt=[jnp.exp(nt(kb,qs[h])).astype(BF) for h in range(2)]
            return tuple(carry[h]+nn(vt[80*h:80*h+80,pl.ds(k0,FK)],pt[h]) for h in range(2))
        init=jnp.zeros((80,BQ),F32)
        res=lax.fori_loop(0,count,step,(init,init))
        outs=[]
        for h in range(2):
            l=jnp.maximum(res[h][64:65],1e-30)
            outs.append(res[h][0:64]/l)
            lse[0,h:h+1,pl.ds(r0,BQ)]=jnp.where(l>1e-30,jnp.log(l),1e30)
        put(i,jnp.concatenate(outs,axis=0).T.astype(BF))
        return 0
    def qblock(i,_):
        r0=pl.multiple_of(i*BQ,BQ)
        base,count=key_range(i,e0,e1,FK)
        qs=(q0[pl.ds(r0,BQ),:],q1[pl.ds(r0,BQ),:])
        def step(j,carry):
            k0=pl.multiple_of(base+j*FK,128)
            kb=kaug[pl.ds(k0,FK),:]
            scores=[nt(kb,qs[h]) for h in range(2)]
            out=[]
            for h in range(2):
                m,acc=carry[h]
                mn=jnp.maximum(m,jnp.max(scores[h],axis=0,keepdims=True))
                pt=jnp.exp(scores[h]-mn).astype(BF)
                acc=acc*jnp.exp(m-mn)+nn(vt[80*h:80*h+80,pl.ds(k0,FK)],pt)
                out.append((mn,acc))
            return tuple(out)
        init=(jnp.full((1,BQ),-jnp.inf,F32),jnp.zeros((80,BQ),F32))
        res=lax.fori_loop(0,count,step,(init,init))
        outs=[]
        for h in range(2):
            m,acc=res[h]
            l=acc[64:65]
            outs.append(acc[0:64]/l)
            lse[0,h:h+1,pl.ds(r0,BQ)]=jnp.where(m>-1e29,m+jnp.log(l),1e30)
        ob=jnp.concatenate(outs,axis=0).T.astype(BF)
        put(i,ob)
        return 0
    def put(i,ob):
        local=i*BQ-pos*half
        @pl.when((local>=0)&(local<half))
        def _(): oo[pl.ds(pl.multiple_of(local,BQ),BQ),:]=ob
        @pl.when((local<0)|(local>=half))
        def _(): ox[pl.ds(pl.multiple_of(i*BQ-(1-pos)*half,BQ),BQ),:]=ob
    used=(e1+BQ-1)//BQ
    @pl.when(narrow)
    def _(): lax.fori_loop(0,used,qnarrow,0)
    @pl.when(jnp.logical_not(narrow))
    def _(): lax.fori_loop(0,used,qblock,0)
    def blank(i,_):
        r0=pl.multiple_of(i*BQ,BQ)
        lse[0,:,pl.ds(r0,BQ)]=jnp.zeros((8,BQ),F32)
        put(i,jnp.zeros((BQ,128),BF))
        return 0
    lax.fori_loop(used,rows//BQ,blank,0)

def attend_fwd(ctl,own,recv):
    half,width=own.shape
    pairs=width//384
    rows=2*half
    sp=[pl.BlockSpec((half,128),(lambda p,c,s=s:(0,s*pairs+p))) for s in range(3)]
    outw=pairs*128
    return pl.pallas_call(fwd_kernel,
        grid_spec=pltpu.PrefetchScalarGridSpec(num_scalar_prefetch=1,grid=(pairs,),
          in_specs=sp+sp,
          out_specs=[pl.BlockSpec((half,128),lambda p,c:(0,p))]*2+[pl.BlockSpec((1,8,rows),lambda p,c:(p,0,0))],
          scratch_shapes=[pltpu.VMEM((rows+FK,256),BF),pltpu.VMEM((rows,256),BF),pltpu.VMEM((rows,256),BF),pltpu.VMEM((160,rows+FK),BF)]),
        out_shape=[jax.ShapeDtypeStruct((half,outw),BF)]*2+[jax.ShapeDtypeStruct((pairs,8,rows),F32)],
        compiler_params=pltpu.CompilerParams(vmem_limit_bytes=60<<20,dimension_semantics=("arbitrary",)),
        cost_estimate=pl.CostEstimate(flops=4*rows*rows*64*2*pairs//2,bytes_accessed=10*half*width,transcendentals=rows*rows*pairs),
        name="attend_fwd",
    )(ctl,own,own,own,recv,recv,recv)

def bwd_kernel(ctl,qo,ko,vo,qr,kr,vr,do_o,do_r,oo,ox,lse,cos,sin,g0,g1,g2,x0,x1,x2,kaug,q0,q1,vs,d0,d1,kt,delta,dk,dv):
    rows=kaug.shape[0]-BK
    half=rows//2
    pos,e0,e1=ctl[0],ctl[1],ctl[2]
    p=pl.program_id(0)
    @pl.when(p==0)
    def _():
        fill_masks(e0,e1,kaug,q0,q1,rows,kaug.shape[0]-rows)
        kaug[rows:,0:128]=jnp.zeros((BK,128),BF)
        vs[rows:,:]=jnp.zeros((BK,128),BF)
        kt[:,rows:]=jnp.zeros((128,BK),BF)
    lane=lax.broadcasted_iota(jnp.int32,(half,128),1)
    pick_r=lax.broadcasted_iota(jnp.int32,(16,128),0)
    pick_l=lax.broadcasted_iota(jnp.int32,(16,128),1)
    pick=jnp.where(pick_l//64==pick_r,1.0,0.0).astype(BF)
    for own,(q,k,v,d,o) in ((True,(qo,ko,vo,do_o,oo)),(False,(qr,kr,vr,do_r,ox))):
        at=pl.multiple_of((pos if own else 1-pos)*half,half)
        scaled=q[...]*jnp.asarray(0.125,BF)
        zero=jnp.zeros_like(scaled)
        q0[pl.ds(at,half),0:128]=jnp.where(lane<64,scaled,zero)
        q1[pl.ds(at,half),0:128]=jnp.where(lane<64,zero,scaled)
        kb=k[...]
        kaug[pl.ds(at,half),0:128]=kb
        kt[:,pl.ds(at,half)]=kb.T
        vs[pl.ds(at,half),:]=v[...]
        db=d[...]
        d0[pl.ds(at,half),:]=jnp.where(lane<64,db,zero)
        d1[pl.ds(at,half),:]=jnp.where(lane<64,zero,db)
        prod=db.astype(F32)*o[...].astype(F32)
        hi=prod.astype(BF)
        lo=(prod-hi.astype(F32)).astype(BF)
        delta[:,pl.ds(at,half)]=nt(pick,hi)+nt(pick,lo)
    dk[...]=jnp.zeros_like(dk)
    dv[...]=jnp.zeros_like(dv)
    def spread(i,col,val):
        local=i*ROWS-pos*half
        @pl.when((local>=0)&(local<half))
        def _(): (g0,g1,g2)[col][pl.ds(pl.multiple_of(local,ROWS),ROWS),:]=val
        @pl.when((local<0)|(local>=half))
        def _(): (x0,x1,x2)[col][pl.ds(pl.multiple_of(i*ROWS-(1-pos)*half,ROWS),ROWS),:]=val
    def unturn(x,r0):
        ln=lax.broadcasted_iota(jnp.int32,x.shape,1)
        swapped=jnp.where((ln%64)<32,pltpu.roll(x,96,1),pltpu.roll(x,32,1))
        return x*cos[pl.ds(r0,ROWS),:]-swapped*sin[pl.ds(r0,ROWS),:]
    def qblock(i,_):
        r0=pl.multiple_of(i*BQ,BQ)
        base,count=key_range(i,e0,e1,BK)
        qs=(q0[pl.ds(r0,BQ),:],q1[pl.ds(r0,BQ),:])
        ds_=(d0[pl.ds(r0,BQ),:],d1[pl.ds(r0,BQ),:])
        ls=[lse[0,h:h+1,pl.ds(r0,BQ)] for h in range(2)]
        de=[delta[h:h+1,pl.ds(r0,BQ)] for h in range(2)]
        def step(j,carry):
            k0=pl.multiple_of(base+j*BK,128)
            kb=kaug[pl.ds(k0,BK),:]
            vb=vs[pl.ds(k0,BK),:]
            both=range(2)
            st=[nt(kb,qs[h]) for h in both]
            dpt=[nt(vb,ds_[h]) for h in both]
            pt=[jnp.exp(st[h]-ls[h]) for h in both]
            dst=[(pt[h]*(dpt[h]-de[h])).astype(BF) for h in both]
            pb=[pt[h].astype(BF) for h in both]
            dv[pl.ds(k0,BK),:]+=nn(pb[0],ds_[0])+nn(pb[1],ds_[1])
            dk[pl.ds(k0,BK),:]+=nn(dst[0],qs[0][:,0:128])+nn(dst[1],qs[1][:,0:128])
            out=[carry[h]+nn(kt[64*h:64*h+64,pl.ds(k0,BK)],dst[h]) for h in both]
            return tuple(out)
        init=jnp.zeros((64,BQ),F32)
        res=lax.fori_loop(0,count,step,(init,init))
        dq=jnp.concatenate(res,axis=0).T*0.125
        for t in range(BQ//ROWS):
            at=pl.multiple_of(r0+t*ROWS,ROWS)
            spread(i*(BQ//ROWS)+t,0,unturn(dq[t*ROWS:(t+1)*ROWS],at).astype(BF))
        return 0
    used=(e1+BQ-1)//BQ
    lax.fori_loop(0,used,qblock,0)
    def blank(i,_):
        spread(i,0,jnp.zeros((ROWS,128),BF))
        return 0
    lax.fori_loop(used*(BQ//ROWS),rows//ROWS,blank,0)
    def last(i,_):
        r0=pl.multiple_of(i*ROWS,ROWS)
        spread(i,1,unturn(dk[pl.ds(r0,ROWS),:],r0).astype(BF))
        spread(i,2,dv[pl.ds(r0,ROWS),:].astype(BF))
        return 0
    lax.fori_loop(0,rows//ROWS,last,0)

def attend_bwd(ctl,own,recv,d_own,d_recv,o_own,o_oth,lse,cos,sin):
    half,width=own.shape
    pairs=width//384
    rows=2*half
    sp=[pl.BlockSpec((half,128),(lambda p,c,s=s:(0,s*pairs+p))) for s in range(3)]
    one=pl.BlockSpec((half,128),lambda p,c:(0,p))
    full=pl.BlockSpec((rows,128),lambda p,c:(0,0))
    return pl.pallas_call(bwd_kernel,
        grid_spec=pltpu.PrefetchScalarGridSpec(num_scalar_prefetch=1,grid=(pairs,),
          in_specs=sp+sp+[one]*4+[pl.BlockSpec((1,8,rows),lambda p,c:(p,0,0)),full,full],
          out_specs=[one]*6,
          scratch_shapes=[pltpu.VMEM((rows+BK,256),BF),pltpu.VMEM((rows,256),BF),pltpu.VMEM((rows,256),BF),
             pltpu.VMEM((rows+BK,128),BF),pltpu.VMEM((rows,128),BF),pltpu.VMEM((rows,128),BF),
             pltpu.VMEM((128,rows+BK),BF),pltpu.VMEM((16,rows),F32),pltpu.VMEM((rows+BK,128),F32),pltpu.VMEM((rows+BK,128),F32)]),
        out_shape=[jax.ShapeDtypeStruct((half,width//3),BF)]*6,
        compiler_params=pltpu.CompilerParams(vmem_limit_bytes=60<<20,dimension_semantics=("arbitrary",)),
        cost_estimate=pl.CostEstimate(flops=10*rows*rows*64*2*pairs//2,bytes_accessed=20*half*width,transcendentals=rows*rows*pairs),
        name="attend_bwd",
    )(ctl,own,own,own,recv,recv,recv,d_own,d_recv,o_own,o_oth,lse,cos,sin)

BLOCK=256

def spread_mean(x):
    return jnp.mean(x,axis=1,keepdims=True)

def row_docs(ctl,block):
    i=pl.program_id(0)
    r=ctl[0]*(block*pl.num_programs(0))+i*block+lax.broadcasted_iota(jnp.int32,(block,1),0)
    return (r>=ctl[1]).astype(jnp.int32)+(r>=ctl[2]).astype(jnp.int32)

def ffn_fwd_kernel(ctl,ao,ax,tok,w_exp,w_con,w_out,norm,u1,u2,rs,yb,h0,h1,h2,h3,pf,pooled):
    block,width=tok.shape
    hidden=pf.shape[1]//2
    kept=(h0,h1,h2,h3)
    share=width//2
    pos=ctl[0]
    mine=pl.multiple_of(pos*share,share)
    other=pl.multiple_of((1-pos)*share,share)
    f=tok[...].astype(F32)+nn(ao[...],w_out[pl.ds(mine,share),:])+nn(ax[...],w_out[pl.ds(other,share),:])
    cent=f-spread_mean(f)
    scale=lax.rsqrt(spread_mean(cent*cent)+NORM_EPSILON)
    unit=cent*scale
    u1[...]=unit
    rs[:,0:128]=jnp.broadcast_to(scale,(block,128))
    y=unit*norm[0:1,:]+norm[1:2,:]
    ylow=y.astype(BF)
    yb[...]=ylow
    acc=y
    count=hidden//width
    spans=[(slice(c*width,(c+1)*width),slice(hidden+c*width,hidden+(c+1)*width)) for c in range(count)]
    pre=lambda c: (nn(ylow,w_exp[:,spans[c][0]]),nn(ylow,w_exp[:,spans[c][1]]))
    ahead=pre(0)
    for c in range(count):
        gate,up=ahead
        if c+1<count: ahead=pre(c+1)
        gc,uc=spans[c]
        sig=jax.nn.sigmoid(gate)
        act=gate*sig
        low=(act*up).astype(BF)
        kept[c][...]=low
        pf[:,gc]=(up*(sig+act*(1.0-sig))).astype(BF)
        pf[:,uc]=act.astype(BF)
        acc=acc+nn(low,w_con[:,gc])
    cent=acc-spread_mean(acc)
    scale=lax.rsqrt(spread_mean(cent*cent)+NORM_EPSILON)
    unit=cent*scale
    u2[...]=unit
    rs[:,128:256]=jnp.broadcast_to(scale,(block,128))
    out=unit*norm[2:3,:]+norm[3:4,:]
    docs=row_docs(ctl,block)
    @pl.when(pl.program_id(0)==0)
    def _(): pooled[...]=jnp.zeros_like(pooled)
    for d in range(2):
        pooled[d:d+1,:]+=jnp.sum(jnp.where(docs==d,out,0.0),axis=0,keepdims=True)

def ffn_fwd(ctl,ao,ax,tok,bundle,norm,hidden):
    rows,width=tok.shape
    row=lambda n: pl.BlockSpec((BLOCK,n),lambda i,c:(i,0))
    held=lambda n,at: pl.BlockSpec((width,n),lambda i,c:(0,at//n),pipeline_mode=pl.Buffered(1))
    flat=pl.BlockSpec((8,width),lambda i,c:(0,0))
    return pl.pallas_call(ffn_fwd_kernel,
        grid_spec=pltpu.PrefetchScalarGridSpec(num_scalar_prefetch=1,grid=(rows//BLOCK,),
          in_specs=[row(width//2),row(width//2),row(width),held(2*hidden,0),held(hidden,2*hidden),held(width,3*hidden),flat],
          out_specs=[row(width),row(width),row(256),*[row(width)]*5,row(2*hidden),flat]),
        out_shape=[jax.ShapeDtypeStruct((rows,width),F32),jax.ShapeDtypeStruct((rows,width),F32),jax.ShapeDtypeStruct((rows,256),F32),
          *[jax.ShapeDtypeStruct((rows,width),BF)]*5,jax.ShapeDtypeStruct((rows,2*hidden),BF),
          jax.ShapeDtypeStruct((8,width),F32)],
        compiler_params=pltpu.CompilerParams(vmem_limit_bytes=60<<20,dimension_semantics=("arbitrary",)),
        cost_estimate=pl.CostEstimate(flops=2*rows*width*(width+3*hidden),bytes_accessed=rows*(width*14+hidden*6)+2*width*(width+3*hidden),transcendentals=rows*hidden),
        name="ffn_fwd",
    )(ctl,ao,ax,tok,bundle,bundle,bundle,norm)

def loss_grad(pool,targets,len0,len1):
    width=pool.shape[1]
    docs=lax.broadcasted_iota(jnp.int32,pool.shape,0)
    length=jnp.where(docs==0,len0,len1)
    emb=pool/length
    lane=lax.broadcasted_iota(jnp.int32,pool.shape,1)
    d_target=jnp.zeros_like(pool)
    d_self=jnp.zeros_like(pool)
    for cut in (width//12,width//6,width//3,2*width//3,width):
        keep=lane<cut
        total=lambda v: jnp.sum(jnp.where(keep,v,0.0),axis=1,keepdims=True)
        own_root=lax.rsqrt(total(emb*emb)+COSINE_EPSILON)
        other_root=lax.rsqrt(total(targets*targets)+COSINE_EPSILON)
        cosine=total(emb*targets)*own_root*other_root
        d_target=d_target+jnp.where(keep,own_root*other_root,0.0)
        d_self=d_self+jnp.where(keep,cosine*own_root*own_root,0.0)
    d_emb=length*(d_self*emb-d_target*targets)
    return emb,d_emb/length

def ffn_bwd_kernel(ctl,flen,pool_a,pool_b,targets,u1,u2,rs,pf,w_exp,w_con,w_out,norm,
                   emb,mb,ub,df,ab,do,dx,gn,de):
    block,width=u1.shape
    hidden=pf.shape[1]//2
    share=width//2
    pos=ctl[0]
    @pl.when(pl.program_id(0)==0)
    def _():
        e,d=loss_grad(pool_a[...]+pool_b[...],targets[...],flen[0],flen[1])
        emb[...]=e
        de[...]=d
        gn[...]=jnp.zeros_like(gn)
    docs=row_docs(ctl,block)
    dout=jnp.where(docs==0,de[0:1,:],jnp.where(docs==1,de[1:2,:],0.0))
    unit=u2[...]
    gn[2:3,:]+=jnp.sum(dout*unit,axis=0,keepdims=True)
    gn[3:4,:]+=jnp.sum(dout,axis=0,keepdims=True)
    gu=dout*norm[2:3,:]
    dg=rs[:,128:129]*(gu-spread_mean(gu)-unit*spread_mean(gu*unit))
    mlow=dg.astype(BF)
    mb[...]=mlow
    acc=dg
    for c in range(hidden//width):
        gc=slice(c*width,(c+1)*width)
        uc=slice(hidden+c*width,hidden+(c+1)*width)
        dh=nt(mlow,w_con[:,gc])
        dgate=(dh*pf[:,gc].astype(F32)).astype(BF)
        dup=(dh*pf[:,uc].astype(F32)).astype(BF)
        ub[:,gc]=dgate
        ub[:,uc]=dup
        acc=acc+nt(dgate,w_exp[:,gc])+nt(dup,w_exp[:,uc])
    unit=u1[...]
    gn[0:1,:]+=jnp.sum(acc*unit,axis=0,keepdims=True)
    gn[1:2,:]+=jnp.sum(acc,axis=0,keepdims=True)
    gu=acc*norm[0:1,:]
    dfirst=rs[:,0:1]*(gu-spread_mean(gu)-unit*spread_mean(gu*unit))
    df[...]=dfirst
    alow=dfirst.astype(BF)
    ab[...]=alow
    do[...]=nt(alow,w_out[pl.ds(pl.multiple_of(pos*share,share),share),:]).astype(BF)
    dx[...]=nt(alow,w_out[pl.ds(pl.multiple_of((1-pos)*share,share),share),:]).astype(BF)

def ffn_bwd(ctl,flen,pool_a,pool_b,targets,u1,u2,rs,pf,bundle,norm):
    rows,width=u1.shape
    hidden=pf.shape[1]//2
    row=lambda n: pl.BlockSpec((BLOCK,n),lambda i,c,l:(i,0))
    held=lambda n,at: pl.BlockSpec((width,n),lambda i,c,l:(0,at//n),pipeline_mode=pl.Buffered(1))
    flat=pl.BlockSpec((8,width),lambda i,c,l:(0,0))
    sds=jax.ShapeDtypeStruct
    return pl.pallas_call(ffn_bwd_kernel,
        grid_spec=pltpu.PrefetchScalarGridSpec(num_scalar_prefetch=2,grid=(rows//BLOCK,),
          in_specs=[flat,flat,flat,row(width),row(width),row(256),row(2*hidden),held(2*hidden,0),held(hidden,2*hidden),held(width,3*hidden),flat],
          out_specs=[flat,row(width),row(2*hidden),row(width),row(width),row(width//2),row(width//2),flat],
          scratch_shapes=[pltpu.VMEM((8,width),F32)]),
        out_shape=[sds((8,width),F32),sds((rows,width),BF),sds((rows,2*hidden),BF),sds((rows,width),F32),sds((rows,width),BF),
          sds((rows,width//2),BF),sds((rows,width//2),BF),sds((8,width),F32)],
        compiler_params=pltpu.CompilerParams(vmem_limit_bytes=60<<20,dimension_semantics=("arbitrary",)),
        cost_estimate=pl.CostEstimate(flops=2*rows*width*(width+3*hidden),bytes_accessed=rows*(width*18+hidden*8)+2*width*(width+3*hidden),transcendentals=0),
        name="ffn_bwd",
    )(ctl,flen,pool_a,pool_b,targets,u1,u2,rs,pf,bundle,bundle,bundle,norm)

MESH=pl.DeviceIdType.MESH

def place():
    dp=lax.axis_index("dp")
    core=lax.axis_index("dim")
    return dp//4,(dp//2)%2,dp%2,core

def meet(z,y,x,core):
    chip=lambda a,b,c: a*4+b*2+c
    peers=[(chip(z,y,x),1-core),(chip(z,y,1-x),core),(chip(z,1-y,x),core)]
    peers+=[(chip(lax.rem(z+k,4),y,x),core) for k in (1,2,3)]
    barrier=pltpu.get_barrier_semaphore()
    for peer in peers:
        pl.semaphore_signal(barrier,inc=1,device_id=peer,device_id_type=MESH)
    pl.semaphore_wait(barrier,len(peers))
    return peers

def lanes_of(cols):
    tiles=cols//128
    widths=[tiles-tiles//4*3]+[tiles//4]*3
    widths=[widths[0],widths[2],widths[1],widths[3]]
    widths=[5,5,4,4] if tiles==18 else widths
    out=[]
    at=0
    for n,w in enumerate(widths):
        out.append((at*128,w*128,n%2==0))
        at+=w
    return out

def send(src,dst,sems,n,k,peer):
    copy=pltpu.make_async_remote_copy(src_ref=src,dst_ref=dst,send_sem=sems[0].at[n,k],recv_sem=sems[1].at[n,k],device_id=peer,device_id_type=MESH)
    copy.start()
    return copy

def gather_kernel(w,out,low,local,s_sem,r_sem):
    z,y,x,core=place()
    low[...]=w[...].astype(BF)
    keep=pltpu.make_async_copy(low,out.at[z,y,x,core],local)
    keep.start()
    pair,xn,yn,z1,z2,z3=meet(z,y,x,core)
    sems=(s_sem,r_sem)
    lanes=lanes_of(w.shape[1])
    every=[]
    def go(n,k,peer,*index,src=None):
        at,width,_=lanes[n]
        dst=out.at[(*index,slice(None),pl.ds(at,width))]
        if src is None: src=dst
        copy=send(src,dst,sems,n,k,peer)
        every.append(copy)
        return copy
    whole=slice(None)
    first=[]
    for n,(at,width,_) in enumerate(lanes):
        piece=low.at[:,pl.ds(at,width)]
        first.append([go(n,k,peer,z,y,x,core,src=piece) for k,peer in enumerate((z1,z2,z3))])
    keep.wait()
    second=[]
    for n,(_,_,flip) in enumerate(lanes):
        for copy in first[n]: copy.wait_recv()
        second.append(go(n,3,yn if flip else xn,whole,y,x,core))
        go(n,5,pair,whole,y,x,core)
    third=[]
    for n,(_,_,flip) in enumerate(lanes):
        second[n].wait_recv()
        if flip:
            third.append(go(n,4,xn,whole,whole,x,core))
            go(n,6,pair,whole,1-y,x,core)
        else:
            third.append(go(n,4,yn,whole,y,whole,core))
            go(n,6,pair,whole,y,1-x,core)
    for n,(_,_,flip) in enumerate(lanes):
        third[n].wait_recv()
        if flip: go(n,7,pair,whole,whole,1-x,core)
        else: go(n,7,pair,whole,1-y,whole,core)
    done=set(id(c) for c in second+third+[c for f in first for c in f])
    for copy in every:
        copy.wait_send()
        if id(copy) not in done: copy.wait_recv()

def ring_gather(w):
    share,cols=w.shape
    out=pl.pallas_call(gather_kernel,
        in_specs=[pl.BlockSpec(memory_space=pltpu.VMEM)],
        out_specs=pl.BlockSpec(memory_space=pl.ANY),
        scratch_shapes=[pltpu.VMEM((share,cols),BF),pltpu.SemaphoreType.DMA,pltpu.SemaphoreType.DMA((4,8)),pltpu.SemaphoreType.DMA((4,8))],
        out_shape=jax.ShapeDtypeStruct((4,2,2,2,share,cols),BF),
        compiler_params=pltpu.CompilerParams(collective_id=1,has_side_effects=True,vmem_limit_bytes=60<<20),
        cost_estimate=pl.CostEstimate(flops=0,bytes_accessed=64*share*cols*20,transcendentals=0),
        name="comm_gather",
    )(w)
    return out.reshape(32*share,cols)

def scatter_kernel(g,out,gl,r0,b1,k1,r1,b2,k2,r2,b3,k3,r3,local,s_sem,r_sem):
    z,y,x,core=place()
    keep=pltpu.make_async_copy(g.at[:,core],gl,local)
    keep.start()
    pair,xn,yn,z1,z2,z3=meet(z,y,x,core)
    sems=(s_sem,r_sem)
    lanes=lanes_of(out.shape[1])
    span=[pl.ds(at,width) for at,width,_ in lanes]
    every=[]
    def go(n,k,peer,src,dst):
        copy=send(src,dst,sems,n,k,peer)
        every.append(copy)
        return copy
    n_lanes=range(len(lanes))
    zero=[go(n,0,pair,g.at[:,1-core,:,span[n]],r0.at[:,:,span[n]]) for n in n_lanes]
    def split1(n,iz,j,side):
        row=iz*4+(j*2+side if lanes[n][2] else side*2+j)
        c=span[n]
        return gl[row,:,c].astype(F32)+r0[row,:,c].astype(F32)
    one=[]
    keep.wait()
    for n in n_lanes:
        flip=lanes[n][2]
        side=x if flip else y
        zero[n].wait_recv()
        for iz in range(4):
            for j in range(2):
                b1[iz,j,:,span[n]]=split1(n,iz,j,1-side).astype(BF)
        one.append(go(n,1,xn if flip else yn,b1.at[:,:,:,span[n]],r1.at[:,:,:,span[n]]))
        for iz in range(4):
            for j in range(2):
                k1[iz,j,:,span[n]]=split1(n,iz,j,side)
    two=[]
    for n in n_lanes:
        flip=lanes[n][2]
        side=y if flip else x
        c=span[n]
        one[n].wait_recv()
        for iz in range(4):
            b2[iz,:,c]=(k1[iz,1-side,:,c]+r1[iz,1-side,:,c].astype(F32)).astype(BF)
        two.append(go(n,2,yn if flip else xn,b2.at[:,:,c],r2.at[:,:,c]))
        for iz in range(4):
            k2[iz,:,c]=k1[iz,side,:,c]+r1[iz,side,:,c].astype(F32)
    three=[]
    for n in n_lanes:
        c=span[n]
        two[n].wait_recv()
        for k in (1,2,3):
            to=lax.rem(z+k,4)
            b3[k-1,:,c]=(k2[to,:,c]+r2[to,:,c].astype(F32)).astype(BF)
        three.append([go(n,2+k,(z1,z2,z3)[k-1],b3.at[k-1,:,c],r3.at[k-1,:,c]) for k in (1,2,3)])
        k3[:,c]=k2[z,:,c]+r2[z,:,c].astype(F32)
    for n in n_lanes:
        c=span[n]
        for copy in three[n]: copy.wait_recv()
        out[:,c]=k3[:,c]+r3[0,:,c].astype(F32)+r3[1,:,c].astype(F32)+r3[2,:,c].astype(F32)
    for copy in every: copy.wait_send()

def ring_scatter(g):
    rows,cols=g.shape
    share=rows//32
    v=lambda *s: pltpu.VMEM((*s,share,cols),BF)
    f=lambda *s: pltpu.VMEM((*s,share,cols),F32)
    return pl.pallas_call(scatter_kernel,
        in_specs=[pl.BlockSpec(memory_space=pl.ANY)],
        out_specs=pl.BlockSpec(memory_space=pltpu.VMEM),
        scratch_shapes=[v(16),v(16),v(4,2),f(4,2),v(4,2),v(4),f(4),v(4),v(3),f(),v(3),pltpu.SemaphoreType.DMA,pltpu.SemaphoreType.DMA((4,6)),pltpu.SemaphoreType.DMA((4,6))],
        out_shape=jax.ShapeDtypeStruct((share,cols),F32),
        compiler_params=pltpu.CompilerParams(collective_id=2,has_side_effects=True,vmem_limit_bytes=60<<20),
        cost_estimate=pl.CostEstimate(flops=0,bytes_accessed=64*share*cols*20,transcendentals=0),
        name="comm_scatter",
    )(g.reshape(16,2,share,cols))

def selector(forward):
    r=lax.broadcasted_iota(jnp.int32,(512,512),0)
    c=lax.broadcasted_iota(jnp.int32,(512,512),1)
    a,b=(r,c) if forward else (c,r)
    return jnp.where(a==4*(b%128)+b//128,1.0,0.0).astype(BF)

def bundle_kernel(exp,con,out,norm,bundle,tiles):
    share,width=out.shape
    hidden=exp.shape[1]//2
    pick=selector(True)
    for b in range(exp.shape[1]//512):
        half,at=divmod(b*512,hidden)
        y=nn(exp[:,b*512:(b+1)*512].astype(BF),pick).astype(BF)
        for j in range(4):
            to=half*hidden+j*width+at//4
            bundle[:,to:to+128]=y[:,j*128:(j+1)*128]
    for t in range(width//128):
        tiles[t]=con[:,t*128:(t+1)*128]
        for j in range(4):
            to=2*hidden+j*width+t*128
            bundle[:,to:to+128]=tiles[t,pl.ds(j,share,stride=4),:].astype(BF)
    bundle[:,3*hidden:3*hidden+width]=out[...].astype(BF)
    flat=jnp.concatenate([norm[...],jnp.zeros((4,128-share),F32)],1)
    bundle[:,3*hidden+width:]=jnp.concatenate([flat,jnp.zeros((share-4,128),F32)],0).astype(BF)

def make_bundle(exp,con,out,norm):
    share,width=out.shape
    total=exp.shape[1]+4*width+width+128
    return pl.pallas_call(bundle_kernel,
        out_shape=jax.ShapeDtypeStruct((share,total),BF),
        scratch_shapes=[pltpu.VMEM((width//128,4*share,128),F32)],
        compiler_params=pltpu.CompilerParams(vmem_limit_bytes=60<<20),
        cost_estimate=pl.CostEstimate(flops=2*share*512*exp.shape[1],bytes_accessed=6*share*total,transcendentals=0),
        name="make_bundle",
    )(exp,con,out,norm)

def update_kernel(rates,sums,*refs):
    ins,outs,tiles=refs[:12],refs[12:32],refs[32]
    exp_w,con_w,out_w,norm_w=(ins[3*k:3*k+3] for k in range(4))
    share,width=out_w[0].shape
    hidden=exp_w[0].shape[1]//2
    def step(kind,index,g,rate):
        w,m,a=(ref[index] for ref in ins[3*kind:3*kind+3])
        grad,nxt,mom,avg,low=outs[5*kind:5*kind+5]
        mn=MOMENTUM*m+g
        wn=w-rate*(g+MOMENTUM*mn)
        grad[index]=g
        nxt[index]=wn
        mom[index]=mn
        avg[index]=AVERAGE_DECAY*a+(1.0-AVERAGE_DECAY)*wn
        low[index]=wn.astype(BF)
    pick=selector(False)
    for b in range(2*hidden//512):
        half,at=divmod(b*512,hidden)
        z=jnp.concatenate([sums[:,half*hidden+j*width+at//4:half*hidden+j*width+at//4+128] for j in range(4)],1)
        step(0,(slice(None),slice(b*512,(b+1)*512)),nn(z,pick),rates[0])
    for t in range(width//128):
        for j in range(4):
            at=2*hidden+j*width+t*128
            tiles[t,pl.ds(j,share,stride=4),:]=sums[:,at:at+128].astype(F32)
        step(1,(slice(None),slice(t*128,(t+1)*128)),tiles[t],rates[0])
    step(2,(slice(None),slice(None)),sums[:,3*hidden:3*hidden+width].astype(F32),rates[0])
    step(3,(slice(None),slice(None)),sums[0:8,3*hidden+width:].astype(F32)[0:4,0:share],rates[1])

def update(sums,rates,params):
    sds=jax.ShapeDtypeStruct
    shapes=[]
    for w,_,_ in params:
        shapes+=[sds(w.shape,F32)]*4+[sds(w.shape,BF)]
    flat=[x for p in params for x in p]
    import_vmem=pl.BlockSpec(memory_space=pltpu.VMEM)
    outs=pl.pallas_call(lambda *refs: update_kernel(rates,*refs),
        in_specs=[import_vmem]*13,
        out_specs=[import_vmem]*20,
        out_shape=shapes,
        scratch_shapes=[pltpu.VMEM((params[2][0].shape[1]//128,params[1][0].shape[0],128),F32)],
        compiler_params=pltpu.CompilerParams(vmem_limit_bytes=60<<20),
        cost_estimate=pl.CostEstimate(flops=2*24*512*6144,bytes_accessed=12<<20,transcendentals=0),
        name="update",
    )(sums,*flat)
    return [outs[5*k:5*k+5] for k in range(4)]

def tail_kernel(ctl,x,qo,ko,vo,qr,kr,vr,w,df,tok,gm,acc):
    pos=ctl[0]
    i=pl.program_id(0)
    width=x.shape[1]
    turned=x[...].T
    total=df[...]
    @pl.when(i==0)
    def _(): acc[...]=jnp.zeros_like(acc)
    for s,(mine,theirs) in enumerate(((qo,qr),(ko,kr),(vo,vr))):
        a=mine[...]
        b=theirs[...]
        grad=jnp.concatenate([jnp.where(pos==0,a,b),jnp.where(pos==0,b,a)],1)
        cols=slice(s*width,(s+1)*width)
        total=total+nt(grad,w[:,cols])
        acc[:,cols]+=nn(turned,grad)
    tok[...]=total
    @pl.when(i==pl.num_programs(0)-1)
    def _(): gm[...]=acc[...].astype(BF)

def tail(ctl,x,own,recv,w,df):
    rows,width=x.shape
    cols=w.shape[1]
    row=lambda n: pl.BlockSpec((512,n),lambda i,c:(i,0))
    held=pl.BlockSpec((width,cols),lambda i,c:(0,0),pipeline_mode=pl.Buffered(1))
    return pl.pallas_call(tail_kernel,
        grid_spec=pltpu.PrefetchScalarGridSpec(num_scalar_prefetch=1,grid=(rows//512,),
          in_specs=[row(width)]+[row(width//2)]*6+[held,row(width)],
          out_specs=[row(width),pl.BlockSpec((width,cols),lambda i,c:(0,0))],
          scratch_shapes=[pltpu.VMEM((width,cols),F32)]),
        out_shape=[jax.ShapeDtypeStruct((rows,width),F32),jax.ShapeDtypeStruct((width,cols),BF)],
        compiler_params=pltpu.CompilerParams(vmem_limit_bytes=60<<20,dimension_semantics=("arbitrary",)),
        cost_estimate=pl.CostEstimate(flops=4*rows*width*cols,bytes_accessed=rows*width*16+8*width*cols,transcendentals=0),
        name="tail",
    )(ctl,x,*own,*recv,w,df)

def mix_kernel(ctl,x,w,cos,sin,own,oth):
    pos=ctl[0]
    width=x.shape[1]
    share=width//2
    xb=x[...]
    c=cos[...]
    s=sin[...]
    lane=lax.broadcasted_iota(jnp.int32,c.shape,1)
    first=(lane%64)<32
    for part in range(3):
        y=nn(xb,w[:,part*width:(part+1)*width])
        tiles=[]
        for t in range(width//128):
            z=y[:,t*128:(t+1)*128]
            if part<2:
                swapped=jnp.where(first,pltpu.roll(z,96,1),pltpu.roll(z,32,1))
                z=z*c+swapped*s
            tiles.append(z.astype(BF))
        count=share//128
        for t in range(count):
            cols=slice(part*share+t*128,part*share+(t+1)*128)
            own[:,cols]=jnp.where(pos==0,tiles[t],tiles[count+t])
            oth[:,cols]=jnp.where(pos==0,tiles[count+t],tiles[t])

def mix(ctl,x,w,cos,sin):
    rows,width=x.shape
    cols=w.shape[1]
    block=256
    row=lambda n: pl.BlockSpec((block,n),lambda i,c:(i,0))
    angle=pl.BlockSpec((block,128),lambda i,c:(c[0]*(rows//block)+i,0))
    return pl.pallas_call(mix_kernel,
        grid_spec=pltpu.PrefetchScalarGridSpec(num_scalar_prefetch=1,grid=(rows//block,),
          in_specs=[row(width),pl.BlockSpec((width,cols),lambda i,c:(0,0)),angle,angle],
          out_specs=[row(cols//2)]*2),
        out_shape=[jax.ShapeDtypeStruct((rows,cols//2),BF)]*2,
        compiler_params=pltpu.CompilerParams(vmem_limit_bytes=60<<20,dimension_semantics=("arbitrary",)),
        cost_estimate=pl.CostEstimate(flops=2*rows*width*cols,bytes_accessed=2*(rows*width+width*cols+rows*cols),transcendentals=0),
        name="mix",
    )(ctl,x,w,cos,sin)

def swap_cores(x):
    return lax.ppermute(x,"dim",[(0,1),(1,0)])

def join(pos,own,recv,axis=1):
    return jnp.where(pos==0,jnp.concatenate([own,recv],axis),jnp.concatenate([recv,own],axis))

def body(tokens,doc_lengths,pair_index,target_bank,mixer_in,mixer_out,expand,contract,norm_params,*rest):
    slices=lax.axis_size("dim")
    if slices!=2 or lax.axis_size("dp")!=16 or doc_lengths.shape[1]!=2:
        return body_general(tokens,doc_lengths,pair_index,target_bank,mixer_in,mixer_out,expand,contract,norm_params,*rest)
    (mixer_in_moment,mixer_out_moment,expand_moment,contract_moment,norm_moment,
     mixer_in_average,mixer_out_average,expand_average,contract_average,norm_average)=rest
    local_rows,model_width=tokens.shape
    group_rows=local_rows*slices
    pos=lax.axis_index("dim")
    doc_count=2
    w_mix=ring_gather(mixer_in[0])
    share_rows=mixer_out.shape[1]
    per=contract.shape[1]//share_rows
    count=model_width//share_rows
    hidden_width=contract.shape[1]*count
    bundle=make_bundle(expand[0],contract[0],mixer_out[0],norm_params[0])
    bundle=lax.all_gather(bundle,("dp","dim"),axis=0,tiled=True)
    at1=2*hidden_width
    at2=at1+per*model_width
    at3=at2+model_width
    w_norm=bundle[:,at3:].reshape(count,share_rows,128)[:,0:4,0:share_rows].transpose(1,0,2).reshape(4,model_width)
    lengths=doc_lengths[0]
    e0=lengths[0]
    e1=lengths[0]+lengths[1]
    ctl=jnp.stack([pos.astype(jnp.int32),e0,e1])
    ids=jnp.arange(group_rows,dtype=jnp.int32)
    seg=(ids>=e0).astype(jnp.int32)+(ids>=e1).astype(jnp.int32)
    begin=jnp.where(seg==0,0,jnp.where(seg==1,e0,e1))
    lane=jnp.arange(128,dtype=jnp.int32)
    frequency=jnp.power(1000.0,-(2*(lane%32)).astype(F32)/HEAD)
    angles=(ids-begin).astype(F32)[:,None]*frequency[None,:]
    cos=jnp.cos(angles)
    sin=jnp.sin(angles)*jnp.where((lane%64)<32,-1.0,1.0)[None,:]
    own,oth=mix(ctl,tokens,w_mix,cos,sin)
    recv=swap_cores(oth)
    pick=(pair_index[:,None]==jnp.arange(target_bank.shape[0],dtype=jnp.int32)[None,:]).astype(BF)
    some=matmul(pick,target_bank)
    targets=jnp.pad(join(pos,some,swap_cores(some)),((0,6),(0,0)))
    o_own,o_oth,lse=attend_fwd(ctl,own,recv)
    o_recv=swap_cores(o_oth)
    norm_gains=jnp.pad(w_norm.astype(F32),((0,4),(0,0)))
    u1,u2,rs,y_low,*hidden,factors,pooled=ffn_fwd(ctl,o_own,o_recv,tokens,bundle,norm_gains,hidden_width)
    embeds,grad_m_low,grad_both,grad_first,grad_a_low,d_own,d_oth,grad_norm=ffn_bwd(
        ctl,lengths.astype(F32),pooled,swap_cores(pooled),targets,u1,u2,rs,factors,bundle,norm_gains)
    share=model_width//2
    embeddings=lax.dynamic_slice(embeds,(0,pos*share),(doc_count,share))
    d_recv=swap_cores(d_oth)
    grad_exp=inner_rows(y_low,grad_both)
    grad_con=[inner_rows(h,grad_m_low).astype(BF) for h in hidden]
    grad_out=join(pos,inner_rows(o_own,grad_a_low),inner_rows(o_recv,grad_a_low),0)
    grad_norm=grad_norm[0:4].reshape(4,count,share_rows).transpose(1,0,2)
    grad_norm=jnp.pad(grad_norm,((0,0),(0,share_rows-4),(0,128-share_rows))).reshape(model_width,128)
    terms=jnp.concatenate([grad_exp.astype(BF),*grad_con,grad_out.astype(BF),grad_norm.astype(BF)],1)
    terms,d_own,d_recv=lax.optimization_barrier((terms,d_own,d_recv))
    sums=lax.psum_scatter(terms,("dp","dim"),scatter_dimension=0,tiled=True)
    backs=attend_bwd(ctl,own,recv,d_own,d_recv,o_own,o_oth,lse,cos,sin)
    token_grads,grad_mix=tail(ctl,tokens,backs[0:3],[swap_cores(g) for g in backs[3:6]],w_mix,grad_first)
    total_rows=group_rows*lax.axis_size("dp")
    matrix_rate=1.0/math.sqrt(total_rows)
    norm_rate=0.3/math.sqrt(total_rows)
    new_exp,new_con,new_out,new_norm=update(sums,(matrix_rate,norm_rate),[
        (expand[0],expand_moment[0],expand_average[0]),(contract[0],contract_moment[0],contract_average[0]),
        (mixer_out[0],mixer_out_moment[0],mixer_out_average[0]),(norm_params[0],norm_moment[0],norm_average[0])])
    sum_mix=ring_scatter(grad_mix)
    nxt,mom,avg,low=advance(mixer_in[0],mixer_in_moment[0],mixer_in_average[0],sum_mix,matrix_rate)
    results=[[sum_mix,nxt,mom,avg,low],new_out,new_exp,new_con,new_norm]
    return (embeddings,token_grads,*[results[k][f][None] for f in range(5) for k in range(5)])

def solution(mesh):
    placed = (
        P(("dp", "dim"), None),
        P("dp", None),
        P("dp"),
        P(None, "dim"),
        P(None, ("dp", "dim"), None),
        P(None, ("dp", "dim"), None),
        P(None, ("dp", "dim"), None),
        P(None, ("dp", "dim"), None),
        P(None, None, ("dp", "dim")),
        P(None, ("dp", "dim"), None),
        P(None, ("dp", "dim"), None),
        P(None, ("dp", "dim"), None),
        P(None, ("dp", "dim"), None),
        P(None, None, ("dp", "dim")),
        P(None, ("dp", "dim"), None),
        P(None, ("dp", "dim"), None),
        P(None, ("dp", "dim"), None),
        P(None, ("dp", "dim"), None),
        P(None, None, ("dp", "dim")),
    )
    return jax.shard_map(
        body,
        mesh=mesh,
        in_specs=placed,
        out_specs=(
            P("dp", "dim"),
            P(("dp", "dim"), None),
            P(None, ("dp", "dim"), None),
            P(None, ("dp", "dim"), None),
            P(None, ("dp", "dim"), None),
            P(None, ("dp", "dim"), None),
            P(None, None, ("dp", "dim")),
            P(None, ("dp", "dim"), None),
            P(None, ("dp", "dim"), None),
            P(None, ("dp", "dim"), None),
            P(None, ("dp", "dim"), None),
            P(None, None, ("dp", "dim")),
            P(None, ("dp", "dim"), None),
            P(None, ("dp", "dim"), None),
            P(None, ("dp", "dim"), None),
            P(None, ("dp", "dim"), None),
            P(None, None, ("dp", "dim")),
            P(None, ("dp", "dim"), None),
            P(None, ("dp", "dim"), None),
            P(None, ("dp", "dim"), None),
            P(None, ("dp", "dim"), None),
            P(None, None, ("dp", "dim")),
            P(None, ("dp", "dim"), None),
            P(None, ("dp", "dim"), None),
            P(None, ("dp", "dim"), None),
            P(None, ("dp", "dim"), None),
            P(None, None, ("dp", "dim")),
        ),
        check_vma=False,
    )
```

```python
import functools
import math

import jax
import jax.numpy as jnp
from jax import lax
from jax.experimental import pallas as pl
from jax.experimental.pallas import tpu as pltpu
from jax.sharding import PartitionSpec as P

HEAD = 64


NORM_EPSILON = 1e-05
COSINE_EPSILON = 1e-06
MOMENTUM = 0.5
AVERAGE_DECAY = 0.5
PRECISE = lax.Precision.HIGHEST
MASKED = -1e30


def matmul(left_op, right_op):
    return jnp.dot(left_op, right_op, preferred_element_type=jnp.float32)


def matmul_exact(left_op, right_op):
    return jnp.dot(left_op, right_op, precision=PRECISE, preferred_element_type=jnp.float32)


def inner_rows(left_op, right_op):
    return lax.dot_general(
        left_op, right_op, (((0,), (0,)), ((), ())), preferred_element_type=jnp.float32
    )


def inner_cols(left_op, right_op):
    return lax.dot_general(
        left_op, right_op, (((1,), (1,)), ((), ())), preferred_element_type=jnp.float32
    )


def rotate(values, cosines, sines):
    row_count = values.shape[0]
    shaped = values.reshape(row_count, -1, 2, HEAD // 2)
    former = shaped[:, :, 0, :]
    latter = shaped[:, :, 1, :]
    cosine_b = cosines[:, None, :]
    sine_b = sines[:, None, :]
    turned = jnp.stack(
        [former * cosine_b - latter * sine_b, latter * cosine_b + former * sine_b], axis=2
    )
    return turned.reshape(values.shape)


def rotate_back(grads_in, cosines, sines):
    row_count = grads_in.shape[0]
    shaped = grads_in.reshape(row_count, -1, 2, HEAD // 2)
    former = shaped[:, :, 0, :]
    latter = shaped[:, :, 1, :]
    cosine_b = cosines[:, None, :]
    sine_b = sines[:, None, :]
    turned = jnp.stack(
        [former * cosine_b + latter * sine_b, latter * cosine_b - former * sine_b], axis=2
    )
    return turned.reshape(grads_in.shape)


def normalize(summed, gain_vec, bias_vec):
    centred = summed - jnp.mean(summed, axis=1, keepdims=True)
    scaling = lax.rsqrt(jnp.mean(centred * centred, axis=1, keepdims=True) + NORM_EPSILON)
    return centred * scaling * gain_vec + bias_vec


def normalize_back(grad_in, summed, gain_vec):
    centred = summed - jnp.mean(summed, axis=1, keepdims=True)
    scaling = lax.rsqrt(jnp.mean(centred * centred, axis=1, keepdims=True) + NORM_EPSILON)
    unit = centred * scaling
    grad_unit = grad_in * gain_vec
    grad_sum = scaling * (
        grad_unit
        - jnp.mean(grad_unit, axis=1, keepdims=True)
        - unit * jnp.mean(grad_unit * unit, axis=1, keepdims=True)
    )
    return (grad_sum, jnp.sum(grad_in * unit, axis=0), jnp.sum(grad_in, axis=0))


def flatten(stacked):
    return stacked.transpose(1, 0, 2).reshape(stacked.shape[1], -1)


def attend(q_rot, all_keys, all_values, same_doc):
    head_count = q_rot.shape[1] // HEAD

    def one_head(head_pos):
        offset = head_pos * HEAD
        query_part = lax.dynamic_slice_in_dim(q_rot, offset, HEAD, 1)
        key_part = lax.dynamic_slice_in_dim(all_keys, offset, HEAD, 1)
        value_part = lax.dynamic_slice_in_dim(all_values, offset, HEAD, 1)
        scores = jnp.where(same_doc, inner_cols(query_part, key_part) * 0.125, MASKED)
        row_max = jnp.max(scores, axis=1, keepdims=True)
        exponent = jnp.exp(scores - row_max)
        row_total = jnp.sum(exponent, axis=1, keepdims=True)
        attn_probs = (exponent / row_total).astype(jnp.bfloat16)
        return (matmul(attn_probs, value_part), (row_max + jnp.log(row_total))[:, 0])

    outputs, log_totals = lax.map(one_head, jnp.arange(head_count, dtype=jnp.int32))
    return (flatten(outputs), log_totals)


def attend_back(q_rot, all_keys, all_values, same_doc, grad_out, log_totals):
    head_count = q_rot.shape[1] // HEAD

    def one_head(pack):
        head_pos, log_total = pack
        offset = head_pos * HEAD
        query_part = lax.dynamic_slice_in_dim(q_rot, offset, HEAD, 1)
        key_part = lax.dynamic_slice_in_dim(all_keys, offset, HEAD, 1)
        value_part = lax.dynamic_slice_in_dim(all_values, offset, HEAD, 1)
        grad_part = lax.dynamic_slice_in_dim(grad_out, offset, HEAD, 1)
        scores = jnp.where(same_doc, inner_cols(query_part, key_part) * 0.125, MASKED)
        attn_probs = jnp.exp(scores - log_total[:, None])
        grad_probs = inner_cols(grad_part, value_part)
        row_dot = jnp.sum(attn_probs * grad_probs, axis=1, keepdims=True)
        grad_scores = (attn_probs * (grad_probs - row_dot)).astype(jnp.bfloat16)
        grad_query = matmul(grad_scores, key_part) * 0.125
        grad_key = inner_rows(grad_scores, query_part) * 0.125
        grad_value = inner_rows(attn_probs.astype(jnp.bfloat16), grad_part)
        return (grad_query, grad_key, grad_value)

    mapped = lax.map(one_head, (jnp.arange(head_count, dtype=jnp.int32), log_totals))
    return (flatten(mapped[0]), flatten(mapped[1]), flatten(mapped[2]))


def advance(weight, moment, average, grad_in, rate):
    moment_next = MOMENTUM * moment + grad_in
    weight_next = weight - rate * (grad_in + MOMENTUM * moment_next)
    average_next = AVERAGE_DECAY * average + (1.0 - AVERAGE_DECAY) * weight_next
    return (weight_next, moment_next, average_next, weight_next.astype(jnp.bfloat16))


def body_general(
    tokens,
    doc_lengths,
    pair_index,
    target_bank,
    mixer_in,
    mixer_out,
    expand,
    contract,
    norm_params,
    mixer_in_moment,
    mixer_out_moment,
    expand_moment,
    contract_moment,
    norm_moment,
    mixer_in_average,
    mixer_out_average,
    expand_average,
    contract_average,
    norm_average,
):
    local_rows, model_width = tokens.shape
    slices = lax.axis_size("dim")
    group_rows = local_rows * slices
    position = lax.axis_index("dim")
    layer_count = mixer_in.shape[0]
    doc_count = doc_lengths.shape[1]
    lengths = doc_lengths[0]
    doc_ends = jnp.cumsum(lengths)
    doc_starts = doc_ends - lengths
    row_ids = position * local_rows + jnp.arange(local_rows, dtype=jnp.int32)
    key_ids = jnp.arange(group_rows, dtype=jnp.int32)
    seg_rows = jnp.sum((row_ids[:, None] >= doc_ends[None, :]).astype(jnp.int32), axis=1)
    seg_keys = jnp.sum((key_ids[:, None] >= doc_ends[None, :]).astype(jnp.int32), axis=1)
    first_rows = jnp.concatenate([doc_starts, doc_ends[-1:]])
    segment_ids = jnp.arange(doc_count + 1, dtype=jnp.int32)
    row_begin = jnp.sum(
        jnp.where(seg_rows[:, None] == segment_ids[None, :], first_rows[None, :], 0), axis=1
    )
    frequency = jnp.power(1000.0, -jnp.arange(0, HEAD, 2).astype(jnp.float32) / HEAD)
    angles = (row_ids - row_begin).astype(jnp.float32)[:, None] * frequency[None, :]
    cosines = jnp.cos(angles)
    sines = jnp.sin(angles)
    same_doc = seg_rows[:, None] == seg_keys[None, :]
    stream = tokens.astype(jnp.float32)
    layer_pos = 0
    layer_weights = (
        lax.all_gather(mixer_in[layer_pos].astype(jnp.bfloat16), ("dp", "dim"), axis=0, tiled=True),
        lax.all_gather(
            mixer_out[layer_pos].astype(jnp.bfloat16), ("dp", "dim"), axis=0, tiled=True
        ),
        lax.all_gather(expand[layer_pos].astype(jnp.bfloat16), ("dp", "dim"), axis=0, tiled=True),
        lax.all_gather(contract[layer_pos].astype(jnp.bfloat16), ("dp", "dim"), axis=0, tiled=True),
        lax.all_gather(
            norm_params[layer_pos].astype(jnp.bfloat16), ("dp", "dim"), axis=1, tiled=True
        ),
    )
    w_mix, w_out, w_exp, w_con, w_norm = layer_weights
    norm_gains = w_norm.astype(jnp.float32)
    x_low = stream.astype(jnp.bfloat16)
    mixed = matmul(x_low, w_mix)
    q_rot = rotate(mixed[:, 0:model_width], cosines, sines).astype(jnp.bfloat16)
    k_rot = rotate(mixed[:, model_width : 2 * model_width], cosines, sines).astype(jnp.bfloat16)
    v_low = mixed[:, 2 * model_width : 3 * model_width].astype(jnp.bfloat16)
    all_keys = lax.all_gather(k_rot, "dim", axis=0, tiled=True)
    all_values = lax.all_gather(v_low, "dim", axis=0, tiled=True)
    attended, log_totals = attend(q_rot, all_keys, all_values, same_doc)
    att_low = attended.astype(jnp.bfloat16)
    first_sum = stream + matmul(att_low, w_out)
    normed = normalize(first_sum, norm_gains[0], norm_gains[1])
    y_low = normed.astype(jnp.bfloat16)
    gate_up = matmul(y_low, w_exp)
    half = gate_up.shape[1] // 2
    hidden = (jax.nn.silu(gate_up[:, 0:half]) * gate_up[:, half : 2 * half]).astype(jnp.bfloat16)
    second_sum = normed + matmul(hidden, w_con)
    saved = [
        (
            stream,
            layer_weights,
            q_rot,
            k_rot,
            v_low,
            all_keys,
            all_values,
            log_totals,
            attended,
            att_low,
            first_sum,
            normed,
            y_low,
            gate_up,
            hidden,
            second_sum,
        )
    ]
    stream = normalize(second_sum, norm_gains[2], norm_gains[3])
    member = (seg_rows[None, :] == jnp.arange(doc_count, dtype=jnp.int32)[:, None]).astype(
        jnp.float32
    )
    partial_value = matmul_exact(member, stream)
    pooled = lax.psum_scatter(partial_value, "dim", scatter_dimension=1, tiled=True)
    length_f = lengths.astype(jnp.float32)
    embeddings = pooled / length_f[:, None]
    share = embeddings.shape[1]
    pick = (
        pair_index[:, None] == jnp.arange(target_bank.shape[0], dtype=jnp.int32)[None, :]
    ).astype(jnp.bfloat16)
    targets = matmul(pick, target_bank)
    feature_ids = position * share + jnp.arange(share, dtype=jnp.int32)
    cuts = jnp.array(
        [model_width // 12, model_width // 6, model_width // 3, 2 * model_width // 3, model_width],
        dtype=jnp.int32,
    )
    masks = (feature_ids[None, :] < cuts[:, None]).astype(jnp.float32)
    cross = matmul_exact(embeddings * targets, masks.T)
    own = matmul_exact(embeddings * embeddings, masks.T)
    other = matmul_exact(targets * targets, masks.T)
    cross, own, other = lax.psum((cross, own, other), "dim")
    own_root = lax.rsqrt(own + COSINE_EPSILON)
    other_root = lax.rsqrt(other + COSINE_EPSILON)
    cosine = cross * own_root * other_root
    coef_target = -length_f[:, None] * own_root * other_root
    coef_self = length_f[:, None] * cosine * own_root * own_root
    grad_emb = (
        matmul_exact(coef_target, masks) * targets + matmul_exact(coef_self, masks) * embeddings
    )
    grad_full = lax.all_gather(grad_emb, "dim", axis=1, tiled=True)
    spread_rows = member / length_f[:, None]
    grad_stream = lax.dot_general(
        spread_rows,
        grad_full,
        (((0,), (0,)), ((), ())),
        precision=PRECISE,
        preferred_element_type=jnp.float32,
    )
    grad_list = [None] * layer_count
    for layer_pos in reversed(range(layer_count)):
        (
            layer_input,
            layer_weights,
            q_rot,
            k_rot,
            v_low,
            all_keys,
            all_values,
            log_totals,
            attended,
            att_low,
            first_sum,
            normed,
            y_low,
            gate_up,
            hidden,
            second_sum,
        ) = saved[layer_pos]
        w_mix = lax.all_gather(
            mixer_in[layer_pos].astype(jnp.bfloat16), ("dp", "dim"), axis=0, tiled=True
        )
        w_out = lax.all_gather(
            mixer_out[layer_pos].astype(jnp.bfloat16), ("dp", "dim"), axis=0, tiled=True
        )
        w_exp = lax.all_gather(
            expand[layer_pos].astype(jnp.bfloat16), ("dp", "dim"), axis=0, tiled=True
        )
        w_con = lax.all_gather(
            contract[layer_pos].astype(jnp.bfloat16), ("dp", "dim"), axis=0, tiled=True
        )
        w_norm = lax.all_gather(
            norm_params[layer_pos].astype(jnp.bfloat16), ("dp", "dim"), axis=1, tiled=True
        )
        norm_gains = w_norm.astype(jnp.float32)
        grad_second, grad_gain2, grad_bias2 = normalize_back(grad_stream, second_sum, norm_gains[2])
        grad_m_low = grad_second.astype(jnp.bfloat16)
        grad_con = inner_rows(hidden, grad_m_low)
        grad_hidden = inner_cols(grad_m_low, w_con)
        half = gate_up.shape[1] // 2
        gate_part = gate_up[:, 0:half]
        up_part = gate_up[:, half : 2 * half]
        sigmoid_gate = jax.nn.sigmoid(gate_part)
        activated = gate_part * sigmoid_gate
        grad_gate = grad_hidden * up_part * sigmoid_gate * (1.0 + gate_part * (1.0 - sigmoid_gate))
        grad_up = grad_hidden * activated
        grad_both = jnp.concatenate([grad_gate, grad_up], axis=1).astype(jnp.bfloat16)
        grad_exp = inner_rows(y_low, grad_both)
        grad_normed = grad_second + inner_cols(grad_both, w_exp)
        grad_first, grad_gain1, grad_bias1 = normalize_back(grad_normed, first_sum, norm_gains[0])
        grad_a_low = grad_first.astype(jnp.bfloat16)
        grad_out = inner_rows(att_low, grad_a_low)
        grad_attended = inner_cols(grad_a_low, w_out).astype(jnp.bfloat16)
        keys_back, values_back = (
            lax.all_gather(k_rot, "dim", axis=0, tiled=True),
            lax.all_gather(v_low, "dim", axis=0, tiled=True),
        )
        grad_query, grad_key_all, grad_value_all = attend_back(
            q_rot, keys_back, values_back, same_doc, grad_attended, log_totals
        )
        grad_kv = lax.psum_scatter(
            jnp.concatenate([grad_key_all, grad_value_all], axis=1).astype(jnp.bfloat16),
            "dim",
            scatter_dimension=0,
            tiled=True,
        ).astype(jnp.float32)
        grad_mixed = jnp.concatenate(
            [
                rotate_back(grad_query, cosines, sines),
                rotate_back(grad_kv[:, 0:model_width], cosines, sines),
                grad_kv[:, model_width : 2 * model_width],
            ],
            axis=1,
        ).astype(jnp.bfloat16)
        x_low = layer_input.astype(jnp.bfloat16)
        grad_mix = inner_rows(x_low, grad_mixed)
        grad_stream = grad_first + inner_cols(grad_mixed, w_mix)
        grad_norm = jnp.stack([grad_gain1, grad_bias1, grad_gain2, grad_bias2])
        grad_list[layer_pos] = (
            lax.psum_scatter(grad_mix, ("dp", "dim"), scatter_dimension=0, tiled=True),
            lax.psum_scatter(grad_out, ("dp", "dim"), scatter_dimension=0, tiled=True),
            lax.psum_scatter(grad_exp, ("dp", "dim"), scatter_dimension=0, tiled=True),
            lax.psum_scatter(grad_con, ("dp", "dim"), scatter_dimension=0, tiled=True),
            lax.psum_scatter(grad_norm, ("dp", "dim"), scatter_dimension=1, tiled=True),
        )
    total_rows = group_rows * lax.axis_size("dp")
    matrix_rate = 1.0 / math.sqrt(total_rows)
    norm_rate = 0.3 / math.sqrt(total_rows)
    grads = [jnp.stack([grad_list[0][kind]]) for kind in range(5)]
    weights = (mixer_in, mixer_out, expand, contract, norm_params)
    moments = (mixer_in_moment, mixer_out_moment, expand_moment, contract_moment, norm_moment)
    averages = (mixer_in_average, mixer_out_average, expand_average, contract_average, norm_average)
    rates = (matrix_rate, matrix_rate, matrix_rate, matrix_rate, norm_rate)
    results = [
        advance(weights[kind], moments[kind], averages[kind], grads[kind], rates[kind])
        for kind in range(5)
    ]
    return (
        embeddings,
        grad_stream,
        grads[0],
        grads[1],
        grads[2],
        grads[3],
        grads[4],
        results[0][0],
        results[1][0],
        results[2][0],
        results[3][0],
        results[4][0],
        results[0][1],
        results[1][1],
        results[2][1],
        results[3][1],
        results[4][1],
        results[0][2],
        results[1][2],
        results[2][2],
        results[3][2],
        results[4][2],
        results[0][3],
        results[1][3],
        results[2][3],
        results[3][3],
        results[4][3],
    )


NEG=-1e30
BQ=512
ROWS=256
BK=384
FK=512
F32=jnp.float32
BF=jnp.bfloat16

def nt(a,b): return lax.dot_general(a,b,(((1,),(1,)),((),())),preferred_element_type=F32)
def nn(a,b): return jnp.dot(a,b,preferred_element_type=F32)

def fill_masks(e0,e1,kaug,q0,q1,rows,pad):
    r=lax.broadcasted_iota(jnp.int32,(rows+pad,128),0)
    l=lax.broadcasted_iota(jnp.int32,(rows+pad,128),1)
    seg=(r>=e0).astype(jnp.int32)+(r>=e1).astype(jnp.int32)
    kaug[:,128:256]=jnp.where((l<3)&(l!=seg),NEG,0.0).astype(BF)
    qm=jnp.where(l==seg,1.0,0.0).astype(BF)[0:rows]
    q0[:,128:256]=qm
    q1[:,128:256]=qm

def key_range(i,e0,e1,step):
    first=i*BQ
    last=jnp.minimum(first+BQ,e1)-1
    lo=jnp.where(first>=e0,e0,0)
    hi=jnp.where(last>=e0,e1,e0)
    base=(lo//128)*128
    return pl.multiple_of(base,128),(hi-base+step-1)//step

def wide_fits(i,e0,e1):
    return key_range(i,e0,e1,FK)[1]*FK<=key_range(i,e0,e1,BK)[1]*BK

def fwd_kernel(ctl,qo,ko,vo,qr,kr,vr,oo,ox,lse,kaug,q0,q1,vt):
    rows=kaug.shape[0]-FK
    half=rows//2
    pos,e0,e1=ctl[0],ctl[1],ctl[2]
    p=pl.program_id(0)
    @pl.when(p==0)
    def _():
        fill_masks(e0,e1,kaug,q0,q1,rows,FK)
        kaug[rows:,0:128]=jnp.zeros((FK,128),BF)
        vt[:,:]=jnp.where(lax.broadcasted_iota(jnp.int32,vt.shape,0)%80>=64,1.0,0.0).astype(BF)
    pick_r=lax.broadcasted_iota(jnp.int32,(16,128),0)
    pick_l=lax.broadcasted_iota(jnp.int32,(16,128),1)
    pick=jnp.where(pick_l//64==pick_r,1.0,0.0).astype(BF)
    q_top=jnp.zeros((16,1),F32)
    k_top=jnp.zeros((16,1),F32)
    lane=lax.broadcasted_iota(jnp.int32,(half,128),1)
    for own,(q,k,v) in ((True,(qo,ko,vo)),(False,(qr,kr,vr))):
        at=pl.multiple_of((pos if own else 1-pos)*half,half)
        scaled=q[...]*jnp.asarray(0.125,BF)
        zero=jnp.zeros_like(scaled)
        q0[pl.ds(at,half),0:128]=jnp.where(lane<64,scaled,zero)
        q1[pl.ds(at,half),0:128]=jnp.where(lane<64,zero,scaled)
        kb=k[...]
        kaug[pl.ds(at,half),0:128]=kb
        q_top=jnp.maximum(q_top,jnp.max(nt(pick,scaled*scaled),axis=1,keepdims=True))
        k_top=jnp.maximum(k_top,jnp.max(nt(pick,kb*kb),axis=1,keepdims=True))
        turned=v[...].T
        vt[0:64,pl.ds(at,half)]=turned[0:64]
        vt[80:144,pl.ds(at,half)]=turned[64:128]
    narrow=jnp.max(q_top*k_top)*1.05<=1600.0
    def qnarrow(i,_):
        r0=pl.multiple_of(i*BQ,BQ)
        base,count=key_range(i,e0,e1,FK)
        qs=(q0[pl.ds(r0,BQ),:],q1[pl.ds(r0,BQ),:])
        def step(j,carry):
            k0=pl.multiple_of(base+j*FK,128)
            kb=kaug[pl.ds(k0,FK),:]
            pt=[jnp.exp(nt(kb,qs[h])).astype(BF) for h in range(2)]
            return tuple(carry[h]+nn(vt[80*h:80*h+80,pl.ds(k0,FK)],pt[h]) for h in range(2))
        init=jnp.zeros((80,BQ),F32)
        res=lax.fori_loop(0,count,step,(init,init))
        outs=[]
        for h in range(2):
            l=jnp.maximum(res[h][64:65],1e-30)
            outs.append(res[h][0:64]/l)
            lse[0,h:h+1,pl.ds(r0,BQ)]=jnp.where(l>1e-30,jnp.log(l),1e30)
        put(i,jnp.concatenate(outs,axis=0).T.astype(BF))
        return 0
    def qblock(i,_):
        r0=pl.multiple_of(i*BQ,BQ)
        base,count=key_range(i,e0,e1,FK)
        qs=(q0[pl.ds(r0,BQ),:],q1[pl.ds(r0,BQ),:])
        def step(j,carry):
            k0=pl.multiple_of(base+j*FK,128)
            kb=kaug[pl.ds(k0,FK),:]
            scores=[nt(kb,qs[h]) for h in range(2)]
            out=[]
            for h in range(2):
                m,acc=carry[h]
                mn=jnp.maximum(m,jnp.max(scores[h],axis=0,keepdims=True))
                pt=jnp.exp(scores[h]-mn).astype(BF)
                acc=acc*jnp.exp(m-mn)+nn(vt[80*h:80*h+80,pl.ds(k0,FK)],pt)
                out.append((mn,acc))
            return tuple(out)
        init=(jnp.full((1,BQ),-jnp.inf,F32),jnp.zeros((80,BQ),F32))
        res=lax.fori_loop(0,count,step,(init,init))
        outs=[]
        for h in range(2):
            m,acc=res[h]
            l=acc[64:65]
            outs.append(acc[0:64]/l)
            lse[0,h:h+1,pl.ds(r0,BQ)]=jnp.where(m>-1e29,m+jnp.log(l),1e30)
        ob=jnp.concatenate(outs,axis=0).T.astype(BF)
        put(i,ob)
        return 0
    def put(i,ob):
        local=i*BQ-pos*half
        @pl.when((local>=0)&(local<half))
        def _(): oo[pl.ds(pl.multiple_of(local,BQ),BQ),:]=ob
        @pl.when((local<0)|(local>=half))
        def _(): ox[pl.ds(pl.multiple_of(i*BQ-(1-pos)*half,BQ),BQ),:]=ob
    used=(e1+BQ-1)//BQ
    @pl.when(narrow)
    def _(): lax.fori_loop(0,used,qnarrow,0)
    @pl.when(jnp.logical_not(narrow))
    def _(): lax.fori_loop(0,used,qblock,0)
    def blank(i,_):
        r0=pl.multiple_of(i*BQ,BQ)
        lse[0,:,pl.ds(r0,BQ)]=jnp.zeros((8,BQ),F32)
        put(i,jnp.zeros((BQ,128),BF))
        return 0
    lax.fori_loop(used,rows//BQ,blank,0)

def attend_fwd(ctl,own,recv):
    half,width=own.shape
    pairs=width//384
    rows=2*half
    sp=[pl.BlockSpec((half,128),(lambda p,c,s=s:(0,s*pairs+p))) for s in range(3)]
    outw=pairs*128
    return pl.pallas_call(fwd_kernel,
        grid_spec=pltpu.PrefetchScalarGridSpec(num_scalar_prefetch=1,grid=(pairs,),
          in_specs=sp+sp,
          out_specs=[pl.BlockSpec((half,128),lambda p,c:(0,p))]*2+[pl.BlockSpec((1,8,rows),lambda p,c:(p,0,0))],
          scratch_shapes=[pltpu.VMEM((rows+FK,256),BF),pltpu.VMEM((rows,256),BF),pltpu.VMEM((rows,256),BF),pltpu.VMEM((160,rows+FK),BF)]),
        out_shape=[jax.ShapeDtypeStruct((half,outw),BF)]*2+[jax.ShapeDtypeStruct((pairs,8,rows),F32)],
        compiler_params=pltpu.CompilerParams(vmem_limit_bytes=60<<20,dimension_semantics=("arbitrary",)),
        cost_estimate=pl.CostEstimate(flops=4*rows*rows*64*2*pairs//2,bytes_accessed=10*half*width,transcendentals=rows*rows*pairs),
        name="attend_fwd",
    )(ctl,own,own,own,recv,recv,recv)

def bwd_kernel(ctl,qo,ko,vo,qr,kr,vr,do_o,do_r,oo,ox,lse,cos,sin,g0,g1,g2,x0,x1,x2,kaug,q0,q1,vs,d0,d1,kt,delta,dk,dv):
    rows=kaug.shape[0]-FK
    half=rows//2
    pos,e0,e1=ctl[0],ctl[1],ctl[2]
    p=pl.program_id(0)
    @pl.when(p==0)
    def _():
        fill_masks(e0,e1,kaug,q0,q1,rows,kaug.shape[0]-rows)
        kaug[rows:,0:128]=jnp.zeros((FK,128),BF)
        vs[rows:,:]=jnp.zeros((FK,128),BF)
        kt[:,rows:]=jnp.zeros((128,FK),BF)
    lane=lax.broadcasted_iota(jnp.int32,(half,128),1)
    pick_r=lax.broadcasted_iota(jnp.int32,(16,128),0)
    pick_l=lax.broadcasted_iota(jnp.int32,(16,128),1)
    pick=jnp.where(pick_l//64==pick_r,1.0,0.0).astype(BF)
    for own,(q,k,v,d,o) in ((True,(qo,ko,vo,do_o,oo)),(False,(qr,kr,vr,do_r,ox))):
        at=pl.multiple_of((pos if own else 1-pos)*half,half)
        scaled=q[...]*jnp.asarray(0.125,BF)
        zero=jnp.zeros_like(scaled)
        q0[pl.ds(at,half),0:128]=jnp.where(lane<64,scaled,zero)
        q1[pl.ds(at,half),0:128]=jnp.where(lane<64,zero,scaled)
        kb=k[...]
        kaug[pl.ds(at,half),0:128]=kb
        kt[:,pl.ds(at,half)]=kb.T
        vs[pl.ds(at,half),:]=v[...]
        db=d[...]
        d0[pl.ds(at,half),:]=jnp.where(lane<64,db,zero)
        d1[pl.ds(at,half),:]=jnp.where(lane<64,zero,db)
        prod=db.astype(F32)*o[...].astype(F32)
        hi=prod.astype(BF)
        lo=(prod-hi.astype(F32)).astype(BF)
        delta[:,pl.ds(at,half)]=nt(pick,hi)+nt(pick,lo)
    dk[...]=jnp.zeros_like(dk)
    dv[...]=jnp.zeros_like(dv)
    def spread(i,col,val):
        local=i*ROWS-pos*half
        @pl.when((local>=0)&(local<half))
        def _(): (g0,g1,g2)[col][pl.ds(pl.multiple_of(local,ROWS),ROWS),:]=val
        @pl.when((local<0)|(local>=half))
        def _(): (x0,x1,x2)[col][pl.ds(pl.multiple_of(i*ROWS-(1-pos)*half,ROWS),ROWS),:]=val
    def unturn(x,r0):
        ln=lax.broadcasted_iota(jnp.int32,x.shape,1)
        swapped=jnp.where((ln%64)<32,pltpu.roll(x,96,1),pltpu.roll(x,32,1))
        return x*cos[pl.ds(r0,ROWS),:]-swapped*sin[pl.ds(r0,ROWS),:]
    def qblock(i,_):
        r0=pl.multiple_of(i*BQ,BQ)
        qs=(q0[pl.ds(r0,BQ),:],q1[pl.ds(r0,BQ),:])
        ds_=(d0[pl.ds(r0,BQ),:],d1[pl.ds(r0,BQ),:])
        ls=[lse[0,h:h+1,pl.ds(r0,BQ)] for h in range(2)]
        de=[delta[h:h+1,pl.ds(r0,BQ)] for h in range(2)]
        def walk(size):
            base,count=key_range(i,e0,e1,size)
            def step(j,carry):
                k0=pl.multiple_of(base+j*size,128)
                kb=kaug[pl.ds(k0,size),:]
                vb=vs[pl.ds(k0,size),:]
                both=range(2)
                st=[nt(kb,qs[h]) for h in both]
                dpt=[nt(vb,ds_[h]) for h in both]
                pt=[jnp.exp(st[h]-ls[h]) for h in both]
                dst=[(pt[h]*(dpt[h]-de[h])).astype(BF) for h in both]
                pb=[pt[h].astype(BF) for h in both]
                dv[pl.ds(k0,size),:]+=nn(pb[0],ds_[0])+nn(pb[1],ds_[1])
                dk[pl.ds(k0,size),:]+=nn(dst[0],qs[0][:,0:128])+nn(dst[1],qs[1][:,0:128])
                out=[carry[h]+nn(kt[64*h:64*h+64,pl.ds(k0,size)],dst[h]) for h in both]
                return tuple(out)
            init=jnp.zeros((64,BQ),F32)
            return lax.fori_loop(0,count,step,(init,init))
        res=lax.cond(wide_fits(i,e0,e1),lambda: walk(FK),lambda: walk(BK))
        dq=jnp.concatenate(res,axis=0).T*0.125
        for t in range(BQ//ROWS):
            at=pl.multiple_of(r0+t*ROWS,ROWS)
            spread(i*(BQ//ROWS)+t,0,unturn(dq[t*ROWS:(t+1)*ROWS],at).astype(BF))
        return 0
    used=(e1+BQ-1)//BQ
    lax.fori_loop(0,used,qblock,0)
    def blank(i,_):
        spread(i,0,jnp.zeros((ROWS,128),BF))
        return 0
    lax.fori_loop(used*(BQ//ROWS),rows//ROWS,blank,0)
    def last(i,_):
        r0=pl.multiple_of(i*ROWS,ROWS)
        spread(i,1,unturn(dk[pl.ds(r0,ROWS),:],r0).astype(BF))
        spread(i,2,dv[pl.ds(r0,ROWS),:].astype(BF))
        return 0
    lax.fori_loop(0,rows//ROWS,last,0)

def attend_bwd(ctl,own,recv,d_own,d_recv,o_own,o_oth,lse,cos,sin):
    half,width=own.shape
    pairs=width//384
    rows=2*half
    sp=[pl.BlockSpec((half,128),(lambda p,c,s=s:(0,s*pairs+p))) for s in range(3)]
    one=pl.BlockSpec((half,128),lambda p,c:(0,p))
    full=pl.BlockSpec((rows,128),lambda p,c:(0,0))
    return pl.pallas_call(bwd_kernel,
        grid_spec=pltpu.PrefetchScalarGridSpec(num_scalar_prefetch=1,grid=(pairs,),
          in_specs=sp+sp+[one]*4+[pl.BlockSpec((1,8,rows),lambda p,c:(p,0,0)),full,full],
          out_specs=[one]*6,
          scratch_shapes=[pltpu.VMEM((rows+FK,256),BF),pltpu.VMEM((rows,256),BF),pltpu.VMEM((rows,256),BF),
             pltpu.VMEM((rows+FK,128),BF),pltpu.VMEM((rows,128),BF),pltpu.VMEM((rows,128),BF),
             pltpu.VMEM((128,rows+FK),BF),pltpu.VMEM((16,rows),F32),pltpu.VMEM((rows+FK,128),F32),pltpu.VMEM((rows+FK,128),F32)]),
        out_shape=[jax.ShapeDtypeStruct((half,width//3),BF)]*6,
        compiler_params=pltpu.CompilerParams(vmem_limit_bytes=60<<20,dimension_semantics=("arbitrary",)),
        cost_estimate=pl.CostEstimate(flops=10*rows*rows*64*2*pairs//2,bytes_accessed=20*half*width,transcendentals=rows*rows*pairs),
        name="attend_bwd",
    )(ctl,own,own,own,recv,recv,recv,d_own,d_recv,o_own,o_oth,lse,cos,sin)

BLOCK=256

def spread_mean(x):
    return jnp.mean(x,axis=1,keepdims=True)

def row_docs(ctl,block):
    i=pl.program_id(0)
    r=ctl[0]*(block*pl.num_programs(0))+i*block+lax.broadcasted_iota(jnp.int32,(block,1),0)
    return (r>=ctl[1]).astype(jnp.int32)+(r>=ctl[2]).astype(jnp.int32)

def ffn_fwd_kernel(ctl,ao,ax,tok,w_exp,w_con,w_out,norm,u1,u2,rs,yb,h0,h1,h2,h3,pf,pooled):
    block,width=tok.shape
    hidden=pf.shape[1]//2
    kept=(h0,h1,h2,h3)
    share=width//2
    pos=ctl[0]
    mine=pl.multiple_of(pos*share,share)
    other=pl.multiple_of((1-pos)*share,share)
    f=tok[...].astype(F32)+nn(ao[...],w_out[pl.ds(mine,share),:])+nn(ax[...],w_out[pl.ds(other,share),:])
    cent=f-spread_mean(f)
    scale=lax.rsqrt(spread_mean(cent*cent)+NORM_EPSILON)
    unit=cent*scale
    u1[...]=unit
    rs[:,0:128]=jnp.broadcast_to(scale,(block,128))
    y=unit*norm[0:1,:]+norm[1:2,:]
    ylow=y.astype(BF)
    yb[...]=ylow
    acc=y
    count=hidden//width
    spans=[(slice(c*width,(c+1)*width),slice(hidden+c*width,hidden+(c+1)*width)) for c in range(count)]
    pre=lambda c: (nn(ylow,w_exp[:,spans[c][0]]),nn(ylow,w_exp[:,spans[c][1]]))
    ahead=pre(0)
    for c in range(count):
        gate,up=ahead
        if c+1<count: ahead=pre(c+1)
        gc,uc=spans[c]
        sig=jax.nn.sigmoid(gate)
        act=gate*sig
        low=(act*up).astype(BF)
        kept[c][...]=low
        pf[:,gc]=(up*(sig+act*(1.0-sig))).astype(BF)
        pf[:,uc]=act.astype(BF)
        acc=acc+nn(low,w_con[:,gc])
    cent=acc-spread_mean(acc)
    scale=lax.rsqrt(spread_mean(cent*cent)+NORM_EPSILON)
    unit=cent*scale
    u2[...]=unit
    rs[:,128:256]=jnp.broadcast_to(scale,(block,128))
    out=unit*norm[2:3,:]+norm[3:4,:]
    docs=row_docs(ctl,block)
    @pl.when(pl.program_id(0)==0)
    def _(): pooled[...]=jnp.zeros_like(pooled)
    for d in range(2):
        pooled[d:d+1,:]+=jnp.sum(jnp.where(docs==d,out,0.0),axis=0,keepdims=True)

def ffn_fwd(ctl,ao,ax,tok,bundle,norm,hidden):
    rows,width=tok.shape
    row=lambda n: pl.BlockSpec((BLOCK,n),lambda i,c:(i,0))
    held=lambda n,at: pl.BlockSpec((width,n),lambda i,c:(0,at//n),pipeline_mode=pl.Buffered(1))
    flat=pl.BlockSpec((8,width),lambda i,c:(0,0))
    return pl.pallas_call(ffn_fwd_kernel,
        grid_spec=pltpu.PrefetchScalarGridSpec(num_scalar_prefetch=1,grid=(rows//BLOCK,),
          in_specs=[row(width//2),row(width//2),row(width),held(2*hidden,0),held(hidden,2*hidden),held(width,3*hidden),flat],
          out_specs=[row(width),row(width),row(256),*[row(width)]*5,row(2*hidden),flat]),
        out_shape=[jax.ShapeDtypeStruct((rows,width),F32),jax.ShapeDtypeStruct((rows,width),F32),jax.ShapeDtypeStruct((rows,256),F32),
          *[jax.ShapeDtypeStruct((rows,width),BF)]*5,jax.ShapeDtypeStruct((rows,2*hidden),BF),
          jax.ShapeDtypeStruct((8,width),F32)],
        compiler_params=pltpu.CompilerParams(vmem_limit_bytes=60<<20,dimension_semantics=("arbitrary",)),
        cost_estimate=pl.CostEstimate(flops=2*rows*width*(width+3*hidden),bytes_accessed=rows*(width*14+hidden*6)+2*width*(width+3*hidden),transcendentals=rows*hidden),
        name="ffn_fwd",
    )(ctl,ao,ax,tok,bundle,bundle,bundle,norm)

def loss_grad(pool,targets,len0,len1):
    width=pool.shape[1]
    docs=lax.broadcasted_iota(jnp.int32,pool.shape,0)
    length=jnp.where(docs==0,len0,len1)
    emb=pool/length
    lane=lax.broadcasted_iota(jnp.int32,pool.shape,1)
    d_target=jnp.zeros_like(pool)
    d_self=jnp.zeros_like(pool)
    for cut in (width//12,width//6,width//3,2*width//3,width):
        keep=lane<cut
        total=lambda v: jnp.sum(jnp.where(keep,v,0.0),axis=1,keepdims=True)
        own_root=lax.rsqrt(total(emb*emb)+COSINE_EPSILON)
        other_root=lax.rsqrt(total(targets*targets)+COSINE_EPSILON)
        cosine=total(emb*targets)*own_root*other_root
        d_target=d_target+jnp.where(keep,own_root*other_root,0.0)
        d_self=d_self+jnp.where(keep,cosine*own_root*own_root,0.0)
    d_emb=length*(d_self*emb-d_target*targets)
    return emb,d_emb/length

def ffn_bwd_kernel(ctl,flen,pool_a,pool_b,targets,u1,u2,rs,pf,w_exp,w_con,w_out,norm,
                   emb,mb,ub,df,ab,do,dx,gn,de):
    block,width=u1.shape
    hidden=pf.shape[1]//2
    share=width//2
    pos=ctl[0]
    @pl.when(pl.program_id(0)==0)
    def _():
        e,d=loss_grad(pool_a[...]+pool_b[...],targets[...],flen[0],flen[1])
        emb[...]=e
        de[...]=d
        gn[...]=jnp.zeros_like(gn)
    docs=row_docs(ctl,block)
    dout=jnp.where(docs==0,de[0:1,:],jnp.where(docs==1,de[1:2,:],0.0))
    unit=u2[...]
    gn[2:3,:]+=jnp.sum(dout*unit,axis=0,keepdims=True)
    gn[3:4,:]+=jnp.sum(dout,axis=0,keepdims=True)
    gu=dout*norm[2:3,:]
    dg=rs[:,128:129]*(gu-spread_mean(gu)-unit*spread_mean(gu*unit))
    mlow=dg.astype(BF)
    mb[...]=mlow
    acc=dg
    for c in range(hidden//width):
        gc=slice(c*width,(c+1)*width)
        uc=slice(hidden+c*width,hidden+(c+1)*width)
        dh=nt(mlow,w_con[:,gc])
        dgate=(dh*pf[:,gc].astype(F32)).astype(BF)
        dup=(dh*pf[:,uc].astype(F32)).astype(BF)
        ub[:,gc]=dgate
        ub[:,uc]=dup
        acc=acc+nt(dgate,w_exp[:,gc])+nt(dup,w_exp[:,uc])
    unit=u1[...]
    gn[0:1,:]+=jnp.sum(acc*unit,axis=0,keepdims=True)
    gn[1:2,:]+=jnp.sum(acc,axis=0,keepdims=True)
    gu=acc*norm[0:1,:]
    dfirst=rs[:,0:1]*(gu-spread_mean(gu)-unit*spread_mean(gu*unit))
    df[...]=dfirst
    alow=dfirst.astype(BF)
    ab[...]=alow
    do[...]=nt(alow,w_out[pl.ds(pl.multiple_of(pos*share,share),share),:]).astype(BF)
    dx[...]=nt(alow,w_out[pl.ds(pl.multiple_of((1-pos)*share,share),share),:]).astype(BF)

def ffn_bwd(ctl,flen,pool_a,pool_b,targets,u1,u2,rs,pf,bundle,norm):
    rows,width=u1.shape
    hidden=pf.shape[1]//2
    row=lambda n: pl.BlockSpec((BLOCK,n),lambda i,c,l:(i,0))
    held=lambda n,at: pl.BlockSpec((width,n),lambda i,c,l:(0,at//n),pipeline_mode=pl.Buffered(1))
    flat=pl.BlockSpec((8,width),lambda i,c,l:(0,0))
    sds=jax.ShapeDtypeStruct
    return pl.pallas_call(ffn_bwd_kernel,
        grid_spec=pltpu.PrefetchScalarGridSpec(num_scalar_prefetch=2,grid=(rows//BLOCK,),
          in_specs=[flat,flat,flat,row(width),row(width),row(256),row(2*hidden),held(2*hidden,0),held(hidden,2*hidden),held(width,3*hidden),flat],
          out_specs=[flat,row(width),row(2*hidden),row(width),row(width),row(width//2),row(width//2),flat],
          scratch_shapes=[pltpu.VMEM((8,width),F32)]),
        out_shape=[sds((8,width),F32),sds((rows,width),BF),sds((rows,2*hidden),BF),sds((rows,width),F32),sds((rows,width),BF),
          sds((rows,width//2),BF),sds((rows,width//2),BF),sds((8,width),F32)],
        compiler_params=pltpu.CompilerParams(vmem_limit_bytes=60<<20,dimension_semantics=("arbitrary",)),
        cost_estimate=pl.CostEstimate(flops=2*rows*width*(width+3*hidden),bytes_accessed=rows*(width*18+hidden*8)+2*width*(width+3*hidden),transcendentals=0),
        name="ffn_bwd",
    )(ctl,flen,pool_a,pool_b,targets,u1,u2,rs,pf,bundle,bundle,bundle,norm)

MESH=pl.DeviceIdType.MESH

def place():
    dp=lax.axis_index("dp")
    core=lax.axis_index("dim")
    return dp//4,(dp//2)%2,dp%2,core

def meet(z,y,x,core):
    chip=lambda a,b,c: a*4+b*2+c
    peers=[(chip(z,y,x),1-core),(chip(z,y,1-x),core),(chip(z,1-y,x),core)]
    peers+=[(chip(lax.rem(z+k,4),y,x),core) for k in (1,2,3)]
    barrier=pltpu.get_barrier_semaphore()
    for peer in peers:
        pl.semaphore_signal(barrier,inc=1,device_id=peer,device_id_type=MESH)
    pl.semaphore_wait(barrier,len(peers))
    return peers

def lanes_of(cols):
    tiles=cols//128
    widths=[tiles-tiles//4*3]+[tiles//4]*3
    widths=[widths[0],widths[2],widths[1],widths[3]]
    widths=[5,5,4,4] if tiles==18 else widths
    out=[]
    at=0
    for n,w in enumerate(widths):
        out.append((at*128,w*128,n%2==0))
        at+=w
    return out

def send(src,dst,sems,n,k,peer):
    copy=pltpu.make_async_remote_copy(src_ref=src,dst_ref=dst,send_sem=sems[0].at[n,k],recv_sem=sems[1].at[n,k],device_id=peer,device_id_type=MESH)
    copy.start()
    return copy

def gather_kernel(w,out,low,local,s_sem,r_sem):
    z,y,x,core=place()
    low[...]=w[...].astype(BF)
    keep=pltpu.make_async_copy(low,out.at[z,y,x,core],local)
    keep.start()
    pair,xn,yn,z1,z2,z3=meet(z,y,x,core)
    sems=(s_sem,r_sem)
    lanes=lanes_of(w.shape[1])
    every=[]
    def go(n,k,peer,*index,src=None):
        at,width,_=lanes[n]
        dst=out.at[(*index,slice(None),pl.ds(at,width))]
        if src is None: src=dst
        copy=send(src,dst,sems,n,k,peer)
        every.append(copy)
        return copy
    whole=slice(None)
    first=[]
    for n,(at,width,_) in enumerate(lanes):
        piece=low.at[:,pl.ds(at,width)]
        first.append([go(n,k,peer,z,y,x,core,src=piece) for k,peer in enumerate((z1,z2,z3))])
    keep.wait()
    second=[]
    for n,(_,_,flip) in enumerate(lanes):
        for copy in first[n]: copy.wait_recv()
        second.append(go(n,3,yn if flip else xn,whole,y,x,core))
        go(n,5,pair,whole,y,x,core)
    third=[]
    for n,(_,_,flip) in enumerate(lanes):
        second[n].wait_recv()
        if flip:
            third.append(go(n,4,xn,whole,whole,x,core))
            go(n,6,pair,whole,1-y,x,core)
        else:
            third.append(go(n,4,yn,whole,y,whole,core))
            go(n,6,pair,whole,y,1-x,core)
    for n,(_,_,flip) in enumerate(lanes):
        third[n].wait_recv()
        if flip: go(n,7,pair,whole,whole,1-x,core)
        else: go(n,7,pair,whole,1-y,whole,core)
    done=set(id(c) for c in second+third+[c for f in first for c in f])
    for copy in every:
        copy.wait_send()
        if id(copy) not in done: copy.wait_recv()

def ring_gather(w):
    share,cols=w.shape
    out=pl.pallas_call(gather_kernel,
        in_specs=[pl.BlockSpec(memory_space=pltpu.VMEM)],
        out_specs=pl.BlockSpec(memory_space=pl.ANY),
        scratch_shapes=[pltpu.VMEM((share,cols),BF),pltpu.SemaphoreType.DMA,pltpu.SemaphoreType.DMA((4,8)),pltpu.SemaphoreType.DMA((4,8))],
        out_shape=jax.ShapeDtypeStruct((4,2,2,2,share,cols),BF),
        compiler_params=pltpu.CompilerParams(collective_id=1,has_side_effects=True,vmem_limit_bytes=60<<20),
        cost_estimate=pl.CostEstimate(flops=0,bytes_accessed=64*share*cols*20,transcendentals=0),
        name="comm_gather",
    )(w)
    return out.reshape(32*share,cols)

def scatter_kernel(g,out,gl,r0,b1,k1,r1,b2,k2,r2,b3,k3,r3,local,s_sem,r_sem):
    z,y,x,core=place()
    keep=pltpu.make_async_copy(g.at[:,core],gl,local)
    keep.start()
    pair,xn,yn,z1,z2,z3=meet(z,y,x,core)
    sems=(s_sem,r_sem)
    lanes=lanes_of(out.shape[1])
    span=[pl.ds(at,width) for at,width,_ in lanes]
    every=[]
    def go(n,k,peer,src,dst):
        copy=send(src,dst,sems,n,k,peer)
        every.append(copy)
        return copy
    n_lanes=range(len(lanes))
    zero=[go(n,0,pair,g.at[:,1-core,:,span[n]],r0.at[:,:,span[n]]) for n in n_lanes]
    def split1(n,iz,j,side):
        row=iz*4+(j*2+side if lanes[n][2] else side*2+j)
        c=span[n]
        return gl[row,:,c].astype(F32)+r0[row,:,c].astype(F32)
    one=[]
    keep.wait()
    for n in n_lanes:
        flip=lanes[n][2]
        side=x if flip else y
        zero[n].wait_recv()
        for iz in range(4):
            for j in range(2):
                b1[iz,j,:,span[n]]=split1(n,iz,j,1-side).astype(BF)
        one.append(go(n,1,xn if flip else yn,b1.at[:,:,:,span[n]],r1.at[:,:,:,span[n]]))
        for iz in range(4):
            for j in range(2):
                k1[iz,j,:,span[n]]=split1(n,iz,j,side)
    two=[]
    for n in n_lanes:
        flip=lanes[n][2]
        side=y if flip else x
        c=span[n]
        one[n].wait_recv()
        for iz in range(4):
            b2[iz,:,c]=(k1[iz,1-side,:,c]+r1[iz,1-side,:,c].astype(F32)).astype(BF)
        two.append(go(n,2,yn if flip else xn,b2.at[:,:,c],r2.at[:,:,c]))
        for iz in range(4):
            k2[iz,:,c]=k1[iz,side,:,c]+r1[iz,side,:,c].astype(F32)
    three=[]
    for n in n_lanes:
        c=span[n]
        two[n].wait_recv()
        for k in (1,2,3):
            to=lax.rem(z+k,4)
            b3[k-1,:,c]=(k2[to,:,c]+r2[to,:,c].astype(F32)).astype(BF)
        three.append([go(n,2+k,(z1,z2,z3)[k-1],b3.at[k-1,:,c],r3.at[k-1,:,c]) for k in (1,2,3)])
        k3[:,c]=k2[z,:,c]+r2[z,:,c].astype(F32)
    for n in n_lanes:
        c=span[n]
        for copy in three[n]: copy.wait_recv()
        out[:,c]=k3[:,c]+r3[0,:,c].astype(F32)+r3[1,:,c].astype(F32)+r3[2,:,c].astype(F32)
    for copy in every: copy.wait_send()

def ring_scatter(g):
    rows,cols=g.shape
    share=rows//32
    v=lambda *s: pltpu.VMEM((*s,share,cols),BF)
    f=lambda *s: pltpu.VMEM((*s,share,cols),F32)
    return pl.pallas_call(scatter_kernel,
        in_specs=[pl.BlockSpec(memory_space=pl.ANY)],
        out_specs=pl.BlockSpec(memory_space=pltpu.VMEM),
        scratch_shapes=[v(16),v(16),v(4,2),f(4,2),v(4,2),v(4),f(4),v(4),v(3),f(),v(3),pltpu.SemaphoreType.DMA,pltpu.SemaphoreType.DMA((4,6)),pltpu.SemaphoreType.DMA((4,6))],
        out_shape=jax.ShapeDtypeStruct((share,cols),F32),
        compiler_params=pltpu.CompilerParams(collective_id=2,has_side_effects=True,vmem_limit_bytes=60<<20),
        cost_estimate=pl.CostEstimate(flops=0,bytes_accessed=64*share*cols*20,transcendentals=0),
        name="comm_scatter",
    )(g.reshape(16,2,share,cols))

def selector(forward):
    r=lax.broadcasted_iota(jnp.int32,(512,512),0)
    c=lax.broadcasted_iota(jnp.int32,(512,512),1)
    a,b=(r,c) if forward else (c,r)
    return jnp.where(a==4*(b%128)+b//128,1.0,0.0).astype(BF)

def bundle_kernel(exp,con,out,norm,bundle,tiles):
    share,width=out.shape
    hidden=exp.shape[1]//2
    pick=selector(True)
    for b in range(exp.shape[1]//512):
        half,at=divmod(b*512,hidden)
        y=nn(exp[:,b*512:(b+1)*512].astype(BF),pick).astype(BF)
        for j in range(4):
            to=half*hidden+j*width+at//4
            bundle[:,to:to+128]=y[:,j*128:(j+1)*128]
    for t in range(width//128):
        tiles[t]=con[:,t*128:(t+1)*128]
        for j in range(4):
            to=2*hidden+j*width+t*128
            bundle[:,to:to+128]=tiles[t,pl.ds(j,share,stride=4),:].astype(BF)
    bundle[:,3*hidden:3*hidden+width]=out[...].astype(BF)
    flat=jnp.concatenate([norm[...],jnp.zeros((4,128-share),F32)],1)
    bundle[:,3*hidden+width:]=jnp.concatenate([flat,jnp.zeros((share-4,128),F32)],0).astype(BF)

def make_bundle(exp,con,out,norm):
    share,width=out.shape
    total=exp.shape[1]+4*width+width+128
    return pl.pallas_call(bundle_kernel,
        out_shape=jax.ShapeDtypeStruct((share,total),BF),
        scratch_shapes=[pltpu.VMEM((width//128,4*share,128),F32)],
        compiler_params=pltpu.CompilerParams(vmem_limit_bytes=60<<20),
        cost_estimate=pl.CostEstimate(flops=2*share*512*exp.shape[1],bytes_accessed=6*share*total,transcendentals=0),
        name="make_bundle",
    )(exp,con,out,norm)

def update_kernel(rates,sums,*refs):
    ins,outs,tiles=refs[:12],refs[12:32],refs[32]
    exp_w,con_w,out_w,norm_w=(ins[3*k:3*k+3] for k in range(4))
    share,width=out_w[0].shape
    hidden=exp_w[0].shape[1]//2
    def step(kind,index,g,rate):
        w,m,a=(ref[index] for ref in ins[3*kind:3*kind+3])
        grad,nxt,mom,avg,low=outs[5*kind:5*kind+5]
        mn=MOMENTUM*m+g
        wn=w-rate*(g+MOMENTUM*mn)
        grad[index]=g
        nxt[index]=wn
        mom[index]=mn
        avg[index]=AVERAGE_DECAY*a+(1.0-AVERAGE_DECAY)*wn
        low[index]=wn.astype(BF)
    pick=selector(False)
    for b in range(2*hidden//512):
        half,at=divmod(b*512,hidden)
        z=jnp.concatenate([sums[:,half*hidden+j*width+at//4:half*hidden+j*width+at//4+128] for j in range(4)],1)
        step(0,(slice(None),slice(b*512,(b+1)*512)),nn(z,pick),rates[0])
    for t in range(width//128):
        for j in range(4):
            at=2*hidden+j*width+t*128
            tiles[t,pl.ds(j,share,stride=4),:]=sums[:,at:at+128].astype(F32)
        step(1,(slice(None),slice(t*128,(t+1)*128)),tiles[t],rates[0])
    step(2,(slice(None),slice(None)),sums[:,3*hidden:3*hidden+width].astype(F32),rates[0])
    step(3,(slice(None),slice(None)),sums[0:8,3*hidden+width:].astype(F32)[0:4,0:share],rates[1])

def update(sums,rates,params):
    sds=jax.ShapeDtypeStruct
    shapes=[]
    for w,_,_ in params:
        shapes+=[sds(w.shape,F32)]*4+[sds(w.shape,BF)]
    flat=[x for p in params for x in p]
    import_vmem=pl.BlockSpec(memory_space=pltpu.VMEM)
    outs=pl.pallas_call(lambda *refs: update_kernel(rates,*refs),
        in_specs=[import_vmem]*13,
        out_specs=[import_vmem]*20,
        out_shape=shapes,
        scratch_shapes=[pltpu.VMEM((params[2][0].shape[1]//128,params[1][0].shape[0],128),F32)],
        compiler_params=pltpu.CompilerParams(vmem_limit_bytes=60<<20),
        cost_estimate=pl.CostEstimate(flops=2*24*512*6144,bytes_accessed=12<<20,transcendentals=0),
        name="update",
    )(sums,*flat)
    return [outs[5*k:5*k+5] for k in range(4)]

def tail_kernel(ctl,x,qo,ko,vo,qr,kr,vr,w,df,tok,gm,acc):
    pos=ctl[0]
    i=pl.program_id(0)
    width=x.shape[1]
    turned=x[...].T
    total=df[...]
    @pl.when(i==0)
    def _(): acc[...]=jnp.zeros_like(acc)
    for s,(mine,theirs) in enumerate(((qo,qr),(ko,kr),(vo,vr))):
        a=mine[...]
        b=theirs[...]
        grad=jnp.concatenate([jnp.where(pos==0,a,b),jnp.where(pos==0,b,a)],1)
        cols=slice(s*width,(s+1)*width)
        total=total+nt(grad,w[:,cols])
        acc[:,cols]+=nn(turned,grad)
    tok[...]=total
    @pl.when(i==pl.num_programs(0)-1)
    def _(): gm[...]=acc[...].astype(BF)

def tail(ctl,x,own,recv,w,df):
    rows,width=x.shape
    cols=w.shape[1]
    row=lambda n: pl.BlockSpec((512,n),lambda i,c:(i,0))
    held=pl.BlockSpec((width,cols),lambda i,c:(0,0),pipeline_mode=pl.Buffered(1))
    return pl.pallas_call(tail_kernel,
        grid_spec=pltpu.PrefetchScalarGridSpec(num_scalar_prefetch=1,grid=(rows//512,),
          in_specs=[row(width)]+[row(width//2)]*6+[held,row(width)],
          out_specs=[row(width),pl.BlockSpec((width,cols),lambda i,c:(0,0))],
          scratch_shapes=[pltpu.VMEM((width,cols),F32)]),
        out_shape=[jax.ShapeDtypeStruct((rows,width),F32),jax.ShapeDtypeStruct((width,cols),BF)],
        compiler_params=pltpu.CompilerParams(vmem_limit_bytes=60<<20,dimension_semantics=("arbitrary",)),
        cost_estimate=pl.CostEstimate(flops=4*rows*width*cols,bytes_accessed=rows*width*16+8*width*cols,transcendentals=0),
        name="tail",
    )(ctl,x,*own,*recv,w,df)

def spread_kernel(c,s,cos,sin):
    lane=lax.broadcasted_iota(jnp.int32,c.shape,1)
    count=c.shape[0]
    for src,dst in ((c,cos),(s,sin)):
        table=src[...]
        for t in range(4):
            z=table if t==0 else pltpu.roll(table,128-32*t,1)
            z=jnp.where(lane<32,z,pltpu.roll(z,32,1))
            z=jnp.where(lane<64,z,pltpu.roll(z,64,1))
            if dst is sin: z=jnp.where((lane%64)<32,-z,z)
            dst[pl.ds(t,count,stride=4),:]=z

def spread_angles(c,s):
    return pl.pallas_call(spread_kernel,
        out_shape=[jax.ShapeDtypeStruct((4*c.shape[0],128),F32)]*2,
        compiler_params=pltpu.CompilerParams(vmem_limit_bytes=60<<20),
        cost_estimate=pl.CostEstimate(flops=40*c.size,bytes_accessed=40*c.size,transcendentals=0),
        name="spread_angles",
    )(c,s)

def mix_kernel(ctl,x,w,cos,sin,own,oth):
    pos=ctl[0]
    width=x.shape[1]
    share=width//2
    xb=x[...]
    c=cos[...]
    s=sin[...]
    lane=lax.broadcasted_iota(jnp.int32,c.shape,1)
    first=(lane%64)<32
    for part in range(3):
        y=nn(xb,w[:,part*width:(part+1)*width])
        tiles=[]
        for t in range(width//128):
            z=y[:,t*128:(t+1)*128]
            if part<2:
                swapped=jnp.where(first,pltpu.roll(z,96,1),pltpu.roll(z,32,1))
                z=z*c+swapped*s
            tiles.append(z.astype(BF))
        count=share//128
        for t in range(count):
            cols=slice(part*share+t*128,part*share+(t+1)*128)
            own[:,cols]=jnp.where(pos==0,tiles[t],tiles[count+t])
            oth[:,cols]=jnp.where(pos==0,tiles[count+t],tiles[t])

def mix(ctl,x,w,cos,sin):
    rows,width=x.shape
    cols=w.shape[1]
    block=256
    row=lambda n: pl.BlockSpec((block,n),lambda i,c:(i,0))
    angle=pl.BlockSpec((block,128),lambda i,c:(c[0]*(rows//block)+i,0))
    return pl.pallas_call(mix_kernel,
        grid_spec=pltpu.PrefetchScalarGridSpec(num_scalar_prefetch=1,grid=(rows//block,),
          in_specs=[row(width),pl.BlockSpec((width,cols),lambda i,c:(0,0)),angle,angle],
          out_specs=[row(cols//2)]*2),
        out_shape=[jax.ShapeDtypeStruct((rows,cols//2),BF)]*2,
        compiler_params=pltpu.CompilerParams(vmem_limit_bytes=60<<20,dimension_semantics=("arbitrary",)),
        cost_estimate=pl.CostEstimate(flops=2*rows*width*cols,bytes_accessed=2*(rows*width+width*cols+rows*cols),transcendentals=0),
        name="mix",
    )(ctl,x,w,cos,sin)

def swap_cores(x):
    return lax.ppermute(x,"dim",[(0,1),(1,0)])

def join(pos,own,recv,axis=1):
    return jnp.where(pos==0,jnp.concatenate([own,recv],axis),jnp.concatenate([recv,own],axis))

def body(tokens,doc_lengths,pair_index,target_bank,mixer_in,mixer_out,expand,contract,norm_params,*rest):
    slices=lax.axis_size("dim")
    if slices!=2 or lax.axis_size("dp")!=16 or doc_lengths.shape[1]!=2:
        return body_general(tokens,doc_lengths,pair_index,target_bank,mixer_in,mixer_out,expand,contract,norm_params,*rest)
    (mixer_in_moment,mixer_out_moment,expand_moment,contract_moment,norm_moment,
     mixer_in_average,mixer_out_average,expand_average,contract_average,norm_average)=rest
    local_rows,model_width=tokens.shape
    group_rows=local_rows*slices
    pos=lax.axis_index("dim")
    doc_count=2
    w_mix=ring_gather(mixer_in[0])
    share_rows=mixer_out.shape[1]
    per=contract.shape[1]//share_rows
    count=model_width//share_rows
    hidden_width=contract.shape[1]*count
    bundle=make_bundle(expand[0],contract[0],mixer_out[0],norm_params[0])
    bundle=lax.all_gather(bundle,("dp","dim"),axis=0,tiled=True)
    at1=2*hidden_width
    at2=at1+per*model_width
    at3=at2+model_width
    w_norm=bundle[:,at3:].reshape(count,share_rows,128)[:,0:4,0:share_rows].transpose(1,0,2).reshape(4,model_width)
    lengths=doc_lengths[0]
    e0=lengths[0]
    e1=lengths[0]+lengths[1]
    ctl=jnp.stack([pos.astype(jnp.int32),e0,e1])
    lane=jnp.arange(128,dtype=jnp.int32)
    ids=4*jnp.arange(group_rows//4,dtype=jnp.int32)[:,None]+(lane//32)[None,:]
    begin=jnp.where(ids>=e1,e1,jnp.where(ids>=e0,e0,0))
    frequency=jnp.power(1000.0,-(2*(lane%32)).astype(F32)/HEAD)
    angles=(ids-begin).astype(F32)*frequency[None,:]
    cos,sin=spread_angles(jnp.cos(angles),jnp.sin(angles))
    own,oth=mix(ctl,tokens,w_mix,cos,sin)
    recv=swap_cores(oth)
    pick=(pair_index[:,None]==jnp.arange(target_bank.shape[0],dtype=jnp.int32)[None,:]).astype(BF)
    some=matmul(pick,target_bank)
    targets=jnp.pad(join(pos,some,swap_cores(some)),((0,6),(0,0)))
    o_own,o_oth,lse=attend_fwd(ctl,own,recv)
    o_recv=swap_cores(o_oth)
    norm_gains=jnp.pad(w_norm.astype(F32),((0,4),(0,0)))
    u1,u2,rs,y_low,*hidden,factors,pooled=ffn_fwd(ctl,o_own,o_recv,tokens,bundle,norm_gains,hidden_width)
    embeds,grad_m_low,grad_both,grad_first,grad_a_low,d_own,d_oth,grad_norm=ffn_bwd(
        ctl,lengths.astype(F32),pooled,swap_cores(pooled),targets,u1,u2,rs,factors,bundle,norm_gains)
    share=model_width//2
    embeddings=lax.dynamic_slice(embeds,(0,pos*share),(doc_count,share))
    d_recv=swap_cores(d_oth)
    grad_exp=inner_rows(y_low,grad_both)
    grad_con=[inner_rows(h,grad_m_low).astype(BF) for h in hidden]
    grad_out=join(pos,inner_rows(o_own,grad_a_low),inner_rows(o_recv,grad_a_low),0)
    grad_norm=grad_norm[0:4].reshape(4,count,share_rows).transpose(1,0,2)
    grad_norm=jnp.pad(grad_norm,((0,0),(0,share_rows-4),(0,128-share_rows))).reshape(model_width,128)
    terms=jnp.concatenate([grad_exp.astype(BF),*grad_con,grad_out.astype(BF),grad_norm.astype(BF)],1)
    terms,d_own,d_recv=lax.optimization_barrier((terms,d_own,d_recv))
    sums=lax.psum_scatter(terms,("dp","dim"),scatter_dimension=0,tiled=True)
    backs=attend_bwd(ctl,own,recv,d_own,d_recv,o_own,o_oth,lse,cos,sin)
    token_grads,grad_mix=tail(ctl,tokens,backs[0:3],[swap_cores(g) for g in backs[3:6]],w_mix,grad_first)
    total_rows=group_rows*lax.axis_size("dp")
    matrix_rate=1.0/math.sqrt(total_rows)
    norm_rate=0.3/math.sqrt(total_rows)
    new_exp,new_con,new_out,new_norm=update(sums,(matrix_rate,norm_rate),[
        (expand[0],expand_moment[0],expand_average[0]),(contract[0],contract_moment[0],contract_average[0]),
        (mixer_out[0],mixer_out_moment[0],mixer_out_average[0]),(norm_params[0],norm_moment[0],norm_average[0])])
    sum_mix=ring_scatter(grad_mix)
    nxt,mom,avg,low=advance(mixer_in[0],mixer_in_moment[0],mixer_in_average[0],sum_mix,matrix_rate)
    results=[[sum_mix,nxt,mom,avg,low],new_out,new_exp,new_con,new_norm]
    return (embeddings,token_grads,*[results[k][f][None] for f in range(5) for k in range(5)])

def solution(mesh):
    placed = (
        P(("dp", "dim"), None),
        P("dp", None),
        P("dp"),
        P(None, "dim"),
        P(None, ("dp", "dim"), None),
        P(None, ("dp", "dim"), None),
        P(None, ("dp", "dim"), None),
        P(None, ("dp", "dim"), None),
        P(None, None, ("dp", "dim")),
        P(None, ("dp", "dim"), None),
        P(None, ("dp", "dim"), None),
        P(None, ("dp", "dim"), None),
        P(None, ("dp", "dim"), None),
        P(None, None, ("dp", "dim")),
        P(None, ("dp", "dim"), None),
        P(None, ("dp", "dim"), None),
        P(None, ("dp", "dim"), None),
        P(None, ("dp", "dim"), None),
        P(None, None, ("dp", "dim")),
    )
    return jax.shard_map(
        body,
        mesh=mesh,
        in_specs=placed,
        out_specs=(
            P("dp", "dim"),
            P(("dp", "dim"), None),
            P(None, ("dp", "dim"), None),
            P(None, ("dp", "dim"), None),
            P(None, ("dp", "dim"), None),
            P(None, ("dp", "dim"), None),
            P(None, None, ("dp", "dim")),
            P(None, ("dp", "dim"), None),
            P(None, ("dp", "dim"), None),
            P(None, ("dp", "dim"), None),
            P(None, ("dp", "dim"), None),
            P(None, None, ("dp", "dim")),
            P(None, ("dp", "dim"), None),
            P(None, ("dp", "dim"), None),
            P(None, ("dp", "dim"), None),
            P(None, ("dp", "dim"), None),
            P(None, None, ("dp", "dim")),
            P(None, ("dp", "dim"), None),
            P(None, ("dp", "dim"), None),
            P(None, ("dp", "dim"), None),
            P(None, ("dp", "dim"), None),
            P(None, None, ("dp", "dim")),
            P(None, ("dp", "dim"), None),
            P(None, ("dp", "dim"), None),
            P(None, ("dp", "dim"), None),
            P(None, ("dp", "dim"), None),
            P(None, None, ("dp", "dim")),
        ),
        check_vma=False,
    )
```
